32 devices in a mesh: dp: 4 (over x, core), tensor: 8 (over z, y).
Axes of the slice: x: 2, y: 2, z: 4, core: 2. Of those that a mesh axis runs over, the one named last changes fastest.
Arguments:
- tokens: bfloat16 [8192, 2048], P(('dp', 'tensor')), may hold values from -6 to 6
- attn_gain: bfloat16 [2048], replicated, may hold values from 0.099609375 to 1.8984375
- w_query: bfloat16 [2048, 2048], P(None, 'tensor'), may hold values from -0.125 to 0.125
- w_key: bfloat16 [2048, 2048], P(None, 'tensor'), may hold values from -0.125 to 0.125
- w_value: bfloat16 [2048, 2048], P(None, 'tensor'), may hold values from -0.125 to 0.125
- conv_query: bfloat16 [4, 2048], P(None, 'tensor'), may hold values from -3 to 3
- conv_key: bfloat16 [4, 2048], P(None, 'tensor'), may hold values from -3 to 3
- conv_value: bfloat16 [4, 2048], P(None, 'tensor'), may hold values from -3 to 3
- w_beta: bfloat16 [2048, 16], P(None, 'tensor'), may hold values from -0.125 to 0.125
- w_gate_out: bfloat16 [2048, 2048], P(None, 'tensor'), may hold values from -0.125 to 0.125
- head_gain: bfloat16 [128], replicated, may hold values from 0.099609375 to 1.8984375
- w_out: bfloat16 [2048, 2048], P('tensor'), may hold values from -0.25 to 0.25
- ffn_gain: bfloat16 [2048], replicated, may hold values from 0.099609375 to 1.8984375
- w_gate: bfloat16 [2048, 5632], P(None, 'tensor'), may hold values from -0.125 to 0.125
- w_up: bfloat16 [2048, 5632], P(None, 'tensor'), may hold values from -0.125 to 0.125
- w_down: bfloat16 [5632, 2048], P('tensor'), may hold values from -0.15625 to 0.15625
- seq_starts: int32 [4, 2], P('dp'), may hold values from 0 to 1536, as said below
- seq_lengths: int32 [4, 2], P('dp'), may hold values from 512 to 1024, as said below
- cotangent: bfloat16 [8192, 2048], P(('dp', 'tensor')), may hold values from -6 to 6
Outputs:
- output: bfloat16 [8192, 2048], P(('dp', 'tensor'))
- grad_tokens: float32 [8192, 2048], P(('dp', 'tensor'))
- grad_attn_gain: float32 [2048], replicated
- grad_w_query: float32 [2048, 2048], P(None, 'tensor')
- grad_w_key: float32 [2048, 2048], P(None, 'tensor')
- grad_w_value: float32 [2048, 2048], P(None, 'tensor')
- grad_conv_query: float32 [4, 2048], P(None, 'tensor')
- grad_conv_key: float32 [4, 2048], P(None, 'tensor')
- grad_conv_value: float32 [4, 2048], P(None, 'tensor')
- grad_w_beta: float32 [2048, 16], P(None, 'tensor')
- grad_w_gate_out: float32 [2048, 2048], P(None, 'tensor')
- grad_head_gain: float32 [128], replicated
- grad_w_out: float32 [2048, 2048], P('tensor')
- grad_ffn_gain: float32 [2048], replicated
- grad_w_gate: float32 [2048, 5632], P(None, 'tensor')
- grad_w_up: float32 [2048, 5632], P(None, 'tensor')
- grad_w_down: float32 [5632, 2048], P('tensor')
The draws below stay inside these ranges and needn't reach their ends.
Inputs may be any that keep to these rules, and one draw needn't show every extreme that they name: `seq_lengths`: each shard holds 2 sequences; the first shard's first sequence has 1024 tokens and its last one 2048 // 4. `seq_starts`: the sequences of a shard lie in order within its 2048 slots and do not intersect, the first starting at slot 0; the other slots are padding. The first shard's last sequence ends at its last slot.
All inputs are finite; a program needn't handle non-finite values.
Results may differ from the reference program's by a relative error of at most 0.02.
Values may be sent and summed in bfloat16 or wider, within the bound.
A program may use at most 320 MiB of HBM per device.

```python
from functools import partial
import jax
import jax.numpy as jnp
from jax import lax

D = 2048
HEADS = 16
HD = 128
FF = 5632
CONV = 4
STRETCH = 64
SLOTS = 2048
SEQS = 2
GROUPS = 4
TOKENS = 8192


def shard_layout(key):
    base = jax.random.fold_in(key, 29)
    key_lengths, key_gaps = jax.random.split(base)
    lengths = jax.random.randint(key_lengths, (GROUPS, SEQS), SLOTS // (2 * SEQS), SLOTS // SEQS + 1)
    group_index = jnp.arange(GROUPS)[:, None]
    seq_index = jnp.arange(SEQS)[None, :]
    first_corner = (group_index == 0) & (seq_index == 0)
    last_corner = (group_index == 0) & (seq_index == SEQS - 1)
    lengths = jnp.where(first_corner, SLOTS // SEQS, lengths)
    lengths = jnp.where(last_corner, SLOTS // (2 * SEQS), lengths).astype(jnp.int32)
    spare_slots = SLOTS - jnp.sum(lengths, axis=1)
    shares = jax.random.randint(key_gaps, (GROUPS, SEQS), 1, 64)
    shares = jnp.where(seq_index == 0, 0, shares)
    gap_sizes = spare_slots[:, None] * shares // (jnp.sum(shares, axis=1, keepdims=True) + 1)
    gap_sizes = jnp.where(group_index == 0, jnp.where(seq_index == SEQS - 1, spare_slots[:, None], 0), gap_sizes)
    before = jnp.concatenate([jnp.zeros((GROUPS, 1), jnp.int32), jnp.cumsum(lengths, axis=1)[:, :-1]], axis=1)
    starts = jnp.cumsum(gap_sizes, axis=1) + before
    return (starts.astype(jnp.int32), lengths)


def draw_seq_starts(key, part):
    return shard_layout(key)[0]


def draw_seq_lengths(key, part):
    return shard_layout(key)[1]


def level_of(own_key, dims, cuts, low, high):
    def one(dim, shards_of):
        heights = jax.random.uniform(jax.random.fold_in(jax.random.fold_in(own_key, 6), dim), (shards_of,), jnp.float32, low / len(cuts), high / len(cuts))
        return jnp.repeat(jnp.exp(heights), dims[dim] // shards_of).reshape((-1,) + (1,) * (len(dims) - dim - 1))

    level = one(*cuts[0])
    for cut in cuts[1:]:
        level = level * one(*cut)
    return level


def centred(own_key, dims, scale, most, cuts=(), kind=jnp.bfloat16):
    loudness = level_of(own_key, dims, cuts, -0.22, 0.18) if cuts else 1.0
    values = jax.random.normal(own_key, dims, jnp.float32) * scale * loudness
    return jnp.minimum(jnp.maximum(values, -most), most).astype(kind)


def setup_inputs(seed: int = 0) -> dict:
    seeds = jax.random.split(jax.random.key(seed), 20)
    return {
        "tokens": centred(seeds[0], (TOKENS, D), 1.0, 6.0, ((0, 32),)),
        "attn_gain": jnp.clip(1.0 + 0.18 * jax.random.normal(seeds[1], (D,), jnp.float32), 0.099609375, 1.8984375).astype(jnp.bfloat16),
        "w_query": centred(seeds[2], (D, HEADS * HD), D ** -0.5, 0.125, ((1, 8),)),
        "w_key": centred(seeds[3], (D, HEADS * HD), D ** -0.5, 0.125, ((1, 8),)),
        "w_value": centred(seeds[4], (D, HEADS * HD), D ** -0.5, 0.125, ((1, 8),)),
        "conv_query": centred(seeds[5], (CONV, HEADS * HD), CONV ** -0.5, 3.0, ((1, 8),)),
        "conv_key": centred(seeds[6], (CONV, HEADS * HD), CONV ** -0.5, 3.0, ((1, 8),)),
        "conv_value": centred(seeds[7], (CONV, HEADS * HD), CONV ** -0.5, 3.0, ((1, 8),)),
        "w_beta": centred(seeds[8], (D, HEADS), D ** -0.5, 0.125, ((1, 8),)),
        "w_gate_out": centred(seeds[9], (D, HEADS * HD), D ** -0.5, 0.125, ((1, 8),)),
        "head_gain": jnp.clip(1.0 + 0.18 * jax.random.normal(seeds[10], (HD,), jnp.float32), 0.099609375, 1.8984375).astype(jnp.bfloat16),
        "w_out": centred(seeds[11], (HEADS * HD, D), (HEADS * HD // 4) ** -0.5, 0.25, ((0, 8),)),
        "ffn_gain": jnp.clip(1.0 + 0.18 * jax.random.normal(seeds[12], (D,), jnp.float32), 0.099609375, 1.8984375).astype(jnp.bfloat16),
        "w_gate": centred(seeds[13], (D, FF), D ** -0.5, 0.125, ((1, 8),)),
        "w_up": centred(seeds[14], (D, FF), D ** -0.5, 0.125, ((1, 8),)),
        "w_down": centred(seeds[15], (FF, D), (FF // 4) ** -0.5, 0.15625, ((0, 8),)),
        "seq_starts": draw_seq_starts(jax.random.fold_in(seeds[19], 71), 0),
        "seq_lengths": draw_seq_lengths(jax.random.fold_in(seeds[19], 71), 0),
        "cotangent": centred(seeds[18], (TOKENS, D), 1.0, 6.0, ((0, 32),)),
    }


highest = lax.Precision.HIGHEST

@jax.custom_vjp
def low(v):
    return lax.optimization_barrier(v.astype(jnp.bfloat16)).astype(jnp.float32)

@jax.custom_vjp
def low_back(v):
    return v

def low_keep(v):
    return (low(v), None)

def low_pass(kept, grad):
    return (grad,)

def back_keep(v):
    return (v, None)

def back_low(kept, grad):
    return (low(grad),)
low.defvjp(low_keep, low_pass)
low_back.defvjp(back_keep, back_low)

def positions(starts, lengths, slot_count):
    places = jnp.arange(slot_count, dtype=jnp.int32)
    begun = (places[:, None] >= starts[None, :]).astype(jnp.int32)
    ended = (places[:, None] >= (starts + lengths)[None, :]).astype(jnp.int32)
    segment = lax.optimization_barrier(jnp.sum(begun + ended, axis=1)).astype(jnp.int32)
    live = (segment % 2).astype(jnp.float32)
    return (segment, live)

def short_conv(inputs, taps, segment):
    result = inputs * taps[0]
    for offset in range(1, taps.shape[0]):
        moved = jnp.concatenate([jnp.zeros((offset, inputs.shape[1]), jnp.float32), inputs[:-offset]], 0)
        earlier = jnp.concatenate([jnp.full((offset,), -1, jnp.int32), segment[:-offset]], 0)
        result = result + moved * taps[offset] * (earlier == segment).astype(jnp.float32)[:, None]
    return result

def unit_rows(inputs):
    return inputs * lax.rsqrt(lax.optimization_barrier(jnp.sum(inputs * inputs, axis=-1, keepdims=True)) + 1e-06)

def delta_rule(queries, key_rows, values, strength, segment):
    slot_count, head_width = queries.shape
    blocks = slot_count // STRETCH
    query_blocks = (queries * head_width ** (-0.5)).reshape(blocks, STRETCH, head_width)
    key_blocks = key_rows.reshape(blocks, STRETCH, head_width)
    value_blocks = values.reshape(blocks, STRETCH, head_width)
    beta_blocks = strength.reshape(blocks, STRETCH)
    seg_blocks = segment.reshape(blocks, STRETCH)
    same_seg = (seg_blocks[:, :, None] == seg_blocks[:, None, :]).astype(jnp.float32)
    places = jnp.arange(STRETCH)
    strict = (places[:, None] > places[None, :]).astype(jnp.float32)
    inclusive = (places[:, None] >= places[None, :]).astype(jnp.float32)
    key_inner = jnp.einsum('nik,njk->nij', key_blocks, key_blocks, precision=highest)
    system = jnp.eye(STRETCH, dtype=jnp.float32)[None] + beta_blocks[:, :, None] * key_inner * same_seg * strict
    weighted = lax.linalg.triangular_solve(system, beta_blocks[:, :, None] * key_blocks, left_side=True, lower=True, unit_diagonal=True)
    updates = lax.linalg.triangular_solve(system, beta_blocks[:, :, None] * value_blocks, left_side=True, lower=True, unit_diagonal=True)
    within = jnp.einsum('nik,njk->nij', query_blocks, key_blocks, precision=highest) * same_seg * inclusive
    earlier_last = jnp.concatenate([jnp.full((1,), -1, jnp.int32), seg_blocks[:-1, STRETCH - 1]], 0)
    continued = (seg_blocks[:, 0] == earlier_last).astype(jnp.float32)
    carried = same_seg[:, :, 0] * continued[:, None]
    ending = same_seg[:, :, STRETCH - 1]
    kept_state = continued * same_seg[:, 0, STRETCH - 1]

    def advance(memory, pieces):
        query_part, key_part, weight_part, update_part, mixing, carry_part, end_part, keep_part = pieces
        change = update_part - carry_part[:, None] * jnp.dot(weight_part, memory.T, precision=highest)
        result = carry_part[:, None] * jnp.dot(query_part, memory.T, precision=highest) + jnp.dot(mixing, change, precision=highest)
        memory = keep_part * memory + jnp.dot((end_part[:, None] * change).T, key_part, precision=highest)
        return (memory, result)
    start_memory = jnp.zeros((head_width, head_width), jnp.float32)
    last_memory, outputs = lax.scan(jax.checkpoint(advance), start_memory, (query_blocks, key_blocks, weighted, updates, within, carried, ending, kept_state))
    return outputs.reshape(slot_count, head_width)

def mixer_local(proj_query, proj_key, proj_value, proj_beta, proj_gate, taps_query, taps_key, taps_value, gain_head, segment, live):
    slot_count = proj_query.shape[0]
    head_count = proj_beta.shape[1]
    head_width = proj_query.shape[1] // head_count

    def feature(projected, taps):
        return jax.nn.silu(short_conv(projected, taps, segment)).reshape(slot_count, head_count, head_width)
    queries = low(unit_rows(feature(proj_query, taps_query)))
    key_rows = low(unit_rows(feature(proj_key, taps_key)))
    values = low(feature(proj_value, taps_value))
    strength = jax.nn.sigmoid(proj_beta)
    delta_out = jax.vmap(delta_rule, in_axes=(1, 1, 1, 1, None), out_axes=1)(queries, key_rows, values, strength, segment)
    head_normed = delta_out * lax.rsqrt(lax.optimization_barrier(jnp.mean(delta_out * delta_out, axis=-1, keepdims=True)) + 1e-05) * gain_head
    gated = head_normed * jax.nn.silu(proj_gate.reshape(slot_count, head_count, head_width)) * live[:, None, None]
    return gated.reshape(slot_count, head_count * head_width)

def rms_scale(inputs, gain):
    return inputs * lax.rsqrt(lax.optimization_barrier(jnp.mean(inputs * inputs, axis=-1, keepdims=True)) + 1e-06) * gain

def block_forward(tokens, attn_gain, w_query, w_key, w_value, conv_query, conv_key, conv_value, w_beta, w_gate_out, head_gain, w_out, ffn_gain, w_gate, w_up, w_down, segment, live):
    normed = low(rms_scale(tokens, attn_gain))

    def project(weight):
        return low_back(jnp.dot(normed, weight, precision=highest))

    def grouped(inputs):
        return inputs.reshape(GROUPS, SLOTS, inputs.shape[1])
    proj_query = grouped(project(w_query))
    proj_key = grouped(project(w_key))
    proj_value = grouped(project(w_value))
    proj_beta = grouped(project(w_beta))
    proj_gate = grouped(project(w_gate_out))
    mixed = jax.vmap(mixer_local, in_axes=(0, 0, 0, 0, 0, None, None, None, None, 0, 0))(proj_query, proj_key, proj_value, proj_beta, proj_gate, conv_query, conv_key, conv_value, head_gain, segment, live)
    mixed = low(mixed.reshape(TOKENS, HEADS * HD))
    attended = low_back(jnp.dot(mixed, w_out, precision=highest))
    resid = tokens + attended
    ffn_in = low(rms_scale(resid, ffn_gain))
    gate_pre = low_back(jnp.dot(ffn_in, w_gate, precision=highest))
    up_pre = low_back(jnp.dot(ffn_in, w_up, precision=highest))
    hidden = low(jax.nn.silu(gate_pre) * up_pre)
    return resid + jnp.dot(hidden, w_down, precision=highest)

def reference(tokens, attn_gain, w_query, w_key, w_value, conv_query, conv_key, conv_value, w_beta, w_gate_out, head_gain, w_out, ffn_gain, w_gate, w_up, w_down, seq_starts, seq_lengths, cotangent):
    segment, live = jax.vmap(positions, in_axes=(0, 0, None))(seq_starts, seq_lengths, SLOTS)
    floats = [array.astype(jnp.float32) for array in (tokens, attn_gain, w_query, w_key, w_value, conv_query, conv_key, conv_value, w_beta, w_gate_out, head_gain, w_out, ffn_gain, w_gate, w_up, w_down)]
    output, pullback = jax.vjp(partial(block_forward, segment=segment, live=live), *floats)
    grads = pullback(cotangent.astype(jnp.float32))
    return (output.astype(jnp.bfloat16), grads[0], grads[1], grads[2], grads[3], grads[4], grads[5], grads[6], grads[7], grads[8], grads[9], grads[10], grads[11], grads[12], grads[13], grads[14], grads[15])
```

```python
import functools
import jax
import jax.numpy as jnp
from jax import lax
from jax.experimental import pallas as pl
from jax.experimental.pallas import tpu as pltpu
from jax.sharding import PartitionSpec as P

CHUNK = 256
F32, BF16 = jnp.float32, jnp.bfloat16


def mm(a, b, contract=(1, 0)):
    return lax.dot_general(
        a.astype(BF16),
        b.astype(BF16),
        (((contract[0],), (contract[1],)), ((), ())),
        preferred_element_type=F32,
    )


def segment_at(places, starts, lengths, seqs):
    segment = jnp.zeros_like(places)
    for s in range(seqs):
        begin = starts[0, s]
        stop = begin + lengths[0, s]
        segment = segment + jnp.where(places >= begin, 1, 0) + jnp.where(places >= stop, 1, 0)
    return jnp.where(places < 0, -1, segment)


def chunk_masks(starts, lengths, seqs, first, size):
    rows = first + lax.broadcasted_iota(jnp.int32, (size, 1), 0)
    columns = first + lax.broadcasted_iota(jnp.int32, (1, size), 1)
    seg_rows = segment_at(rows, starts, lengths, seqs)
    seg_columns = segment_at(columns, starts, lengths, seqs)
    before = segment_at(jnp.full((1, 1), first - 1, jnp.int32), starts, lengths, seqs)
    last = segment_at(jnp.full((1, 1), first + size - 1, jnp.int32), starts, lengths, seqs)
    return rows, seg_rows, seg_columns, before, last


def inverse_unit_lower(lower, size):
    i = lax.broadcasted_iota(jnp.int32, (size, size), 0)
    j = lax.broadcasted_iota(jnp.int32, (size, size), 1)

    def corner(width):
        shift = width.bit_length() - 1
        pair = (i >> (shift + 1)) == (j >> (shift + 1))
        return pair & (((i >> shift) & 1) == 1) & (((j >> shift) & 1) == 0)

    inverse = jnp.where(i == j, 1.0, 0.0) - jnp.where(corner(1), lower, 0.0)
    width = 2
    while width < size:
        low = inverse.astype(BF16)
        if 2 * width == size:
            part = mm(mm(low[width:, width:], lower[width:, :width]), low[:width, :width])
            inverse = jnp.concatenate(
                [
                    inverse[:width],
                    jnp.concatenate([-part, inverse[width:, width:]], axis=1),
                ],
                axis=0,
            )
        else:
            between = jnp.where(corner(width), lower, 0.0)
            inverse = inverse - mm(mm(low, between), low)
        width *= 2
    return inverse


def sigmoid(v):
    return 1.0 / (1.0 + jnp.exp(-v))


def forward_kernel(
    heads, width, seqs,
    starts, lengths, normed, w_query, w_key, w_value, w_gate, w_beta,
    taps_query, taps_key, taps_value, gain,
    mixed, p_query, p_key, p_value, p_gate, p_beta, z_query, z_key, z_value,
    delta_out, change_out, inverse_out, state_out,
    tail_query, tail_key, tail_value, state,
):
    step = pl.program_id(0)
    size = normed.shape[0]
    first = step * size

    @pl.when(step == 0)
    def _():
        for tail in (tail_query, tail_key, tail_value):
            tail[...] = jnp.zeros_like(tail)
        state[...] = jnp.zeros_like(state)

    rows, seg_rows, seg_columns, before, last = chunk_masks(starts, lengths, seqs, first, size)
    same = seg_rows == seg_columns
    i = lax.broadcasted_iota(jnp.int32, (size, size), 0)
    j = lax.broadcasted_iota(jnp.int32, (size, size), 1)
    strict = jnp.where(same & (i > j), 1.0, 0.0)
    inclusive = jnp.where(same & (i >= j), 1.0, 0.0)
    carried = jnp.where(seg_rows == before, 1.0, 0.0)
    ending = jnp.where(seg_rows == last, 1.0, 0.0)
    kept = jnp.where(before == last, 1.0, 0.0)
    live = jnp.where(seg_rows % 2 == 1, 1.0, 0.0)
    joined = [
        jnp.where(segment_at(rows - offset, starts, lengths, seqs) == seg_rows, 1.0, 0.0)
        for offset in range(1, taps_query.shape[0])
    ]
    inputs = normed[...]

    def feature(weight, taps, tail, p_out, z_out):
        projected = jnp.dot(inputs, weight[...], preferred_element_type=F32)
        p_out[...] = projected
        tail[8:, :] = projected
        tap = taps[...].astype(F32)
        result = projected * tap[0:1]
        for offset in range(1, tap.shape[0]):
            result = result + tail[8 - offset : 8 - offset + size, :] * tap[offset : offset + 1] * joined[offset - 1]
        tail[0:8, :] = projected[size - 8 :, :]
        z_out[...] = result
        return result * sigmoid(result)

    u_query = feature(w_query, taps_query, tail_query, p_query, z_query)
    u_key = feature(w_key, taps_key, tail_key, p_key, z_key)
    u_value = feature(w_value, taps_value, tail_value, p_value, z_value)
    gate = jnp.dot(inputs, w_gate[...], preferred_element_type=F32)
    p_gate[...] = gate
    beta_pre = jnp.dot(inputs, w_beta[...], preferred_element_type=F32)
    p_beta[...] = beta_pre
    strength = sigmoid(beta_pre)
    opened = gate * sigmoid(gate)
    scale = width ** (-0.5)
    head_gain = gain[...].astype(F32)
    for h in range(heads):
        cols = slice(h * width, (h + 1) * width)
        uq, uk = u_query[:, cols], u_key[:, cols]
        query = (uq * lax.rsqrt(jnp.sum(uq * uq, axis=1, keepdims=True) + 1e-6)).astype(BF16)
        key = (uk * lax.rsqrt(jnp.sum(uk * uk, axis=1, keepdims=True) + 1e-6)).astype(BF16)
        value = u_value[:, cols].astype(BF16).astype(F32)
        beta = strength[:, h : h + 1]
        memory = state[h]
        low_memory = memory.astype(BF16)
        state_out[0, h] = low_memory
        lower = mm(key, key, (1, 1)) * strict * beta
        inverse = inverse_unit_lower(lower, size).astype(BF16)
        inverse_out[0, h] = inverse
        within = mm(query, key, (1, 1)) * inclusive
        change = mm(inverse, beta * (value - carried * mm(key, low_memory)))
        low_change = change.astype(BF16)
        change_out[:, cols] = low_change
        out = scale * (carried * mm(query, low_memory) + mm(within, low_change))
        state[h] = kept * memory + mm(key, ending * change, (0, 0))
        delta_out[:, cols] = out
        normal = out * lax.rsqrt(jnp.mean(out * out, axis=1, keepdims=True) + 1e-5) * head_gain
        mixed[:, cols] = (normal * opened[:, cols] * live).astype(BF16)


def forward_mixer(normed, w_query, w_key, w_value, w_gate, w_beta, taps_query, taps_key, taps_value, gain, starts, lengths):
    slots, model = normed.shape
    wide = w_query.shape[1]
    width = gain.shape[0]
    heads = wide // width
    seqs = starts.shape[1]
    chunks = slots // CHUNK
    taps = taps_query.shape[0]
    smem = pl.BlockSpec(memory_space=pltpu.SMEM)
    whole = lambda shape: pl.BlockSpec(shape, lambda n: (0,) * len(shape))
    piece = lambda shape: pl.BlockSpec(shape, lambda n: (n,) + (0,) * (len(shape) - 1))
    outs = [
        ((slots, wide), BF16), ((slots, wide), F32), ((slots, wide), F32), ((slots, wide), F32), ((slots, wide), F32),
        ((slots, heads), F32), ((slots, wide), F32), ((slots, wide), F32), ((slots, wide), F32),
        ((slots, wide), F32), ((slots, wide), BF16),
    ]
    return pl.pallas_call(
        functools.partial(forward_kernel, heads, width, seqs),
        name="mixer_forward",
        grid=(chunks,),
        out_shape=[jax.ShapeDtypeStruct(s, d) for s, d in outs]
        + [
            jax.ShapeDtypeStruct((chunks, heads, CHUNK, CHUNK), BF16),
            jax.ShapeDtypeStruct((chunks, heads, width, width), BF16),
        ],
        in_specs=[smem, smem, piece((CHUNK, model))]
        + [whole((model, wide))] * 4
        + [whole((model, heads))]
        + [whole((taps, wide))] * 3
        + [whole((1, width))],
        out_specs=[piece((CHUNK, s[1])) for s, d in outs]
        + [piece((1, heads, CHUNK, CHUNK)), piece((1, heads, width, width))],
        scratch_shapes=[pltpu.VMEM((CHUNK + 8, wide), F32)] * 3 + [pltpu.VMEM((heads, width, width), F32)],
        compiler_params=pltpu.CompilerParams(vmem_limit_bytes=56 << 20),
        cost_estimate=pl.CostEstimate(
            flops=2 * slots * model * wide * 4 + slots * heads * CHUNK * 2 * CHUNK * 20,
            bytes_accessed=slots * model * 2 + 4 * model * wide * 2 + slots * wide * 36,
            transcendentals=slots * wide * 4,
        ),
    )(starts, lengths, normed, w_query, w_key, w_value, w_gate, w_beta, taps_query, taps_key, taps_value, gain.reshape(1, width))


def backward_kernel(
    heads, width, seqs, chunks,
    starts, lengths, normed, grad_attended, mixed, p_query, p_key, p_value, p_gate, p_beta,
    z_query, z_key, z_value, delta_out, change_in, inverse_in, state_in,
    w_query, w_key, w_value, w_gate, w_beta, w_out, taps_query, taps_key, taps_value, gain,
    grad_normed, gw_query, gw_key, gw_value, gw_gate, gw_beta, gw_out,
    gt_query, gt_key, gt_value, g_gain,
    a_query, a_key, a_value, a_gate, a_beta, a_out, head_query, head_key, head_value, flow,
):
    step = pl.program_id(0)
    size = normed.shape[0]
    first = (chunks - 1 - step) * size

    @pl.when(step == 0)
    def _():
        for ref in (a_query, a_key, a_value, a_gate, a_beta, a_out, gt_query, gt_key, gt_value, g_gain, flow):
            ref[...] = jnp.zeros_like(ref)
        for ref in (head_query, head_key, head_value):
            ref[size:, :] = jnp.zeros((8, ref.shape[1]), F32)

    rows, seg_rows, seg_columns, before, last = chunk_masks(starts, lengths, seqs, first, size)
    same = seg_rows == seg_columns
    i = lax.broadcasted_iota(jnp.int32, (size, size), 0)
    j = lax.broadcasted_iota(jnp.int32, (size, size), 1)
    strict = jnp.where(same & (i > j), 1.0, 0.0)
    inclusive = jnp.where(same & (i >= j), 1.0, 0.0)
    carried = jnp.where(seg_rows == before, 1.0, 0.0)
    ending = jnp.where(seg_rows == last, 1.0, 0.0)
    kept = jnp.where(before == last, 1.0, 0.0)
    live = jnp.where(seg_rows % 2 == 1, 1.0, 0.0)
    taps = taps_query.shape[0]
    joined = [
        jnp.where(segment_at(rows + offset, starts, lengths, seqs) == seg_rows, 1.0, 0.0)
        for offset in range(1, taps)
    ]
    inputs = normed[...]
    grad_rows = grad_attended[...]
    grad_mixed = mm(grad_rows, w_out[...], (1, 1))
    a_out[...] += mm(mixed[...], grad_rows, (0, 0))
    strength = sigmoid(p_beta[...])
    scale = width ** (-0.5)
    head_gain = gain[...].astype(F32)

    grads_query, grads_key, grads_value, grads_gate, grads_beta = [], [], [], [], []
    for h in range(heads):
        cols = slice(h * width, (h + 1) * width)
        out = delta_out[:, cols]
        gate = p_gate[:, cols]
        sig_gate = sigmoid(gate)
        silu_gate = gate * sig_gate
        root = lax.rsqrt(jnp.mean(out * out, axis=1, keepdims=True) + 1e-5)
        grad = grad_mixed[:, cols] * live
        unit = out * root
        grads_gate.append(grad * unit * head_gain * (sig_gate * (1.0 + gate * (1.0 - sig_gate))))
        grad_normal = grad * silu_gate
        g_gain[...] += jnp.sum(grad_normal * unit, axis=0, keepdims=True)
        push = grad_normal * head_gain
        grad_out = scale * root * (push - unit * jnp.mean(push * unit, axis=1, keepdims=True))

        zq, zk, zv = z_query[:, cols], z_key[:, cols], z_value[:, cols]
        sq, sk, sv = sigmoid(zq), sigmoid(zk), sigmoid(zv)
        uq, uk = zq * sq, zk * sk
        nq = lax.rsqrt(jnp.sum(uq * uq, axis=1, keepdims=True) + 1e-6)
        nk = lax.rsqrt(jnp.sum(uk * uk, axis=1, keepdims=True) + 1e-6)
        unit_q, unit_k = uq * nq, uk * nk
        query, key = unit_q.astype(BF16), unit_k.astype(BF16)
        beta = strength[:, h : h + 1]
        change = change_in[:, cols]
        inverse = inverse_in[0, h]
        memory = state_in[0, h]
        flowing = flow[h]
        low_flow = flowing.astype(BF16)
        low_out = grad_out.astype(BF16)

        within = mm(query, key, (1, 1)) * inclusive
        grad_within = (mm(low_out, change, (1, 1)) * inclusive).astype(BF16)
        grad_change = mm(within, low_out, (0, 0)) + ending * mm(key, low_flow)
        grad_mid = mm(inverse, grad_change, (0, 0))
        grad_value = beta * grad_mid
        low_value = grad_value.astype(BF16)
        cross = (mm(low_value, change, (1, 1)) * strict).astype(BF16)
        grad_query = carried * mm(low_out, memory, (1, 1)) + mm(grad_within, key)
        grad_key = (
            mm(grad_within, query, (0, 0))
            + ending * mm(change, low_flow, (1, 1))
            - carried * mm(low_value, memory, (1, 1))
            - mm(cross, key)
            - mm(cross, key, (0, 0))
        )
        flow[h] = (
            kept * flowing
            + mm(query, carried * grad_out, (0, 0))
            - mm(key, carried * grad_value, (0, 0))
        )
        grads_beta.append((1.0 - beta) * jnp.sum(grad_mid * change.astype(F32), axis=1, keepdims=True))
        du_q = nq * (grad_query - unit_q * jnp.sum(grad_query * unit_q, axis=1, keepdims=True))
        du_k = nk * (grad_key - unit_k * jnp.sum(grad_key * unit_k, axis=1, keepdims=True))
        grads_query.append(du_q * sq * (1.0 + zq * (1.0 - sq)))
        grads_key.append(du_k * sk * (1.0 + zk * (1.0 - sk)))
        grads_value.append(grad_value * sv * (1.0 + zv * (1.0 - sv)))

    def unconv(parts, taps_ref, head, projected, grad_taps):
        grad = jnp.concatenate(parts, axis=1)
        head[0:size, :] = grad
        tap = taps_ref[...].astype(F32)
        p = projected[...]
        result = grad * tap[0:1]
        grad_taps[0:1, :] += jnp.sum(p * grad, axis=0, keepdims=True)
        for offset in range(1, taps):
            moved = head[offset : offset + size, :] * joined[offset - 1]
            result = result + moved * tap[offset : offset + 1]
            grad_taps[offset : offset + 1, :] += jnp.sum(p * moved, axis=0, keepdims=True)
        head[size:, :] = grad[0:8, :]
        return result.astype(BF16)

    d_query = unconv(grads_query, taps_query, head_query, p_query, gt_query)
    d_key = unconv(grads_key, taps_key, head_key, p_key, gt_key)
    d_value = unconv(grads_value, taps_value, head_value, p_value, gt_value)
    d_gate = jnp.concatenate(grads_gate, axis=1).astype(BF16)
    d_beta = jnp.concatenate(grads_beta, axis=1).astype(BF16)
    grad_normed[...] = (
        mm(d_query, w_query[...], (1, 1))
        + mm(d_key, w_key[...], (1, 1))
        + mm(d_value, w_value[...], (1, 1))
        + mm(d_gate, w_gate[...], (1, 1))
        + mm(d_beta, w_beta[...], (1, 1))
    ).astype(BF16)
    a_query[...] += mm(inputs, d_query, (0, 0))
    a_key[...] += mm(inputs, d_key, (0, 0))
    a_value[...] += mm(inputs, d_value, (0, 0))
    a_gate[...] += mm(inputs, d_gate, (0, 0))
    a_beta[...] += mm(inputs, d_beta, (0, 0))

    @pl.when(step == chunks - 1)
    def _():
        for target, source in (
            (gw_query, a_query), (gw_key, a_key), (gw_value, a_value), (gw_gate, a_gate),
            (gw_beta, a_beta), (gw_out, a_out),
        ):
            target[...] = source[...].astype(target.dtype)


def backward_mixer(normed, grad_attended, saved, w_query, w_key, w_value, w_gate, w_beta, w_out, taps_query, taps_key, taps_value, gain, starts, lengths):
    slots, model = normed.shape
    wide = w_query.shape[1]
    width = gain.shape[0]
    heads = wide // width
    seqs = starts.shape[1]
    chunks = slots // CHUNK
    taps = taps_query.shape[0]
    smem = pl.BlockSpec(memory_space=pltpu.SMEM)
    whole = lambda shape: pl.BlockSpec(shape, lambda n: (0,) * len(shape))
    fixed = lambda shape: pl.BlockSpec(shape, lambda n: (0,) * len(shape), pipeline_mode=pl.Buffered(1))
    piece = lambda shape: pl.BlockSpec(shape, lambda n: (chunks - 1 - n,) + (0,) * (len(shape) - 1))
    rows = lambda a: piece((CHUNK, a.shape[1]))
    outs = (
        [((slots, model), BF16)] + [((model, wide), BF16)] * 4 + [((model, heads), BF16), ((wide, model), BF16)]
        + [((taps, wide), F32)] * 3 + [((1, width), F32)]
    )
    return pl.pallas_call(
        functools.partial(backward_kernel, heads, width, seqs, chunks),
        name="mixer_backward",
        grid=(chunks,),
        out_shape=[jax.ShapeDtypeStruct(s, d) for s, d in outs],
        in_specs=[smem, smem, rows(normed), rows(grad_attended)]
        + [rows(a) for a in saved[:11]]
        + [piece((1, heads, CHUNK, CHUNK)), piece((1, heads, width, width))]
        + [fixed((model, wide))] * 4
        + [fixed((model, heads)), fixed((wide, model))]
        + [fixed((taps, wide))] * 3
        + [fixed((1, width))],
        out_specs=[piece((CHUNK, model))] + [whole(s) for s, d in outs[1:]],
        scratch_shapes=[pltpu.VMEM((model, wide), F32)] * 4
        + [pltpu.VMEM((model, heads), F32), pltpu.VMEM((wide, model), F32)]
        + [pltpu.VMEM((CHUNK + 8, wide), F32)] * 3
        + [pltpu.VMEM((heads, width, width), F32)],
        compiler_params=pltpu.CompilerParams(vmem_limit_bytes=60 << 20),
        cost_estimate=pl.CostEstimate(
            flops=2 * slots * model * wide * 10 + slots * heads * CHUNK * 2 * CHUNK * 8,
            bytes_accessed=slots * model * 6 + 10 * model * wide * 2 + slots * wide * 36,
            transcendentals=slots * wide * 8,
        ),
    )(starts, lengths, normed, grad_attended, *saved, w_query, w_key, w_value, w_gate, w_beta, w_out, taps_query, taps_key, taps_value, gain.reshape(1, width))


def norm_back(inputs, scale, gain, grad_normed):
    weighted_grad = gain * grad_normed
    inner = jnp.mean(weighted_grad * inputs, axis=1, keepdims=True)
    grad_inputs = scale * weighted_grad - inputs * scale * scale * scale * inner
    grad_gain = jnp.sum(grad_normed * inputs * scale, axis=0)
    return (grad_inputs, grad_gain)


def shards(
    tokens,
    attn_gain,
    w_query,
    w_key,
    w_value,
    conv_query,
    conv_key,
    conv_value,
    w_beta,
    w_gate_out,
    head_gain,
    w_out,
    ffn_gain,
    w_gate,
    w_up,
    w_down,
    seq_starts,
    seq_lengths,
    cotangent,
):
    inputs = tokens.astype(jnp.float32)
    gain_first = attn_gain.astype(jnp.float32)
    scale_first = lax.rsqrt(jnp.mean(inputs * inputs, axis=1, keepdims=True) + 1e-06)
    normed = (inputs * scale_first * gain_first).astype(jnp.bfloat16)
    normed_full = lax.all_gather(normed, "tensor", axis=0, tiled=True)
    saved = forward_mixer(
        normed_full, w_query, w_key, w_value, w_gate_out, w_beta,
        conv_query, conv_key, conv_value, head_gain, seq_starts, seq_lengths,
    )
    mixed_low = saved[0]
    attended = lax.psum_scatter(
        jnp.dot(mixed_low, w_out, preferred_element_type=jnp.float32).astype(jnp.bfloat16),
        "tensor",
        scatter_dimension=0,
        tiled=True,
    ).astype(jnp.float32)
    resid = inputs + attended
    gain_second = ffn_gain.astype(jnp.float32)
    scale_second = lax.rsqrt(jnp.mean(resid * resid, axis=1, keepdims=True) + 1e-06)
    ffn_in = (resid * scale_second * gain_second).astype(jnp.bfloat16)
    ffn_full = lax.all_gather(ffn_in, "tensor", axis=0, tiled=True)
    gate_pre = jnp.dot(ffn_full, w_gate, preferred_element_type=jnp.float32)
    up_pre = jnp.dot(ffn_full, w_up, preferred_element_type=jnp.float32)
    sigmoid_gate = jax.nn.sigmoid(gate_pre)
    silu_gate = gate_pre * sigmoid_gate
    hidden = (silu_gate * up_pre).astype(jnp.bfloat16)
    output = resid + lax.psum_scatter(
        jnp.dot(hidden, w_down, preferred_element_type=jnp.float32).astype(jnp.bfloat16),
        "tensor",
        scatter_dimension=0,
        tiled=True,
    ).astype(jnp.float32)
    grad_full = lax.all_gather(cotangent, "tensor", axis=0, tiled=True)
    grad_hidden = jnp.einsum("sd,fd->sf", grad_full, w_down, preferred_element_type=jnp.float32)
    grad_w_down = jnp.einsum("sf,sd->fd", hidden, grad_full, preferred_element_type=jnp.float32)
    grad_gate = (
        grad_hidden * up_pre * sigmoid_gate * (1.0 + gate_pre * (1.0 - sigmoid_gate))
    ).astype(jnp.bfloat16)
    grad_up = (grad_hidden * silu_gate).astype(jnp.bfloat16)
    grad_w_gate = jnp.einsum("sd,sf->df", ffn_full, grad_gate, preferred_element_type=jnp.float32)
    grad_w_up = jnp.einsum("sd,sf->df", ffn_full, grad_up, preferred_element_type=jnp.float32)
    grad_ffn_in = lax.psum_scatter(
        (
            jnp.einsum("sf,df->sd", grad_gate, w_gate, preferred_element_type=jnp.float32)
            + jnp.einsum("sf,df->sd", grad_up, w_up, preferred_element_type=jnp.float32)
        ).astype(jnp.bfloat16),
        "tensor",
        scatter_dimension=0,
        tiled=True,
    ).astype(jnp.float32)
    grad_through, grad_ffn_gain = norm_back(resid, scale_second, gain_second, grad_ffn_in)
    grad_resid = cotangent.astype(jnp.float32) + grad_through
    grad_attended = lax.all_gather(grad_resid.astype(jnp.bfloat16), "tensor", axis=0, tiled=True)
    pulled = backward_mixer(
        normed_full, grad_attended, saved, w_query, w_key, w_value, w_gate_out, w_beta, w_out,
        conv_query, conv_key, conv_value, head_gain, seq_starts, seq_lengths,
    )
    grad_normed = lax.psum_scatter(
        pulled[0], "tensor", scatter_dimension=0, tiled=True
    ).astype(jnp.float32)
    grad_first, grad_attn_gain = norm_back(inputs, scale_first, gain_first, grad_normed)
    grad_tokens = grad_resid + grad_first
    grad_attn_gain, grad_ffn_gain, grad_head_gain = lax.psum(
        (grad_attn_gain, grad_ffn_gain, pulled[10][0]), ("dp", "tensor")
    )
    mixer_grads = (
        pulled[1], pulled[2], pulled[3], pulled[7], pulled[8], pulled[9], pulled[5], pulled[4], pulled[6],
    )
    summed_all = (
        lax.psum(mixer_grads[0].astype(jnp.bfloat16), "dp").astype(jnp.float32),
        lax.psum(mixer_grads[1].astype(jnp.bfloat16), "dp").astype(jnp.float32),
        lax.psum(mixer_grads[2].astype(jnp.bfloat16), "dp").astype(jnp.float32),
        lax.psum(mixer_grads[3].astype(jnp.bfloat16), "dp").astype(jnp.float32),
        lax.psum(mixer_grads[4].astype(jnp.bfloat16), "dp").astype(jnp.float32),
        lax.psum(mixer_grads[5].astype(jnp.bfloat16), "dp").astype(jnp.float32),
        lax.psum(mixer_grads[6].astype(jnp.bfloat16), "dp").astype(jnp.float32),
        lax.psum(mixer_grads[7].astype(jnp.bfloat16), "dp").astype(jnp.float32),
        lax.psum(mixer_grads[8].astype(jnp.bfloat16), "dp").astype(jnp.float32),
        lax.psum(grad_w_gate.astype(jnp.bfloat16), "dp").astype(jnp.float32),
        lax.psum(grad_w_up.astype(jnp.bfloat16), "dp").astype(jnp.float32),
        lax.psum(grad_w_down.astype(jnp.bfloat16), "dp").astype(jnp.float32),
    )
    mixer_grads = summed_all[:9]
    grad_w_gate, grad_w_up, grad_w_down = (summed_all[9], summed_all[10], summed_all[11])
    return (
        output.astype(jnp.bfloat16),
        grad_tokens,
        grad_attn_gain,
        mixer_grads[0],
        mixer_grads[1],
        mixer_grads[2],
        mixer_grads[3],
        mixer_grads[4],
        mixer_grads[5],
        mixer_grads[6],
        mixer_grads[7],
        grad_head_gain,
        mixer_grads[8],
        grad_ffn_gain,
        grad_w_gate,
        grad_w_up,
        grad_w_down,
    )


def solution(mesh):
    placed = (
        P(("dp", "tensor"), None),
        P(),
        P(None, "tensor"),
        P(None, "tensor"),
        P(None, "tensor"),
        P(None, "tensor"),
        P(None, "tensor"),
        P(None, "tensor"),
        P(None, "tensor"),
        P(None, "tensor"),
        P(),
        P("tensor", None),
        P(),
        P(None, "tensor"),
        P(None, "tensor"),
        P("tensor", None),
        P("dp", None),
        P("dp", None),
        P(("dp", "tensor"), None),
    )
    return jax.shard_map(
        shards,
        mesh=mesh,
        in_specs=placed,
        out_specs=(
            P(("dp", "tensor"), None),
            P(("dp", "tensor"), None),
            P(),
            P(None, "tensor"),
            P(None, "tensor"),
            P(None, "tensor"),
            P(None, "tensor"),
            P(None, "tensor"),
            P(None, "tensor"),
            P(None, "tensor"),
            P(None, "tensor"),
            P(),
            P("tensor", None),
            P(),
            P(None, "tensor"),
            P(None, "tensor"),
            P("tensor", None),
        ),
        check_vma=False,
    )
```

```python
import functools
import jax
import jax.numpy as jnp
from jax import lax
from jax.experimental import pallas as pl
from jax.experimental.pallas import tpu as pltpu
from jax.sharding import PartitionSpec as P

CHUNK = 256
F32, BF16 = jnp.float32, jnp.bfloat16


def mm(a, b, contract=(1, 0)):
    return lax.dot_general(
        a.astype(BF16),
        b.astype(BF16),
        (((contract[0],), (contract[1],)), ((), ())),
        preferred_element_type=F32,
    )


def segment_at(places, starts, lengths, seqs):
    segment = jnp.zeros_like(places)
    for s in range(seqs):
        begin = starts[0, s]
        stop = begin + lengths[0, s]
        segment = segment + jnp.where(places >= begin, 1, 0) + jnp.where(places >= stop, 1, 0)
    return jnp.where(places < 0, -1, segment)


def chunk_masks(starts, lengths, seqs, first, size):
    rows = first + lax.broadcasted_iota(jnp.int32, (size, 1), 0)
    columns = first + lax.broadcasted_iota(jnp.int32, (1, size), 1)
    seg_rows = segment_at(rows, starts, lengths, seqs)
    seg_columns = segment_at(columns, starts, lengths, seqs)
    before = segment_at(jnp.full((1, 1), first - 1, jnp.int32), starts, lengths, seqs)
    last = segment_at(jnp.full((1, 1), first + size - 1, jnp.int32), starts, lengths, seqs)
    return rows, seg_rows, seg_columns, before, last


def inverse_unit_lower(lower, size):
    i = lax.broadcasted_iota(jnp.int32, (size, size), 0)
    j = lax.broadcasted_iota(jnp.int32, (size, size), 1)

    def corner(width):
        shift = width.bit_length() - 1
        pair = (i >> (shift + 1)) == (j >> (shift + 1))
        return pair & (((i >> shift) & 1) == 1) & (((j >> shift) & 1) == 0)

    inverse = jnp.where(i == j, 1.0, 0.0) - jnp.where(corner(1), lower, 0.0)
    width = 2
    while width < size:
        low = inverse.astype(BF16)
        if 2 * width == size:
            part = mm(mm(low[width:, width:], lower[width:, :width]), low[:width, :width])
            inverse = jnp.concatenate(
                [
                    inverse[:width],
                    jnp.concatenate([-part, inverse[width:, width:]], axis=1),
                ],
                axis=0,
            )
        else:
            between = jnp.where(corner(width), lower, 0.0)
            inverse = inverse - mm(mm(low, between), low)
        width *= 2
    return inverse


def sigmoid(v):
    return 1.0 / (1.0 + jnp.exp(-v))


def normed_rows(tokens, gain):
    value = tokens[...].astype(F32)
    unit = value * lax.rsqrt(jnp.mean(value * value, axis=1, keepdims=True) + 1e-6)
    return unit * gain[...].astype(F32), unit


def forward_kernel(
    heads, width, seqs,
    starts, lengths, tokens, w_query, w_key, w_value, w_gate, w_beta,
    taps_query, taps_key, taps_value, gain, gain_first,
    mixed, p_query, p_key, p_value, p_gate, p_beta, z_query, z_key, z_value,
    delta_out, change_out, inverse_out, state_out,
    tail_query, tail_key, tail_value, state,
):
    step = pl.program_id(0)
    size = tokens.shape[0]
    first = step * size

    @pl.when(step == 0)
    def _():
        for tail in (tail_query, tail_key, tail_value):
            tail[...] = jnp.zeros_like(tail)
        state[...] = jnp.zeros_like(state)

    rows, seg_rows, seg_columns, before, last = chunk_masks(starts, lengths, seqs, first, size)
    same = seg_rows == seg_columns
    i = lax.broadcasted_iota(jnp.int32, (size, size), 0)
    j = lax.broadcasted_iota(jnp.int32, (size, size), 1)
    strict = jnp.where(same & (i > j), 1.0, 0.0)
    inclusive = jnp.where(same & (i >= j), 1.0, 0.0)
    carried = jnp.where(seg_rows == before, 1.0, 0.0)
    ending = jnp.where(seg_rows == last, 1.0, 0.0)
    kept = jnp.where(before == last, 1.0, 0.0)
    live = jnp.where(seg_rows % 2 == 1, 1.0, 0.0)
    joined = [
        jnp.where(segment_at(rows - offset, starts, lengths, seqs) == seg_rows, 1.0, 0.0)
        for offset in range(1, taps_query.shape[0])
    ]
    inputs = normed_rows(tokens, gain_first)[0].astype(BF16)

    def feature(weight, taps, tail, p_out, z_out):
        projected = jnp.dot(inputs, weight[...], preferred_element_type=F32)
        p_out[...] = projected
        tail[8:, :] = projected
        tap = taps[...].astype(F32)
        result = projected * tap[0:1]
        for offset in range(1, tap.shape[0]):
            result = result + tail[8 - offset : 8 - offset + size, :] * tap[offset : offset + 1] * joined[offset - 1]
        tail[0:8, :] = projected[size - 8 :, :]
        z_out[...] = result
        return result * sigmoid(result)

    u_query = feature(w_query, taps_query, tail_query, p_query, z_query)
    u_key = feature(w_key, taps_key, tail_key, p_key, z_key)
    u_value = feature(w_value, taps_value, tail_value, p_value, z_value)
    gate = jnp.dot(inputs, w_gate[...], preferred_element_type=F32)
    p_gate[...] = gate
    beta_pre = jnp.dot(inputs, w_beta[...], preferred_element_type=F32)
    p_beta[...] = beta_pre
    strength = sigmoid(beta_pre)
    opened = gate * sigmoid(gate)
    scale = width ** (-0.5)
    head_gain = gain[...].astype(F32)
    for h in range(heads):
        cols = slice(h * width, (h + 1) * width)
        uq, uk = u_query[:, cols], u_key[:, cols]
        query = (uq * lax.rsqrt(jnp.sum(uq * uq, axis=1, keepdims=True) + 1e-6)).astype(BF16)
        key = (uk * lax.rsqrt(jnp.sum(uk * uk, axis=1, keepdims=True) + 1e-6)).astype(BF16)
        value = u_value[:, cols].astype(BF16).astype(F32)
        beta = strength[:, h : h + 1]
        memory = state[h]
        low_memory = memory.astype(BF16)
        state_out[0, h] = low_memory
        lower = mm(key, key, (1, 1)) * strict * beta
        inverse = inverse_unit_lower(lower, size).astype(BF16)
        inverse_out[0, h] = inverse
        within = mm(query, key, (1, 1)) * inclusive
        change = mm(inverse, beta * (value - carried * mm(key, low_memory)))
        low_change = change.astype(BF16)
        change_out[:, cols] = low_change
        out = scale * (carried * mm(query, low_memory) + mm(within, low_change))
        state[h] = kept * memory + mm(key, ending * change, (0, 0))
        delta_out[:, cols] = out
        normal = out * lax.rsqrt(jnp.mean(out * out, axis=1, keepdims=True) + 1e-5) * head_gain
        mixed[:, cols] = (normal * opened[:, cols] * live).astype(BF16)


def forward_mixer(tokens, w_query, w_key, w_value, w_gate, w_beta, taps_query, taps_key, taps_value, gain, gain_first, starts, lengths):
    slots, model = tokens.shape
    wide = w_query.shape[1]
    width = gain.shape[0]
    heads = wide // width
    seqs = starts.shape[1]
    chunks = slots // CHUNK
    taps = taps_query.shape[0]
    smem = pl.BlockSpec(memory_space=pltpu.SMEM)
    whole = lambda shape: pl.BlockSpec(shape, lambda n: (0,) * len(shape))
    piece = lambda shape: pl.BlockSpec(shape, lambda n: (n,) + (0,) * (len(shape) - 1))
    outs = [
        ((slots, wide), BF16), ((slots, wide), F32), ((slots, wide), F32), ((slots, wide), F32), ((slots, wide), F32),
        ((slots, heads), F32), ((slots, wide), F32), ((slots, wide), F32), ((slots, wide), F32),
        ((slots, wide), F32), ((slots, wide), BF16),
    ]
    return pl.pallas_call(
        functools.partial(forward_kernel, heads, width, seqs),
        name="mixer_forward",
        grid=(chunks,),
        out_shape=[jax.ShapeDtypeStruct(s, d) for s, d in outs]
        + [
            jax.ShapeDtypeStruct((chunks, heads, CHUNK, CHUNK), BF16),
            jax.ShapeDtypeStruct((chunks, heads, width, width), BF16),
        ],
        in_specs=[smem, smem, piece((CHUNK, model))]
        + [whole((model, wide))] * 4
        + [whole((model, heads))]
        + [whole((taps, wide))] * 3
        + [whole((1, width)), whole((1, model))],
        out_specs=[piece((CHUNK, s[1])) for s, d in outs]
        + [piece((1, heads, CHUNK, CHUNK)), piece((1, heads, width, width))],
        scratch_shapes=[pltpu.VMEM((CHUNK + 8, wide), F32)] * 3 + [pltpu.VMEM((heads, width, width), F32)],
        compiler_params=pltpu.CompilerParams(vmem_limit_bytes=56 << 20),
        cost_estimate=pl.CostEstimate(
            flops=2 * slots * model * wide * 4 + slots * heads * CHUNK * 2 * CHUNK * 20,
            bytes_accessed=slots * model * 2 + 4 * model * wide * 2 + slots * wide * 36,
            transcendentals=slots * wide * 4,
        ),
    )(starts, lengths, tokens, w_query, w_key, w_value, w_gate, w_beta, taps_query, taps_key, taps_value, gain.reshape(1, width), gain_first.reshape(1, model))


def backward_kernel(
    heads, width, seqs, chunks,
    starts, lengths, tokens, grad_attended, mixed, p_query, p_key, p_value, p_gate, p_beta,
    z_query, z_key, z_value, delta_out, change_in, inverse_in, state_in,
    w_query, w_key, w_value, w_gate, w_beta, w_out, taps_query, taps_key, taps_value, gain, gain_first,
    grad_normed, gw_query, gw_key, gw_value, gw_gate, gw_beta, gw_out,
    gt_query, gt_key, gt_value, g_gain, g_first,
    a_query, a_key, a_value, a_gate, a_out, head_query, head_key, head_value, flow,
):
    step = pl.program_id(0)
    size = tokens.shape[0]
    first = (chunks - 1 - step) * size

    @pl.when(step == 0)
    def _():
        for ref in (a_query, a_key, a_value, a_gate, gw_beta, a_out, gt_query, gt_key, gt_value, g_gain, g_first, flow):
            ref[...] = jnp.zeros_like(ref)
        for ref in (head_query, head_key, head_value):
            ref[size:, :] = jnp.zeros((8, ref.shape[1]), F32)

    rows, seg_rows, seg_columns, before, last = chunk_masks(starts, lengths, seqs, first, size)
    same = seg_rows == seg_columns
    i = lax.broadcasted_iota(jnp.int32, (size, size), 0)
    j = lax.broadcasted_iota(jnp.int32, (size, size), 1)
    strict = jnp.where(same & (i > j), 1.0, 0.0)
    inclusive = jnp.where(same & (i >= j), 1.0, 0.0)
    carried = jnp.where(seg_rows == before, 1.0, 0.0)
    ending = jnp.where(seg_rows == last, 1.0, 0.0)
    kept = jnp.where(before == last, 1.0, 0.0)
    live = jnp.where(seg_rows % 2 == 1, 1.0, 0.0)
    taps = taps_query.shape[0]
    joined = [
        jnp.where(segment_at(rows + offset, starts, lengths, seqs) == seg_rows, 1.0, 0.0)
        for offset in range(1, taps)
    ]
    normal_rows, unit_rows = normed_rows(tokens, gain_first)
    inputs = normal_rows.astype(BF16)
    grad_rows = grad_attended[...]
    grad_mixed = mm(grad_rows, w_out[...], (1, 1))
    a_out[...] += mm(mixed[...], grad_rows, (0, 0))
    strength = sigmoid(p_beta[...])
    scale = width ** (-0.5)
    head_gain = gain[...].astype(F32)

    grads_query, grads_key, grads_value, grads_gate, grads_beta = [], [], [], [], []
    for h in range(heads):
        cols = slice(h * width, (h + 1) * width)
        out = delta_out[:, cols]
        gate = p_gate[:, cols]
        sig_gate = sigmoid(gate)
        silu_gate = gate * sig_gate
        root = lax.rsqrt(jnp.mean(out * out, axis=1, keepdims=True) + 1e-5)
        grad = grad_mixed[:, cols] * live
        unit = out * root
        grads_gate.append(grad * unit * head_gain * (sig_gate * (1.0 + gate * (1.0 - sig_gate))))
        grad_normal = grad * silu_gate
        g_gain[...] += jnp.sum(grad_normal * unit, axis=0, keepdims=True)
        push = grad_normal * head_gain
        grad_out = scale * root * (push - unit * jnp.mean(push * unit, axis=1, keepdims=True))

        zq, zk, zv = z_query[:, cols], z_key[:, cols], z_value[:, cols]
        sq, sk, sv = sigmoid(zq), sigmoid(zk), sigmoid(zv)
        uq, uk = zq * sq, zk * sk
        nq = lax.rsqrt(jnp.sum(uq * uq, axis=1, keepdims=True) + 1e-6)
        nk = lax.rsqrt(jnp.sum(uk * uk, axis=1, keepdims=True) + 1e-6)
        unit_q, unit_k = uq * nq, uk * nk
        query, key = unit_q.astype(BF16), unit_k.astype(BF16)
        beta = strength[:, h : h + 1]
        change = change_in[:, cols]
        inverse = inverse_in[0, h]
        memory = state_in[0, h]
        flowing = flow[h]
        low_flow = flowing.astype(BF16)
        low_out = grad_out.astype(BF16)

        within = mm(query, key, (1, 1)) * inclusive
        grad_within = (mm(low_out, change, (1, 1)) * inclusive).astype(BF16)
        grad_change = mm(within, low_out, (0, 0)) + ending * mm(key, low_flow)
        grad_mid = mm(inverse, grad_change, (0, 0))
        grad_value = beta * grad_mid
        low_value = grad_value.astype(BF16)
        cross = (mm(low_value, change, (1, 1)) * strict).astype(BF16)
        grad_query = carried * mm(low_out, memory, (1, 1)) + mm(grad_within, key)
        grad_key = (
            mm(grad_within, query, (0, 0))
            + ending * mm(change, low_flow, (1, 1))
            - carried * mm(low_value, memory, (1, 1))
            - mm(cross, key)
            - mm(cross, key, (0, 0))
        )
        flow[h] = (
            kept * flowing
            + mm(query, carried * grad_out, (0, 0))
            - mm(key, carried * grad_value, (0, 0))
        )
        grads_beta.append((1.0 - beta) * jnp.sum(grad_mid * change.astype(F32), axis=1, keepdims=True))
        du_q = nq * (grad_query - unit_q * jnp.sum(grad_query * unit_q, axis=1, keepdims=True))
        du_k = nk * (grad_key - unit_k * jnp.sum(grad_key * unit_k, axis=1, keepdims=True))
        grads_query.append(du_q * sq * (1.0 + zq * (1.0 - sq)))
        grads_key.append(du_k * sk * (1.0 + zk * (1.0 - sk)))
        grads_value.append(grad_value * sv * (1.0 + zv * (1.0 - sv)))

    def unconv(parts, taps_ref, head, projected, grad_taps):
        grad = jnp.concatenate(parts, axis=1)
        head[0:size, :] = grad
        tap = taps_ref[...].astype(F32)
        p = projected[...]
        result = grad * tap[0:1]
        grad_taps[0:1, :] += jnp.sum(p * grad, axis=0, keepdims=True)
        for offset in range(1, taps):
            moved = head[offset : offset + size, :] * joined[offset - 1]
            result = result + moved * tap[offset : offset + 1]
            grad_taps[offset : offset + 1, :] += jnp.sum(p * moved, axis=0, keepdims=True)
        head[size:, :] = grad[0:8, :]
        return result.astype(BF16)

    d_query = unconv(grads_query, taps_query, head_query, p_query, gt_query)
    d_key = unconv(grads_key, taps_key, head_key, p_key, gt_key)
    d_value = unconv(grads_value, taps_value, head_value, p_value, gt_value)
    d_gate = jnp.concatenate(grads_gate, axis=1).astype(BF16)
    d_beta = jnp.concatenate(grads_beta, axis=1).astype(BF16)
    grad_inputs = (
        mm(d_query, w_query[...], (1, 1))
        + mm(d_key, w_key[...], (1, 1))
        + mm(d_value, w_value[...], (1, 1))
        + mm(d_gate, w_gate[...], (1, 1))
        + mm(d_beta, w_beta[...], (1, 1))
    )
    grad_normed[...] = grad_inputs.astype(BF16)
    g_first[...] += jnp.sum(grad_inputs * unit_rows, axis=0, keepdims=True)
    a_query[...] += mm(inputs, d_query, (0, 0))
    a_key[...] += mm(inputs, d_key, (0, 0))
    a_value[...] += mm(inputs, d_value, (0, 0))
    a_gate[...] += mm(inputs, d_gate, (0, 0))
    gw_beta[...] += mm(d_beta, inputs, (0, 0))

    @pl.when(step == chunks - 1)
    def _():
        for target, source in (
            (gw_query, a_query), (gw_key, a_key), (gw_value, a_value), (gw_gate, a_gate),
            (gw_out, a_out),
        ):
            target[...] = source[...].astype(target.dtype)


def backward_mixer(tokens, grad_attended, saved, w_query, w_key, w_value, w_gate, w_beta, w_out, taps_query, taps_key, taps_value, gain, gain_first, starts, lengths):
    slots, model = tokens.shape
    wide = w_query.shape[1]
    width = gain.shape[0]
    heads = wide // width
    seqs = starts.shape[1]
    chunks = slots // CHUNK
    taps = taps_query.shape[0]
    smem = pl.BlockSpec(memory_space=pltpu.SMEM)
    whole = lambda shape: pl.BlockSpec(shape, lambda n: (0,) * len(shape))
    fixed = lambda shape: pl.BlockSpec(shape, lambda n: (0,) * len(shape), pipeline_mode=pl.Buffered(1))
    piece = lambda shape: pl.BlockSpec(shape, lambda n: (chunks - 1 - n,) + (0,) * (len(shape) - 1))
    rows = lambda a: piece((CHUNK, a.shape[1]))
    outs = (
        [((slots, model), BF16)] + [((model, wide), BF16)] * 4 + [((heads, model), F32), ((wide, model), BF16)]
        + [((taps, wide), F32)] * 3 + [((1, width), F32), ((1, model), F32)]
    )
    return pl.pallas_call(
        functools.partial(backward_kernel, heads, width, seqs, chunks),
        name="mixer_backward",
        grid=(chunks,),
        out_shape=[jax.ShapeDtypeStruct(s, d) for s, d in outs],
        in_specs=[smem, smem, rows(tokens), rows(grad_attended)]
        + [rows(a) for a in saved[:11]]
        + [piece((1, heads, CHUNK, CHUNK)), piece((1, heads, width, width))]
        + [fixed((model, wide))] * 4
        + [fixed((model, heads)), fixed((wide, model))]
        + [fixed((taps, wide))] * 3
        + [fixed((1, width)), fixed((1, model))],
        out_specs=[piece((CHUNK, model))] + [whole(s) for s, d in outs[1:]],
        scratch_shapes=[pltpu.VMEM((model, wide), F32)] * 4
        + [pltpu.VMEM((wide, model), F32)]
        + [pltpu.VMEM((CHUNK + 8, wide), F32)] * 3
        + [pltpu.VMEM((heads, width, width), F32)],
        compiler_params=pltpu.CompilerParams(vmem_limit_bytes=60 << 20),
        cost_estimate=pl.CostEstimate(
            flops=2 * slots * model * wide * 10 + slots * heads * CHUNK * 2 * CHUNK * 8,
            bytes_accessed=slots * model * 6 + 10 * model * wide * 2 + slots * wide * 36,
            transcendentals=slots * wide * 8,
        ),
    )(starts, lengths, tokens, grad_attended, *saved, w_query, w_key, w_value, w_gate, w_beta, w_out, taps_query, taps_key, taps_value, gain.reshape(1, width), gain_first.reshape(1, model))


MESH = pl.DeviceIdType.MESH
SUBS = 2


def ring_position(device, count):
    half, odd = device // 2, device % 2
    return half + odd * (count - 1 - 2 * half)


def ring_device(position, count):
    back = position // (count // 2)
    return (1 - back) * 2 * position + back * (2 * (count - 1 - position) + 1)


class Ring:
    def __init__(self, count):
        self.count = count
        self.me = lax.axis_index("tensor")
        self.place = ring_position(self.me, count)
        self.group = lax.axis_index("dp")

    def at(self, offset):
        return ring_device((self.place + offset + 2 * self.count) % self.count, self.count)

    def next(self, way):
        return (self.group, self.at(1 if way == 0 else -1))

    def greet(self):
        barrier = pltpu.get_barrier_semaphore()
        for way in (0, 1):
            pl.semaphore_signal(barrier, inc=1, device_id=self.next(way), device_id_type=MESH)
        pl.semaphore_wait(barrier, 2)


def gather_copy(ring, source, target, sends, recvs, way, sub, step, origin, rows):
    piece = rows // (2 * SUBS)
    inside = way * (rows // 2) + sub * piece
    start = pl.multiple_of(origin * rows + inside, piece)
    src = target.at[pl.ds(start, piece), :] if source is None else source.at[pl.ds(inside, piece), :]
    return pltpu.make_async_remote_copy(
        src_ref=src,
        dst_ref=target.at[pl.ds(start, piece), :],
        send_sem=sends.at[way, sub, step],
        recv_sem=recvs.at[way, sub, step],
        device_id=ring.next(way),
        device_id_type=MESH,
    )


def ring_gather(ring, source, target, sends, recvs, local, rows):
    count = ring.count
    keep = pltpu.make_async_copy(
        source, target.at[pl.ds(pl.multiple_of(ring.me * rows, rows), rows), :], local
    )
    keep.start()
    pairs = [(sub, way) for sub in range(SUBS) for way in (0, 1)]
    for sub, way in pairs:
        gather_copy(ring, source, target, sends, recvs, way, sub, 0, ring.me, rows).start()

    def origin(way, step):
        return ring.at(-step if way == 0 else step)

    def forward(step, carry):
        for sub, way in pairs:
            gather_copy(
                ring, None, target, sends, recvs, way, sub, step - 1, origin(way, step), rows
            ).wait_recv()
            gather_copy(
                ring, None, target, sends, recvs, way, sub, step, origin(way, step), rows
            ).start()
        return carry

    lax.fori_loop(1, count - 1, forward, 0)
    for sub, way in pairs:
        gather_copy(
            ring, None, target, sends, recvs, way, sub, count - 2, origin(way, count - 1), rows
        ).wait_recv()

    def drain(step, carry):
        for sub, way in pairs:
            gather_copy(ring, None, target, sends, recvs, way, sub, step, ring.me, rows).wait_send()
        return carry

    lax.fori_loop(0, count - 1, drain, 0)
    keep.wait()


def scatter_copy(ring, slots, sends, recvs, way, sub, step):
    return pltpu.make_async_remote_copy(
        src_ref=slots.at[way, sub, step],
        dst_ref=slots.at[way, sub, step + 1],
        send_sem=sends.at[way, sub, step],
        recv_sem=recvs.at[way, sub, step],
        device_id=ring.next(way),
        device_id_type=MESH,
    )


def ring_scatter(ring, partial, slots, sends, recvs, rows, finish):
    count = ring.count
    piece = rows // (2 * SUBS)
    pairs = [(sub, way) for sub in range(SUBS) for way in (0, 1)]

    def begin(way, sub, owner):
        return pl.multiple_of(owner * rows + way * (rows // 2) + sub * piece, piece)

    def owner_at(way, step):
        return ring.at(-1 - step if way == 0 else 1 + step)

    for sub, way in pairs:
        slots[way, sub, 0] = partial(begin(way, sub, owner_at(way, 0)), piece).astype(BF16)
        scatter_copy(ring, slots, sends, recvs, way, sub, 0).start()

    def hop(step, carry):
        for sub, way in pairs:
            term = partial(begin(way, sub, owner_at(way, step)), piece)
            scatter_copy(ring, slots, sends, recvs, way, sub, step - 1).wait_recv()
            slots[way, sub, step] = (slots[way, sub, step].astype(F32) + term).astype(BF16)
            scatter_copy(ring, slots, sends, recvs, way, sub, step).start()
        return carry

    lax.fori_loop(1, count - 1, hop, 0)
    for sub, way in pairs:
        term = partial(begin(way, sub, ring.me), piece)
        scatter_copy(ring, slots, sends, recvs, way, sub, count - 2).wait_recv()
        finish(way * (rows // 2) + sub * piece, piece, slots[way, sub, count - 1].astype(F32) + term)

    def drain(step, carry):
        for sub, way in pairs:
            scatter_copy(ring, slots, sends, recvs, way, sub, step).wait_send()
        return carry

    lax.fori_loop(0, count - 1, drain, 0)


def ring_semaphores(count):
    return [pltpu.SemaphoreType.DMA((2, SUBS, count - 1))] * 2


def ring_slots(count, rows, columns):
    return pltpu.VMEM((2, SUBS, count, rows // (2 * SUBS), columns), BF16)


ANY = pl.BlockSpec(memory_space=pl.ANY)
VMEM = pl.BlockSpec(memory_space=pltpu.VMEM)


def ring_params(number):
    return pltpu.CompilerParams(
        collective_id=number, has_side_effects=True, vmem_limit_bytes=56 << 20
    )


def gather_kernel(count, rows, source, target, sends, recvs, local):
    ring = Ring(count)
    ring.greet()
    ring_gather(ring, source, target, sends, recvs, local, rows)


def gather_tokens(tokens, count):
    rows, model = tokens.shape
    return pl.pallas_call(
        functools.partial(gather_kernel, count, rows),
        name="gather_tokens",
        out_shape=jax.ShapeDtypeStruct((count * rows, model), tokens.dtype),
        in_specs=[ANY],
        out_specs=ANY,
        scratch_shapes=ring_semaphores(count) + [pltpu.SemaphoreType.DMA],
        compiler_params=ring_params(1),
        cost_estimate=pl.CostEstimate(flops=0, bytes_accessed=300 << 20, transcendentals=0),
    )(tokens)


def attend_kernel(
    count, rows, mixed, w_out, tokens, gain, resid, full,
    slots, low, sends, recvs, sends_two, recvs_two, local,
):
    ring = Ring(count)
    ring.greet()

    def partial(start, size):
        return mm(mixed[pl.ds(start, size), :], w_out[...])

    def finish(start, size, attended):
        value = tokens[start : start + size, :].astype(F32) + attended
        resid[start : start + size, :] = value
        scale = lax.rsqrt(jnp.mean(value * value, axis=1, keepdims=True) + 1e-6)
        low[start : start + size, :] = (value * scale * gain[...].astype(F32)).astype(BF16)

    ring_scatter(ring, partial, slots, sends, recvs, rows, finish)
    ring_gather(ring, low, full, sends_two, recvs_two, local, rows)


def attend(mixed, w_out, tokens, gain, count):
    rows, model = tokens.shape
    return pl.pallas_call(
        functools.partial(attend_kernel, count, rows),
        name="attend",
        out_shape=[
            jax.ShapeDtypeStruct((rows, model), F32),
            jax.ShapeDtypeStruct((count * rows, model), BF16),
        ],
        in_specs=[VMEM] * 4,
        out_specs=[VMEM, ANY],
        scratch_shapes=[ring_slots(count, rows, model), pltpu.VMEM((rows, model), BF16)]
        + ring_semaphores(count) * 2
        + [pltpu.SemaphoreType.DMA],
        compiler_params=ring_params(2),
        cost_estimate=pl.CostEstimate(
            flops=2 * count * rows * model * mixed.shape[1], bytes_accessed=600 << 20, transcendentals=0
        ),
    )(mixed, w_out, tokens, gain.reshape(1, model))


def norm_back(inputs, scale, gain, grad_normed):
    weighted = gain * grad_normed
    inner = jnp.mean(weighted * inputs, axis=1, keepdims=True)
    unit = inputs * scale
    return scale * weighted - unit * (scale * scale * inner), grad_normed * unit


def ffn_back_kernel(
    count, rows, grad_gate, grad_up, w_gate, w_up, resid, cotangent, gain, grad_resid, full, grad_gain,
    slots, low, sends, recvs, sends_two, recvs_two, local,
):
    ring = Ring(count)
    ring.greet()
    grad_gain[...] = jnp.zeros_like(grad_gain)

    def partial(start, size):
        return mm(grad_gate[pl.ds(start, size), :], w_gate[...], (1, 1)) + mm(
            grad_up[pl.ds(start, size), :], w_up[...], (1, 1)
        )

    def finish(start, size, grad):
        value = resid[start : start + size, :]
        scale = lax.rsqrt(jnp.mean(value * value, axis=1, keepdims=True) + 1e-6)
        through, pieces = norm_back(value, scale, gain[...].astype(F32), grad)
        result = cotangent[start : start + size, :].astype(F32) + through
        grad_resid[start : start + size, :] = result
        grad_gain[...] += jnp.sum(pieces, axis=0, keepdims=True)
        low[start : start + size, :] = result.astype(BF16)

    ring_scatter(ring, partial, slots, sends, recvs, rows, finish)
    ring_gather(ring, low, full, sends_two, recvs_two, local, rows)


def ffn_back(grad_gate, grad_up, w_gate, w_up, resid, cotangent, gain, count):
    rows, model = resid.shape
    return pl.pallas_call(
        functools.partial(ffn_back_kernel, count, rows),
        name="ffn_back",
        out_shape=[
            jax.ShapeDtypeStruct((rows, model), F32),
            jax.ShapeDtypeStruct((count * rows, model), BF16),
            jax.ShapeDtypeStruct((1, model), F32),
        ],
        in_specs=[VMEM] * 7,
        out_specs=[VMEM, ANY, VMEM],
        scratch_shapes=[ring_slots(count, rows, model), pltpu.VMEM((rows, model), BF16)]
        + ring_semaphores(count) * 2
        + [pltpu.SemaphoreType.DMA],
        compiler_params=ring_params(3),
        cost_estimate=pl.CostEstimate(
            flops=4 * count * rows * model * grad_up.shape[1], bytes_accessed=600 << 20, transcendentals=0
        ),
    )(grad_gate, grad_up, w_gate, w_up, resid, cotangent, gain.reshape(1, model))


def last_kernel(
    count, groups, rows, terms, tokens, grad_resid, gain, small, grad_tokens, total,
    slots, first_box, second_box, second_own, sends, recvs, first_sends, first_recvs, second_sends, second_recvs,
):
    ring = Ring(count)
    me, group = ring.me, ring.group
    barrier = pltpu.get_barrier_semaphore()
    first_peers = [(group, (me + k) % count) for k in range(1, count)]
    second_peers = [((group + k) % groups, me) for k in range(1, groups)]
    for peer in first_peers + second_peers:
        pl.semaphore_signal(barrier, inc=1, device_id=peer, device_id_type=MESH)
    pl.semaphore_wait(barrier, count + groups - 2)

    def first(k):
        return pltpu.make_async_remote_copy(
            src_ref=small.at[0:8], dst_ref=first_box.at[k], send_sem=first_sends.at[k],
            recv_sem=first_recvs.at[k], device_id=first_peers[k], device_id_type=MESH,
        )

    def second(k):
        return pltpu.make_async_remote_copy(
            src_ref=second_own, dst_ref=second_box.at[k], send_sem=second_sends.at[k],
            recv_sem=second_recvs.at[k], device_id=second_peers[k], device_id_type=MESH,
        )

    for k in range(count - 1):
        first(k).start()
    for k in range(count - 1):
        first(k).wait()
    mine = small[0:8]
    for k in range(count - 1):
        mine = mine + first_box[k]
    second_own[0:8] = mine
    second_own[8:] = small[8:]
    for k in range(groups - 1):
        second(k).start()

    def partial(start, size):
        return terms[pl.ds(start, size), :].astype(F32)

    def finish(start, size, grad):
        value = tokens[start : start + size, :].astype(F32)
        scale = lax.rsqrt(jnp.mean(value * value, axis=1, keepdims=True) + 1e-6)
        through, pieces = norm_back(value, scale, gain[...].astype(F32), grad)
        grad_tokens[start : start + size, :] = grad_resid[start : start + size, :] + through

    ring_scatter(ring, partial, slots, sends, recvs, rows, finish)
    for k in range(groups - 1):
        second(k).wait()
    mine = second_own[...]
    for k in range(groups - 1):
        mine = mine + second_box[k]
    total[...] = mine


def last_step(terms, tokens, grad_resid, gain, small, count, groups):
    rows, model = tokens.shape
    return pl.pallas_call(
        functools.partial(last_kernel, count, groups, rows),
        name="last_step",
        out_shape=[jax.ShapeDtypeStruct((rows, model), F32), jax.ShapeDtypeStruct(small.shape, F32)],
        in_specs=[VMEM] * 5,
        out_specs=[VMEM, VMEM],
        scratch_shapes=[
            ring_slots(count, rows, model),
            pltpu.VMEM((count - 1, 8, model), F32),
            pltpu.VMEM((groups - 1,) + small.shape, F32),
            pltpu.VMEM(small.shape, F32),
        ]
        + ring_semaphores(count)
        + [pltpu.SemaphoreType.DMA((count - 1,))] * 2
        + [pltpu.SemaphoreType.DMA((groups - 1,))] * 2,
        compiler_params=ring_params(4),
        cost_estimate=pl.CostEstimate(flops=0, bytes_accessed=300 << 20, transcendentals=0),
    )(terms, tokens, grad_resid, gain.reshape(1, model), small)


def swap(value, distance, count):
    if distance == "core":
        pairs = [(i, i + 1 - 2 * (i % 2)) for i in range(count)]
    else:
        pairs = [(i, (i + 2 * distance) % count) for i in range(count)]
    return lax.ppermute(value, "dp", pairs)


def sum_groups(value, count):
    rows = value.shape[0] // 2
    core = lax.axis_index("dp") % 2
    here = lax.dynamic_slice_in_dim(value, core * rows, rows, 0)
    away = lax.dynamic_slice_in_dim(value, (1 - core) * rows, rows, 0)
    here = (here.astype(F32) + swap(away, "core", count).astype(F32)).astype(BF16)
    total = here.astype(F32)
    for distance in range(1, count // 2):
        total = total + swap(here, distance, count).astype(F32)
    here = total.astype(BF16)
    other = swap(here, "core", count)
    lower = jnp.where(core == 0, here, other)
    upper = jnp.where(core == 0, other, here)
    return jnp.concatenate([lower, upper], 0).astype(F32)


def silu_parts(value):
    sig = jax.nn.sigmoid(value)
    return sig, value * sig


def make_shards(groups, count):
    def shards(
        tokens, attn_gain, w_query, w_key, w_value, conv_query, conv_key, conv_value, w_beta, w_gate_out,
        head_gain, w_out, ffn_gain, w_gate, w_up, w_down, seq_starts, seq_lengths, cotangent,
    ):
        model = tokens.shape[1]
        tokens_full = gather_tokens(tokens, count)
        late_cotangent, tokens_full = lax.optimization_barrier((cotangent, tokens_full))
        grad_full = lax.all_gather(late_cotangent, "tensor", axis=0, tiled=True)
        saved = forward_mixer(
            tokens_full, w_query, w_key, w_value, w_gate_out, w_beta,
            conv_query, conv_key, conv_value, head_gain, attn_gain, seq_starts, seq_lengths,
        )
        resid, ffn_full = attend(saved[0], w_out, tokens, ffn_gain, count)
        gate_pre = jnp.dot(ffn_full, w_gate, preferred_element_type=F32)
        up_pre = jnp.dot(ffn_full, w_up, preferred_element_type=F32)
        sig, silu_gate = silu_parts(gate_pre)
        hidden = (silu_gate * up_pre).astype(BF16)
        down = jnp.dot(hidden, w_down, preferred_element_type=F32).astype(BF16)
        grad_hidden = jnp.einsum("sd,fd->sf", grad_full, w_down, preferred_element_type=F32)
        grad_gate = (grad_hidden * up_pre * sig * (1.0 + gate_pre * (1.0 - sig))).astype(BF16)
        grad_up = (grad_hidden * silu_gate).astype(BF16)
        grad_resid, grad_attended, g_second = ffn_back(
            grad_gate, grad_up, w_gate, w_up, resid, cotangent, ffn_gain, count
        )
        gw_down = jnp.einsum("sf,sd->fd", hidden, grad_full, preferred_element_type=F32)
        gw_gate = jnp.einsum("sd,sf->df", ffn_full, grad_gate, preferred_element_type=F32)
        gw_up = jnp.einsum("sd,sf->df", ffn_full, grad_up, preferred_element_type=F32)
        ffn_grads = [sum_groups(g.astype(BF16), groups) for g in (gw_gate, gw_up, gw_down)]
        output = resid + lax.psum_scatter(
            down, "tensor", scatter_dimension=0, tiled=True
        ).astype(F32)
        pulled = backward_mixer(
            tokens_full, grad_attended, saved, w_query, w_key, w_value, w_gate_out, w_beta, w_out,
            conv_query, conv_key, conv_value, head_gain, attn_gain, seq_starts, seq_lengths,
        )
        terms, gw_query, gw_key, gw_value, gw_gate_out, gw_beta, gw_out = pulled[:7]
        gt_query, gt_key, gt_value, g_head, g_first = pulled[7:]
        wide = gt_query.shape[1]
        heads = gw_beta.shape[0]
        taps = gt_query.shape[0]
        small = jnp.concatenate(
            [
                g_first,
                g_second,
                jnp.pad(g_head, ((0, 0), (0, model - g_head.shape[1]))),
                jnp.zeros((5, model), F32),
                gw_beta,
                jnp.pad(
                    jnp.concatenate([gt_query, gt_key, gt_value], 1), ((0, 0), (0, model - 3 * wide))
                ),
                jnp.zeros((-(heads + taps) % 8, model), F32),
            ],
            0,
        )
        grad_tokens, total = last_step(terms, tokens, grad_resid, attn_gain, small, count, groups)
        mixer_grads = [
            sum_groups(g, groups) for g in (gw_query, gw_key, gw_value, gw_gate_out, gw_out)
        ]
        tap_rows = total[8 + heads : 8 + heads + taps]
        return (
            output.astype(BF16),
            grad_tokens,
            total[0],
            mixer_grads[0],
            mixer_grads[1],
            mixer_grads[2],
            tap_rows[:, :wide],
            tap_rows[:, wide : 2 * wide],
            tap_rows[:, 2 * wide : 3 * wide],
            total[8 : 8 + heads].T,
            mixer_grads[3],
            total[2, : head_gain.shape[0]],
            mixer_grads[4],
            total[1],
            ffn_grads[0],
            ffn_grads[1],
            ffn_grads[2],
        )

    return shards


def solution(mesh):
    placed = (
        P(("dp", "tensor"), None),
        P(),
        P(None, "tensor"),
        P(None, "tensor"),
        P(None, "tensor"),
        P(None, "tensor"),
        P(None, "tensor"),
        P(None, "tensor"),
        P(None, "tensor"),
        P(None, "tensor"),
        P(),
        P("tensor", None),
        P(),
        P(None, "tensor"),
        P(None, "tensor"),
        P("tensor", None),
        P("dp", None),
        P("dp", None),
        P(("dp", "tensor"), None),
    )
    return jax.shard_map(
        make_shards(mesh.shape["dp"], mesh.shape["tensor"]),
        mesh=mesh,
        in_specs=placed,
        out_specs=(
            P(("dp", "tensor"), None),
            P(("dp", "tensor"), None),
            P(),
            P(None, "tensor"),
            P(None, "tensor"),
            P(None, "tensor"),
            P(None, "tensor"),
            P(None, "tensor"),
            P(None, "tensor"),
            P(None, "tensor"),
            P(None, "tensor"),
            P(),
            P("tensor", None),
            P(),
            P(None, "tensor"),
            P(None, "tensor"),
            P("tensor", None),
        ),
        check_vma=False,
    )
```

```python
import functools
import jax
import jax.numpy as jnp
from jax import lax
from jax.experimental import pallas as pl
from jax.experimental.pallas import tpu as pltpu
from jax.sharding import PartitionSpec as P

CHUNK = 256
F32, BF16 = jnp.float32, jnp.bfloat16


def mm(a, b, contract=(1, 0)):
    return lax.dot_general(
        a.astype(BF16),
        b.astype(BF16),
        (((contract[0],), (contract[1],)), ((), ())),
        preferred_element_type=F32,
    )


def segment_at(places, starts, lengths, seqs):
    segment = jnp.zeros_like(places)
    for s in range(seqs):
        begin = starts[0, s]
        stop = begin + lengths[0, s]
        segment = segment + jnp.where(places >= begin, 1, 0) + jnp.where(places >= stop, 1, 0)
    return jnp.where(places < 0, -1, segment)


def chunk_masks(starts, lengths, seqs, first, size):
    rows = first + lax.broadcasted_iota(jnp.int32, (size, 1), 0)
    columns = first + lax.broadcasted_iota(jnp.int32, (1, size), 1)
    seg_rows = segment_at(rows, starts, lengths, seqs)
    seg_columns = segment_at(columns, starts, lengths, seqs)
    before = segment_at(jnp.full((1, 1), first - 1, jnp.int32), starts, lengths, seqs)
    last = segment_at(jnp.full((1, 1), first + size - 1, jnp.int32), starts, lengths, seqs)
    return rows, seg_rows, seg_columns, before, last


def inverse_unit_lower(lower, size):
    i = lax.broadcasted_iota(jnp.int32, (size, size), 0)
    j = lax.broadcasted_iota(jnp.int32, (size, size), 1)

    def corner(width):
        shift = width.bit_length() - 1
        pair = (i >> (shift + 1)) == (j >> (shift + 1))
        return pair & (((i >> shift) & 1) == 1) & (((j >> shift) & 1) == 0)

    inverse = jnp.where(i == j, 1.0, 0.0) - jnp.where(corner(1), lower, 0.0)
    width = 2
    while width < size:
        low = inverse.astype(BF16)
        if 2 * width == size:
            part = mm(mm(low[width:, width:], lower[width:, :width]), low[:width, :width])
            inverse = jnp.concatenate(
                [
                    inverse[:width],
                    jnp.concatenate([-part, inverse[width:, width:]], axis=1),
                ],
                axis=0,
            )
        else:
            between = jnp.where(corner(width), lower, 0.0)
            inverse = inverse - mm(mm(low, between), low)
        width *= 2
    return inverse


def sigmoid(v):
    return 1.0 / (1.0 + jnp.exp(-v))


def normed_rows(tokens, gain):
    value = tokens[...].astype(F32)
    unit = value * lax.rsqrt(jnp.mean(value * value, axis=1, keepdims=True) + 1e-6)
    return unit * gain[...].astype(F32), unit


MESH = pl.DeviceIdType.MESH
SUBS = 2


def ring_position(device, count):
    half, odd = device // 2, device % 2
    return half + odd * (count - 1 - 2 * half)


def ring_device(position, count):
    back = position // (count // 2)
    return (1 - back) * 2 * position + back * (2 * (count - 1 - position) + 1)


class Ring:
    def __init__(self, count):
        self.count = count
        self.me = lax.axis_index("tensor")
        self.place = ring_position(self.me, count)
        self.group = lax.axis_index("dp")

    def at(self, offset):
        return ring_device((self.place + offset + 2 * self.count) % self.count, self.count)

    def next(self, way):
        return (self.group, self.at(1 if way == 0 else -1))


def gather_copy(ring, source, target, sends, recvs, way, sub, step, origin, rows):
    piece = rows // (2 * SUBS)
    inside = way * (rows // 2) + sub * piece
    start = pl.multiple_of(origin * rows + inside, piece)
    src = target.at[pl.ds(start, piece), :] if source is None else source.at[pl.ds(inside, piece), :]
    return pltpu.make_async_remote_copy(
        src_ref=src,
        dst_ref=target.at[pl.ds(start, piece), :],
        send_sem=sends.at[way, sub, step],
        recv_sem=recvs.at[way, sub, step],
        device_id=ring.next(way),
        device_id_type=MESH,
    )


PAIRS = [(sub, way) for sub in range(SUBS) for way in (0, 1)]


class Gather:
    def __init__(self, ring, source, target, sends, recvs, local, rows):
        self.ring, self.source, self.target = ring, source, target
        self.sends, self.recvs, self.rows = sends, recvs, rows
        self.keep = pltpu.make_async_copy(
            source, target.at[pl.ds(pl.multiple_of(ring.me * rows, rows), rows), :], local
        )

    def origin(self, way, step):
        return self.ring.at(-step if way == 0 else step)

    def copy(self, way, sub, step, origin, source=None):
        return gather_copy(
            self.ring, source, self.target, self.sends, self.recvs, way, sub, step, origin, self.rows
        )

    def begin(self):
        self.keep.start()
        for sub, way in PAIRS:
            self.copy(way, sub, 0, self.ring.me, self.source).start()

    def arrived(self, step):
        for sub, way in PAIRS:
            self.copy(way, sub, step - 1, self.origin(way, step)).wait_recv()

    def hop(self, step):
        for sub, way in PAIRS:
            self.copy(way, sub, step - 1, self.origin(way, step)).wait_recv()
            self.copy(way, sub, step, self.origin(way, step)).start()

    def end(self):
        def drain(step, carry):
            for sub, way in PAIRS:
                self.copy(way, sub, step, self.ring.me).wait_send()
            return carry

        lax.fori_loop(0, self.ring.count - 1, drain, 0)
        self.keep.wait()


def ring_gather(ring, source, target, sends, recvs, local, rows, between=None):
    gather = Gather(ring, source, target, sends, recvs, local, rows)
    gather.begin()

    def forward(step, carry):
        gather.hop(step)
        if between is not None:
            between(step)
        return carry

    lax.fori_loop(1, ring.count - 1, forward, 0)
    gather.arrived(ring.count - 1)
    if between is not None:
        between(ring.count - 1)
    gather.end()


def scatter_copy(ring, slots, sends, recvs, way, sub, step):
    return pltpu.make_async_remote_copy(
        src_ref=slots.at[way, sub, step],
        dst_ref=slots.at[way, sub, step + 1],
        send_sem=sends.at[way, sub, step],
        recv_sem=recvs.at[way, sub, step],
        device_id=ring.next(way),
        device_id_type=MESH,
    )


class Scatter:
    def __init__(self, ring, partial, slots, sends, recvs, rows, finish):
        self.ring, self.partial, self.slots, self.sends, self.recvs = ring, partial, slots, sends, recvs
        self.half, self.finish = rows // 2, finish
        self.rows, self.piece = rows, rows // (2 * SUBS)

    def terms(self, first, second):
        half = self.half
        return self.partial(
            pl.multiple_of(first * self.rows, half), pl.multiple_of(second * self.rows + half, half)
        )

    def part(self, terms, way, sub):
        start = way * self.half + sub * self.piece
        return terms[start : start + self.piece]

    def copy(self, way, sub, step):
        return scatter_copy(self.ring, self.slots, self.sends, self.recvs, way, sub, step)

    def begin(self):
        terms = self.terms(self.ring.at(-1), self.ring.at(1))
        for sub, way in PAIRS:
            self.slots[way, sub, 0] = self.part(terms, way, sub).astype(BF16)
            self.copy(way, sub, 0).start()

    def hop(self, step):
        terms = self.terms(self.ring.at(-1 - step), self.ring.at(1 + step))
        for sub, way in PAIRS:
            self.copy(way, sub, step - 1).wait_recv()
            self.slots[way, sub, step] = (
                self.slots[way, sub, step].astype(F32) + self.part(terms, way, sub)
            ).astype(BF16)
            self.copy(way, sub, step).start()

    def end(self):
        count = self.ring.count
        terms = self.terms(self.ring.me, self.ring.me)
        for sub, way in PAIRS:
            self.copy(way, sub, count - 2).wait_recv()
            self.finish(
                way * self.half + sub * self.piece,
                self.piece,
                self.slots[way, sub, count - 1].astype(F32) + self.part(terms, way, sub),
            )

        def drain(step, carry):
            for sub, way in PAIRS:
                self.copy(way, sub, step).wait_send()
            return carry

        lax.fori_loop(0, count - 1, drain, 0)


def ring_scatter(ring, partial, slots, sends, recvs, rows, finish, between=None):
    scatter = Scatter(ring, partial, slots, sends, recvs, rows, finish)
    scatter.begin()

    def forward(step, carry):
        scatter.hop(step)
        if between is not None:
            between(step)
        return carry

    lax.fori_loop(1, ring.count - 1, forward, 0)
    scatter.end()


class GroupSum:
    def __init__(self, ring, groups, grads, near, far, targets, near_sems, far_sems, back_sems, keep_sems):
        self.ring, self.groups, self.grads, self.near, self.far, self.targets = ring, groups, grads, near, far, targets
        self.near_sems, self.far_sems, self.back_sems, self.keep_sems = near_sems, far_sems, back_sems, keep_sems
        self.core = ring.group % 2
        self.mate = (ring.group + 1 - 2 * self.core, ring.me)

    def peers(self):
        return [self.mate] + [
            ((self.ring.group + 2 * k) % self.groups, self.ring.me) for k in range(1, self.groups // 2)
        ]

    def half(self, i, core):
        rows = self.near[i].shape[0]
        return pl.ds(pl.multiple_of(core * rows, rows), rows)

    def near_copy(self, i):
        return pltpu.make_async_remote_copy(
            src_ref=self.grads[i].at[self.half(i, 1 - self.core), :], dst_ref=self.near[i],
            send_sem=self.near_sems.at[0, i], recv_sem=self.near_sems.at[1, i],
            device_id=self.mate, device_id_type=MESH,
        )

    def far_copy(self, i, k):
        return pltpu.make_async_remote_copy(
            src_ref=self.near[i], dst_ref=self.far[i].at[k - 1],
            send_sem=self.far_sems.at[0, i, k - 1], recv_sem=self.far_sems.at[1, i, k - 1],
            device_id=((self.ring.group + 2 * k) % self.groups, self.ring.me), device_id_type=MESH,
        )

    def back_copy(self, i):
        return pltpu.make_async_remote_copy(
            src_ref=self.far[i].at[0], dst_ref=self.targets[i].at[self.half(i, self.core), :],
            send_sem=self.back_sems.at[0, i], recv_sem=self.back_sems.at[1, i],
            device_id=self.mate, device_id_type=MESH,
        )

    def keep_copy(self, i):
        return pltpu.make_async_copy(
            self.far[i].at[0], self.targets[i].at[self.half(i, self.core), :], self.keep_sems.at[i]
        )

    def first(self):
        for i in range(len(self.grads)):
            self.near_copy(i).start()

    def second(self):
        for i in range(len(self.grads)):
            self.near_copy(i).wait_recv()
            rows = self.near[i].shape[0]
            block = next(size for size in (64, 32, 16) if rows % size == 0)

            def add(at, carry, i=i, rows=rows, block=block):
                here = pl.ds(pl.multiple_of(at * block, block), block)
                own = pl.ds(pl.multiple_of(self.core * rows + at * block, block), block)
                self.near[i][here, :] = (
                    self.near[i][here, :].astype(F32) + self.grads[i][own, :].astype(F32)
                ).astype(BF16)
                return carry

            lax.fori_loop(0, rows // block, add, 0)
            for k in range(1, self.groups // 2):
                self.far_copy(i, k).start()

    def third(self):
        for i in range(len(self.grads)):
            for k in range(1, self.groups // 2):
                self.far_copy(i, k).wait()
            rows = self.near[i].shape[0]
            block = next(size for size in (64, 32, 16) if rows % size == 0)

            def add(at, carry, i=i, block=block):
                here = pl.ds(pl.multiple_of(at * block, block), block)
                total = self.near[i][here, :].astype(F32)
                for k in range(self.groups // 2 - 1):
                    total = total + self.far[i][k, here, :].astype(F32)
                self.far[i][0, here, :] = total.astype(BF16)
                return carry

            lax.fori_loop(0, rows // block, add, 0)
            self.keep_copy(i).start()
            self.back_copy(i).start()

    def last(self):
        for i in range(len(self.grads)):
            self.near_copy(i).wait_send()
            self.back_copy(i).wait()
            self.keep_copy(i).wait()


def sum_scratch(shapes, groups):
    number = len(shapes)
    return (
        [pltpu.VMEM((rows // 2, columns), BF16) for rows, columns in shapes]
        + [pltpu.VMEM((groups // 2 - 1, rows // 2, columns), BF16) for rows, columns in shapes]
        + [
            pltpu.SemaphoreType.DMA((2, number)),
            pltpu.SemaphoreType.DMA((2, number, groups // 2 - 1)),
            pltpu.SemaphoreType.DMA((2, number)),
            pltpu.SemaphoreType.DMA((number,)),
        ]
    )


def greet(ring, others=()):
    barrier = pltpu.get_barrier_semaphore()
    peers = [ring.next(0), ring.next(1)] + list(others)
    for peer in peers:
        pl.semaphore_signal(barrier, inc=1, device_id=peer, device_id_type=MESH)
    pl.semaphore_wait(barrier, len(peers))


def ring_semaphores(count):
    return [pltpu.SemaphoreType.DMA((2, SUBS, count - 1))] * 2


def ring_slots(count, rows, columns):
    return pltpu.VMEM((2, SUBS, count, rows // (2 * SUBS), columns), BF16)


ANY = pl.BlockSpec(memory_space=pl.ANY)
VMEM = pl.BlockSpec(memory_space=pltpu.VMEM)


def ring_params(number):
    return pltpu.CompilerParams(
        collective_id=number, has_side_effects=True, vmem_limit_bytes=60 << 20
    )


def gather_kernel(count, rows, source, target, sends, recvs, local):
    ring = Ring(count)
    greet(ring)
    ring_gather(ring, source, target, sends, recvs, local, rows)


def gather_tokens(tokens, count):
    rows, model = tokens.shape
    return pl.pallas_call(
        functools.partial(gather_kernel, count, rows),
        name="gather_tokens",
        out_shape=jax.ShapeDtypeStruct((count * rows, model), tokens.dtype),
        in_specs=[ANY],
        out_specs=ANY,
        scratch_shapes=ring_semaphores(count) + [pltpu.SemaphoreType.DMA],
        compiler_params=ring_params(1),
        cost_estimate=pl.CostEstimate(flops=0, bytes_accessed=300 << 20, transcendentals=0),
    )(tokens)


def attend_kernel(
    count, rows, mixed, w_out, tokens, gain, resid, full,
    slots, low, sends, recvs, sends_two, recvs_two, local,
):
    ring = Ring(count)
    greet(ring)

    half = rows // 2

    def partial(first, second):
        return mm(jnp.concatenate([mixed[pl.ds(first, half), :], mixed[pl.ds(second, half), :]], 0), w_out[...])

    def finish(start, size, attended):
        value = tokens[start : start + size, :].astype(F32) + attended
        resid[start : start + size, :] = value
        scale = lax.rsqrt(jnp.mean(value * value, axis=1, keepdims=True) + 1e-6)
        low[start : start + size, :] = (value * scale * gain[...].astype(F32)).astype(BF16)

    ring_scatter(ring, partial, slots, sends, recvs, rows, finish)
    ring_gather(ring, low, full, sends_two, recvs_two, local, rows)


def attend(mixed, w_out, tokens, gain, count):
    rows, model = tokens.shape
    return pl.pallas_call(
        functools.partial(attend_kernel, count, rows),
        name="attend",
        out_shape=[
            jax.ShapeDtypeStruct((rows, model), F32),
            jax.ShapeDtypeStruct((count * rows, model), BF16),
        ],
        in_specs=[VMEM] * 4,
        out_specs=[VMEM, ANY],
        scratch_shapes=[ring_slots(count, rows, model), pltpu.VMEM((rows, model), BF16)]
        + ring_semaphores(count) * 2
        + [pltpu.SemaphoreType.DMA],
        compiler_params=ring_params(2),
        cost_estimate=pl.CostEstimate(
            flops=2 * count * rows * model * mixed.shape[1], bytes_accessed=600 << 20, transcendentals=0
        ),
    )(mixed, w_out, tokens, gain.reshape(1, model))


def norm_back(inputs, scale, gain, grad_normed):
    weighted = gain * grad_normed
    inner = jnp.mean(weighted * inputs, axis=1, keepdims=True)
    unit = inputs * scale
    return scale * weighted - unit * (scale * scale * inner), grad_normed * unit


def ffn_back_kernel(
    count, groups, rows, grad_gate, grad_up, w_gate, w_up, resid, cotangent, gain, gw_one, gw_two, gw_three,
    grad_resid, full, grad_gain, sum_one, sum_two, sum_three,
    slots, low, *rest,
):
    ring = Ring(count)
    sends, recvs, sends_two, recvs_two, local = rest[:5]
    sums = GroupSum(
        ring, groups, (gw_one, gw_two, gw_three), rest[5:8], rest[8:11], (sum_one, sum_two, sum_three), *rest[11:]
    )
    greet(ring, sums.peers())
    sums.first()
    grad_gain[...] = jnp.zeros_like(grad_gain)
    half = rows // 2

    def partial(first, second):
        gates = jnp.concatenate([grad_gate[pl.ds(first, half), :], grad_gate[pl.ds(second, half), :]], 0)
        ups = jnp.concatenate([grad_up[pl.ds(first, half), :], grad_up[pl.ds(second, half), :]], 0)
        return mm(gates, w_gate[...]) + mm(ups, w_up[...])

    def finish(start, size, grad):
        value = resid[start : start + size, :]
        scale = lax.rsqrt(jnp.mean(value * value, axis=1, keepdims=True) + 1e-6)
        through, pieces = norm_back(value, scale, gain[...].astype(F32), grad)
        result = cotangent[start : start + size, :].astype(F32) + through
        grad_resid[start : start + size, :] = result
        grad_gain[...] += jnp.sum(pieces, axis=0, keepdims=True)
        low[start : start + size, :] = result.astype(BF16)

    def between(step):
        @pl.when(step == 2)
        def _():
            sums.second()

    def between_two(step):
        @pl.when(step == count - 2)
        def _():
            sums.third()

    ring_scatter(ring, partial, slots, sends, recvs, rows, finish, between)
    ring_gather(ring, low, full, sends_two, recvs_two, local, rows, between_two)
    sums.last()


def ffn_back(grad_gate, grad_up, w_gate, w_up, resid, cotangent, gain, grads, count, groups):
    rows, model = resid.shape
    return pl.pallas_call(
        functools.partial(ffn_back_kernel, count, groups, rows),
        name="ffn_back",
        out_shape=[
            jax.ShapeDtypeStruct((rows, model), F32),
            jax.ShapeDtypeStruct((count * rows, model), BF16),
            jax.ShapeDtypeStruct((1, model), F32),
        ]
        + [jax.ShapeDtypeStruct(g.shape, BF16) for g in grads],
        in_specs=[VMEM] * 10,
        out_specs=[VMEM, ANY, VMEM] + [ANY] * 3,
        scratch_shapes=[ring_slots(count, rows, model), pltpu.VMEM((rows, model), BF16)]
        + ring_semaphores(count) * 2
        + [pltpu.SemaphoreType.DMA]
        + sum_scratch([g.shape for g in grads], groups),
        compiler_params=ring_params(3),
        cost_estimate=pl.CostEstimate(
            flops=4 * count * rows * model * grad_up.shape[1], bytes_accessed=600 << 20, transcendentals=0
        ),
    )(grad_gate, grad_up, w_gate, w_up, resid, cotangent, gain.reshape(1, model), *grads)


def last_kernel(
    count, groups, rows, terms, tokens, grad_resid, gain, small, *rest,
):
    grads, rest = rest[:5], rest[5:]
    grad_tokens, total = rest[:2]
    targets, rest = rest[2:7], rest[7:]
    slots, first_box, second_box, second_own, sends, recvs = rest[:6]
    first_sends, first_recvs, second_sends, second_recvs = rest[6:10]
    ring = Ring(count)
    sums = GroupSum(ring, groups, grads, rest[10:15], rest[15:20], targets, *rest[20:])
    me, group = ring.me, ring.group
    first_peers = [(group, (me + k) % count) for k in range(1, count)]
    second_peers = [((group + k) % groups, me) for k in range(1, groups)]
    barrier = pltpu.get_barrier_semaphore()
    for peer in first_peers + second_peers:
        pl.semaphore_signal(barrier, inc=1, device_id=peer, device_id_type=MESH)
    pl.semaphore_wait(barrier, count + groups - 2)

    def first(k):
        return pltpu.make_async_remote_copy(
            src_ref=small.at[0:8], dst_ref=first_box.at[k], send_sem=first_sends.at[k],
            recv_sem=first_recvs.at[k], device_id=first_peers[k], device_id_type=MESH,
        )

    def second(k):
        return pltpu.make_async_remote_copy(
            src_ref=second_own, dst_ref=second_box.at[k], send_sem=second_sends.at[k],
            recv_sem=second_recvs.at[k], device_id=second_peers[k], device_id_type=MESH,
        )

    sums.first()
    for k in range(count - 1):
        first(k).start()
    half = rows // 2

    def partial(first, second):
        return jnp.concatenate([terms[pl.ds(first, half), :], terms[pl.ds(second, half), :]], 0).astype(F32)

    def finish(start, size, grad):
        value = tokens[start : start + size, :].astype(F32)
        scale = lax.rsqrt(jnp.mean(value * value, axis=1, keepdims=True) + 1e-6)
        through, pieces = norm_back(value, scale, gain[...].astype(F32), grad)
        grad_tokens[start : start + size, :] = grad_resid[start : start + size, :] + through

    def between(step):
        @pl.when(step == 1)
        def _():
            sums.second()
            for k in range(count - 1):
                first(k).wait()
            mine = small[0:8]
            for k in range(count - 1):
                mine = mine + first_box[k]
            second_own[0:8] = mine
            second_own[8:] = small[8:]
            for k in range(groups - 1):
                second(k).start()

        @pl.when(step == count - 2)
        def _():
            for k in range(groups - 1):
                second(k).wait()
            mine = second_own[...]
            for k in range(groups - 1):
                mine = mine + second_box[k]
            total[...] = mine
            sums.third()

    ring_scatter(ring, partial, slots, sends, recvs, rows, finish, between)
    sums.last()


def last_step(terms, tokens, grad_resid, gain, small, grads, count, groups):
    rows, model = tokens.shape
    return pl.pallas_call(
        functools.partial(last_kernel, count, groups, rows),
        name="last_step",
        out_shape=[jax.ShapeDtypeStruct((rows, model), F32), jax.ShapeDtypeStruct(small.shape, F32)]
        + [jax.ShapeDtypeStruct(g.shape, BF16) for g in grads],
        in_specs=[VMEM] * (5 + len(grads)),
        out_specs=[VMEM, VMEM] + [ANY] * len(grads),
        scratch_shapes=[
            ring_slots(count, rows, model),
            pltpu.VMEM((count - 1, 8, model), F32),
            pltpu.VMEM((groups - 1,) + small.shape, F32),
            pltpu.VMEM(small.shape, F32),
        ]
        + ring_semaphores(count)
        + [pltpu.SemaphoreType.DMA((count - 1,))] * 2
        + [pltpu.SemaphoreType.DMA((groups - 1,))] * 2
        + sum_scratch([g.shape for g in grads], groups),
        compiler_params=ring_params(4),
        cost_estimate=pl.CostEstimate(flops=0, bytes_accessed=300 << 20, transcendentals=0),
    )(terms, tokens, grad_resid, gain.reshape(1, model), small, *grads)


def spread_hops(step, chunks, count, begin, hop, end):
    each = -(-(count - 1) // (chunks - 1))

    @pl.when(step == 0)
    def _():
        begin()

    for place in range(each):
        number = step * each + place

        @pl.when((number > 0) & (number < count - 1))
        def _():
            hop(number)

    @pl.when(step == chunks - 1)
    def _():
        end()


def forward_kernel(
    heads, width, seqs, count, rows_own, chunks,
    starts, lengths, tokens, w_query, w_key, w_value, w_gate, w_beta,
    taps_query, taps_key, taps_value, gain, gain_first, side,
    mixed, p_query, p_key, p_value, p_gate, p_beta, z_query, z_key, z_value,
    delta_out, change_out, inverse_out, state_out, side_full,
    tail_query, tail_key, tail_value, state, sends, recvs, local,
):
    step = pl.program_id(0)
    size = tokens.shape[0]
    first = step * size

    @pl.when(step == 0)
    def _():
        for tail in (tail_query, tail_key, tail_value):
            tail[...] = jnp.zeros_like(tail)
        state[...] = jnp.zeros_like(state)

    ring = Ring(count)
    gather = Gather(ring, side, side_full, sends, recvs, local, rows_own)
    spread_hops(
        step, chunks, count,
        lambda: (greet(ring), gather.begin()),
        gather.hop,
        lambda: (gather.arrived(count - 1), gather.end()),
    )
    rows, seg_rows, seg_columns, before, last = chunk_masks(starts, lengths, seqs, first, size)
    same = seg_rows == seg_columns
    i = lax.broadcasted_iota(jnp.int32, (size, size), 0)
    j = lax.broadcasted_iota(jnp.int32, (size, size), 1)
    strict = jnp.where(same & (i > j), 1.0, 0.0)
    inclusive = jnp.where(same & (i >= j), 1.0, 0.0)
    carried = jnp.where(seg_rows == before, 1.0, 0.0)
    ending = jnp.where(seg_rows == last, 1.0, 0.0)
    kept = jnp.where(before == last, 1.0, 0.0)
    live = jnp.where(seg_rows % 2 == 1, 1.0, 0.0)
    joined = [
        jnp.where(segment_at(rows - offset, starts, lengths, seqs) == seg_rows, 1.0, 0.0)
        for offset in range(1, taps_query.shape[0])
    ]
    inputs = normed_rows(tokens, gain_first)[0].astype(BF16)

    def feature(weight, taps, tail, p_out, z_out):
        projected = jnp.dot(inputs, weight[...], preferred_element_type=F32)
        p_out[...] = projected
        tail[8:, :] = projected
        tap = taps[...].astype(F32)
        result = projected * tap[0:1]
        for offset in range(1, tap.shape[0]):
            result = result + tail[8 - offset : 8 - offset + size, :] * tap[offset : offset + 1] * joined[offset - 1]
        tail[0:8, :] = projected[size - 8 :, :]
        z_out[...] = result
        return result * sigmoid(result)

    u_query = feature(w_query, taps_query, tail_query, p_query, z_query)
    u_key = feature(w_key, taps_key, tail_key, p_key, z_key)
    u_value = feature(w_value, taps_value, tail_value, p_value, z_value)
    gate = jnp.dot(inputs, w_gate[...], preferred_element_type=F32)
    p_gate[...] = gate
    beta_pre = mm(inputs, w_beta[...], (1, 1))
    p_beta[...] = beta_pre
    strength = sigmoid(beta_pre)
    opened = gate * sigmoid(gate)
    scale = width ** (-0.5)
    head_gain = gain[...].astype(F32)
    for h in range(heads):
        cols = slice(h * width, (h + 1) * width)
        uq, uk = u_query[:, cols], u_key[:, cols]
        query = (uq * lax.rsqrt(jnp.sum(uq * uq, axis=1, keepdims=True) + 1e-6)).astype(BF16)
        key = (uk * lax.rsqrt(jnp.sum(uk * uk, axis=1, keepdims=True) + 1e-6)).astype(BF16)
        value = u_value[:, cols].astype(BF16).astype(F32)
        beta = strength[:, h : h + 1]
        memory = state[h]
        low_memory = memory.astype(BF16)
        state_out[0, h] = low_memory
        lower = mm(key, key, (1, 1)) * strict * beta
        inverse = inverse_unit_lower(lower, size).astype(BF16)
        inverse_out[0, h] = inverse
        within = mm(query, key, (1, 1)) * inclusive
        change = mm(inverse, beta * (value - carried * mm(key, low_memory)))
        low_change = change.astype(BF16)
        change_out[:, cols] = low_change
        out = scale * (carried * mm(query, low_memory) + mm(within, low_change))
        state[h] = kept * memory + mm(key, ending * change, (0, 0))
        delta_out[:, cols] = out
        normal = out * lax.rsqrt(jnp.mean(out * out, axis=1, keepdims=True) + 1e-5) * head_gain
        mixed[:, cols] = (normal * opened[:, cols] * live).astype(BF16)


def forward_mixer(tokens, w_query, w_key, w_value, w_gate, w_beta, taps_query, taps_key, taps_value, gain, gain_first, starts, lengths, side, count):
    slots, model = tokens.shape
    wide = w_query.shape[1]
    width = gain.shape[0]
    heads = wide // width
    seqs = starts.shape[1]
    chunks = slots // CHUNK
    taps = taps_query.shape[0]
    smem = pl.BlockSpec(memory_space=pltpu.SMEM)
    whole = lambda shape: pl.BlockSpec(shape, lambda n: (0,) * len(shape))
    piece = lambda shape: pl.BlockSpec(shape, lambda n: (n,) + (0,) * (len(shape) - 1))
    outs = [
        ((slots, wide), BF16), ((slots, wide), F32), ((slots, wide), F32), ((slots, wide), F32), ((slots, wide), F32),
        ((slots, w_beta.shape[0]), F32), ((slots, wide), F32), ((slots, wide), F32), ((slots, wide), F32),
        ((slots, wide), F32), ((slots, wide), BF16),
    ]
    return pl.pallas_call(
        functools.partial(forward_kernel, heads, width, seqs, count, slots // count, chunks),
        name="mixer_forward",
        grid=(chunks,),
        out_shape=[jax.ShapeDtypeStruct(s, d) for s, d in outs]
        + [
            jax.ShapeDtypeStruct((chunks, heads, CHUNK, CHUNK), BF16),
            jax.ShapeDtypeStruct((chunks, heads, width, width), BF16),
            jax.ShapeDtypeStruct((slots, model), BF16),
        ],
        in_specs=[smem, smem, piece((CHUNK, model))]
        + [whole((model, wide))] * 4
        + [whole(w_beta.shape)]
        + [whole((taps, wide))] * 3
        + [whole((1, width)), whole((1, model)), ANY],
        out_specs=[piece((CHUNK, s[1])) for s, d in outs]
        + [piece((1, heads, CHUNK, CHUNK)), piece((1, heads, width, width)), ANY],
        scratch_shapes=[pltpu.VMEM((CHUNK + 8, wide), F32)] * 3
        + [pltpu.VMEM((heads, width, width), F32)]
        + ring_semaphores(count)
        + [pltpu.SemaphoreType.DMA],
        compiler_params=ring_params(5),
        cost_estimate=pl.CostEstimate(
            flops=2 * slots * model * wide * 4 + slots * heads * CHUNK * 2 * CHUNK * 20,
            bytes_accessed=slots * model * 2 + 4 * model * wide * 2 + slots * wide * 36,
            transcendentals=slots * wide * 4,
        ),
    )(starts, lengths, tokens, w_query, w_key, w_value, w_gate, w_beta, taps_query, taps_key, taps_value, gain.reshape(1, width), gain_first.reshape(1, model), side)


def backward_kernel(
    heads, width, seqs, chunks, count, rows_own,
    starts, lengths, tokens, grad_attended, mixed, p_query, p_key, p_value, p_gate, p_beta,
    z_query, z_key, z_value, delta_out, change_in, inverse_in, state_in,
    w_query, w_key, w_value, w_gate, w_beta, w_out, taps_query, taps_key, taps_value, gain, gain_first,
    hidden, w_down, resid, grad_normed, gw_query, gw_key, gw_value, gw_gate, gw_beta, gw_out,
    gt_query, gt_key, gt_value, g_gain, g_first, output,
    a_query, a_key, a_value, a_gate, a_out, head_query, head_key, head_value, flow, slots, sends, recvs,
):
    step = pl.program_id(0)
    size = tokens.shape[0]
    first = (chunks - 1 - step) * size

    @pl.when(step == 0)
    def _():
        for ref in (a_query, a_key, a_value, a_gate, gw_beta, a_out, gt_query, gt_key, gt_value, g_gain, g_first, flow):
            ref[...] = jnp.zeros_like(ref)
        for ref in (head_query, head_key, head_value):
            ref[size:, :] = jnp.zeros((8, ref.shape[1]), F32)

    half = rows_own // 2

    def partial(one, two):
        return mm(jnp.concatenate([hidden[pl.ds(one, half), :], hidden[pl.ds(two, half), :]], 0), w_down[...])

    def finish(start, length, down):
        output[start : start + length, :] = (resid[start : start + length, :] + down).astype(BF16)

    ring = Ring(count)
    scatter = Scatter(ring, partial, slots, sends, recvs, rows_own, finish)
    spread_hops(
        step, chunks, count,
        lambda: (greet(ring), scatter.begin()),
        scatter.hop,
        scatter.end,
    )
    rows, seg_rows, seg_columns, before, last = chunk_masks(starts, lengths, seqs, first, size)
    same = seg_rows == seg_columns
    i = lax.broadcasted_iota(jnp.int32, (size, size), 0)
    j = lax.broadcasted_iota(jnp.int32, (size, size), 1)
    strict = jnp.where(same & (i > j), 1.0, 0.0)
    inclusive = jnp.where(same & (i >= j), 1.0, 0.0)
    carried = jnp.where(seg_rows == before, 1.0, 0.0)
    ending = jnp.where(seg_rows == last, 1.0, 0.0)
    kept = jnp.where(before == last, 1.0, 0.0)
    live = jnp.where(seg_rows % 2 == 1, 1.0, 0.0)
    taps = taps_query.shape[0]
    joined = [
        jnp.where(segment_at(rows + offset, starts, lengths, seqs) == seg_rows, 1.0, 0.0)
        for offset in range(1, taps)
    ]
    normal_rows, unit_rows = normed_rows(tokens, gain_first)
    inputs = normal_rows.astype(BF16)
    grad_rows = grad_attended[...]
    grad_mixed = mm(grad_rows, w_out[...], (1, 1))
    a_out[...] += mm(mixed[...], grad_rows, (0, 0))
    strength = sigmoid(p_beta[...])
    scale = width ** (-0.5)
    head_gain = gain[...].astype(F32)

    grads_query, grads_key, grads_value, grads_gate, grads_beta = [], [], [], [], []
    for h in range(heads):
        cols = slice(h * width, (h + 1) * width)
        out = delta_out[:, cols]
        gate = p_gate[:, cols]
        sig_gate = sigmoid(gate)
        silu_gate = gate * sig_gate
        root = lax.rsqrt(jnp.mean(out * out, axis=1, keepdims=True) + 1e-5)
        grad = grad_mixed[:, cols] * live
        unit = out * root
        grads_gate.append(grad * unit * head_gain * (sig_gate * (1.0 + gate * (1.0 - sig_gate))))
        grad_normal = grad * silu_gate
        g_gain[...] += jnp.sum(grad_normal * unit, axis=0, keepdims=True)
        push = grad_normal * head_gain
        grad_out = scale * root * (push - unit * jnp.mean(push * unit, axis=1, keepdims=True))

        zq, zk, zv = z_query[:, cols], z_key[:, cols], z_value[:, cols]
        sq, sk, sv = sigmoid(zq), sigmoid(zk), sigmoid(zv)
        uq, uk = zq * sq, zk * sk
        nq = lax.rsqrt(jnp.sum(uq * uq, axis=1, keepdims=True) + 1e-6)
        nk = lax.rsqrt(jnp.sum(uk * uk, axis=1, keepdims=True) + 1e-6)
        unit_q, unit_k = uq * nq, uk * nk
        query, key = unit_q.astype(BF16), unit_k.astype(BF16)
        beta = strength[:, h : h + 1]
        change = change_in[:, cols]
        inverse = inverse_in[0, h]
        memory = state_in[0, h]
        flowing = flow[h]
        low_flow = flowing.astype(BF16)
        low_out = grad_out.astype(BF16)

        within = mm(query, key, (1, 1)) * inclusive
        grad_within = (mm(low_out, change, (1, 1)) * inclusive).astype(BF16)
        grad_change = mm(within, low_out, (0, 0)) + ending * mm(key, low_flow)
        grad_mid = mm(inverse, grad_change, (0, 0))
        grad_value = beta * grad_mid
        low_value = grad_value.astype(BF16)
        cross = (mm(low_value, change, (1, 1)) * strict).astype(BF16)
        grad_query = carried * mm(low_out, memory, (1, 1)) + mm(grad_within, key)
        grad_key = (
            mm(grad_within, query, (0, 0))
            + ending * mm(change, low_flow, (1, 1))
            - carried * mm(low_value, memory, (1, 1))
            - mm(cross, key)
            - mm(cross, key, (0, 0))
        )
        flow[h] = (
            kept * flowing
            + mm(query, carried * grad_out, (0, 0))
            - mm(key, carried * grad_value, (0, 0))
        )
        grads_beta.append((1.0 - beta) * jnp.sum(grad_mid * change.astype(F32), axis=1, keepdims=True))
        du_q = nq * (grad_query - unit_q * jnp.sum(grad_query * unit_q, axis=1, keepdims=True))
        du_k = nk * (grad_key - unit_k * jnp.sum(grad_key * unit_k, axis=1, keepdims=True))
        grads_query.append(du_q * sq * (1.0 + zq * (1.0 - sq)))
        grads_key.append(du_k * sk * (1.0 + zk * (1.0 - sk)))
        grads_value.append(grad_value * sv * (1.0 + zv * (1.0 - sv)))

    def unconv(parts, taps_ref, head, projected, grad_taps):
        grad = jnp.concatenate(parts, axis=1)
        head[0:size, :] = grad
        tap = taps_ref[...].astype(F32)
        p = projected[...]
        result = grad * tap[0:1]
        grad_taps[0:1, :] += jnp.sum(p * grad, axis=0, keepdims=True)
        for offset in range(1, taps):
            moved = head[offset : offset + size, :] * joined[offset - 1]
            result = result + moved * tap[offset : offset + 1]
            grad_taps[offset : offset + 1, :] += jnp.sum(p * moved, axis=0, keepdims=True)
        head[size:, :] = grad[0:8, :]
        return result.astype(BF16)

    d_query = unconv(grads_query, taps_query, head_query, p_query, gt_query)
    d_key = unconv(grads_key, taps_key, head_key, p_key, gt_key)
    d_value = unconv(grads_value, taps_value, head_value, p_value, gt_value)
    d_gate = jnp.concatenate(grads_gate, axis=1).astype(BF16)
    spare = [jnp.zeros((size, 1), F32)] * (w_beta.shape[0] - heads)
    d_beta = jnp.concatenate(grads_beta + spare, axis=1).astype(BF16)
    grad_inputs = (
        mm(d_query, w_query[...], (1, 1))
        + mm(d_key, w_key[...], (1, 1))
        + mm(d_value, w_value[...], (1, 1))
        + mm(d_gate, w_gate[...], (1, 1))
        + mm(d_beta, w_beta[...])
    )
    grad_normed[...] = grad_inputs.astype(BF16)
    g_first[...] += jnp.sum(grad_inputs * unit_rows, axis=0, keepdims=True)
    a_query[...] += mm(inputs, d_query, (0, 0))
    a_key[...] += mm(inputs, d_key, (0, 0))
    a_value[...] += mm(inputs, d_value, (0, 0))
    a_gate[...] += mm(inputs, d_gate, (0, 0))
    gw_beta[...] += mm(d_beta, inputs, (0, 0))

    @pl.when(step == chunks - 1)
    def _():
        for target, source in (
            (gw_query, a_query), (gw_key, a_key), (gw_value, a_value), (gw_gate, a_gate),
            (gw_out, a_out),
        ):
            target[...] = source[...].astype(target.dtype)


def backward_mixer(tokens, grad_attended, saved, w_query, w_key, w_value, w_gate, w_beta, w_out, taps_query, taps_key, taps_value, gain, gain_first, starts, lengths, hidden, w_down, resid, count):
    slots, model = tokens.shape
    wide = w_query.shape[1]
    width = gain.shape[0]
    heads = wide // width
    seqs = starts.shape[1]
    chunks = slots // CHUNK
    taps = taps_query.shape[0]
    smem = pl.BlockSpec(memory_space=pltpu.SMEM)
    fixed = lambda shape: pl.BlockSpec(shape, lambda n: (0,) * len(shape), pipeline_mode=pl.Buffered(1))
    piece = lambda shape: pl.BlockSpec(shape, lambda n: (chunks - 1 - n,) + (0,) * (len(shape) - 1))
    rows = lambda a: piece((CHUNK, a.shape[1]))
    outs = (
        [((slots, model), BF16)] + [((model, wide), BF16)] * 4 + [(w_beta.shape, F32), ((wide, model), BF16)]
        + [((taps, wide), F32)] * 3 + [((1, width), F32), ((1, model), F32), (resid.shape, BF16)]
    )
    return pl.pallas_call(
        functools.partial(backward_kernel, heads, width, seqs, chunks, count, slots // count),
        name="mixer_backward",
        grid=(chunks,),
        out_shape=[jax.ShapeDtypeStruct(s, d) for s, d in outs],
        in_specs=[smem, smem, rows(tokens), rows(grad_attended)]
        + [rows(a) for a in saved[:11]]
        + [piece((1, heads, CHUNK, CHUNK)), piece((1, heads, width, width))]
        + [fixed((model, wide))] * 4
        + [fixed(w_beta.shape), fixed((wide, model))]
        + [fixed((taps, wide))] * 3
        + [fixed((1, width)), fixed((1, model)), fixed(hidden.shape), fixed(w_down.shape), fixed(resid.shape)],
        out_specs=[piece((CHUNK, model))] + [fixed(s) for s, d in outs[1:]],
        scratch_shapes=[pltpu.VMEM((model, wide), F32)] * 4
        + [pltpu.VMEM((wide, model), F32)]
        + [pltpu.VMEM((CHUNK + 8, wide), F32)] * 3
        + [pltpu.VMEM((heads, width, width), F32), ring_slots(count, slots // count, model)]
        + ring_semaphores(count),
        compiler_params=ring_params(6),
        cost_estimate=pl.CostEstimate(
            flops=2 * slots * model * wide * 10 + slots * heads * CHUNK * 2 * CHUNK * 8,
            bytes_accessed=slots * model * 6 + 10 * model * wide * 2 + slots * wide * 36,
            transcendentals=slots * wide * 8,
        ),
    )(starts, lengths, tokens, grad_attended, *saved, w_query, w_key, w_value, w_gate, w_beta, w_out, taps_query, taps_key, taps_value, gain.reshape(1, width), gain_first.reshape(1, model), hidden, w_down, resid)


def silu_parts(value):
    sig = jax.nn.sigmoid(value)
    return sig, value * sig


def make_shards(groups, count):
    def shards(
        tokens, attn_gain, w_query, w_key, w_value, conv_query, conv_key, conv_value, w_beta, w_gate_out,
        head_gain, w_out, ffn_gain, w_gate, w_up, w_down, seq_starts, seq_lengths, cotangent,
    ):
        model = tokens.shape[1]
        heads = w_beta.shape[1]
        beta_rows = w_beta.T if heads > 1 else jnp.pad(w_beta.T, ((0, 1), (0, 0)))
        tokens_full = gather_tokens(tokens, count)
        saved = forward_mixer(
            tokens_full, w_query, w_key, w_value, w_gate_out, beta_rows,
            conv_query, conv_key, conv_value, head_gain, attn_gain, seq_starts, seq_lengths, cotangent, count,
        )
        grad_full, saved = saved[-1], saved[:-1]
        resid, ffn_full = attend(saved[0], w_out, tokens, ffn_gain, count)
        gate_pre = jnp.dot(ffn_full, w_gate, preferred_element_type=F32)
        up_pre = jnp.dot(ffn_full, w_up, preferred_element_type=F32)
        sig, silu_gate = silu_parts(gate_pre)
        hidden = (silu_gate * up_pre).astype(BF16)
        grad_hidden = jnp.einsum("sd,fd->sf", grad_full, w_down, preferred_element_type=F32)
        grad_gate = (grad_hidden * up_pre * sig * (1.0 + gate_pre * (1.0 - sig))).astype(BF16)
        grad_up = (grad_hidden * silu_gate).astype(BF16)
        gw_down = jnp.einsum("sf,sd->fd", hidden, grad_full, preferred_element_type=F32)
        gw_gate = jnp.einsum("sd,sf->fd", ffn_full, grad_gate, preferred_element_type=F32)
        gw_up = jnp.einsum("sd,sf->fd", ffn_full, grad_up, preferred_element_type=F32)
        grad_resid, grad_attended, g_second, *ffn_grads = ffn_back(
            grad_gate, grad_up, w_gate.T, w_up.T, resid, cotangent, ffn_gain,
            [g.astype(BF16) for g in (gw_gate, gw_up, gw_down)], count, groups,
        )
        pulled = backward_mixer(
            tokens_full, grad_attended, saved, w_query, w_key, w_value, w_gate_out, beta_rows, w_out,
            conv_query, conv_key, conv_value, head_gain, attn_gain, seq_starts, seq_lengths,
            hidden, w_down, resid, count,
        )
        terms, gw_query, gw_key, gw_value, gw_gate_out, gw_beta, gw_out = pulled[:7]
        gt_query, gt_key, gt_value, g_head, g_first, output = pulled[7:]
        wide = gt_query.shape[1]
        gw_beta = gw_beta[:heads]
        taps = gt_query.shape[0]
        small = jnp.concatenate(
            [
                g_first,
                g_second,
                jnp.pad(g_head, ((0, 0), (0, model - g_head.shape[1]))),
                jnp.zeros((5, model), F32),
                gw_beta,
                jnp.pad(
                    jnp.concatenate([gt_query, gt_key, gt_value], 1), ((0, 0), (0, model - 3 * wide))
                ),
                jnp.zeros((-(heads + taps) % 8, model), F32),
            ],
            0,
        )
        grad_tokens, total, *mixer_grads = last_step(
            terms, tokens, grad_resid, attn_gain, small,
            (gw_query, gw_key, gw_value, gw_gate_out, gw_out), count, groups,
        )
        mixer_grads = [g.astype(F32) for g in mixer_grads]
        tap_rows = total[8 + heads : 8 + heads + taps]
        return (
            output,
            grad_tokens,
            total[0],
            mixer_grads[0],
            mixer_grads[1],
            mixer_grads[2],
            tap_rows[:, :wide],
            tap_rows[:, wide : 2 * wide],
            tap_rows[:, 2 * wide : 3 * wide],
            total[8 : 8 + heads].T,
            mixer_grads[3],
            total[2, : head_gain.shape[0]],
            mixer_grads[4],
            total[1],
            ffn_grads[0].astype(F32).T,
            ffn_grads[1].astype(F32).T,
            ffn_grads[2].astype(F32),
        )

    return shards


def solution(mesh):
    placed = (
        P(("dp", "tensor"), None),
        P(),
        P(None, "tensor"),
        P(None, "tensor"),
        P(None, "tensor"),
        P(None, "tensor"),
        P(None, "tensor"),
        P(None, "tensor"),
        P(None, "tensor"),
        P(None, "tensor"),
        P(),
        P("tensor", None),
        P(),
        P(None, "tensor"),
        P(None, "tensor"),
        P("tensor", None),
        P("dp", None),
        P("dp", None),
        P(("dp", "tensor"), None),
    )
    return jax.shard_map(
        make_shards(mesh.shape["dp"], mesh.shape["tensor"]),
        mesh=mesh,
        in_specs=placed,
        out_specs=(
            P(("dp", "tensor"), None),
            P(("dp", "tensor"), None),
            P(),
            P(None, "tensor"),
            P(None, "tensor"),
            P(None, "tensor"),
            P(None, "tensor"),
            P(None, "tensor"),
            P(None, "tensor"),
            P(None, "tensor"),
            P(None, "tensor"),
            P(),
            P("tensor", None),
            P(),
            P(None, "tensor"),
            P(None, "tensor"),
            P("tensor", None),
        ),
        check_vma=False,
    )
```

```python
import functools
import jax
import jax.numpy as jnp
from jax import lax
from jax.experimental import pallas as pl
from jax.experimental.pallas import tpu as pltpu
from jax.sharding import PartitionSpec as P

CHUNK = 256
F32, BF16 = jnp.float32, jnp.bfloat16


def mm(a, b, contract=(1, 0)):
    return lax.dot_general(
        a.astype(BF16),
        b.astype(BF16),
        (((contract[0],), (contract[1],)), ((), ())),
        preferred_element_type=F32,
    )


def segment_at(places, starts, lengths, seqs):
    segment = jnp.zeros_like(places)
    for s in range(seqs):
        begin = starts[0, s]
        stop = begin + lengths[0, s]
        segment = segment + jnp.where(places >= begin, 1, 0) + jnp.where(places >= stop, 1, 0)
    return jnp.where(places < 0, -1, segment)


def chunk_masks(starts, lengths, seqs, first, size):
    rows = first + lax.broadcasted_iota(jnp.int32, (size, 1), 0)
    columns = first + lax.broadcasted_iota(jnp.int32, (1, size), 1)
    seg_rows = segment_at(rows, starts, lengths, seqs)
    seg_columns = segment_at(columns, starts, lengths, seqs)
    before = segment_at(jnp.full((1, 1), first - 1, jnp.int32), starts, lengths, seqs)
    last = segment_at(jnp.full((1, 1), first + size - 1, jnp.int32), starts, lengths, seqs)
    return rows, seg_rows, seg_columns, before, last


def inverse_unit_lower(lower, size):
    i = lax.broadcasted_iota(jnp.int32, (size, size), 0)
    j = lax.broadcasted_iota(jnp.int32, (size, size), 1)

    def corner(width):
        shift = width.bit_length() - 1
        pair = (i >> (shift + 1)) == (j >> (shift + 1))
        return pair & (((i >> shift) & 1) == 1) & (((j >> shift) & 1) == 0)

    inverse = jnp.where(i == j, 1.0, 0.0) - jnp.where(corner(1), lower, 0.0)
    width = 2
    while width < size:
        low = inverse.astype(BF16)
        if 2 * width == size:
            part = mm(mm(low[width:, width:], lower[width:, :width]), low[:width, :width])
            inverse = jnp.concatenate(
                [
                    inverse[:width],
                    jnp.concatenate([-part, inverse[width:, width:]], axis=1),
                ],
                axis=0,
            )
        else:
            between = jnp.where(corner(width), lower, 0.0)
            inverse = inverse - mm(mm(low, between), low)
        width *= 2
    return inverse


def sigmoid(v):
    return 1.0 / (1.0 + jnp.exp(-v))


def normed_rows(tokens, gain):
    value = tokens[...].astype(F32)
    unit = value * lax.rsqrt(jnp.mean(value * value, axis=1, keepdims=True) + 1e-6)
    return unit * gain[...].astype(F32), unit


MESH = pl.DeviceIdType.MESH
SUBS = 2


def ring_position(device, count):
    half, odd = device // 2, device % 2
    return half + odd * (count - 1 - 2 * half)


def ring_device(position, count):
    back = position // (count // 2)
    return (1 - back) * 2 * position + back * (2 * (count - 1 - position) + 1)


class Ring:
    def __init__(self, count):
        self.count = count
        self.me = lax.axis_index("tensor")
        self.place = ring_position(self.me, count)
        self.group = lax.axis_index("dp")

    def at(self, offset):
        return ring_device((self.place + offset + 2 * self.count) % self.count, self.count)

    def next(self, way):
        return (self.group, self.at(1 if way == 0 else -1))


def gather_copy(ring, source, target, sends, recvs, way, sub, step, origin, rows):
    piece = rows // (2 * SUBS)
    inside = way * (rows // 2) + sub * piece
    start = pl.multiple_of(origin * rows + inside, piece)
    src = target.at[pl.ds(start, piece), :] if source is None else source.at[pl.ds(inside, piece), :]
    return pltpu.make_async_remote_copy(
        src_ref=src,
        dst_ref=target.at[pl.ds(start, piece), :],
        send_sem=sends.at[way, sub, step],
        recv_sem=recvs.at[way, sub, step],
        device_id=ring.next(way),
        device_id_type=MESH,
    )


PAIRS = [(sub, way) for sub in range(SUBS) for way in (0, 1)]


class Gather:
    def __init__(self, ring, source, target, sends, recvs, local, rows):
        self.ring, self.source, self.target = ring, source, target
        self.sends, self.recvs, self.rows = sends, recvs, rows
        self.keep = None
        if source is not None:
            self.keep = pltpu.make_async_copy(
                source, target.at[pl.ds(pl.multiple_of(ring.me * rows, rows), rows), :], local
            )

    def origin(self, way, step):
        return self.ring.at(-step if way == 0 else step)

    def copy(self, way, sub, step, origin, source=None):
        return gather_copy(
            self.ring, source, self.target, self.sends, self.recvs, way, sub, step, origin, self.rows
        )

    def begin(self):
        if self.keep is not None:
            self.keep.start()
        for sub, way in PAIRS:
            self.copy(way, sub, 0, self.ring.me, self.source).start()

    def arrived(self, step):
        for sub, way in PAIRS:
            self.copy(way, sub, step - 1, self.origin(way, step)).wait_recv()

    def hop(self, step):
        for sub, way in PAIRS:
            self.copy(way, sub, step - 1, self.origin(way, step)).wait_recv()
            self.copy(way, sub, step, self.origin(way, step)).start()

    def end(self):
        def drain(step, carry):
            for sub, way in PAIRS:
                self.copy(way, sub, step, self.ring.me).wait_send()
            return carry

        lax.fori_loop(0, self.ring.count - 1, drain, 0)
        if self.keep is not None:
            self.keep.wait()


def ring_gather(ring, source, target, sends, recvs, local, rows, between=None):
    gather = Gather(ring, source, target, sends, recvs, local, rows)
    gather.begin()
    if between is not None:
        between(0)

    def forward(step, carry):
        gather.hop(step)
        if between is not None:
            between(step)
        return carry

    lax.fori_loop(1, ring.count - 1, forward, 0)
    gather.arrived(ring.count - 1)
    if between is not None:
        between(ring.count - 1)
    gather.end()


def scatter_copy(ring, slots, sends, recvs, way, sub, step):
    return pltpu.make_async_remote_copy(
        src_ref=slots.at[way, sub, step],
        dst_ref=slots.at[way, sub, step + 1],
        send_sem=sends.at[way, sub, step],
        recv_sem=recvs.at[way, sub, step],
        device_id=ring.next(way),
        device_id_type=MESH,
    )


class Scatter:
    def __init__(self, ring, partial, slots, sends, recvs, rows, finish):
        self.ring, self.partial, self.slots, self.sends, self.recvs = ring, partial, slots, sends, recvs
        self.half, self.finish = rows // 2, finish
        self.rows, self.piece = rows, rows // (2 * SUBS)

    def terms(self, first, second):
        half = self.half
        return self.partial(
            pl.multiple_of(first * self.rows, half), pl.multiple_of(second * self.rows + half, half)
        )

    def part(self, terms, way, sub):
        start = way * self.half + sub * self.piece
        return terms[start : start + self.piece]

    def copy(self, way, sub, step):
        return scatter_copy(self.ring, self.slots, self.sends, self.recvs, way, sub, step)

    def begin(self):
        terms = self.terms(self.ring.at(-1), self.ring.at(1))
        for sub, way in PAIRS:
            self.slots[way, sub, 0] = self.part(terms, way, sub).astype(BF16)
            self.copy(way, sub, 0).start()

    def hop(self, step):
        terms = self.terms(self.ring.at(-1 - step), self.ring.at(1 + step))
        for sub, way in PAIRS:
            self.copy(way, sub, step - 1).wait_recv()
            self.slots[way, sub, step] = (
                self.slots[way, sub, step].astype(F32) + self.part(terms, way, sub)
            ).astype(BF16)
            self.copy(way, sub, step).start()

    def end(self):
        count = self.ring.count
        terms = self.terms(self.ring.me, self.ring.me)
        for sub, way in PAIRS:
            self.copy(way, sub, count - 2).wait_recv()
            self.finish(
                way * self.half + sub * self.piece,
                self.piece,
                self.slots[way, sub, count - 1].astype(F32) + self.part(terms, way, sub),
            )

        def drain(step, carry):
            for sub, way in PAIRS:
                self.copy(way, sub, step).wait_send()
            return carry

        lax.fori_loop(0, count - 1, drain, 0)


def ring_scatter(ring, partial, slots, sends, recvs, rows, finish, between=None):
    scatter = Scatter(ring, partial, slots, sends, recvs, rows, finish)
    scatter.begin()
    if between is not None:
        between(0)

    def forward(step, carry):
        scatter.hop(step)
        if between is not None:
            between(step)
        return carry

    lax.fori_loop(1, ring.count - 1, forward, 0)
    if between is not None:
        between(ring.count - 1)
    scatter.end()


class GroupSum:
    def __init__(self, ring, groups, grads, near, far, targets, near_sems, far_sems, back_sems, keep_sems):
        self.ring, self.groups, self.grads, self.near, self.far, self.targets = ring, groups, grads, near, far, targets
        self.near_sems, self.far_sems, self.back_sems, self.keep_sems = near_sems, far_sems, back_sems, keep_sems
        self.core = ring.group % 2
        self.mate = (ring.group + 1 - 2 * self.core, ring.me)

    def peers(self):
        return [self.mate] + [
            ((self.ring.group + 2 * k) % self.groups, self.ring.me) for k in range(1, self.groups // 2)
        ]

    def half(self, i, core):
        rows = self.near[i].shape[0]
        return pl.ds(pl.multiple_of(core * rows, rows), rows)

    def near_copy(self, i):
        return pltpu.make_async_remote_copy(
            src_ref=self.grads[i].at[self.half(i, 1 - self.core), :], dst_ref=self.near[i],
            send_sem=self.near_sems.at[0, i], recv_sem=self.near_sems.at[1, i],
            device_id=self.mate, device_id_type=MESH,
        )

    def far_copy(self, i, k):
        return pltpu.make_async_remote_copy(
            src_ref=self.near[i], dst_ref=self.far[i].at[k - 1],
            send_sem=self.far_sems.at[0, i, k - 1], recv_sem=self.far_sems.at[1, i, k - 1],
            device_id=((self.ring.group + 2 * k) % self.groups, self.ring.me), device_id_type=MESH,
        )

    def back_copy(self, i):
        return pltpu.make_async_remote_copy(
            src_ref=self.far[i].at[0], dst_ref=self.targets[i].at[self.half(i, self.core), :],
            send_sem=self.back_sems.at[0, i], recv_sem=self.back_sems.at[1, i],
            device_id=self.mate, device_id_type=MESH,
        )

    def keep_copy(self, i):
        return pltpu.make_async_copy(
            self.far[i].at[0], self.targets[i].at[self.half(i, self.core), :], self.keep_sems.at[i]
        )

    def first(self, chosen):
        for i in chosen:
            self.near_copy(i).start()

    def each_block(self, i, body):
        rows = self.near[i].shape[0]
        block = next(size for size in (64, 32, 16) if rows % size == 0)

        def step(at, carry):
            start = pl.multiple_of(at * block, block)
            body(pl.ds(start, block), pl.ds(pl.multiple_of(self.core * rows + start, block), block))
            return carry

        lax.fori_loop(0, rows // block, step, 0)

    def second(self, chosen):
        for i in chosen:
            self.near_copy(i).wait_recv()

            def add(here, own, i=i):
                self.near[i][here, :] = (
                    self.near[i][here, :].astype(F32) + self.grads[i][own, :].astype(F32)
                ).astype(BF16)

            self.each_block(i, add)
            for k in range(1, self.groups // 2):
                self.far_copy(i, k).start()

    def third(self, chosen):
        for i in chosen:
            for k in range(1, self.groups // 2):
                self.far_copy(i, k).wait()

            def add(here, own, i=i):
                total = self.near[i][here, :].astype(F32)
                for k in range(self.groups // 2 - 1):
                    total = total + self.far[i][k, here, :].astype(F32)
                self.far[i][0, here, :] = total.astype(BF16)

            self.each_block(i, add)
            self.keep_copy(i).start()
            self.back_copy(i).start()

    def last(self):
        for i in range(len(self.grads)):
            self.near_copy(i).wait_send()
            self.back_copy(i).wait()
            self.keep_copy(i).wait()


def sum_scratch(shapes, groups):
    number = len(shapes)
    return (
        [pltpu.VMEM((rows // 2, columns), BF16) for rows, columns in shapes]
        + [pltpu.VMEM((groups // 2 - 1, rows // 2, columns), BF16) for rows, columns in shapes]
        + [
            pltpu.SemaphoreType.DMA((2, number)),
            pltpu.SemaphoreType.DMA((2, number, groups // 2 - 1)),
            pltpu.SemaphoreType.DMA((2, number)),
            pltpu.SemaphoreType.DMA((number,)),
        ]
    )


def greet(ring, others=()):
    barrier = pltpu.get_barrier_semaphore()
    peers = [ring.next(0), ring.next(1)] + list(others)
    for peer in peers:
        pl.semaphore_signal(barrier, inc=1, device_id=peer, device_id_type=MESH)
    pl.semaphore_wait(barrier, len(peers))


def ring_semaphores(count):
    return [pltpu.SemaphoreType.DMA((2, SUBS, count - 1))] * 2


def ring_slots(count, rows, columns):
    return pltpu.VMEM((2, SUBS, count, rows // (2 * SUBS), columns), BF16)


ANY = pl.BlockSpec(memory_space=pl.ANY)
VMEM = pl.BlockSpec(memory_space=pltpu.VMEM)


def ring_params(number):
    return pltpu.CompilerParams(
        collective_id=number, has_side_effects=True, vmem_limit_bytes=60 << 20
    )


def gather_kernel(count, rows, source, target, sends, recvs, local):
    ring = Ring(count)
    greet(ring)
    ring_gather(ring, source, target, sends, recvs, local, rows)


def gather_tokens(tokens, count):
    rows, model = tokens.shape
    return pl.pallas_call(
        functools.partial(gather_kernel, count, rows),
        name="gather_tokens",
        out_shape=jax.ShapeDtypeStruct((count * rows, model), tokens.dtype),
        in_specs=[ANY],
        out_specs=ANY,
        scratch_shapes=ring_semaphores(count) + [pltpu.SemaphoreType.DMA],
        compiler_params=ring_params(1),
        cost_estimate=pl.CostEstimate(flops=0, bytes_accessed=300 << 20, transcendentals=0),
    )(tokens)


def logistic(v):
    return 1.0 / (1.0 + jnp.exp(-v))


def attend_kernel(
    count, rows, mixed, w_out, tokens, gain, w_gate, w_up, w_down, cotangents,
    resid, full, hidden, grad_gate, grad_up,
    slots, gathered, grad_hidden, boxes, sends, recvs, sends_two, recvs_two, box_sems, out_sems,
):
    ring = Ring(count)
    half = rows // 2

    def box_copy(block):
        return pltpu.make_async_copy(
            cotangents.at[pl.ds(pl.multiple_of(block * rows, rows), rows), :],
            boxes.at[block % 2],
            box_sems.at[block % 2],
        )

    box_copy(0).start()
    greet(ring)

    def partial(first, second):
        return mm(jnp.concatenate([mixed[pl.ds(first, half), :], mixed[pl.ds(second, half), :]], 0), w_out[...])

    def finish(start, size, attended):
        value = tokens[start : start + size, :].astype(F32) + attended
        resid[start : start + size, :] = value
        scale = lax.rsqrt(jnp.mean(value * value, axis=1, keepdims=True) + 1e-6)
        gathered[pl.ds(pl.multiple_of(ring.me * rows + start, size), size), :] = (
            value * scale * gain[...].astype(F32)
        ).astype(BF16)

    def hide(block):
        box_copy(block).wait()

        @pl.when(block + 1 < count)
        def _():
            box_copy(block + 1).start()

        grad_hidden[pl.ds(pl.multiple_of(block * rows, rows), rows), :] = mm(
            boxes[block % 2], w_down[...], (1, 1)
        )

    ring_scatter(ring, partial, slots, sends, recvs, rows, finish, hide)
    gather = Gather(ring, None, gathered, sends_two, recvs_two, None, rows)

    def places(step):
        return [
            pl.ds(pl.multiple_of(gather.origin(way, step) * rows + way * half, half), half) for way in (0, 1)
        ]

    def out_copy(way, step):
        at = places(step)[way]
        return pltpu.make_async_copy(gathered.at[at, :], full.at[at, :], out_sems.at[way, step])

    def feed(step):
        one, two = places(step)
        for way in (0, 1):
            out_copy(way, step).start()
        inputs = jnp.concatenate([gathered[one, :], gathered[two, :]], 0)
        gate = mm(inputs, w_gate[...], (1, 1))
        up = mm(inputs, w_up[...], (1, 1))
        grad = jnp.concatenate([grad_hidden[one, :], grad_hidden[two, :]], 0)
        sig = logistic(gate)
        opened = gate * sig
        for target, value in (
            (hidden, opened * up),
            (grad_gate, grad * up * sig * (1.0 + gate * (1.0 - sig))),
            (grad_up, grad * opened),
        ):
            low = value.astype(BF16)
            target[one, :] = low[:half]
            target[two, :] = low[half:]

    ring_gather(ring, None, gathered, sends_two, recvs_two, None, rows, feed)

    def drain(step, carry):
        for way in (0, 1):
            out_copy(way, step).wait()
        return carry

    lax.fori_loop(0, count, drain, 0)


def attend(mixed, w_out, tokens, gain, w_gate, w_up, w_down, cotangents, count):
    rows, model = tokens.shape
    slots, inner = count * rows, w_down.shape[0]
    return pl.pallas_call(
        functools.partial(attend_kernel, count, rows),
        name="attend",
        out_shape=[
            jax.ShapeDtypeStruct((rows, model), F32),
            jax.ShapeDtypeStruct((slots, model), BF16),
        ]
        + [jax.ShapeDtypeStruct((slots, inner), BF16)] * 3,
        in_specs=[VMEM] * 7 + [ANY],
        out_specs=[VMEM, ANY] + [VMEM] * 3,
        scratch_shapes=[
            ring_slots(count, rows, model),
            pltpu.VMEM((slots, model), BF16),
            pltpu.VMEM((slots, inner), F32),
            pltpu.VMEM((2, rows, model), BF16),
        ]
        + ring_semaphores(count) * 2
        + [pltpu.SemaphoreType.DMA((2,)), pltpu.SemaphoreType.DMA((2, count))],
        compiler_params=ring_params(2),
        cost_estimate=pl.CostEstimate(
            flops=2 * slots * model * (mixed.shape[1] + 3 * inner), bytes_accessed=600 << 20,
            transcendentals=slots * inner,
        ),
    )(mixed, w_out, tokens, gain.reshape(1, model), w_gate, w_up, w_down, cotangents)


def norm_back(inputs, scale, gain, grad_normed):
    weighted = gain * grad_normed
    inner = jnp.mean(weighted * inputs, axis=1, keepdims=True)
    unit = inputs * scale
    return scale * weighted - unit * (scale * scale * inner), grad_normed * unit


JOBS = 8


def ffn_back_kernel(
    count, groups, rows, grad_gate, grad_up, hidden, w_gate, w_up, resid, cotangent, gain, inputs, cotangents,
    grad_resid, full, grad_gain, sum_gate, sum_up, sum_down,
    slots, low, gw_gate, gw_up, gw_down, boxes, box_sems, *rest,
):
    ring = Ring(count)
    sends, recvs, sends_two, recvs_two, local = rest[:5]
    sums = GroupSum(
        ring, groups, (gw_gate, gw_up, gw_down), rest[5:8], rest[8:11], (sum_gate, sum_up, sum_down), *rest[11:]
    )
    wide = boxes.shape[2]

    def box_copy(job):
        source = inputs if job < JOBS // 2 else cotangents
        at = job % (JOBS // 2) * wide
        return pltpu.make_async_copy(
            source.at[:, at : at + wide], boxes.at[job % 2], box_sems.at[job % 2]
        )

    box_copy(0).start()
    greet(ring, sums.peers())
    grad_gain[...] = jnp.zeros_like(grad_gain)
    half = rows // 2

    def partial(first, second):
        gates = jnp.concatenate([grad_gate[pl.ds(first, half), :], grad_gate[pl.ds(second, half), :]], 0)
        ups = jnp.concatenate([grad_up[pl.ds(first, half), :], grad_up[pl.ds(second, half), :]], 0)
        return mm(gates, w_gate[...]) + mm(ups, w_up[...])

    def finish(start, size, grad):
        value = resid[start : start + size, :]
        scale = lax.rsqrt(jnp.mean(value * value, axis=1, keepdims=True) + 1e-6)
        through, pieces = norm_back(value, scale, gain[...].astype(F32), grad)
        result = cotangent[start : start + size, :].astype(F32) + through
        grad_resid[start : start + size, :] = result
        grad_gain[...] += jnp.sum(pieces, axis=0, keepdims=True)
        low[start : start + size, :] = result.astype(BF16)

    def work(job):
        box_copy(job).wait()
        if job + 1 < JOBS:
            box_copy(job + 1).start()
        at = job % (JOBS // 2) * wide
        box = boxes[job % 2]
        if job < JOBS // 2:
            gw_gate[:, at : at + wide] = mm(grad_gate[...], box, (0, 0)).astype(BF16)
            gw_up[:, at : at + wide] = mm(grad_up[...], box, (0, 0)).astype(BF16)
        else:
            gw_down[:, at : at + wide] = mm(hidden[...], box, (0, 0)).astype(BF16)

    each = JOBS // 4
    events = {step: [functools.partial(work, step * each + k) for k in range(each)] for step in range(4)}
    events[1].append(lambda: sums.first((0, 1)))
    events[3].insert(0, lambda: sums.second((0, 1)))
    events[3].append(lambda: sums.first((2,)))
    events[5] = [lambda: sums.second((2,))]
    events_two = {count - 3: [lambda: sums.third((0, 1))], count - 2: [lambda: sums.third((2,))]}

    def between(table):
        def run(step):
            for when, actions in table.items():
                def act(actions=actions):
                    for action in actions:
                        action()

                if isinstance(step, int):
                    if step == when:
                        act()
                else:
                    pl.when(step == when)(act)

        return run

    ring_scatter(ring, partial, slots, sends, recvs, rows, finish, between(events))
    ring_gather(ring, low, full, sends_two, recvs_two, local, rows, between(events_two))
    sums.last()


def ffn_back(grad_gate, grad_up, hidden, w_gate, w_up, resid, cotangent, gain, inputs, cotangents, count, groups):
    rows, model = resid.shape
    slots, inner = grad_up.shape
    shapes = [(inner, model)] * 3
    return pl.pallas_call(
        functools.partial(ffn_back_kernel, count, groups, rows),
        name="ffn_back",
        out_shape=[
            jax.ShapeDtypeStruct((rows, model), F32),
            jax.ShapeDtypeStruct((slots, model), BF16),
            jax.ShapeDtypeStruct((1, model), F32),
        ]
        + [jax.ShapeDtypeStruct(shape, BF16) for shape in shapes],
        in_specs=[VMEM] * 8 + [ANY] * 2,
        out_specs=[VMEM, ANY, VMEM] + [ANY] * 3,
        scratch_shapes=[ring_slots(count, rows, model), pltpu.VMEM((rows, model), BF16)]
        + [pltpu.VMEM(shape, BF16) for shape in shapes]
        + [pltpu.VMEM((2, slots, model // (JOBS // 2)), BF16), pltpu.SemaphoreType.DMA((2,))]
        + ring_semaphores(count) * 2
        + [pltpu.SemaphoreType.DMA]
        + sum_scratch(shapes, groups),
        compiler_params=ring_params(3),
        cost_estimate=pl.CostEstimate(
            flops=10 * slots * model * inner, bytes_accessed=600 << 20, transcendentals=0
        ),
    )(grad_gate, grad_up, hidden, w_gate, w_up, resid, cotangent, gain.reshape(1, model), inputs, cotangents)


def last_kernel(
    count, groups, rows, terms, tokens, grad_resid, gain, small, *rest,
):
    grads, rest = rest[:5], rest[5:]
    grad_tokens, total = rest[:2]
    targets, rest = rest[2:7], rest[7:]
    slots, first_box, second_box, second_own, sends, recvs = rest[:6]
    first_sends, first_recvs, second_sends, second_recvs = rest[6:10]
    ring = Ring(count)
    sums = GroupSum(ring, groups, grads, rest[10:15], rest[15:20], targets, *rest[20:])
    me, group = ring.me, ring.group
    first_peers = [(group, (me + k) % count) for k in range(1, count)]
    second_peers = [((group + k) % groups, me) for k in range(1, groups)]
    barrier = pltpu.get_barrier_semaphore()
    for peer in first_peers + second_peers:
        pl.semaphore_signal(barrier, inc=1, device_id=peer, device_id_type=MESH)
    pl.semaphore_wait(barrier, count + groups - 2)

    def first(k):
        return pltpu.make_async_remote_copy(
            src_ref=small.at[0:8], dst_ref=first_box.at[k], send_sem=first_sends.at[k],
            recv_sem=first_recvs.at[k], device_id=first_peers[k], device_id_type=MESH,
        )

    def second(k):
        return pltpu.make_async_remote_copy(
            src_ref=second_own, dst_ref=second_box.at[k], send_sem=second_sends.at[k],
            recv_sem=second_recvs.at[k], device_id=second_peers[k], device_id_type=MESH,
        )

    every = range(len(grads))
    sums.first(every)
    for k in range(count - 1):
        first(k).start()
    half = rows // 2

    def partial(first, second):
        return jnp.concatenate([terms[pl.ds(first, half), :], terms[pl.ds(second, half), :]], 0).astype(F32)

    def finish(start, size, grad):
        value = tokens[start : start + size, :].astype(F32)
        scale = lax.rsqrt(jnp.mean(value * value, axis=1, keepdims=True) + 1e-6)
        through, pieces = norm_back(value, scale, gain[...].astype(F32), grad)
        grad_tokens[start : start + size, :] = grad_resid[start : start + size, :] + through

    def between(step):
        if isinstance(step, int):
            return

        @pl.when(step == 1)
        def _():
            sums.second(every)
            for k in range(count - 1):
                first(k).wait()
            mine = small[0:8]
            for k in range(count - 1):
                mine = mine + first_box[k]
            second_own[0:8] = mine
            second_own[8:] = small[8:]
            for k in range(groups - 1):
                second(k).start()

        @pl.when(step == count - 2)
        def _():
            for k in range(groups - 1):
                second(k).wait()
            mine = second_own[...]
            for k in range(groups - 1):
                mine = mine + second_box[k]
            total[...] = mine
            sums.third(every)

    ring_scatter(ring, partial, slots, sends, recvs, rows, finish, between)
    sums.last()


def last_step(terms, tokens, grad_resid, gain, small, grads, count, groups):
    rows, model = tokens.shape
    return pl.pallas_call(
        functools.partial(last_kernel, count, groups, rows),
        name="last_step",
        out_shape=[jax.ShapeDtypeStruct((rows, model), F32), jax.ShapeDtypeStruct(small.shape, F32)]
        + [jax.ShapeDtypeStruct(g.shape, BF16) for g in grads],
        in_specs=[VMEM] * (5 + len(grads)),
        out_specs=[VMEM, VMEM] + [ANY] * len(grads),
        scratch_shapes=[
            ring_slots(count, rows, model),
            pltpu.VMEM((count - 1, 8, model), F32),
            pltpu.VMEM((groups - 1,) + small.shape, F32),
            pltpu.VMEM(small.shape, F32),
        ]
        + ring_semaphores(count)
        + [pltpu.SemaphoreType.DMA((count - 1,))] * 2
        + [pltpu.SemaphoreType.DMA((groups - 1,))] * 2
        + sum_scratch([g.shape for g in grads], groups),
        compiler_params=ring_params(4),
        cost_estimate=pl.CostEstimate(flops=0, bytes_accessed=300 << 20, transcendentals=0),
    )(terms, tokens, grad_resid, gain.reshape(1, model), small, *grads)


def spread_hops(step, chunks, count, begin, hop):
    each = -(-(count - 1) // (chunks - 1))

    @pl.when(step == 0)
    def _():
        begin()

    for place in range(each):
        number = step * each + place

        @pl.when((number > 0) & (number < count - 1))
        def _():
            hop(number)


def forward_kernel(
    heads, width, seqs, count, rows_own, chunks,
    starts, lengths, tokens, w_query, w_key, w_value, w_gate, w_beta,
    taps_query, taps_key, taps_value, gain, gain_first, side,
    mixed, p_query, p_key, p_value, p_gate, p_beta, z_query, z_key, z_value,
    delta_out, change_out, inverse_out, state_out, side_full,
    tail_query, tail_key, tail_value, state, sends, recvs, local,
):
    step = pl.program_id(0)
    size = tokens.shape[0]
    first = step * size

    @pl.when(step == 0)
    def _():
        for tail in (tail_query, tail_key, tail_value):
            tail[...] = jnp.zeros_like(tail)
        state[...] = jnp.zeros_like(state)

    ring = Ring(count)
    gather = Gather(ring, side, side_full, sends, recvs, local, rows_own)
    spread_hops(
        step, chunks, count,
        lambda: (greet(ring), gather.begin()),
        gather.hop,
    )
    rows, seg_rows, seg_columns, before, last = chunk_masks(starts, lengths, seqs, first, size)
    same = seg_rows == seg_columns
    i = lax.broadcasted_iota(jnp.int32, (size, size), 0)
    j = lax.broadcasted_iota(jnp.int32, (size, size), 1)
    strict = jnp.where(same & (i > j), 1.0, 0.0)
    inclusive = jnp.where(same & (i >= j), 1.0, 0.0)
    carried = jnp.where(seg_rows == before, 1.0, 0.0)
    ending = jnp.where(seg_rows == last, 1.0, 0.0)
    kept = jnp.where(before == last, 1.0, 0.0)
    live = jnp.where(seg_rows % 2 == 1, 1.0, 0.0)
    joined = [
        jnp.where(segment_at(rows - offset, starts, lengths, seqs) == seg_rows, 1.0, 0.0)
        for offset in range(1, taps_query.shape[0])
    ]
    inputs = normed_rows(tokens, gain_first)[0].astype(BF16)

    def feature(weight, taps, tail, p_out, z_out):
        projected = jnp.dot(inputs, weight[...], preferred_element_type=F32)
        p_out[...] = projected
        tail[8:, :] = projected
        tap = taps[...].astype(F32)
        result = projected * tap[0:1]
        for offset in range(1, tap.shape[0]):
            result = result + tail[8 - offset : 8 - offset + size, :] * tap[offset : offset + 1] * joined[offset - 1]
        tail[0:8, :] = projected[size - 8 :, :]
        z_out[...] = result
        return result * sigmoid(result)

    u_query = feature(w_query, taps_query, tail_query, p_query, z_query)
    u_key = feature(w_key, taps_key, tail_key, p_key, z_key)
    u_value = feature(w_value, taps_value, tail_value, p_value, z_value)
    gate = jnp.dot(inputs, w_gate[...], preferred_element_type=F32)
    p_gate[...] = gate
    beta_pre = mm(inputs, w_beta[...], (1, 1))
    p_beta[...] = beta_pre
    strength = sigmoid(beta_pre)
    opened = gate * sigmoid(gate)
    scale = width ** (-0.5)
    head_gain = gain[...].astype(F32)
    for h in range(heads):
        cols = slice(h * width, (h + 1) * width)
        uq, uk = u_query[:, cols], u_key[:, cols]
        query = (uq * lax.rsqrt(jnp.sum(uq * uq, axis=1, keepdims=True) + 1e-6)).astype(BF16)
        key = (uk * lax.rsqrt(jnp.sum(uk * uk, axis=1, keepdims=True) + 1e-6)).astype(BF16)
        value = u_value[:, cols].astype(BF16).astype(F32)
        beta = strength[:, h : h + 1]
        memory = state[h]
        low_memory = memory.astype(BF16)
        state_out[0, h] = low_memory
        lower = mm(key, key, (1, 1)) * strict * beta
        inverse = inverse_unit_lower(lower, size).astype(BF16)
        inverse_out[0, h] = inverse
        within = mm(query, key, (1, 1)) * inclusive
        change = mm(inverse, beta * (value - carried * mm(key, low_memory)))
        low_change = change.astype(BF16)
        change_out[:, cols] = low_change
        out = scale * (carried * mm(query, low_memory) + mm(within, low_change))
        state[h] = kept * memory + mm(key, ending * change, (0, 0))
        delta_out[:, cols] = out
        normal = out * lax.rsqrt(jnp.mean(out * out, axis=1, keepdims=True) + 1e-5) * head_gain
        mixed[:, cols] = (normal * opened[:, cols] * live).astype(BF16)

    @pl.when(step == chunks - 1)
    def _():
        gather.arrived(count - 1)
        gather.end()


def forward_mixer(tokens, w_query, w_key, w_value, w_gate, w_beta, taps_query, taps_key, taps_value, gain, gain_first, starts, lengths, side, count):
    slots, model = tokens.shape
    wide = w_query.shape[1]
    width = gain.shape[0]
    heads = wide // width
    seqs = starts.shape[1]
    chunks = slots // CHUNK
    taps = taps_query.shape[0]
    smem = pl.BlockSpec(memory_space=pltpu.SMEM)
    whole = lambda shape: pl.BlockSpec(shape, lambda n: (0,) * len(shape))
    piece = lambda shape: pl.BlockSpec(shape, lambda n: (n,) + (0,) * (len(shape) - 1))
    outs = [
        ((slots, wide), BF16), ((slots, wide), F32), ((slots, wide), F32), ((slots, wide), F32), ((slots, wide), F32),
        ((slots, w_beta.shape[0]), F32), ((slots, wide), F32), ((slots, wide), F32), ((slots, wide), F32),
        ((slots, wide), F32), ((slots, wide), BF16),
    ]
    return pl.pallas_call(
        functools.partial(forward_kernel, heads, width, seqs, count, slots // count, chunks),
        name="mixer_forward",
        grid=(chunks,),
        out_shape=[jax.ShapeDtypeStruct(s, d) for s, d in outs]
        + [
            jax.ShapeDtypeStruct((chunks, heads, CHUNK, CHUNK), BF16),
            jax.ShapeDtypeStruct((chunks, heads, width, width), BF16),
            jax.ShapeDtypeStruct((slots, model), BF16),
        ],
        in_specs=[smem, smem, piece((CHUNK, model))]
        + [whole((model, wide))] * 4
        + [whole(w_beta.shape)]
        + [whole((taps, wide))] * 3
        + [whole((1, width)), whole((1, model)), ANY],
        out_specs=[piece((CHUNK, s[1])) for s, d in outs]
        + [piece((1, heads, CHUNK, CHUNK)), piece((1, heads, width, width)), ANY],
        scratch_shapes=[pltpu.VMEM((CHUNK + 8, wide), F32)] * 3
        + [pltpu.VMEM((heads, width, width), F32)]
        + ring_semaphores(count)
        + [pltpu.SemaphoreType.DMA],
        compiler_params=ring_params(5),
        cost_estimate=pl.CostEstimate(
            flops=2 * slots * model * wide * 4 + slots * heads * CHUNK * 2 * CHUNK * 20,
            bytes_accessed=slots * model * 2 + 4 * model * wide * 2 + slots * wide * 36,
            transcendentals=slots * wide * 4,
        ),
    )(starts, lengths, tokens, w_query, w_key, w_value, w_gate, w_beta, taps_query, taps_key, taps_value, gain.reshape(1, width), gain_first.reshape(1, model), side)


def backward_kernel(
    heads, width, seqs, chunks, count, rows_own,
    starts, lengths, tokens, grad_attended, mixed, p_query, p_key, p_value, p_gate, p_beta,
    z_query, z_key, z_value, delta_out, change_in, inverse_in, state_in,
    w_query, w_key, w_value, w_gate, w_beta, w_out, taps_query, taps_key, taps_value, gain, gain_first,
    hidden, w_down, resid, grad_normed, gw_query, gw_key, gw_value, gw_gate, gw_beta, gw_out,
    gt_query, gt_key, gt_value, g_gain, g_first, output,
    a_query, a_key, a_value, a_gate, a_out, head_query, head_key, head_value, flow, slots, sends, recvs,
):
    step = pl.program_id(0)
    size = tokens.shape[0]
    first = (chunks - 1 - step) * size

    @pl.when(step == 0)
    def _():
        for ref in (a_query, a_key, a_value, a_gate, gw_beta, a_out, gt_query, gt_key, gt_value, g_gain, g_first, flow):
            ref[...] = jnp.zeros_like(ref)
        for ref in (head_query, head_key, head_value):
            ref[size:, :] = jnp.zeros((8, ref.shape[1]), F32)

    half = rows_own // 2

    def partial(one, two):
        return mm(jnp.concatenate([hidden[pl.ds(one, half), :], hidden[pl.ds(two, half), :]], 0), w_down[...])

    def finish(start, length, down):
        output[start : start + length, :] = (resid[start : start + length, :] + down).astype(BF16)

    ring = Ring(count)
    scatter = Scatter(ring, partial, slots, sends, recvs, rows_own, finish)
    spread_hops(
        step, chunks, count,
        lambda: (greet(ring), scatter.begin()),
        scatter.hop,
    )
    rows, seg_rows, seg_columns, before, last = chunk_masks(starts, lengths, seqs, first, size)
    same = seg_rows == seg_columns
    i = lax.broadcasted_iota(jnp.int32, (size, size), 0)
    j = lax.broadcasted_iota(jnp.int32, (size, size), 1)
    strict = jnp.where(same & (i > j), 1.0, 0.0)
    inclusive = jnp.where(same & (i >= j), 1.0, 0.0)
    carried = jnp.where(seg_rows == before, 1.0, 0.0)
    ending = jnp.where(seg_rows == last, 1.0, 0.0)
    kept = jnp.where(before == last, 1.0, 0.0)
    live = jnp.where(seg_rows % 2 == 1, 1.0, 0.0)
    taps = taps_query.shape[0]
    joined = [
        jnp.where(segment_at(rows + offset, starts, lengths, seqs) == seg_rows, 1.0, 0.0)
        for offset in range(1, taps)
    ]
    normal_rows, unit_rows = normed_rows(tokens, gain_first)
    inputs = normal_rows.astype(BF16)
    grad_rows = grad_attended[...]
    grad_mixed = mm(grad_rows, w_out[...], (1, 1))
    a_out[...] += mm(mixed[...], grad_rows, (0, 0))
    strength = sigmoid(p_beta[...])
    scale = width ** (-0.5)
    head_gain = gain[...].astype(F32)

    grads_query, grads_key, grads_value, grads_gate, grads_beta = [], [], [], [], []
    for h in range(heads):
        cols = slice(h * width, (h + 1) * width)
        out = delta_out[:, cols]
        gate = p_gate[:, cols]
        sig_gate = sigmoid(gate)
        silu_gate = gate * sig_gate
        root = lax.rsqrt(jnp.mean(out * out, axis=1, keepdims=True) + 1e-5)
        grad = grad_mixed[:, cols] * live
        unit = out * root
        grads_gate.append(grad * unit * head_gain * (sig_gate * (1.0 + gate * (1.0 - sig_gate))))
        grad_normal = grad * silu_gate
        g_gain[...] += jnp.sum(grad_normal * unit, axis=0, keepdims=True)
        push = grad_normal * head_gain
        grad_out = scale * root * (push - unit * jnp.mean(push * unit, axis=1, keepdims=True))

        zq, zk, zv = z_query[:, cols], z_key[:, cols], z_value[:, cols]
        sq, sk, sv = sigmoid(zq), sigmoid(zk), sigmoid(zv)
        uq, uk = zq * sq, zk * sk
        nq = lax.rsqrt(jnp.sum(uq * uq, axis=1, keepdims=True) + 1e-6)
        nk = lax.rsqrt(jnp.sum(uk * uk, axis=1, keepdims=True) + 1e-6)
        unit_q, unit_k = uq * nq, uk * nk
        query, key = unit_q.astype(BF16), unit_k.astype(BF16)
        beta = strength[:, h : h + 1]
        change = change_in[:, cols]
        inverse = inverse_in[0, h]
        memory = state_in[0, h]
        flowing = flow[h]
        low_flow = flowing.astype(BF16)
        low_out = grad_out.astype(BF16)

        within = mm(query, key, (1, 1)) * inclusive
        grad_within = (mm(low_out, change, (1, 1)) * inclusive).astype(BF16)
        grad_change = mm(within, low_out, (0, 0)) + ending * mm(key, low_flow)
        grad_mid = mm(inverse, grad_change, (0, 0))
        grad_value = beta * grad_mid
        low_value = grad_value.astype(BF16)
        cross = (mm(low_value, change, (1, 1)) * strict).astype(BF16)
        grad_query = carried * mm(low_out, memory, (1, 1)) + mm(grad_within, key)
        grad_key = (
            mm(grad_within, query, (0, 0))
            + ending * mm(change, low_flow, (1, 1))
            - carried * mm(low_value, memory, (1, 1))
            - mm(cross, key)
            - mm(cross, key, (0, 0))
        )
        flow[h] = (
            kept * flowing
            + mm(query, carried * grad_out, (0, 0))
            - mm(key, carried * grad_value, (0, 0))
        )
        grads_beta.append((1.0 - beta) * jnp.sum(grad_mid * change.astype(F32), axis=1, keepdims=True))
        du_q = nq * (grad_query - unit_q * jnp.sum(grad_query * unit_q, axis=1, keepdims=True))
        du_k = nk * (grad_key - unit_k * jnp.sum(grad_key * unit_k, axis=1, keepdims=True))
        grads_query.append(du_q * sq * (1.0 + zq * (1.0 - sq)))
        grads_key.append(du_k * sk * (1.0 + zk * (1.0 - sk)))
        grads_value.append(grad_value * sv * (1.0 + zv * (1.0 - sv)))

    def unconv(parts, taps_ref, head, projected, grad_taps):
        grad = jnp.concatenate(parts, axis=1)
        head[0:size, :] = grad
        tap = taps_ref[...].astype(F32)
        p = projected[...]
        result = grad * tap[0:1]
        grad_taps[0:1, :] += jnp.sum(p * grad, axis=0, keepdims=True)
        for offset in range(1, taps):
            moved = head[offset : offset + size, :] * joined[offset - 1]
            result = result + moved * tap[offset : offset + 1]
            grad_taps[offset : offset + 1, :] += jnp.sum(p * moved, axis=0, keepdims=True)
        head[size:, :] = grad[0:8, :]
        return result.astype(BF16)

    d_query = unconv(grads_query, taps_query, head_query, p_query, gt_query)
    d_key = unconv(grads_key, taps_key, head_key, p_key, gt_key)
    d_value = unconv(grads_value, taps_value, head_value, p_value, gt_value)
    d_gate = jnp.concatenate(grads_gate, axis=1).astype(BF16)
    spare = [jnp.zeros((size, 1), F32)] * (w_beta.shape[0] - heads)
    d_beta = jnp.concatenate(grads_beta + spare, axis=1).astype(BF16)
    grad_inputs = (
        mm(d_query, w_query[...], (1, 1))
        + mm(d_key, w_key[...], (1, 1))
        + mm(d_value, w_value[...], (1, 1))
        + mm(d_gate, w_gate[...], (1, 1))
        + mm(d_beta, w_beta[...])
    )
    grad_normed[...] = grad_inputs.astype(BF16)
    g_first[...] += jnp.sum(grad_inputs * unit_rows, axis=0, keepdims=True)
    a_query[...] += mm(inputs, d_query, (0, 0))
    a_key[...] += mm(inputs, d_key, (0, 0))
    a_value[...] += mm(inputs, d_value, (0, 0))
    a_gate[...] += mm(inputs, d_gate, (0, 0))
    gw_beta[...] += mm(d_beta, inputs, (0, 0))

    @pl.when(step == chunks - 1)
    def _():
        for target, source in (
            (gw_query, a_query), (gw_key, a_key), (gw_value, a_value), (gw_gate, a_gate),
            (gw_out, a_out),
        ):
            target[...] = source[...].astype(target.dtype)
        scatter.end()


def backward_mixer(tokens, grad_attended, saved, w_query, w_key, w_value, w_gate, w_beta, w_out, taps_query, taps_key, taps_value, gain, gain_first, starts, lengths, hidden, w_down, resid, count):
    slots, model = tokens.shape
    wide = w_query.shape[1]
    width = gain.shape[0]
    heads = wide // width
    seqs = starts.shape[1]
    chunks = slots // CHUNK
    taps = taps_query.shape[0]
    smem = pl.BlockSpec(memory_space=pltpu.SMEM)
    fixed = lambda shape: pl.BlockSpec(shape, lambda n: (0,) * len(shape), pipeline_mode=pl.Buffered(1))
    piece = lambda shape: pl.BlockSpec(shape, lambda n: (chunks - 1 - n,) + (0,) * (len(shape) - 1))
    rows = lambda a: piece((CHUNK, a.shape[1]))
    outs = (
        [((slots, model), BF16)] + [((model, wide), BF16)] * 4 + [(w_beta.shape, F32), ((wide, model), BF16)]
        + [((taps, wide), F32)] * 3 + [((1, width), F32), ((1, model), F32), (resid.shape, BF16)]
    )
    return pl.pallas_call(
        functools.partial(backward_kernel, heads, width, seqs, chunks, count, slots // count),
        name="mixer_backward",
        grid=(chunks,),
        out_shape=[jax.ShapeDtypeStruct(s, d) for s, d in outs],
        in_specs=[smem, smem, rows(tokens), rows(grad_attended)]
        + [rows(a) for a in saved[:11]]
        + [piece((1, heads, CHUNK, CHUNK)), piece((1, heads, width, width))]
        + [fixed((model, wide))] * 4
        + [fixed(w_beta.shape), fixed((wide, model))]
        + [fixed((taps, wide))] * 3
        + [fixed((1, width)), fixed((1, model)), fixed(hidden.shape), fixed(w_down.shape), fixed(resid.shape)],
        out_specs=[piece((CHUNK, model))] + [fixed(s) for s, d in outs[1:]],
        scratch_shapes=[pltpu.VMEM((model, wide), F32)] * 4
        + [pltpu.VMEM((wide, model), F32)]
        + [pltpu.VMEM((CHUNK + 8, wide), F32)] * 3
        + [pltpu.VMEM((heads, width, width), F32), ring_slots(count, slots // count, model)]
        + ring_semaphores(count),
        compiler_params=ring_params(6),
        cost_estimate=pl.CostEstimate(
            flops=2 * slots * model * wide * 10 + slots * heads * CHUNK * 2 * CHUNK * 8,
            bytes_accessed=slots * model * 6 + 10 * model * wide * 2 + slots * wide * 36,
            transcendentals=slots * wide * 8,
        ),
    )(starts, lengths, tokens, grad_attended, *saved, w_query, w_key, w_value, w_gate, w_beta, w_out, taps_query, taps_key, taps_value, gain.reshape(1, width), gain_first.reshape(1, model), hidden, w_down, resid)


def make_shards(groups, count):
    def shards(
        tokens, attn_gain, w_query, w_key, w_value, conv_query, conv_key, conv_value, w_beta, w_gate_out,
        head_gain, w_out, ffn_gain, w_gate, w_up, w_down, seq_starts, seq_lengths, cotangent,
    ):
        model = tokens.shape[1]
        heads = w_beta.shape[1]
        beta_rows = w_beta.T if heads > 1 else jnp.pad(w_beta.T, ((0, 1), (0, 0)))
        tokens_full = gather_tokens(tokens, count)
        saved = forward_mixer(
            tokens_full, w_query, w_key, w_value, w_gate_out, beta_rows,
            conv_query, conv_key, conv_value, head_gain, attn_gain, seq_starts, seq_lengths, cotangent, count,
        )
        grad_full, saved = saved[-1], saved[:-1]
        resid, ffn_full, hidden, grad_gate, grad_up = attend(
            saved[0], w_out, tokens, ffn_gain, w_gate.T, w_up.T, w_down, grad_full, count
        )
        grad_resid, grad_attended, g_second, *ffn_grads = ffn_back(
            grad_gate, grad_up, hidden, w_gate.T, w_up.T, resid, cotangent, ffn_gain, ffn_full, grad_full,
            count, groups,
        )
        pulled = backward_mixer(
            tokens_full, grad_attended, saved, w_query, w_key, w_value, w_gate_out, beta_rows, w_out,
            conv_query, conv_key, conv_value, head_gain, attn_gain, seq_starts, seq_lengths,
            hidden, w_down, resid, count,
        )
        terms, gw_query, gw_key, gw_value, gw_gate_out, gw_beta, gw_out = pulled[:7]
        gt_query, gt_key, gt_value, g_head, g_first, output = pulled[7:]
        wide = gt_query.shape[1]
        gw_beta = gw_beta[:heads]
        taps = gt_query.shape[0]
        small = jnp.concatenate(
            [
                g_first,
                g_second,
                jnp.pad(g_head, ((0, 0), (0, model - g_head.shape[1]))),
                jnp.zeros((5, model), F32),
                gw_beta,
                jnp.pad(
                    jnp.concatenate([gt_query, gt_key, gt_value], 1), ((0, 0), (0, model - 3 * wide))
                ),
                jnp.zeros((-(heads + taps) % 8, model), F32),
            ],
            0,
        )
        grad_tokens, total, *mixer_grads = last_step(
            terms, tokens, grad_resid, attn_gain, small,
            (gw_query, gw_key, gw_value, gw_gate_out, gw_out), count, groups,
        )
        mixer_grads = [g.astype(F32) for g in mixer_grads]
        tap_rows = total[8 + heads : 8 + heads + taps]
        return (
            output,
            grad_tokens,
            total[0],
            mixer_grads[0],
            mixer_grads[1],
            mixer_grads[2],
            tap_rows[:, :wide],
            tap_rows[:, wide : 2 * wide],
            tap_rows[:, 2 * wide : 3 * wide],
            total[8 : 8 + heads].T,
            mixer_grads[3],
            total[2, : head_gain.shape[0]],
            mixer_grads[4],
            total[1],
            ffn_grads[0].astype(F32).T,
            ffn_grads[1].astype(F32).T,
            ffn_grads[2].astype(F32),
        )

    return shards


def solution(mesh):
    placed = (
        P(("dp", "tensor"), None),
        P(),
        P(None, "tensor"),
        P(None, "tensor"),
        P(None, "tensor"),
        P(None, "tensor"),
        P(None, "tensor"),
        P(None, "tensor"),
        P(None, "tensor"),
        P(None, "tensor"),
        P(),
        P("tensor", None),
        P(),
        P(None, "tensor"),
        P(None, "tensor"),
        P("tensor", None),
        P("dp", None),
        P("dp", None),
        P(("dp", "tensor"), None),
    )
    return jax.shard_map(
        make_shards(mesh.shape["dp"], mesh.shape["tensor"]),
        mesh=mesh,
        in_specs=placed,
        out_specs=(
            P(("dp", "tensor"), None),
            P(("dp", "tensor"), None),
            P(),
            P(None, "tensor"),
            P(None, "tensor"),
            P(None, "tensor"),
            P(None, "tensor"),
            P(None, "tensor"),
            P(None, "tensor"),
            P(None, "tensor"),
            P(None, "tensor"),
            P(),
            P("tensor", None),
            P(),
            P(None, "tensor"),
            P(None, "tensor"),
            P("tensor", None),
        ),
        check_vma=False,
    )
```

```python
import functools
import jax
import jax.numpy as jnp
from jax import lax
from jax.experimental import pallas as pl
from jax.experimental.pallas import tpu as pltpu
from jax.sharding import PartitionSpec as P

CHUNK = 256
F32, BF16 = jnp.float32, jnp.bfloat16


def mm(a, b, contract=(1, 0)):
    return lax.dot_general(
        a.astype(BF16),
        b.astype(BF16),
        (((contract[0],), (contract[1],)), ((), ())),
        preferred_element_type=F32,
    )


def segment_at(places, starts, lengths, seqs):
    segment = jnp.zeros_like(places)
    for s in range(seqs):
        begin = starts[0, s]
        stop = begin + lengths[0, s]
        segment = segment + jnp.where(places >= begin, 1, 0) + jnp.where(places >= stop, 1, 0)
    return jnp.where(places < 0, -1, segment)


def chunk_masks(starts, lengths, seqs, first, size):
    rows = first + lax.broadcasted_iota(jnp.int32, (size, 1), 0)
    columns = first + lax.broadcasted_iota(jnp.int32, (1, size), 1)
    seg_rows = segment_at(rows, starts, lengths, seqs)
    seg_columns = segment_at(columns, starts, lengths, seqs)
    before = segment_at(jnp.full((1, 1), first - 1, jnp.int32), starts, lengths, seqs)
    last = segment_at(jnp.full((1, 1), first + size - 1, jnp.int32), starts, lengths, seqs)
    return rows, seg_rows, seg_columns, before, last


def inverse_unit_lower(lower, size):
    i = lax.broadcasted_iota(jnp.int32, (size, size), 0)
    j = lax.broadcasted_iota(jnp.int32, (size, size), 1)

    def corner(width):
        shift = width.bit_length() - 1
        pair = (i >> (shift + 1)) == (j >> (shift + 1))
        return pair & (((i >> shift) & 1) == 1) & (((j >> shift) & 1) == 0)

    inverse = jnp.where(i == j, 1.0, 0.0) - jnp.where(corner(1), lower, 0.0)
    width = 2
    while width < size:
        low = inverse.astype(BF16)
        if 2 * width == size:
            part = mm(mm(low[width:, width:], lower[width:, :width]), low[:width, :width])
            inverse = jnp.concatenate(
                [
                    inverse[:width],
                    jnp.concatenate([-part, inverse[width:, width:]], axis=1),
                ],
                axis=0,
            )
        else:
            between = jnp.where(corner(width), lower, 0.0)
            inverse = inverse - mm(mm(low, between), low)
        width *= 2
    return inverse


def sigmoid(v):
    return 1.0 / (1.0 + jnp.exp(-v))


def normed_rows(tokens, gain):
    value = tokens[...].astype(F32)
    unit = value * lax.rsqrt(jnp.mean(value * value, axis=1, keepdims=True) + 1e-6)
    return unit * gain[...].astype(F32), unit


MESH = pl.DeviceIdType.MESH
SUBS = 2


def ring_position(device, count):
    half, odd = device // 2, device % 2
    return half + odd * (count - 1 - 2 * half)


def ring_device(position, count):
    back = position // (count // 2)
    return (1 - back) * 2 * position + back * (2 * (count - 1 - position) + 1)


class Ring:
    def __init__(self, count):
        self.count = count
        self.me = lax.axis_index("tensor")
        self.place = ring_position(self.me, count)
        self.group = lax.axis_index("dp")

    def at(self, offset):
        return ring_device((self.place + offset + 2 * self.count) % self.count, self.count)

    def next(self, way):
        return (self.group, self.at(1 if way == 0 else -1))


def gather_copy(ring, source, target, sends, recvs, way, sub, step, origin, rows):
    piece = rows // (2 * SUBS)
    inside = way * (rows // 2) + sub * piece
    start = pl.multiple_of(origin * rows + inside, piece)
    src = target.at[pl.ds(start, piece), :] if source is None else source.at[pl.ds(inside, piece), :]
    return pltpu.make_async_remote_copy(
        src_ref=src,
        dst_ref=target.at[pl.ds(start, piece), :],
        send_sem=sends.at[way, sub, step],
        recv_sem=recvs.at[way, sub, step],
        device_id=ring.next(way),
        device_id_type=MESH,
    )


PAIRS = [(sub, way) for sub in range(SUBS) for way in (0, 1)]


class Gather:
    def __init__(self, ring, source, target, sends, recvs, local, rows):
        self.ring, self.source, self.target = ring, source, target
        self.sends, self.recvs, self.rows = sends, recvs, rows
        self.keep = None
        if source is not None:
            self.keep = pltpu.make_async_copy(
                source, target.at[pl.ds(pl.multiple_of(ring.me * rows, rows), rows), :], local
            )

    def origin(self, way, step):
        return self.ring.at(-step if way == 0 else step)

    def copy(self, way, sub, step, origin, source=None):
        return gather_copy(
            self.ring, source, self.target, self.sends, self.recvs, way, sub, step, origin, self.rows
        )

    def begin(self):
        if self.keep is not None:
            self.keep.start()
        for sub, way in PAIRS:
            self.copy(way, sub, 0, self.ring.me, self.source).start()

    def arrived(self, step):
        for sub, way in PAIRS:
            self.copy(way, sub, step - 1, self.origin(way, step)).wait_recv()

    def hop(self, step):
        for sub, way in PAIRS:
            self.copy(way, sub, step - 1, self.origin(way, step)).wait_recv()
            self.copy(way, sub, step, self.origin(way, step)).start()

    def end(self):
        def drain(step, carry):
            for sub, way in PAIRS:
                self.copy(way, sub, step, self.ring.me).wait_send()
            return carry

        lax.fori_loop(0, self.ring.count - 1, drain, 0)
        if self.keep is not None:
            self.keep.wait()


def ring_gather(ring, source, target, sends, recvs, local, rows, between=None):
    gather = Gather(ring, source, target, sends, recvs, local, rows)
    gather.begin()
    if between is not None:
        between(0)

    def forward(step, carry):
        gather.hop(step)
        if between is not None:
            between(step)
        return carry

    lax.fori_loop(1, ring.count - 1, forward, 0)
    gather.arrived(ring.count - 1)
    if between is not None:
        between(ring.count - 1)
    gather.end()


def scatter_copy(ring, slots, sends, recvs, way, sub, step):
    return pltpu.make_async_remote_copy(
        src_ref=slots.at[way, sub, step],
        dst_ref=slots.at[way, sub, step + 1],
        send_sem=sends.at[way, sub, step],
        recv_sem=recvs.at[way, sub, step],
        device_id=ring.next(way),
        device_id_type=MESH,
    )


class Scatter:
    def __init__(self, ring, partial, slots, sends, recvs, rows, finish):
        self.ring, self.partial, self.slots, self.sends, self.recvs = ring, partial, slots, sends, recvs
        self.half, self.finish = rows // 2, finish
        self.rows, self.piece = rows, rows // (2 * SUBS)

    def terms(self, step):
        half, first, second = self.half, self.ring.at(-1 - step), self.ring.at(1 + step)
        return self.partial(
            pl.multiple_of(first * self.rows, half), pl.multiple_of(second * self.rows + half, half), step
        )

    def part(self, terms, way, sub):
        start = way * self.half + sub * self.piece
        return terms[start : start + self.piece]

    def copy(self, way, sub, step):
        return scatter_copy(self.ring, self.slots, self.sends, self.recvs, way, sub, step)

    def begin(self):
        terms = self.terms(0)
        for sub, way in PAIRS:
            self.slots[way, sub, 0] = self.part(terms, way, sub).astype(BF16)
            self.copy(way, sub, 0).start()

    def hop(self, step):
        terms = self.terms(step)
        for sub, way in PAIRS:
            self.copy(way, sub, step - 1).wait_recv()
            self.slots[way, sub, step] = (
                self.slots[way, sub, step].astype(F32) + self.part(terms, way, sub)
            ).astype(BF16)
            self.copy(way, sub, step).start()

    def end(self):
        count = self.ring.count
        terms = self.terms(count - 1)
        for sub, way in PAIRS:
            self.copy(way, sub, count - 2).wait_recv()
            self.finish(
                way * self.half + sub * self.piece,
                self.piece,
                self.slots[way, sub, count - 1].astype(F32) + self.part(terms, way, sub),
            )

        def drain(step, carry):
            for sub, way in PAIRS:
                self.copy(way, sub, step).wait_send()
            return carry

        lax.fori_loop(0, count - 1, drain, 0)


def ring_scatter(ring, partial, slots, sends, recvs, rows, finish, between=None):
    scatter = Scatter(ring, partial, slots, sends, recvs, rows, finish)
    scatter.begin()
    if between is not None:
        between(0)

    def forward(step, carry):
        scatter.hop(step)
        if between is not None:
            between(step)
        return carry

    lax.fori_loop(1, ring.count - 1, forward, 0)
    if between is not None:
        between(ring.count - 1)
    scatter.end()


class GroupSum:
    def __init__(self, ring, groups, grads, near, far, targets, near_sems, far_sems, back_sems, keep_sems):
        self.ring, self.groups, self.grads, self.near, self.far, self.targets = ring, groups, grads, near, far, targets
        self.near_sems, self.far_sems, self.back_sems, self.keep_sems = near_sems, far_sems, back_sems, keep_sems
        self.core = ring.group % 2
        self.mate = (ring.group + 1 - 2 * self.core, ring.me)

    def peers(self):
        return [self.mate] + [
            ((self.ring.group + 2 * k) % self.groups, self.ring.me) for k in range(1, self.groups // 2)
        ]

    def half(self, i, core):
        rows = self.near[i].shape[0]
        return pl.ds(pl.multiple_of(core * rows, rows), rows)

    def near_copy(self, i):
        return pltpu.make_async_remote_copy(
            src_ref=self.grads[i].at[self.half(i, 1 - self.core), :], dst_ref=self.near[i],
            send_sem=self.near_sems.at[0, i], recv_sem=self.near_sems.at[1, i],
            device_id=self.mate, device_id_type=MESH,
        )

    def far_copy(self, i, k):
        return pltpu.make_async_remote_copy(
            src_ref=self.near[i], dst_ref=self.far[i].at[k - 1],
            send_sem=self.far_sems.at[0, i, k - 1], recv_sem=self.far_sems.at[1, i, k - 1],
            device_id=((self.ring.group + 2 * k) % self.groups, self.ring.me), device_id_type=MESH,
        )

    def back_copy(self, i):
        return pltpu.make_async_remote_copy(
            src_ref=self.far[i].at[0], dst_ref=self.targets[i].at[self.half(i, self.core), :],
            send_sem=self.back_sems.at[0, i], recv_sem=self.back_sems.at[1, i],
            device_id=self.mate, device_id_type=MESH,
        )

    def keep_copy(self, i):
        return pltpu.make_async_copy(
            self.far[i].at[0], self.targets[i].at[self.half(i, self.core), :], self.keep_sems.at[i]
        )

    def first(self, chosen):
        for i in chosen:
            self.near_copy(i).start()

    def each_block(self, i, body):
        rows = self.near[i].shape[0]
        block = next(size for size in (64, 32, 16) if rows % size == 0)

        def step(at, carry):
            start = pl.multiple_of(at * block, block)
            body(pl.ds(start, block), pl.ds(pl.multiple_of(self.core * rows + start, block), block))
            return carry

        lax.fori_loop(0, rows // block, step, 0)

    def second(self, chosen):
        for i in chosen:
            self.near_copy(i).wait_recv()

            def add(here, own, i=i):
                self.near[i][here, :] = (
                    self.near[i][here, :].astype(F32) + self.grads[i][own, :].astype(F32)
                ).astype(BF16)

            self.each_block(i, add)
            for k in range(1, self.groups // 2):
                self.far_copy(i, k).start()

    def third(self, chosen):
        for i in chosen:
            for k in range(1, self.groups // 2):
                self.far_copy(i, k).wait()

            def add(here, own, i=i):
                total = self.near[i][here, :].astype(F32)
                for k in range(self.groups // 2 - 1):
                    total = total + self.far[i][k, here, :].astype(F32)
                self.far[i][0, here, :] = total.astype(BF16)

            self.each_block(i, add)
            self.keep_copy(i).start()
            self.back_copy(i).start()

    def last(self):
        for i in range(len(self.grads)):
            self.near_copy(i).wait_send()
            self.back_copy(i).wait()
            self.keep_copy(i).wait()


def sum_scratch(shapes, groups):
    number = len(shapes)
    return (
        [pltpu.VMEM((rows // 2, columns), BF16) for rows, columns in shapes]
        + [pltpu.VMEM((groups // 2 - 1, rows // 2, columns), BF16) for rows, columns in shapes]
        + [
            pltpu.SemaphoreType.DMA((2, number)),
            pltpu.SemaphoreType.DMA((2, number, groups // 2 - 1)),
            pltpu.SemaphoreType.DMA((2, number)),
            pltpu.SemaphoreType.DMA((number,)),
        ]
    )


def greet(ring, others=()):
    barrier = pltpu.get_barrier_semaphore()
    peers = [ring.next(0), ring.next(1)] + list(others)
    for peer in peers:
        pl.semaphore_signal(barrier, inc=1, device_id=peer, device_id_type=MESH)
    pl.semaphore_wait(barrier, len(peers))


def ring_semaphores(count):
    return [pltpu.SemaphoreType.DMA((2, SUBS, count - 1))] * 2


def ring_slots(count, rows, columns):
    return pltpu.VMEM((2, SUBS, count, rows // (2 * SUBS), columns), BF16)


ANY = pl.BlockSpec(memory_space=pl.ANY)
VMEM = pl.BlockSpec(memory_space=pltpu.VMEM)


def ring_params(number):
    return pltpu.CompilerParams(
        collective_id=number, has_side_effects=True, vmem_limit_bytes=60 << 20
    )


def gather_kernel(count, rows, source, target, sends, recvs, local):
    ring = Ring(count)
    greet(ring)
    ring_gather(ring, source, target, sends, recvs, local, rows)


def gather_tokens(tokens, count):
    rows, model = tokens.shape
    return pl.pallas_call(
        functools.partial(gather_kernel, count, rows),
        name="gather_tokens",
        out_shape=jax.ShapeDtypeStruct((count * rows, model), tokens.dtype),
        in_specs=[ANY],
        out_specs=ANY,
        scratch_shapes=ring_semaphores(count) + [pltpu.SemaphoreType.DMA],
        compiler_params=ring_params(1),
        cost_estimate=pl.CostEstimate(flops=0, bytes_accessed=300 << 20, transcendentals=0),
    )(tokens)


def logistic(v):
    return 1.0 / (1.0 + jnp.exp(-v))


def attend_kernel(
    count, rows, mixed, w_out, tokens, gain, w_gate, w_up, w_down, cotangents,
    resid, full, hidden, grad_gate, grad_up,
    slots, gathered, grad_hidden, boxes, sends, recvs, sends_two, recvs_two, box_sems, out_sems,
):
    ring = Ring(count)
    half = rows // 2

    def box_copy(block):
        return pltpu.make_async_copy(
            cotangents.at[pl.ds(pl.multiple_of(block * rows, rows), rows), :],
            boxes.at[block % 2],
            box_sems.at[block % 2],
        )

    box_copy(0).start()
    greet(ring)

    def partial(first, second, step):
        return mm(jnp.concatenate([mixed[pl.ds(first, half), :], mixed[pl.ds(second, half), :]], 0), w_out[...])

    def finish(start, size, attended):
        value = tokens[start : start + size, :].astype(F32) + attended
        resid[start : start + size, :] = value
        scale = lax.rsqrt(jnp.mean(value * value, axis=1, keepdims=True) + 1e-6)
        gathered[pl.ds(pl.multiple_of(ring.me * rows + start, size), size), :] = (
            value * scale * gain[...].astype(F32)
        ).astype(BF16)

    def hide(block):
        box_copy(block).wait()

        @pl.when(block + 1 < count)
        def _():
            box_copy(block + 1).start()

        grad_hidden[pl.ds(pl.multiple_of(block * rows, rows), rows), :] = mm(
            boxes[block % 2], w_down[...], (1, 1)
        )

    ring_scatter(ring, partial, slots, sends, recvs, rows, finish, hide)
    gather = Gather(ring, None, gathered, sends_two, recvs_two, None, rows)

    def places(step):
        return [
            pl.ds(pl.multiple_of(gather.origin(way, step) * rows + way * half, half), half) for way in (0, 1)
        ]

    def out_copy(way, step):
        at = places(step)[way]
        return pltpu.make_async_copy(gathered.at[at, :], full.at[at, :], out_sems.at[way, step])

    def feed(step):
        one, two = places(step)
        for way in (0, 1):
            out_copy(way, step).start()
        inputs = jnp.concatenate([gathered[one, :], gathered[two, :]], 0)
        gate = mm(inputs, w_gate[...], (1, 1))
        up = mm(inputs, w_up[...], (1, 1))
        grad = jnp.concatenate([grad_hidden[one, :], grad_hidden[two, :]], 0)
        sig = logistic(gate)
        opened = gate * sig
        for target, value in (
            (hidden, opened * up),
            (grad_gate, grad * up * sig * (1.0 + gate * (1.0 - sig))),
            (grad_up, grad * opened),
        ):
            low = value.astype(BF16)
            target[one, :] = low[:half]
            target[two, :] = low[half:]

    ring_gather(ring, None, gathered, sends_two, recvs_two, None, rows, feed)

    def drain(step, carry):
        for way in (0, 1):
            out_copy(way, step).wait()
        return carry

    lax.fori_loop(0, count, drain, 0)


def attend(mixed, w_out, tokens, gain, w_gate, w_up, w_down, cotangents, count):
    rows, model = tokens.shape
    slots, inner = count * rows, w_down.shape[0]
    return pl.pallas_call(
        functools.partial(attend_kernel, count, rows),
        name="attend",
        out_shape=[
            jax.ShapeDtypeStruct((rows, model), F32),
            jax.ShapeDtypeStruct((slots, model), BF16),
        ]
        + [jax.ShapeDtypeStruct((slots, inner), BF16)] * 3,
        in_specs=[VMEM] * 7 + [ANY],
        out_specs=[VMEM, ANY] + [VMEM] * 3,
        scratch_shapes=[
            ring_slots(count, rows, model),
            pltpu.VMEM((slots, model), BF16),
            pltpu.VMEM((slots, inner), F32),
            pltpu.VMEM((2, rows, model), BF16),
        ]
        + ring_semaphores(count) * 2
        + [pltpu.SemaphoreType.DMA((2,)), pltpu.SemaphoreType.DMA((2, count))],
        compiler_params=ring_params(2),
        cost_estimate=pl.CostEstimate(
            flops=2 * slots * model * (mixed.shape[1] + 3 * inner), bytes_accessed=600 << 20,
            transcendentals=slots * inner,
        ),
    )(mixed, w_out, tokens, gain.reshape(1, model), w_gate, w_up, w_down, cotangents)


def norm_back(inputs, scale, gain, grad_normed):
    weighted = gain * grad_normed
    inner = jnp.mean(weighted * inputs, axis=1, keepdims=True)
    unit = inputs * scale
    return scale * weighted - unit * (scale * scale * inner), grad_normed * unit


JOBS = 8


def ffn_back_kernel(
    count, groups, rows, grad_gate, grad_up, hidden, w_gate, w_up, resid, cotangent, gain, inputs, cotangents,
    grad_resid, full, grad_gain, sum_gate, sum_up, sum_down,
    slots, low, gw_gate, gw_up, gw_down, boxes, box_sems, *rest,
):
    ring = Ring(count)
    sends, recvs, sends_two, recvs_two, local = rest[:5]
    sums = GroupSum(
        ring, groups, (gw_gate, gw_up, gw_down), rest[5:8], rest[8:11], (sum_gate, sum_up, sum_down), *rest[11:]
    )
    wide = boxes.shape[2]

    def box_copy(job):
        source = inputs if job < JOBS // 2 else cotangents
        at = job % (JOBS // 2) * wide
        return pltpu.make_async_copy(
            source.at[:, at : at + wide], boxes.at[job % 2], box_sems.at[job % 2]
        )

    box_copy(0).start()
    greet(ring, sums.peers())
    grad_gain[...] = jnp.zeros_like(grad_gain)
    half = rows // 2

    def partial(first, second, step):
        gates = jnp.concatenate([grad_gate[pl.ds(first, half), :], grad_gate[pl.ds(second, half), :]], 0)
        ups = jnp.concatenate([grad_up[pl.ds(first, half), :], grad_up[pl.ds(second, half), :]], 0)
        return mm(gates, w_gate[...]) + mm(ups, w_up[...])

    def finish(start, size, grad):
        value = resid[start : start + size, :]
        scale = lax.rsqrt(jnp.mean(value * value, axis=1, keepdims=True) + 1e-6)
        through, pieces = norm_back(value, scale, gain[...].astype(F32), grad)
        result = cotangent[start : start + size, :].astype(F32) + through
        grad_resid[start : start + size, :] = result
        grad_gain[...] += jnp.sum(pieces, axis=0, keepdims=True)
        low[start : start + size, :] = result.astype(BF16)

    def work(job):
        box_copy(job).wait()
        if job + 1 < JOBS:
            box_copy(job + 1).start()
        at = job % (JOBS // 2) * wide
        box = boxes[job % 2]
        if job < JOBS // 2:
            gw_gate[:, at : at + wide] = mm(grad_gate[...], box, (0, 0)).astype(BF16)
            gw_up[:, at : at + wide] = mm(grad_up[...], box, (0, 0)).astype(BF16)
        else:
            gw_down[:, at : at + wide] = mm(hidden[...], box, (0, 0)).astype(BF16)

    each = JOBS // 4
    events = {step: [functools.partial(work, step * each + k) for k in range(each)] for step in range(4)}
    events[1].append(lambda: sums.first((0, 1)))
    events[3].insert(0, lambda: sums.second((0, 1)))
    events[3].append(lambda: sums.first((2,)))
    events[5] = [lambda: sums.second((2,))]
    events_two = {count - 3: [lambda: sums.third((0, 1))], count - 2: [lambda: sums.third((2,))]}

    def between(table):
        def run(step):
            for when, actions in table.items():
                def act(actions=actions):
                    for action in actions:
                        action()

                if isinstance(step, int):
                    if step == when:
                        act()
                else:
                    pl.when(step == when)(act)

        return run

    ring_scatter(ring, partial, slots, sends, recvs, rows, finish, between(events))
    ring_gather(ring, low, full, sends_two, recvs_two, local, rows, between(events_two))
    sums.last()


def ffn_back(grad_gate, grad_up, hidden, w_gate, w_up, resid, cotangent, gain, inputs, cotangents, count, groups):
    rows, model = resid.shape
    slots, inner = grad_up.shape
    shapes = [(inner, model)] * 3
    return pl.pallas_call(
        functools.partial(ffn_back_kernel, count, groups, rows),
        name="ffn_back",
        out_shape=[
            jax.ShapeDtypeStruct((rows, model), F32),
            jax.ShapeDtypeStruct((slots, model), BF16),
            jax.ShapeDtypeStruct((1, model), F32),
        ]
        + [jax.ShapeDtypeStruct(shape, BF16) for shape in shapes],
        in_specs=[VMEM] * 8 + [ANY] * 2,
        out_specs=[VMEM, ANY, VMEM] + [ANY] * 3,
        scratch_shapes=[ring_slots(count, rows, model), pltpu.VMEM((rows, model), BF16)]
        + [pltpu.VMEM(shape, BF16) for shape in shapes]
        + [pltpu.VMEM((2, slots, model // (JOBS // 2)), BF16), pltpu.SemaphoreType.DMA((2,))]
        + ring_semaphores(count) * 2
        + [pltpu.SemaphoreType.DMA]
        + sum_scratch(shapes, groups),
        compiler_params=ring_params(3),
        cost_estimate=pl.CostEstimate(
            flops=10 * slots * model * inner, bytes_accessed=600 << 20, transcendentals=0
        ),
    )(grad_gate, grad_up, hidden, w_gate, w_up, resid, cotangent, gain.reshape(1, model), inputs, cotangents)


def last_kernel(
    count, groups, rows, terms, tokens, grad_resid, gain, small, *rest,
):
    grads, rest = rest[:5], rest[5:]
    grad_tokens, total = rest[:2]
    targets, rest = rest[2:7], rest[7:]
    slots, first_box, second_box, second_own, boxes, box_sems, sends, recvs = rest[:8]
    first_sends, first_recvs, second_sends, second_recvs = rest[8:12]
    ring = Ring(count)
    sums = GroupSum(ring, groups, grads, rest[12:17], rest[17:22], targets, *rest[22:])
    me, group = ring.me, ring.group
    first_peers = [(group, (me + k) % count) for k in range(1, count)]
    second_peers = [((group + k) % groups, me) for k in range(1, groups)]
    barrier = pltpu.get_barrier_semaphore()
    for peer in first_peers + second_peers:
        pl.semaphore_signal(barrier, inc=1, device_id=peer, device_id_type=MESH)
    pl.semaphore_wait(barrier, count + groups - 2)

    def first(k):
        return pltpu.make_async_remote_copy(
            src_ref=small.at[0:8], dst_ref=first_box.at[k], send_sem=first_sends.at[k],
            recv_sem=first_recvs.at[k], device_id=first_peers[k], device_id_type=MESH,
        )

    def second(k):
        return pltpu.make_async_remote_copy(
            src_ref=second_own, dst_ref=second_box.at[k], send_sem=second_sends.at[k],
            recv_sem=second_recvs.at[k], device_id=second_peers[k], device_id_type=MESH,
        )

    every = range(len(grads))
    sums.first(every)
    for k in range(count - 1):
        first(k).start()
    half = rows // 2

    def box_copy(way, start, slot):
        return pltpu.make_async_copy(
            terms.at[pl.ds(start, half), :], boxes.at[slot, way], box_sems.at[slot, way]
        )

    def fetch(step):
        for way, owner in ((0, ring.at(-1 - step)), (1, ring.at(1 + step))):
            box_copy(way, pl.multiple_of(owner * rows + way * half, half), step % 2).start()

    def partial(first, second, step):
        for way, start in ((0, first), (1, second)):
            box_copy(way, start, step % 2).wait()

        @pl.when(step + 1 < count)
        def _():
            fetch(step + 1)

        return jnp.concatenate([boxes[step % 2, 0], boxes[step % 2, 1]], 0).astype(F32)

    def finish(start, size, grad):
        value = tokens[start : start + size, :].astype(F32)
        scale = lax.rsqrt(jnp.mean(value * value, axis=1, keepdims=True) + 1e-6)
        through, pieces = norm_back(value, scale, gain[...].astype(F32), grad)
        grad_tokens[start : start + size, :] = grad_resid[start : start + size, :] + through

    def early():
        sums.second(every)
        for k in range(count - 1):
            first(k).wait()
        mine = small[0:8]
        for k in range(count - 1):
            mine = mine + first_box[k]
        second_own[0:8] = mine
        second_own[8:] = small[8:]
        for k in range(groups - 1):
            second(k).start()

    def late():
        for k in range(groups - 1):
            second(k).wait()
        mine = second_own[...]
        for k in range(groups - 1):
            mine = mine + second_box[k]
        total[...] = mine
        sums.third(every)

    def between(step):
        if isinstance(step, int):
            if step == 0:
                early()
        else:
            pl.when(step == count - 2)(late)

    fetch(0)
    ring_scatter(ring, partial, slots, sends, recvs, rows, finish, between)
    sums.last()


def last_step(terms, tokens, grad_resid, gain, small, grads, count, groups):
    rows, model = tokens.shape
    return pl.pallas_call(
        functools.partial(last_kernel, count, groups, rows),
        name="last_step",
        out_shape=[jax.ShapeDtypeStruct((rows, model), F32), jax.ShapeDtypeStruct(small.shape, F32)]
        + [jax.ShapeDtypeStruct(g.shape, BF16) for g in grads],
        in_specs=[ANY] + [VMEM] * (4 + len(grads)),
        out_specs=[VMEM, VMEM] + [ANY] * len(grads),
        scratch_shapes=[
            ring_slots(count, rows, model),
            pltpu.VMEM((count - 1, 8, model), F32),
            pltpu.VMEM((groups - 1,) + small.shape, F32),
            pltpu.VMEM(small.shape, F32),
            pltpu.VMEM((2, 2, rows // 2, model), BF16),
            pltpu.SemaphoreType.DMA((2, 2)),
        ]
        + ring_semaphores(count)
        + [pltpu.SemaphoreType.DMA((count - 1,))] * 2
        + [pltpu.SemaphoreType.DMA((groups - 1,))] * 2
        + sum_scratch([g.shape for g in grads], groups),
        compiler_params=ring_params(4),
        cost_estimate=pl.CostEstimate(flops=0, bytes_accessed=300 << 20, transcendentals=0),
    )(terms, tokens, grad_resid, gain.reshape(1, model), small, *grads)


def results_kernel(heads, taps, wide, width, total, *refs):
    number = (len(refs) - 7) // 2
    for source, target in zip(refs[:number], refs[number : 2 * number]):
        target[...] = source[...].astype(target.dtype)
    g_first, g_second, g_head, gt_query, gt_key, gt_value, g_beta = refs[2 * number :]

    @pl.when(pl.program_id(0) == 0)
    def _():
        g_first[...] = total[0:1, :]
        g_second[...] = total[1:2, :]
        g_head[...] = total[2:3, 0:width]
        row = 8 + heads
        for place, target in enumerate((gt_query, gt_key, gt_value)):
            target[...] = total[row : row + taps, place * wide : (place + 1) * wide]
        g_beta[...] = total[8 : 8 + heads, :]


def results(total, arrays, heads, taps, wide, width):
    model = total.shape[1]
    steps = next(n for n in (8, 4, 2, 1) if all(a.shape[0] % (8 * n) == 0 for a, _ in arrays))
    small = [(1, model), (1, model), (1, width)] + [(taps, wide)] * 3 + [(heads, model)]
    piece = lambda a: pl.BlockSpec((a.shape[0] // steps, a.shape[1]), lambda n: (n, 0))
    whole = lambda shape: pl.BlockSpec(shape, lambda n: (0, 0))
    return pl.pallas_call(
        functools.partial(results_kernel, heads, taps, wide, width),
        name="results",
        grid=(steps,),
        out_shape=[jax.ShapeDtypeStruct(a.shape, kind) for a, kind in arrays]
        + [jax.ShapeDtypeStruct(shape, F32) for shape in small],
        in_specs=[whole(total.shape)] + [piece(a) for a, _ in arrays],
        out_specs=[piece(a) for a, _ in arrays] + [whole(shape) for shape in small],
        compiler_params=pltpu.CompilerParams(vmem_limit_bytes=56 << 20),
        cost_estimate=pl.CostEstimate(flops=0, bytes_accessed=48 << 20, transcendentals=0),
    )(total, *[a for a, _ in arrays])


def spread_hops(step, chunks, count, begin, hop):
    each = -(-(count - 1) // (chunks - 1))

    @pl.when(step == 0)
    def _():
        begin()

    for place in range(each):
        number = step * each + place

        @pl.when((number > 0) & (number < count - 1))
        def _():
            hop(number)


def forward_kernel(
    heads, width, seqs, count, rows_own, chunks,
    starts, lengths, tokens, w_query, w_key, w_value, w_gate, w_beta,
    taps_query, taps_key, taps_value, gain, gain_first, side,
    mixed, p_query, p_key, p_value, p_gate, p_beta, z_query, z_key, z_value,
    delta_out, change_out, inverse_out, state_out, side_full,
    tail_query, tail_key, tail_value, state, sends, recvs, local,
):
    step = pl.program_id(0)
    size = tokens.shape[0]
    first = step * size

    @pl.when(step == 0)
    def _():
        for tail in (tail_query, tail_key, tail_value):
            tail[...] = jnp.zeros_like(tail)
        state[...] = jnp.zeros_like(state)

    ring = Ring(count)
    gather = Gather(ring, side, side_full, sends, recvs, local, rows_own)
    spread_hops(
        step, chunks, count,
        lambda: (greet(ring), gather.begin()),
        gather.hop,
    )
    rows, seg_rows, seg_columns, before, last = chunk_masks(starts, lengths, seqs, first, size)
    same = seg_rows == seg_columns
    i = lax.broadcasted_iota(jnp.int32, (size, size), 0)
    j = lax.broadcasted_iota(jnp.int32, (size, size), 1)
    strict = jnp.where(same & (i > j), 1.0, 0.0)
    inclusive = jnp.where(same & (i >= j), 1.0, 0.0)
    carried = jnp.where(seg_rows == before, 1.0, 0.0)
    ending = jnp.where(seg_rows == last, 1.0, 0.0)
    kept = jnp.where(before == last, 1.0, 0.0)
    live = jnp.where(seg_rows % 2 == 1, 1.0, 0.0)
    joined = [
        jnp.where(segment_at(rows - offset, starts, lengths, seqs) == seg_rows, 1.0, 0.0)
        for offset in range(1, taps_query.shape[0])
    ]
    inputs = normed_rows(tokens, gain_first)[0].astype(BF16)

    def feature(weight, taps, tail, p_out, z_out):
        projected = jnp.dot(inputs, weight[...], preferred_element_type=F32)
        p_out[...] = projected
        tail[8:, :] = projected
        tap = taps[...].astype(F32)
        result = projected * tap[0:1]
        for offset in range(1, tap.shape[0]):
            result = result + tail[8 - offset : 8 - offset + size, :] * tap[offset : offset + 1] * joined[offset - 1]
        tail[0:8, :] = projected[size - 8 :, :]
        z_out[...] = result
        return result * sigmoid(result)

    u_query = feature(w_query, taps_query, tail_query, p_query, z_query)
    u_key = feature(w_key, taps_key, tail_key, p_key, z_key)
    u_value = feature(w_value, taps_value, tail_value, p_value, z_value)
    gate = jnp.dot(inputs, w_gate[...], preferred_element_type=F32)
    p_gate[...] = gate
    beta_pre = mm(inputs, w_beta[...], (1, 1))
    p_beta[...] = beta_pre
    strength = sigmoid(beta_pre)
    opened = gate * sigmoid(gate)
    scale = width ** (-0.5)
    head_gain = gain[...].astype(F32)
    for h in range(heads):
        cols = slice(h * width, (h + 1) * width)
        uq, uk = u_query[:, cols], u_key[:, cols]
        query = (uq * lax.rsqrt(jnp.sum(uq * uq, axis=1, keepdims=True) + 1e-6)).astype(BF16)
        key = (uk * lax.rsqrt(jnp.sum(uk * uk, axis=1, keepdims=True) + 1e-6)).astype(BF16)
        value = u_value[:, cols].astype(BF16).astype(F32)
        beta = strength[:, h : h + 1]
        memory = state[h]
        low_memory = memory.astype(BF16)
        state_out[0, h] = low_memory
        lower = mm(key, key, (1, 1)) * strict * beta
        inverse = inverse_unit_lower(lower, size).astype(BF16)
        inverse_out[0, h] = inverse
        within = mm(query, key, (1, 1)) * inclusive
        change = mm(inverse, beta * (value - carried * mm(key, low_memory)))
        low_change = change.astype(BF16)
        change_out[:, cols] = low_change
        out = scale * (carried * mm(query, low_memory) + mm(within, low_change))
        state[h] = kept * memory + mm(key, ending * change, (0, 0))
        delta_out[:, cols] = out
        normal = out * lax.rsqrt(jnp.mean(out * out, axis=1, keepdims=True) + 1e-5) * head_gain
        mixed[:, cols] = (normal * opened[:, cols] * live).astype(BF16)

    @pl.when(step == chunks - 1)
    def _():
        gather.arrived(count - 1)
        gather.end()


def forward_mixer(tokens, w_query, w_key, w_value, w_gate, w_beta, taps_query, taps_key, taps_value, gain, gain_first, starts, lengths, side, count):
    slots, model = tokens.shape
    wide = w_query.shape[1]
    width = gain.shape[0]
    heads = wide // width
    seqs = starts.shape[1]
    chunks = slots // CHUNK
    taps = taps_query.shape[0]
    smem = pl.BlockSpec(memory_space=pltpu.SMEM)
    whole = lambda shape: pl.BlockSpec(shape, lambda n: (0,) * len(shape))
    piece = lambda shape: pl.BlockSpec(shape, lambda n: (n,) + (0,) * (len(shape) - 1))
    outs = [
        ((slots, wide), BF16), ((slots, wide), F32), ((slots, wide), F32), ((slots, wide), F32), ((slots, wide), F32),
        ((slots, w_beta.shape[0]), F32), ((slots, wide), F32), ((slots, wide), F32), ((slots, wide), F32),
        ((slots, wide), F32), ((slots, wide), BF16),
    ]
    return pl.pallas_call(
        functools.partial(forward_kernel, heads, width, seqs, count, slots // count, chunks),
        name="mixer_forward",
        grid=(chunks,),
        out_shape=[jax.ShapeDtypeStruct(s, d) for s, d in outs]
        + [
            jax.ShapeDtypeStruct((chunks, heads, CHUNK, CHUNK), BF16),
            jax.ShapeDtypeStruct((chunks, heads, width, width), BF16),
            jax.ShapeDtypeStruct((slots, model), BF16),
        ],
        in_specs=[smem, smem, piece((CHUNK, model))]
        + [whole((model, wide))] * 4
        + [whole(w_beta.shape)]
        + [whole((taps, wide))] * 3
        + [whole((1, width)), whole((1, model)), ANY],
        out_specs=[piece((CHUNK, s[1])) for s, d in outs]
        + [piece((1, heads, CHUNK, CHUNK)), piece((1, heads, width, width)), ANY],
        scratch_shapes=[pltpu.VMEM((CHUNK + 8, wide), F32)] * 3
        + [pltpu.VMEM((heads, width, width), F32)]
        + ring_semaphores(count)
        + [pltpu.SemaphoreType.DMA],
        compiler_params=ring_params(5),
        cost_estimate=pl.CostEstimate(
            flops=2 * slots * model * wide * 4 + slots * heads * CHUNK * 2 * CHUNK * 20,
            bytes_accessed=slots * model * 2 + 4 * model * wide * 2 + slots * wide * 36,
            transcendentals=slots * wide * 4,
        ),
    )(starts, lengths, tokens, w_query, w_key, w_value, w_gate, w_beta, taps_query, taps_key, taps_value, gain.reshape(1, width), gain_first.reshape(1, model), side)


def small_rows(heads, taps):
    return -(-(8 + heads + taps) // 8) * 8


def backward_kernel(
    heads, width, seqs, chunks, count, rows_own,
    starts, lengths, tokens, grad_attended, mixed, p_query, p_key, p_value, p_gate, p_beta,
    z_query, z_key, z_value, delta_out, change_in, inverse_in, state_in,
    w_query, w_key, w_value, w_gate, w_beta, w_out, taps_query, taps_key, taps_value, gain, gain_first,
    hidden, w_down, resid, g_second, grad_normed, gw_query, gw_key, gw_value, gw_gate, gw_out,
    small, output,
    a_query, a_key, a_value, a_gate, a_out, head_query, head_key, head_value, flow, slots, sends, recvs,
):
    step = pl.program_id(0)
    size = tokens.shape[0]
    first = (chunks - 1 - step) * size

    @pl.when(step == 0)
    def _():
        for ref in (a_query, a_key, a_value, a_gate, a_out, small, flow):
            ref[...] = jnp.zeros_like(ref)
        small[1:2, :] = g_second[...]
        for ref in (head_query, head_key, head_value):
            ref[size:, :] = jnp.zeros((8, ref.shape[1]), F32)

    half = rows_own // 2

    def partial(one, two, number):
        return mm(jnp.concatenate([hidden[pl.ds(one, half), :], hidden[pl.ds(two, half), :]], 0), w_down[...])

    def finish(start, length, down):
        output[start : start + length, :] = (resid[start : start + length, :] + down).astype(BF16)

    ring = Ring(count)
    scatter = Scatter(ring, partial, slots, sends, recvs, rows_own, finish)
    spread_hops(
        step, chunks, count,
        lambda: (greet(ring), scatter.begin()),
        scatter.hop,
    )
    rows, seg_rows, seg_columns, before, last = chunk_masks(starts, lengths, seqs, first, size)
    same = seg_rows == seg_columns
    i = lax.broadcasted_iota(jnp.int32, (size, size), 0)
    j = lax.broadcasted_iota(jnp.int32, (size, size), 1)
    strict = jnp.where(same & (i > j), 1.0, 0.0)
    inclusive = jnp.where(same & (i >= j), 1.0, 0.0)
    carried = jnp.where(seg_rows == before, 1.0, 0.0)
    ending = jnp.where(seg_rows == last, 1.0, 0.0)
    kept = jnp.where(before == last, 1.0, 0.0)
    live = jnp.where(seg_rows % 2 == 1, 1.0, 0.0)
    taps = taps_query.shape[0]
    joined = [
        jnp.where(segment_at(rows + offset, starts, lengths, seqs) == seg_rows, 1.0, 0.0)
        for offset in range(1, taps)
    ]
    normal_rows, unit_rows = normed_rows(tokens, gain_first)
    inputs = normal_rows.astype(BF16)
    grad_rows = grad_attended[...]
    grad_mixed = mm(grad_rows, w_out[...], (1, 1))
    a_out[...] += mm(mixed[...], grad_rows, (0, 0))
    strength = sigmoid(p_beta[...])
    scale = width ** (-0.5)
    head_gain = gain[...].astype(F32)

    grads_query, grads_key, grads_value, grads_gate, grads_beta = [], [], [], [], []
    for h in range(heads):
        cols = slice(h * width, (h + 1) * width)
        out = delta_out[:, cols]
        gate = p_gate[:, cols]
        sig_gate = sigmoid(gate)
        silu_gate = gate * sig_gate
        root = lax.rsqrt(jnp.mean(out * out, axis=1, keepdims=True) + 1e-5)
        grad = grad_mixed[:, cols] * live
        unit = out * root
        grads_gate.append(grad * unit * head_gain * (sig_gate * (1.0 + gate * (1.0 - sig_gate))))
        grad_normal = grad * silu_gate
        small[2:3, 0:width] += jnp.sum(grad_normal * unit, axis=0, keepdims=True)
        push = grad_normal * head_gain
        grad_out = scale * root * (push - unit * jnp.mean(push * unit, axis=1, keepdims=True))

        zq, zk, zv = z_query[:, cols], z_key[:, cols], z_value[:, cols]
        sq, sk, sv = sigmoid(zq), sigmoid(zk), sigmoid(zv)
        uq, uk = zq * sq, zk * sk
        nq = lax.rsqrt(jnp.sum(uq * uq, axis=1, keepdims=True) + 1e-6)
        nk = lax.rsqrt(jnp.sum(uk * uk, axis=1, keepdims=True) + 1e-6)
        unit_q, unit_k = uq * nq, uk * nk
        query, key = unit_q.astype(BF16), unit_k.astype(BF16)
        beta = strength[:, h : h + 1]
        change = change_in[:, cols]
        inverse = inverse_in[0, h]
        memory = state_in[0, h]
        flowing = flow[h]
        low_flow = flowing.astype(BF16)
        low_out = grad_out.astype(BF16)

        within = mm(query, key, (1, 1)) * inclusive
        grad_within = (mm(low_out, change, (1, 1)) * inclusive).astype(BF16)
        grad_change = mm(within, low_out, (0, 0)) + ending * mm(key, low_flow)
        grad_mid = mm(inverse, grad_change, (0, 0))
        grad_value = beta * grad_mid
        low_value = grad_value.astype(BF16)
        cross = (mm(low_value, change, (1, 1)) * strict).astype(BF16)
        grad_query = carried * mm(low_out, memory, (1, 1)) + mm(grad_within, key)
        grad_key = (
            mm(grad_within, query, (0, 0))
            + ending * mm(change, low_flow, (1, 1))
            - carried * mm(low_value, memory, (1, 1))
            - mm(cross, key)
            - mm(cross, key, (0, 0))
        )
        flow[h] = (
            kept * flowing
            + mm(query, carried * grad_out, (0, 0))
            - mm(key, carried * grad_value, (0, 0))
        )
        grads_beta.append((1.0 - beta) * jnp.sum(grad_mid * change.astype(F32), axis=1, keepdims=True))
        du_q = nq * (grad_query - unit_q * jnp.sum(grad_query * unit_q, axis=1, keepdims=True))
        du_k = nk * (grad_key - unit_k * jnp.sum(grad_key * unit_k, axis=1, keepdims=True))
        grads_query.append(du_q * sq * (1.0 + zq * (1.0 - sq)))
        grads_key.append(du_k * sk * (1.0 + zk * (1.0 - sk)))
        grads_value.append(grad_value * sv * (1.0 + zv * (1.0 - sv)))

    tap_row = 8 + heads
    wide = heads * width

    def unconv(parts, taps_ref, head, projected, place):
        lanes = slice(place * wide, (place + 1) * wide)
        grad = jnp.concatenate(parts, axis=1)
        head[0:size, :] = grad
        tap = taps_ref[...].astype(F32)
        p = projected[...]
        result = grad * tap[0:1]
        small[tap_row : tap_row + 1, lanes] += jnp.sum(p * grad, axis=0, keepdims=True)
        for offset in range(1, taps):
            moved = head[offset : offset + size, :] * joined[offset - 1]
            result = result + moved * tap[offset : offset + 1]
            row = tap_row + offset
            small[row : row + 1, lanes] += jnp.sum(p * moved, axis=0, keepdims=True)
        head[size:, :] = grad[0:8, :]
        return result.astype(BF16)

    d_query = unconv(grads_query, taps_query, head_query, p_query, 0)
    d_key = unconv(grads_key, taps_key, head_key, p_key, 1)
    d_value = unconv(grads_value, taps_value, head_value, p_value, 2)
    d_gate = jnp.concatenate(grads_gate, axis=1).astype(BF16)
    spare = [jnp.zeros((size, 1), F32)] * (w_beta.shape[0] - heads)
    d_beta = jnp.concatenate(grads_beta + spare, axis=1).astype(BF16)
    grad_inputs = (
        mm(d_query, w_query[...], (1, 1))
        + mm(d_key, w_key[...], (1, 1))
        + mm(d_value, w_value[...], (1, 1))
        + mm(d_gate, w_gate[...], (1, 1))
        + mm(d_beta, w_beta[...])
    )
    grad_normed[...] = grad_inputs.astype(BF16)
    small[0:1, :] += jnp.sum(grad_inputs * unit_rows, axis=0, keepdims=True)
    a_query[...] += mm(inputs, d_query, (0, 0))
    a_key[...] += mm(inputs, d_key, (0, 0))
    a_value[...] += mm(inputs, d_value, (0, 0))
    a_gate[...] += mm(inputs, d_gate, (0, 0))
    small[8 : 8 + heads, :] += mm(d_beta, inputs, (0, 0))[:heads]

    @pl.when(step == chunks - 1)
    def _():
        for target, source in (
            (gw_query, a_query), (gw_key, a_key), (gw_value, a_value), (gw_gate, a_gate),
            (gw_out, a_out),
        ):
            target[...] = source[...].astype(target.dtype)
        scatter.end()


def backward_mixer(tokens, grad_attended, saved, w_query, w_key, w_value, w_gate, w_beta, w_out, taps_query, taps_key, taps_value, gain, gain_first, starts, lengths, hidden, w_down, resid, g_second, count):
    slots, model = tokens.shape
    wide = w_query.shape[1]
    width = gain.shape[0]
    heads = wide // width
    seqs = starts.shape[1]
    chunks = slots // CHUNK
    taps = taps_query.shape[0]
    smem = pl.BlockSpec(memory_space=pltpu.SMEM)
    fixed = lambda shape: pl.BlockSpec(shape, lambda n: (0,) * len(shape), pipeline_mode=pl.Buffered(1))
    piece = lambda shape: pl.BlockSpec(shape, lambda n: (chunks - 1 - n,) + (0,) * (len(shape) - 1))
    rows = lambda a: piece((CHUNK, a.shape[1]))
    outs = (
        [((slots, model), BF16)] + [((model, wide), BF16)] * 4 + [((wide, model), BF16)]
        + [((small_rows(heads, taps), model), F32), (resid.shape, BF16)]
    )
    return pl.pallas_call(
        functools.partial(backward_kernel, heads, width, seqs, chunks, count, slots // count),
        name="mixer_backward",
        grid=(chunks,),
        out_shape=[jax.ShapeDtypeStruct(s, d) for s, d in outs],
        in_specs=[smem, smem, rows(tokens), rows(grad_attended)]
        + [rows(a) for a in saved[:11]]
        + [piece((1, heads, CHUNK, CHUNK)), piece((1, heads, width, width))]
        + [fixed((model, wide))] * 4
        + [fixed(w_beta.shape), fixed((wide, model))]
        + [fixed((taps, wide))] * 3
        + [fixed((1, width)), fixed((1, model)), fixed(hidden.shape), fixed(w_down.shape), fixed(resid.shape), fixed(g_second.shape)],
        out_specs=[piece((CHUNK, model))] + [fixed(s) for s, d in outs[1:]],
        scratch_shapes=[pltpu.VMEM((model, wide), F32)] * 4
        + [pltpu.VMEM((wide, model), F32)]
        + [pltpu.VMEM((CHUNK + 8, wide), F32)] * 3
        + [pltpu.VMEM((heads, width, width), F32), ring_slots(count, slots // count, model)]
        + ring_semaphores(count),
        compiler_params=ring_params(6),
        cost_estimate=pl.CostEstimate(
            flops=2 * slots * model * wide * 10 + slots * heads * CHUNK * 2 * CHUNK * 8,
            bytes_accessed=slots * model * 6 + 10 * model * wide * 2 + slots * wide * 36,
            transcendentals=slots * wide * 8,
        ),
    )(starts, lengths, tokens, grad_attended, *saved, w_query, w_key, w_value, w_gate, w_beta, w_out, taps_query, taps_key, taps_value, gain.reshape(1, width), gain_first.reshape(1, model), hidden, w_down, resid, g_second)


def make_shards(groups, count):
    def shards(
        tokens, attn_gain, w_query, w_key, w_value, conv_query, conv_key, conv_value, w_beta, w_gate_out,
        head_gain, w_out, ffn_gain, w_gate, w_up, w_down, seq_starts, seq_lengths, cotangent,
    ):
        model = tokens.shape[1]
        heads = w_beta.shape[1]
        beta_rows = w_beta.T if heads > 1 else jnp.pad(w_beta.T, ((0, 1), (0, 0)))
        tokens_full = gather_tokens(tokens, count)
        saved = forward_mixer(
            tokens_full, w_query, w_key, w_value, w_gate_out, beta_rows,
            conv_query, conv_key, conv_value, head_gain, attn_gain, seq_starts, seq_lengths, cotangent, count,
        )
        grad_full, saved = saved[-1], saved[:-1]
        resid, ffn_full, hidden, grad_gate, grad_up = attend(
            saved[0], w_out, tokens, ffn_gain, w_gate.T, w_up.T, w_down, grad_full, count
        )
        grad_resid, grad_attended, g_second, *ffn_grads = ffn_back(
            grad_gate, grad_up, hidden, w_gate.T, w_up.T, resid, cotangent, ffn_gain, ffn_full, grad_full,
            count, groups,
        )
        pulled = backward_mixer(
            tokens_full, grad_attended, saved, w_query, w_key, w_value, w_gate_out, beta_rows, w_out,
            conv_query, conv_key, conv_value, head_gain, attn_gain, seq_starts, seq_lengths,
            hidden, w_down, resid, g_second, count,
        )
        terms, gw_query, gw_key, gw_value, gw_gate_out, gw_out, small, output = pulled
        grad_tokens, total, *mixer_grads = last_step(
            terms, tokens, grad_resid, attn_gain, small,
            (gw_query, gw_key, gw_value, gw_gate_out, gw_out), count, groups,
        )
        taps, wide = conv_query.shape
        output, grad_tokens, *rest = results(
            total,
            [(output, BF16), (grad_tokens, F32)] + [(g, F32) for g in (*mixer_grads, *ffn_grads)],
            heads, taps, wide, head_gain.shape[0],
        )
        grads, (g_first, g_second, g_head, gt_query, gt_key, gt_value, g_beta) = rest[:8], rest[8:]
        return (
            output,
            grad_tokens,
            g_first[0],
            grads[0],
            grads[1],
            grads[2],
            gt_query,
            gt_key,
            gt_value,
            g_beta.T,
            grads[3],
            g_head[0],
            grads[4],
            g_second[0],
            grads[5].T,
            grads[6].T,
            grads[7],
        )

    return shards


def solution(mesh):
    placed = (
        P(("dp", "tensor"), None),
        P(),
        P(None, "tensor"),
        P(None, "tensor"),
        P(None, "tensor"),
        P(None, "tensor"),
        P(None, "tensor"),
        P(None, "tensor"),
        P(None, "tensor"),
        P(None, "tensor"),
        P(),
        P("tensor", None),
        P(),
        P(None, "tensor"),
        P(None, "tensor"),
        P("tensor", None),
        P("dp", None),
        P("dp", None),
        P(("dp", "tensor"), None),
    )
    return jax.shard_map(
        make_shards(mesh.shape["dp"], mesh.shape["tensor"]),
        mesh=mesh,
        in_specs=placed,
        out_specs=(
            P(("dp", "tensor"), None),
            P(("dp", "tensor"), None),
            P(),
            P(None, "tensor"),
            P(None, "tensor"),
            P(None, "tensor"),
            P(None, "tensor"),
            P(None, "tensor"),
            P(None, "tensor"),
            P(None, "tensor"),
            P(None, "tensor"),
            P(),
            P("tensor", None),
            P(),
            P(None, "tensor"),
            P(None, "tensor"),
            P("tensor", None),
        ),
        check_vma=False,
    )
```

```python
import functools
import jax
import jax.numpy as jnp
from jax import lax
from jax.experimental import pallas as pl
from jax.experimental.pallas import tpu as pltpu
from jax.sharding import PartitionSpec as P

CHUNK = 256
F32, BF16 = jnp.float32, jnp.bfloat16


def mm(a, b, contract=(1, 0)):
    return lax.dot_general(
        a.astype(BF16),
        b.astype(BF16),
        (((contract[0],), (contract[1],)), ((), ())),
        preferred_element_type=F32,
    )


def segment_at(places, starts, lengths, seqs):
    segment = jnp.zeros_like(places)
    for s in range(seqs):
        begin = starts[0, s]
        stop = begin + lengths[0, s]
        segment = segment + jnp.where(places >= begin, 1, 0) + jnp.where(places >= stop, 1, 0)
    return jnp.where(places < 0, -1, segment)


def chunk_masks(starts, lengths, seqs, first, size):
    rows = first + lax.broadcasted_iota(jnp.int32, (size, 1), 0)
    columns = first + lax.broadcasted_iota(jnp.int32, (1, size), 1)
    seg_rows = segment_at(rows, starts, lengths, seqs)
    seg_columns = segment_at(columns, starts, lengths, seqs)
    before = segment_at(jnp.full((1, 1), first - 1, jnp.int32), starts, lengths, seqs)
    last = segment_at(jnp.full((1, 1), first + size - 1, jnp.int32), starts, lengths, seqs)
    return rows, seg_rows, seg_columns, before, last


def inverse_unit_lower(lower, size):
    i = lax.broadcasted_iota(jnp.int32, (size, size), 0)
    j = lax.broadcasted_iota(jnp.int32, (size, size), 1)

    def corner(width):
        shift = width.bit_length() - 1
        pair = (i >> (shift + 1)) == (j >> (shift + 1))
        return pair & (((i >> shift) & 1) == 1) & (((j >> shift) & 1) == 0)

    inverse = jnp.where(i == j, 1.0, 0.0) - jnp.where(corner(1), lower, 0.0)
    width = 2
    while width < size:
        low = inverse.astype(BF16)
        if 2 * width == size:
            part = mm(mm(low[width:, width:], lower[width:, :width]), low[:width, :width])
            inverse = jnp.concatenate(
                [
                    inverse[:width],
                    jnp.concatenate([-part, inverse[width:, width:]], axis=1),
                ],
                axis=0,
            )
        else:
            between = jnp.where(corner(width), lower, 0.0)
            inverse = inverse - mm(mm(low, between), low)
        width *= 2
    return inverse


def sigmoid(v):
    return 1.0 / (1.0 + jnp.exp(-v))


def normed_rows(tokens, gain):
    value = tokens[...].astype(F32)
    unit = value * lax.rsqrt(jnp.mean(value * value, axis=1, keepdims=True) + 1e-6)
    return unit * gain[...].astype(F32), unit


MESH = pl.DeviceIdType.MESH
SUBS = 2
PAIRS = [(sub, way) for sub in range(SUBS) for way in (0, 1)]


def ring_position(device, count):
    half, odd = device // 2, device % 2
    return half + odd * (count - 1 - 2 * half)


def ring_device(position, count):
    back = position // (count // 2)
    return (1 - back) * 2 * position + back * (2 * (count - 1 - position) + 1)


class Ring:
    def __init__(self, count):
        self.count = count
        self.me = lax.axis_index("tensor")
        self.place = ring_position(self.me, count)
        self.group = lax.axis_index("dp")

    def at(self, offset):
        return ring_device((self.place + offset + 2 * self.count) % self.count, self.count)

    def next(self, way):
        return (self.group, self.at(1 if way == 0 else -1))


class Gather:
    def __init__(self, ring, own, view, sends, recvs, rows, subs=SUBS):
        self.ring, self.own, self.view, self.sends, self.recvs, self.rows = ring, own, view, sends, recvs, rows
        self.piece = rows // (2 * subs)
        self.pairs = [(sub, way) for sub in range(subs) for way in (0, 1)]

    def origin(self, way, step):
        return self.ring.at(-step if way == 0 else step)

    def copy(self, way, sub, step, origin, first=False):
        inside = way * (self.rows // 2) + sub * self.piece
        place = self.view(origin, inside, self.piece)
        return pltpu.make_async_remote_copy(
            src_ref=self.own(inside, self.piece) if first else place,
            dst_ref=place,
            send_sem=self.sends.at[way, sub, step],
            recv_sem=self.recvs.at[way, sub, step],
            device_id=self.ring.next(way),
            device_id_type=MESH,
        )

    def begin(self):
        for sub, way in self.pairs:
            self.copy(way, sub, 0, self.ring.me, True).start()

    def arrived(self, step):
        for sub, way in self.pairs:
            self.copy(way, sub, step - 1, self.origin(way, step)).wait_recv()

    def hop(self, step):
        for sub, way in self.pairs:
            self.copy(way, sub, step - 1, self.origin(way, step)).wait_recv()
            self.copy(way, sub, step, self.origin(way, step)).start()

    def end(self):
        def drain(step, carry):
            for sub, way in self.pairs:
                self.copy(way, sub, step, self.ring.me).wait_send()
            return carry

        lax.fori_loop(0, self.ring.count - 1, drain, 0)


def row_view(ref, rows):
    return lambda origin, start, size: ref.at[pl.ds(pl.multiple_of(origin * rows + start, size), size), :]


def row_own(ref):
    return lambda start, size: ref.at[pl.ds(start, size), :]


def ring_gather(gather, between):
    count = gather.ring.count

    def run(step, carry):
        @pl.when(step == 0)
        def _():
            gather.begin()

        @pl.when((step > 0) & (step < count - 1))
        def _():
            gather.hop(step)

        @pl.when(step == count - 1)
        def _():
            gather.arrived(step)

        between(step)
        return carry

    lax.fori_loop(0, count, run, 0)
    gather.end()


def scatter_copy(ring, slots, sends, recvs, way, sub, step):
    return pltpu.make_async_remote_copy(
        src_ref=slots.at[way, sub, step],
        dst_ref=slots.at[way, sub, step + 1],
        send_sem=sends.at[way, sub, step],
        recv_sem=recvs.at[way, sub, step],
        device_id=ring.next(way),
        device_id_type=MESH,
    )


class Scatter:
    def __init__(self, ring, partial, slots, sends, recvs, rows, finish):
        self.ring, self.partial, self.slots, self.sends, self.recvs = ring, partial, slots, sends, recvs
        self.half, self.finish = rows // 2, finish
        self.rows, self.piece = rows, rows // (2 * SUBS)

    def terms(self, step):
        half, first, second = self.half, self.ring.at(-1 - step), self.ring.at(1 + step)
        return self.partial(
            pl.multiple_of(first * self.rows, half), pl.multiple_of(second * self.rows + half, half), step
        )

    def part(self, terms, way, sub):
        start = way * self.half + sub * self.piece
        return terms[start : start + self.piece]

    def copy(self, way, sub, step):
        return scatter_copy(self.ring, self.slots, self.sends, self.recvs, way, sub, step)

    def hop(self, step):
        terms = self.terms(step)
        for sub, way in PAIRS:
            term = self.part(terms, way, sub)

            @pl.when(step == 0)
            def _():
                self.slots[way, sub, 0] = term.astype(BF16)

            @pl.when(step > 0)
            def _():
                self.copy(way, sub, step - 1).wait_recv()
                self.slots[way, sub, step] = (self.slots[way, sub, step].astype(F32) + term).astype(BF16)

            self.copy(way, sub, step).start()

    def end(self):
        count = self.ring.count
        terms = self.terms(count - 1)
        for sub, way in PAIRS:
            self.copy(way, sub, count - 2).wait_recv()
            self.finish(
                way * self.half + sub * self.piece,
                self.piece,
                self.slots[way, sub, count - 1].astype(F32) + self.part(terms, way, sub),
            )

        def drain(step, carry):
            for sub, way in PAIRS:
                self.copy(way, sub, step).wait_send()
            return carry

        lax.fori_loop(0, count - 1, drain, 0)


def ring_scatter(scatter, between):
    def run(step, carry):
        scatter.hop(step)
        between(step)
        return carry

    lax.fori_loop(0, scatter.ring.count - 1, run, 0)
    scatter.end()


class GroupSum:
    def __init__(self, ring, groups, grads, near, far, targets, near_sems, far_sems, back_sems, keep_sems):
        self.ring, self.groups, self.grads, self.near, self.far, self.targets = ring, groups, grads, near, far, targets
        self.near_sems, self.far_sems, self.back_sems, self.keep_sems = near_sems, far_sems, back_sems, keep_sems
        self.core = ring.group % 2
        self.mate = (ring.group + 1 - 2 * self.core, ring.me)

    def peers(self):
        return [self.mate] + [
            ((self.ring.group + 2 * k) % self.groups, self.ring.me) for k in range(1, self.groups // 2)
        ]

    def half(self, i, core):
        rows = self.near[i].shape[0]
        return pl.ds(pl.multiple_of(core * rows, rows), rows)

    def near_copy(self, i):
        return pltpu.make_async_remote_copy(
            src_ref=self.grads[i].at[self.half(i, 1 - self.core), :], dst_ref=self.near[i],
            send_sem=self.near_sems.at[0, i], recv_sem=self.near_sems.at[1, i],
            device_id=self.mate, device_id_type=MESH,
        )

    def far_copy(self, i, k):
        return pltpu.make_async_remote_copy(
            src_ref=self.near[i], dst_ref=self.far[i].at[k - 1],
            send_sem=self.far_sems.at[0, i, k - 1], recv_sem=self.far_sems.at[1, i, k - 1],
            device_id=((self.ring.group + 2 * k) % self.groups, self.ring.me), device_id_type=MESH,
        )

    def back_copy(self, i):
        return pltpu.make_async_remote_copy(
            src_ref=self.far[i].at[0], dst_ref=self.targets[i].at[self.half(i, self.core), :],
            send_sem=self.back_sems.at[0, i], recv_sem=self.back_sems.at[1, i],
            device_id=self.mate, device_id_type=MESH,
        )

    def keep_copy(self, i):
        return pltpu.make_async_copy(
            self.far[i].at[0], self.targets[i].at[self.half(i, self.core), :], self.keep_sems.at[i]
        )

    def first(self, chosen):
        for i in chosen:
            self.near_copy(i).start()

    def each_block(self, i, body):
        rows = self.near[i].shape[0]
        block = next(size for size in (64, 32, 16) if rows % size == 0)

        def step(at, carry):
            start = pl.multiple_of(at * block, block)
            body(pl.ds(start, block), pl.ds(pl.multiple_of(self.core * rows + start, block), block))
            return carry

        lax.fori_loop(0, rows // block, step, 0)

    def second(self, chosen):
        for i in chosen:
            self.near_copy(i).wait_recv()

            def add(here, own, i=i):
                self.near[i][here, :] = (
                    self.near[i][here, :].astype(F32) + self.grads[i][own, :].astype(F32)
                ).astype(BF16)

            self.each_block(i, add)
            for k in range(1, self.groups // 2):
                self.far_copy(i, k).start()

    def third(self, chosen):
        for i in chosen:
            for k in range(1, self.groups // 2):
                self.far_copy(i, k).wait()

            def add(here, own, i=i):
                total = self.near[i][here, :].astype(F32)
                for k in range(self.groups // 2 - 1):
                    total = total + self.far[i][k, here, :].astype(F32)
                self.far[i][0, here, :] = total.astype(BF16)

            self.each_block(i, add)
            self.keep_copy(i).start()
            self.back_copy(i).start()

    def last(self):
        for i in range(len(self.grads)):
            self.near_copy(i).wait_send()
            self.back_copy(i).wait()
            self.keep_copy(i).wait()


def sum_scratch(shapes, groups):
    number = len(shapes)
    return (
        [pltpu.VMEM((rows // 2, columns), BF16) for rows, columns in shapes]
        + [pltpu.VMEM((groups // 2 - 1, rows // 2, columns), BF16) for rows, columns in shapes]
        + [
            pltpu.SemaphoreType.DMA((2, number)),
            pltpu.SemaphoreType.DMA((2, number, groups // 2 - 1)),
            pltpu.SemaphoreType.DMA((2, number)),
            pltpu.SemaphoreType.DMA((number,)),
        ]
    )


def greet(ring, others=()):
    barrier = pltpu.get_barrier_semaphore()
    peers = [ring.next(0), ring.next(1)] + list(others)
    for peer in peers:
        pl.semaphore_signal(barrier, inc=1, device_id=peer, device_id_type=MESH)
    pl.semaphore_wait(barrier, len(peers))


def ring_semaphores(count, subs=SUBS):
    return [pltpu.SemaphoreType.DMA((2, subs, count - 1))] * 2


def ring_slots(count, rows, columns):
    return pltpu.VMEM((2, SUBS, count, rows // (2 * SUBS), columns), BF16)


ANY = pl.BlockSpec(memory_space=pl.ANY)
VMEM = pl.BlockSpec(memory_space=pltpu.VMEM)


def ring_params(number):
    return pltpu.CompilerParams(
        collective_id=number, has_side_effects=True, vmem_limit_bytes=60 << 20
    )


WEIGHT_HOPS = 3


def gather_kernel(
    count, groups, tokens, w_out, tokens_full, w_full,
    sends, recvs, w_sends, w_recvs, local, far_sems, near_sems,
):
    ring = Ring(count)
    rows = tokens.shape[0]
    group, me = ring.group, ring.me
    part = w_out.shape[0] // groups
    across = groups // 2
    mate = (group + 1 - 2 * (group % 2), me)
    gather = Gather(ring, row_own(tokens), row_view(tokens_full, rows), sends, recvs, rows)
    own_part = lambda start, size: w_out.at[pl.ds(pl.multiple_of(group * part + start, size), size), :]
    weights = Gather(
        ring, own_part, lambda origin, start, size: w_full.at[origin, group, pl.ds(start, size), :],
        w_sends, w_recvs, part, 1,
    )
    keep = pltpu.make_async_copy(
        tokens, tokens_full.at[pl.ds(pl.multiple_of(me * rows, rows), rows), :], local.at[0]
    )
    keep_part = pltpu.make_async_copy(own_part(0, part), w_full.at[me, group], local.at[1])

    def far(k):
        return pltpu.make_async_remote_copy(
            src_ref=w_full.at[:, group], dst_ref=w_full.at[:, group],
            send_sem=far_sems.at[0, k - 1], recv_sem=far_sems.at[1, k - 1],
            device_id=((group + 2 * k) % groups, me), device_id_type=MESH,
        )

    def near(k):
        held = (group + groups - 2 * k) % groups
        return pltpu.make_async_remote_copy(
            src_ref=w_full.at[:, held], dst_ref=w_full.at[:, held],
            send_sem=near_sems.at[0, k], recv_sem=near_sems.at[1, k],
            device_id=mate, device_id_type=MESH,
        )

    greet(ring, [mate] + [((group + 2 * k) % groups, me) for k in range(1, across)])
    weights.begin()
    gather.begin()
    keep.start()
    keep_part.start()
    whole_at = -(-(count - 2) // WEIGHT_HOPS) + 1

    def forward(step, carry):
        for place in range(WEIGHT_HOPS):
            number = (step - 1) * WEIGHT_HOPS + place + 1

            @pl.when(number < count - 1)
            def _():
                weights.hop(number)

        gather.hop(step)

        @pl.when(step == whole_at)
        def _():
            weights.arrived(count - 1)
            keep_part.wait()
            for k in range(1, across):
                far(k).start()
            near(0).start()

        return carry

    lax.fori_loop(1, count - 1, forward, 0)
    for k in range(1, across):
        far(k).wait_recv()
        near(k).start()
    gather.arrived(count - 1)
    for k in range(across):
        near(k).wait()
    for k in range(1, across):
        far(k).wait_send()
    weights.end()
    gather.end()
    keep.wait()


def gather_tokens(tokens, w_out, count, groups):
    rows, model = tokens.shape
    part = w_out.shape[0] // groups
    full, w_full = pl.pallas_call(
        functools.partial(gather_kernel, count, groups),
        name="gather_tokens",
        out_shape=[
            jax.ShapeDtypeStruct((count * rows, model), tokens.dtype),
            jax.ShapeDtypeStruct((count, groups, part, model), w_out.dtype),
        ],
        in_specs=[ANY] * 2,
        out_specs=[ANY] * 2,
        scratch_shapes=ring_semaphores(count)
        + ring_semaphores(count, 1)
        + [
            pltpu.SemaphoreType.DMA((2,)),
            pltpu.SemaphoreType.DMA((2, groups // 2 - 1)),
            pltpu.SemaphoreType.DMA((2, groups // 2)),
        ],
        compiler_params=ring_params(1),
        cost_estimate=pl.CostEstimate(flops=0, bytes_accessed=300 << 20, transcendentals=0),
    )(tokens, w_out)
    return full, w_full.reshape(count * w_out.shape[0], model)


def attend_kernel(
    count, mixed, w_out, tokens, gain, w_gate, w_up, w_down, cotangents,
    resid, full, hidden, grad_gate, grad_up,
    gathered, gate_box, up_box, down_box, boxes, stages, sends, recvs, weight_sems, box_sems, out_sems, stage_sems,
):
    ring = Ring(count)
    rows = tokens.shape[0]
    half = rows // 2
    gather = Gather(
        ring, lambda start, size: row_view(gathered, rows)(ring.me, start, size), row_view(gathered, rows),
        sends, recvs, rows,
    )
    loads = [
        pltpu.make_async_copy(source, box, weight_sems.at[k])
        for k, (source, box) in enumerate(((w_gate, gate_box), (w_up, up_box), (w_down, down_box)))
    ]

    def place(way, step):
        return pl.ds(pl.multiple_of(gather.origin(way, step) * rows + way * half, half), half)

    def box_copy(way, step):
        return pltpu.make_async_copy(
            cotangents.at[place(way, step), :], boxes.at[step % 2, way], box_sems.at[step % 2, way]
        )

    def out_copy(way, step):
        at = place(way, step)
        return pltpu.make_async_copy(gathered.at[at, :], full.at[at, :], out_sems.at[way, step])

    def stage_copy(k, way, step):
        target = (hidden, grad_gate, grad_up)[k]
        return pltpu.make_async_copy(
            stages.at[step % 2, k, way], target.at[place(way, step), :], stage_sems.at[step % 2, k, way]
        )

    def settle(step):
        for k in range(3):
            for way in (0, 1):
                stage_copy(k, way, step).wait()

    for way in (0, 1):
        box_copy(way, 0).start()
    for load in loads:
        load.start()
    greet(ring)
    value = tokens[...].astype(F32) + mm(mixed[...], w_out[...])
    resid[...] = value
    scale = lax.rsqrt(jnp.mean(value * value, axis=1, keepdims=True) + 1e-6)
    gathered[pl.ds(pl.multiple_of(ring.me * rows, rows), rows), :] = (
        value * scale * gain[...].astype(F32)
    ).astype(BF16)

    def feed(step):
        @pl.when(step == 0)
        def _():
            for load in loads:
                load.wait()

        @pl.when(step > 1)
        def _():
            settle(step - 2)

        for way in (0, 1):
            out_copy(way, step).start()
            box_copy(way, step).wait()

        @pl.when(step + 1 < count)
        def _():
            for way in (0, 1):
                box_copy(way, step + 1).start()

        slot = step % 2
        inputs = jnp.concatenate([gathered[place(0, step), :], gathered[place(1, step), :]], 0)
        gate = mm(inputs, gate_box[...], (1, 1))
        up = mm(inputs, up_box[...], (1, 1))
        grad = mm(jnp.concatenate([boxes[slot, 0], boxes[slot, 1]], 0), down_box[...], (1, 1))
        sig = sigmoid(gate)
        opened = gate * sig
        for k, result in enumerate(
            (opened * up, grad * up * sig * (1.0 + gate * (1.0 - sig)), grad * opened)
        ):
            low = result.astype(BF16)
            for way in (0, 1):
                stages[slot, k, way] = low[way * half : way * half + half]
                stage_copy(k, way, step).start()

    ring_gather(gather, feed)
    settle(count - 2)
    settle(count - 1)

    def drain(step, carry):
        for way in (0, 1):
            out_copy(way, step).wait()
        return carry

    lax.fori_loop(0, count, drain, 0)


def attend(mixed, w_out, tokens, gain, w_gate, w_up, w_down, cotangents, count):
    rows, model = tokens.shape
    slots, inner = count * rows, w_down.shape[0]
    return pl.pallas_call(
        functools.partial(attend_kernel, count),
        name="attend",
        out_shape=[
            jax.ShapeDtypeStruct((rows, model), F32),
            jax.ShapeDtypeStruct((slots, model), BF16),
        ]
        + [jax.ShapeDtypeStruct((slots, inner), BF16)] * 3,
        in_specs=[VMEM] * 4 + [ANY] * 4,
        out_specs=[VMEM] + [ANY] * 4,
        scratch_shapes=[pltpu.VMEM((slots, model), BF16)]
        + [pltpu.VMEM((inner, model), BF16)] * 3
        + [pltpu.VMEM((2, 2, rows // 2, model), BF16), pltpu.VMEM((2, 3, 2, rows // 2, inner), BF16)]
        + ring_semaphores(count)
        + [
            pltpu.SemaphoreType.DMA((3,)),
            pltpu.SemaphoreType.DMA((2, 2)),
            pltpu.SemaphoreType.DMA((2, count)),
            pltpu.SemaphoreType.DMA((2, 3, 2)),
        ],
        compiler_params=ring_params(2),
        cost_estimate=pl.CostEstimate(
            flops=2 * rows * model * model + 6 * slots * model * inner, bytes_accessed=300 << 20,
            transcendentals=slots * inner,
        ),
    )(mixed, w_out, tokens, gain.reshape(1, model), w_gate, w_up, w_down, cotangents)


def norm_back(inputs, scale, gain, grad_normed):
    weighted = gain * grad_normed
    inner = jnp.mean(weighted * inputs, axis=1, keepdims=True)
    unit = inputs * scale
    return scale * weighted - unit * (scale * scale * inner), grad_normed * unit


JOBS = 8


def ffn_back_kernel(
    count, groups, rows, grad_gate, grad_up, hidden, w_gate, w_up, resid, cotangent, gain, inputs, cotangents,
    grad_resid, full, grad_gain, sum_gate, sum_up, sum_down,
    slots, low, gw_gate, gw_up, gw_down, boxes, box_sems, *rest,
):
    ring = Ring(count)
    sends, recvs, sends_two, recvs_two, local = rest[:5]
    sums = GroupSum(
        ring, groups, (gw_gate, gw_up, gw_down), rest[5:8], rest[8:11], (sum_gate, sum_up, sum_down), *rest[11:]
    )
    wide = boxes.shape[2]

    def box_copy(job, source):
        at = pl.multiple_of(job % (JOBS // 2) * wide, wide)
        return pltpu.make_async_copy(
            source.at[:, pl.ds(at, wide)], boxes.at[job % 2], box_sems.at[job % 2]
        )

    def fetch(job):
        @pl.when(job < JOBS // 2)
        def _():
            box_copy(job, inputs).start()

        @pl.when(job >= JOBS // 2)
        def _():
            box_copy(job, cotangents).start()

    fetch(0)
    greet(ring, sums.peers())
    grad_gain[...] = jnp.zeros_like(grad_gain)
    half = rows // 2

    def partial(first, second, step):
        gates = jnp.concatenate([grad_gate[pl.ds(first, half), :], grad_gate[pl.ds(second, half), :]], 0)
        ups = jnp.concatenate([grad_up[pl.ds(first, half), :], grad_up[pl.ds(second, half), :]], 0)
        return mm(gates, w_gate[...]) + mm(ups, w_up[...])

    def finish(start, size, grad):
        value = resid[start : start + size, :]
        scale = lax.rsqrt(jnp.mean(value * value, axis=1, keepdims=True) + 1e-6)
        through, pieces = norm_back(value, scale, gain[...].astype(F32), grad)
        result = cotangent[start : start + size, :].astype(F32) + through
        grad_resid[start : start + size, :] = result
        grad_gain[...] += jnp.sum(pieces, axis=0, keepdims=True)
        low[start : start + size, :] = result.astype(BF16)

    def work(job, carry):
        box_copy(job, inputs).wait()

        @pl.when(job + 1 < JOBS)
        def _():
            fetch(job + 1)

        at = pl.ds(pl.multiple_of(job % (JOBS // 2) * wide, wide), wide)

        @pl.when(job < JOBS // 2)
        def _():
            box = boxes[job % 2]
            gw_gate[:, at] = mm(grad_gate[...], box, (0, 0)).astype(BF16)
            gw_up[:, at] = mm(grad_up[...], box, (0, 0)).astype(BF16)

        @pl.when(job >= JOBS // 2)
        def _():
            gw_down[:, at] = mm(hidden[...], boxes[job % 2], (0, 0)).astype(BF16)

        return carry

    each = JOBS // 4

    def beside_scatter(step):
        @pl.when(step == 3)
        def _():
            sums.second((0, 1))

        @pl.when(step < 4)
        def _():
            lax.fori_loop(step * each, step * each + each, work, 0)

        @pl.when(step == 1)
        def _():
            sums.first((0, 1))

        @pl.when(step == 3)
        def _():
            sums.first((2,))

        @pl.when(step == 5)
        def _():
            sums.second((2,))

    def beside_gather(step):
        @pl.when(step == count - 3)
        def _():
            sums.third((0, 1))

        @pl.when(step == count - 2)
        def _():
            sums.third((2,))

    ring_scatter(Scatter(ring, partial, slots, sends, recvs, rows, finish), beside_scatter)
    keep = pltpu.make_async_copy(low, full.at[pl.ds(pl.multiple_of(ring.me * rows, rows), rows), :], local)
    keep.start()
    ring_gather(Gather(ring, row_own(low), row_view(full, rows), sends_two, recvs_two, rows), beside_gather)
    keep.wait()
    sums.last()


def ffn_back(grad_gate, grad_up, hidden, w_gate, w_up, resid, cotangent, gain, inputs, cotangents, count, groups):
    rows, model = resid.shape
    slots, inner = grad_up.shape
    shapes = [(inner, model)] * 3
    return pl.pallas_call(
        functools.partial(ffn_back_kernel, count, groups, rows),
        name="ffn_back",
        out_shape=[
            jax.ShapeDtypeStruct((rows, model), F32),
            jax.ShapeDtypeStruct((slots, model), BF16),
            jax.ShapeDtypeStruct((1, model), F32),
        ]
        + [jax.ShapeDtypeStruct(shape, BF16) for shape in shapes],
        in_specs=[VMEM] * 8 + [ANY] * 2,
        out_specs=[VMEM, ANY, VMEM] + [ANY] * 3,
        scratch_shapes=[ring_slots(count, rows, model), pltpu.VMEM((rows, model), BF16)]
        + [pltpu.VMEM(shape, BF16) for shape in shapes]
        + [pltpu.VMEM((2, slots, model // (JOBS // 2)), BF16), pltpu.SemaphoreType.DMA((2,))]
        + ring_semaphores(count) * 2
        + [pltpu.SemaphoreType.DMA]
        + sum_scratch(shapes, groups),
        compiler_params=ring_params(3),
        cost_estimate=pl.CostEstimate(
            flops=10 * slots * model * inner, bytes_accessed=600 << 20, transcendentals=0
        ),
    )(grad_gate, grad_up, hidden, w_gate, w_up, resid, cotangent, gain.reshape(1, model), inputs, cotangents)


def last_kernel(
    count, groups, rows, terms, tokens, grad_resid, gain, small, *rest,
):
    grads, rest = rest[:5], rest[5:]
    grad_tokens, total = rest[:2]
    targets, rest = rest[2:7], rest[7:]
    slots, first_box, second_box, second_own, boxes, box_sems, sends, recvs = rest[:8]
    first_sends, first_recvs, second_sends, second_recvs = rest[8:12]
    ring = Ring(count)
    sums = GroupSum(ring, groups, grads, rest[12:17], rest[17:22], targets, *rest[22:])
    me, group = ring.me, ring.group
    first_peers = [(group, (me + k) % count) for k in range(1, count)]
    second_peers = [((group + k) % groups, me) for k in range(1, groups)]
    barrier = pltpu.get_barrier_semaphore()
    for peer in first_peers + second_peers:
        pl.semaphore_signal(barrier, inc=1, device_id=peer, device_id_type=MESH)
    pl.semaphore_wait(barrier, count + groups - 2)

    def first(k):
        return pltpu.make_async_remote_copy(
            src_ref=small.at[0:8], dst_ref=first_box.at[k], send_sem=first_sends.at[k],
            recv_sem=first_recvs.at[k], device_id=first_peers[k], device_id_type=MESH,
        )

    def second(k):
        return pltpu.make_async_remote_copy(
            src_ref=second_own, dst_ref=second_box.at[k], send_sem=second_sends.at[k],
            recv_sem=second_recvs.at[k], device_id=second_peers[k], device_id_type=MESH,
        )

    every = range(len(grads))
    sums.first(every)
    for k in range(count - 1):
        first(k).start()
    half = rows // 2

    def box_copy(way, start, slot):
        return pltpu.make_async_copy(
            terms.at[pl.ds(start, half), :], boxes.at[slot, way], box_sems.at[slot, way]
        )

    def fetch(step):
        for way, owner in ((0, ring.at(-1 - step)), (1, ring.at(1 + step))):
            box_copy(way, pl.multiple_of(owner * rows + way * half, half), step % 2).start()

    def partial(first, second, step):
        for way, start in ((0, first), (1, second)):
            box_copy(way, start, step % 2).wait()

        @pl.when(step + 1 < count)
        def _():
            fetch(step + 1)

        return jnp.concatenate([boxes[step % 2, 0], boxes[step % 2, 1]], 0).astype(F32)

    def finish(start, size, grad):
        value = tokens[start : start + size, :].astype(F32)
        scale = lax.rsqrt(jnp.mean(value * value, axis=1, keepdims=True) + 1e-6)
        through, pieces = norm_back(value, scale, gain[...].astype(F32), grad)
        grad_tokens[start : start + size, :] = grad_resid[start : start + size, :] + through

    def early():
        sums.second(every)
        for k in range(count - 1):
            first(k).wait()
        mine = small[0:8]
        for k in range(count - 1):
            mine = mine + first_box[k]
        second_own[0:8] = mine
        second_own[8:] = small[8:]
        for k in range(groups - 1):
            second(k).start()

    def late():
        for k in range(groups - 1):
            second(k).wait()
        mine = second_own[...]
        for k in range(groups - 1):
            mine = mine + second_box[k]
        total[...] = mine
        sums.third(every)

    def beside(step):
        pl.when(step == 0)(early)
        pl.when(step == count - 2)(late)

    fetch(0)
    ring_scatter(Scatter(ring, partial, slots, sends, recvs, rows, finish), beside)
    sums.last()


def last_step(terms, tokens, grad_resid, gain, small, grads, count, groups):
    rows, model = tokens.shape
    return pl.pallas_call(
        functools.partial(last_kernel, count, groups, rows),
        name="last_step",
        out_shape=[jax.ShapeDtypeStruct((rows, model), F32), jax.ShapeDtypeStruct(small.shape, F32)]
        + [jax.ShapeDtypeStruct(g.shape, BF16) for g in grads],
        in_specs=[ANY] + [VMEM] * (4 + len(grads)),
        out_specs=[VMEM, VMEM] + [ANY] * len(grads),
        scratch_shapes=[
            ring_slots(count, rows, model),
            pltpu.VMEM((count - 1, 8, model), F32),
            pltpu.VMEM((groups - 1,) + small.shape, F32),
            pltpu.VMEM(small.shape, F32),
            pltpu.VMEM((2, 2, rows // 2, model), BF16),
            pltpu.SemaphoreType.DMA((2, 2)),
        ]
        + ring_semaphores(count)
        + [pltpu.SemaphoreType.DMA((count - 1,))] * 2
        + [pltpu.SemaphoreType.DMA((groups - 1,))] * 2
        + sum_scratch([g.shape for g in grads], groups),
        compiler_params=ring_params(4),
        cost_estimate=pl.CostEstimate(flops=0, bytes_accessed=300 << 20, transcendentals=0),
    )(terms, tokens, grad_resid, gain.reshape(1, model), small, *grads)


def results_kernel(heads, taps, wide, width, total, *refs):
    number = (len(refs) - 7) // 2
    for source, target in zip(refs[:number], refs[number : 2 * number]):
        target[...] = source[...].astype(target.dtype)
    g_first, g_second, g_head, gt_query, gt_key, gt_value, g_beta = refs[2 * number :]

    @pl.when(pl.program_id(0) == 0)
    def _():
        g_first[...] = total[0:1, :]
        g_second[...] = total[1:2, :]
        g_head[...] = total[2:3, 0:width]
        row = 8 + heads
        for place, target in enumerate((gt_query, gt_key, gt_value)):
            target[...] = total[row : row + taps, place * wide : (place + 1) * wide]
        g_beta[...] = total[8 : 8 + heads, :]


def results(total, arrays, heads, taps, wide, width):
    model = total.shape[1]
    steps = next(n for n in (8, 4, 2, 1) if all(a.shape[0] % (8 * n) == 0 for a, _ in arrays))
    small = [(1, model), (1, model), (1, width)] + [(taps, wide)] * 3 + [(heads, model)]
    piece = lambda a: pl.BlockSpec((a.shape[0] // steps, a.shape[1]), lambda n: (n, 0))
    whole = lambda shape: pl.BlockSpec(shape, lambda n: (0, 0))
    return pl.pallas_call(
        functools.partial(results_kernel, heads, taps, wide, width),
        name="results",
        grid=(steps,),
        out_shape=[jax.ShapeDtypeStruct(a.shape, kind) for a, kind in arrays]
        + [jax.ShapeDtypeStruct(shape, F32) for shape in small],
        in_specs=[whole(total.shape)] + [piece(a) for a, _ in arrays],
        out_specs=[piece(a) for a, _ in arrays] + [whole(shape) for shape in small],
        compiler_params=pltpu.CompilerParams(vmem_limit_bytes=56 << 20),
        cost_estimate=pl.CostEstimate(flops=0, bytes_accessed=48 << 20, transcendentals=0),
    )(total, *[a for a, _ in arrays])


def spread_hops(step, chunks, count, hop, start=0):
    each = -(-(count - 1) // (chunks - 1))
    for place in range(each):
        number = step * each + place

        @pl.when((number >= start) & (number < count - 1))
        def _():
            hop(number)


def forward_kernel(
    heads, width, seqs, count, rows_own, chunks,
    starts, lengths, tokens, w_query, w_key, w_value, w_gate, w_beta,
    taps_query, taps_key, taps_value, gain, gain_first, side,
    mixed_own, mixed, p_query, p_key, p_value, p_gate, p_beta, z_query, z_key, z_value,
    delta_out, change_out, inverse_out, state_out, side_full,
    tail_query, tail_key, tail_value, state, stage, sends, recvs, local, row_sends, row_recvs,
):
    step = pl.program_id(0)
    size = tokens.shape[0]
    first = step * size

    @pl.when(step == 0)
    def _():
        for tail in (tail_query, tail_key, tail_value):
            tail[...] = jnp.zeros_like(tail)
        state[...] = jnp.zeros_like(state)

    ring = Ring(count)
    me, group = ring.me, ring.group
    wide = heads * width
    gather = Gather(ring, row_own(side), row_view(side_full, rows_own), sends, recvs, rows_own)
    keep = pltpu.make_async_copy(
        side, side_full.at[pl.ds(pl.multiple_of(me * rows_own, rows_own), rows_own), :], local.at[0]
    )
    own_columns = pl.ds(pl.multiple_of(me * wide, wide), wide)

    def keep_rows():
        return pltpu.make_async_copy(stage.at[me], mixed_own.at[:, own_columns], local.at[1])

    def row_copy(target):
        return pltpu.make_async_remote_copy(
            src_ref=stage.at[target], dst_ref=mixed_own.at[:, own_columns],
            send_sem=row_sends.at[target], recv_sem=row_recvs.at[me],
            device_id=(group, target), device_id_type=MESH,
        )

    def row_arrival(origin):
        return pltpu.make_async_remote_copy(
            src_ref=stage.at[me], dst_ref=mixed_own.at[:, own_columns],
            send_sem=row_sends.at[origin], recv_sem=row_recvs.at[origin],
            device_id=(group, origin), device_id_type=MESH,
        )

    @pl.when(step == 0)
    def _():
        barrier = pltpu.get_barrier_semaphore()
        for k in range(1, count):
            pl.semaphore_signal(barrier, inc=1, device_id=(group, (me + k) % count), device_id_type=MESH)
        pl.semaphore_wait(barrier, count - 1)
        gather.begin()
        keep.start()

    spread_hops(step, chunks, count, gather.hop, 1)
    rows, seg_rows, seg_columns, before, last = chunk_masks(starts, lengths, seqs, first, size)
    same = seg_rows == seg_columns
    i = lax.broadcasted_iota(jnp.int32, (size, size), 0)
    j = lax.broadcasted_iota(jnp.int32, (size, size), 1)
    strict = jnp.where(same & (i > j), 1.0, 0.0)
    inclusive = jnp.where(same & (i >= j), 1.0, 0.0)
    carried = jnp.where(seg_rows == before, 1.0, 0.0)
    ending = jnp.where(seg_rows == last, 1.0, 0.0)
    kept = jnp.where(before == last, 1.0, 0.0)
    live = jnp.where(seg_rows % 2 == 1, 1.0, 0.0)
    joined = [
        jnp.where(segment_at(rows - offset, starts, lengths, seqs) == seg_rows, 1.0, 0.0)
        for offset in range(1, taps_query.shape[0])
    ]
    inputs = normed_rows(tokens, gain_first)[0].astype(BF16)

    def feature(weight, taps, tail, p_out, z_out):
        projected = jnp.dot(inputs, weight[...], preferred_element_type=F32)
        p_out[...] = projected
        tail[8:, :] = projected
        tap = taps[...].astype(F32)
        result = projected * tap[0:1]
        for offset in range(1, tap.shape[0]):
            result = result + tail[8 - offset : 8 - offset + size, :] * tap[offset : offset + 1] * joined[offset - 1]
        tail[0:8, :] = projected[size - 8 :, :]
        z_out[...] = result
        return result * sigmoid(result)

    u_query = feature(w_query, taps_query, tail_query, p_query, z_query)
    u_key = feature(w_key, taps_key, tail_key, p_key, z_key)
    u_value = feature(w_value, taps_value, tail_value, p_value, z_value)
    gate = jnp.dot(inputs, w_gate[...], preferred_element_type=F32)
    p_gate[...] = gate
    beta_pre = mm(inputs, w_beta[...], (1, 1))
    p_beta[...] = beta_pre
    strength = sigmoid(beta_pre)
    opened = gate * sigmoid(gate)
    scale = width ** (-0.5)
    head_gain = gain[...].astype(F32)
    for h in range(heads):
        cols = slice(h * width, (h + 1) * width)
        uq, uk = u_query[:, cols], u_key[:, cols]
        query = (uq * lax.rsqrt(jnp.sum(uq * uq, axis=1, keepdims=True) + 1e-6)).astype(BF16)
        key = (uk * lax.rsqrt(jnp.sum(uk * uk, axis=1, keepdims=True) + 1e-6)).astype(BF16)
        value = u_value[:, cols].astype(BF16).astype(F32)
        beta = strength[:, h : h + 1]
        memory = state[h]
        low_memory = memory.astype(BF16)
        state_out[0, h] = low_memory
        lower = mm(key, key, (1, 1)) * strict * beta
        inverse = inverse_unit_lower(lower, size).astype(BF16)
        inverse_out[0, h] = inverse
        within = mm(query, key, (1, 1)) * inclusive
        change = mm(inverse, beta * (value - carried * mm(key, low_memory)))
        low_change = change.astype(BF16)
        change_out[:, cols] = low_change
        out = scale * (carried * mm(query, low_memory) + mm(within, low_change))
        state[h] = kept * memory + mm(key, ending * change, (0, 0))
        delta_out[:, cols] = out
        normal = out * lax.rsqrt(jnp.mean(out * out, axis=1, keepdims=True) + 1e-5) * head_gain
        low_mixed = (normal * opened[:, cols] * live).astype(BF16)
        mixed[:, cols] = low_mixed
        for place in range(size // rows_own):
            stage[step * (size // rows_own) + place, :, cols] = low_mixed[place * rows_own : (place + 1) * rows_own]

    for place in range(size // rows_own):
        target = step * (size // rows_own) + place

        @pl.when(target != me)
        def _():
            row_copy(target).start()

        @pl.when(target == me)
        def _():
            keep_rows().start()

    @pl.when(step == chunks - 1)
    def _():
        gather.arrived(count - 1)
        gather.end()
        keep.wait()
        keep_rows().wait()
        for k in range(1, count):
            row_copy((me + k) % count).wait_send()
            row_arrival((me + k) % count).wait_recv()


def forward_mixer(tokens, w_query, w_key, w_value, w_gate, w_beta, taps_query, taps_key, taps_value, gain, gain_first, starts, lengths, side, count):
    slots, model = tokens.shape
    wide = w_query.shape[1]
    width = gain.shape[0]
    heads = wide // width
    seqs = starts.shape[1]
    chunks = slots // CHUNK
    taps = taps_query.shape[0]
    smem = pl.BlockSpec(memory_space=pltpu.SMEM)
    whole = lambda shape: pl.BlockSpec(shape, lambda n: (0,) * len(shape))
    piece = lambda shape: pl.BlockSpec(shape, lambda n: (n,) + (0,) * (len(shape) - 1))
    own = (slots // count, count * wide)
    outs = [
        ((slots, wide), BF16), ((slots, wide), F32), ((slots, wide), F32), ((slots, wide), F32), ((slots, wide), F32),
        ((slots, w_beta.shape[0]), F32), ((slots, wide), F32), ((slots, wide), F32), ((slots, wide), F32),
        ((slots, wide), F32), ((slots, wide), BF16),
    ]
    return pl.pallas_call(
        functools.partial(forward_kernel, heads, width, seqs, count, slots // count, chunks),
        name="mixer_forward",
        grid=(chunks,),
        out_shape=[jax.ShapeDtypeStruct(own, BF16)]
        + [jax.ShapeDtypeStruct(s, d) for s, d in outs]
        + [
            jax.ShapeDtypeStruct((chunks, heads, CHUNK, CHUNK), BF16),
            jax.ShapeDtypeStruct((chunks, heads, width, width), BF16),
            jax.ShapeDtypeStruct((slots, model), BF16),
        ],
        in_specs=[smem, smem, piece((CHUNK, model))]
        + [whole((model, wide))] * 4
        + [whole(w_beta.shape)]
        + [whole((taps, wide))] * 3
        + [whole((1, width)), whole((1, model)), ANY],
        out_specs=[ANY]
        + [piece((CHUNK, s[1])) for s, d in outs]
        + [piece((1, heads, CHUNK, CHUNK)), piece((1, heads, width, width)), ANY],
        scratch_shapes=[pltpu.VMEM((CHUNK + 8, wide), F32)] * 3
        + [pltpu.VMEM((heads, width, width), F32), pltpu.VMEM((count, slots // count, wide), BF16)]
        + ring_semaphores(count)
        + [pltpu.SemaphoreType.DMA((2,))]
        + [pltpu.SemaphoreType.DMA((count,))] * 2,
        compiler_params=ring_params(5),
        cost_estimate=pl.CostEstimate(
            flops=2 * slots * model * wide * 4 + slots * heads * CHUNK * 2 * CHUNK * 20,
            bytes_accessed=slots * model * 2 + 4 * model * wide * 2 + slots * wide * 36,
            transcendentals=slots * wide * 4,
        ),
    )(starts, lengths, tokens, w_query, w_key, w_value, w_gate, w_beta, taps_query, taps_key, taps_value, gain.reshape(1, width), gain_first.reshape(1, model), side)


def small_rows(heads, taps):
    return -(-(8 + heads + taps) // 8) * 8


def backward_kernel(
    heads, width, seqs, chunks, count, rows_own,
    starts, lengths, tokens, grad_attended, mixed, p_query, p_key, p_value, p_gate, p_beta,
    z_query, z_key, z_value, delta_out, change_in, inverse_in, state_in,
    w_query, w_key, w_value, w_gate, w_beta, w_out, taps_query, taps_key, taps_value, gain, gain_first,
    hidden, w_down, resid, g_second, grad_normed, gw_query, gw_key, gw_value, gw_gate, gw_out,
    small, output,
    a_query, a_key, a_value, a_gate, a_out, head_query, head_key, head_value, flow, slots, sends, recvs,
):
    step = pl.program_id(0)
    size = tokens.shape[0]
    first = (chunks - 1 - step) * size

    @pl.when(step == 0)
    def _():
        for ref in (a_query, a_key, a_value, a_gate, a_out, small, flow):
            ref[...] = jnp.zeros_like(ref)
        small[1:2, :] = g_second[...]
        for ref in (head_query, head_key, head_value):
            ref[size:, :] = jnp.zeros((8, ref.shape[1]), F32)

    half = rows_own // 2

    def partial(one, two, number):
        return mm(jnp.concatenate([hidden[pl.ds(one, half), :], hidden[pl.ds(two, half), :]], 0), w_down[...])

    def finish(start, length, down):
        output[start : start + length, :] = (resid[start : start + length, :] + down).astype(BF16)

    ring = Ring(count)
    scatter = Scatter(ring, partial, slots, sends, recvs, rows_own, finish)
    pl.when(step == 0)(lambda: greet(ring))
    spread_hops(step, chunks, count, scatter.hop)
    rows, seg_rows, seg_columns, before, last = chunk_masks(starts, lengths, seqs, first, size)
    same = seg_rows == seg_columns
    i = lax.broadcasted_iota(jnp.int32, (size, size), 0)
    j = lax.broadcasted_iota(jnp.int32, (size, size), 1)
    strict = jnp.where(same & (i > j), 1.0, 0.0)
    inclusive = jnp.where(same & (i >= j), 1.0, 0.0)
    carried = jnp.where(seg_rows == before, 1.0, 0.0)
    ending = jnp.where(seg_rows == last, 1.0, 0.0)
    kept = jnp.where(before == last, 1.0, 0.0)
    live = jnp.where(seg_rows % 2 == 1, 1.0, 0.0)
    taps = taps_query.shape[0]
    joined = [
        jnp.where(segment_at(rows + offset, starts, lengths, seqs) == seg_rows, 1.0, 0.0)
        for offset in range(1, taps)
    ]
    normal_rows, unit_rows = normed_rows(tokens, gain_first)
    inputs = normal_rows.astype(BF16)
    grad_rows = grad_attended[...]
    grad_mixed = mm(grad_rows, w_out[...], (1, 1))
    a_out[...] += mm(mixed[...], grad_rows, (0, 0))
    strength = sigmoid(p_beta[...])
    scale = width ** (-0.5)
    head_gain = gain[...].astype(F32)

    grads_query, grads_key, grads_value, grads_gate, grads_beta = [], [], [], [], []
    for h in range(heads):
        cols = slice(h * width, (h + 1) * width)
        out = delta_out[:, cols]
        gate = p_gate[:, cols]
        sig_gate = sigmoid(gate)
        silu_gate = gate * sig_gate
        root = lax.rsqrt(jnp.mean(out * out, axis=1, keepdims=True) + 1e-5)
        grad = grad_mixed[:, cols] * live
        unit = out * root
        grads_gate.append(grad * unit * head_gain * (sig_gate * (1.0 + gate * (1.0 - sig_gate))))
        grad_normal = grad * silu_gate
        small[2:3, 0:width] += jnp.sum(grad_normal * unit, axis=0, keepdims=True)
        push = grad_normal * head_gain
        grad_out = scale * root * (push - unit * jnp.mean(push * unit, axis=1, keepdims=True))

        zq, zk, zv = z_query[:, cols], z_key[:, cols], z_value[:, cols]
        sq, sk, sv = sigmoid(zq), sigmoid(zk), sigmoid(zv)
        uq, uk = zq * sq, zk * sk
        nq = lax.rsqrt(jnp.sum(uq * uq, axis=1, keepdims=True) + 1e-6)
        nk = lax.rsqrt(jnp.sum(uk * uk, axis=1, keepdims=True) + 1e-6)
        unit_q, unit_k = uq * nq, uk * nk
        query, key = unit_q.astype(BF16), unit_k.astype(BF16)
        beta = strength[:, h : h + 1]
        change = change_in[:, cols]
        inverse = inverse_in[0, h]
        memory = state_in[0, h]
        flowing = flow[h]
        low_flow = flowing.astype(BF16)
        low_out = grad_out.astype(BF16)

        within = mm(query, key, (1, 1)) * inclusive
        grad_within = (mm(low_out, change, (1, 1)) * inclusive).astype(BF16)
        grad_change = mm(within, low_out, (0, 0)) + ending * mm(key, low_flow)
        grad_mid = mm(inverse, grad_change, (0, 0))
        grad_value = beta * grad_mid
        low_value = grad_value.astype(BF16)
        cross = (mm(low_value, change, (1, 1)) * strict).astype(BF16)
        grad_query = carried * mm(low_out, memory, (1, 1)) + mm(grad_within, key)
        grad_key = (
            mm(grad_within, query, (0, 0))
            + ending * mm(change, low_flow, (1, 1))
            - carried * mm(low_value, memory, (1, 1))
            - mm(cross, key)
            - mm(cross, key, (0, 0))
        )
        flow[h] = (
            kept * flowing
            + mm(query, carried * grad_out, (0, 0))
            - mm(key, carried * grad_value, (0, 0))
        )
        grads_beta.append((1.0 - beta) * jnp.sum(grad_mid * change.astype(F32), axis=1, keepdims=True))
        du_q = nq * (grad_query - unit_q * jnp.sum(grad_query * unit_q, axis=1, keepdims=True))
        du_k = nk * (grad_key - unit_k * jnp.sum(grad_key * unit_k, axis=1, keepdims=True))
        grads_query.append(du_q * sq * (1.0 + zq * (1.0 - sq)))
        grads_key.append(du_k * sk * (1.0 + zk * (1.0 - sk)))
        grads_value.append(grad_value * sv * (1.0 + zv * (1.0 - sv)))

    tap_row = 8 + heads
    wide = heads * width

    def unconv(parts, taps_ref, head, projected, place):
        lanes = slice(place * wide, (place + 1) * wide)
        grad = jnp.concatenate(parts, axis=1)
        head[0:size, :] = grad
        tap = taps_ref[...].astype(F32)
        p = projected[...]
        result = grad * tap[0:1]
        small[tap_row : tap_row + 1, lanes] += jnp.sum(p * grad, axis=0, keepdims=True)
        for offset in range(1, taps):
            moved = head[offset : offset + size, :] * joined[offset - 1]
            result = result + moved * tap[offset : offset + 1]
            row = tap_row + offset
            small[row : row + 1, lanes] += jnp.sum(p * moved, axis=0, keepdims=True)
        head[size:, :] = grad[0:8, :]
        return result.astype(BF16)

    d_query = unconv(grads_query, taps_query, head_query, p_query, 0)
    d_key = unconv(grads_key, taps_key, head_key, p_key, 1)
    d_value = unconv(grads_value, taps_value, head_value, p_value, 2)
    d_gate = jnp.concatenate(grads_gate, axis=1).astype(BF16)
    spare = [jnp.zeros((size, 1), F32)] * (w_beta.shape[0] - heads)
    d_beta = jnp.concatenate(grads_beta + spare, axis=1).astype(BF16)
    grad_inputs = (
        mm(d_query, w_query[...], (1, 1))
        + mm(d_key, w_key[...], (1, 1))
        + mm(d_value, w_value[...], (1, 1))
        + mm(d_gate, w_gate[...], (1, 1))
        + mm(d_beta, w_beta[...])
    )
    grad_normed[...] = grad_inputs.astype(BF16)
    small[0:1, :] += jnp.sum(grad_inputs * unit_rows, axis=0, keepdims=True)
    a_query[...] += mm(inputs, d_query, (0, 0))
    a_key[...] += mm(inputs, d_key, (0, 0))
    a_value[...] += mm(inputs, d_value, (0, 0))
    a_gate[...] += mm(inputs, d_gate, (0, 0))
    small[8 : 8 + heads, :] += mm(d_beta, inputs, (0, 0))[:heads]

    @pl.when(step == chunks - 1)
    def _():
        for target, source in (
            (gw_query, a_query), (gw_key, a_key), (gw_value, a_value), (gw_gate, a_gate),
            (gw_out, a_out),
        ):
            target[...] = source[...].astype(target.dtype)
        scatter.end()


def backward_mixer(tokens, grad_attended, saved, w_query, w_key, w_value, w_gate, w_beta, w_out, taps_query, taps_key, taps_value, gain, gain_first, starts, lengths, hidden, w_down, resid, g_second, count):
    slots, model = tokens.shape
    wide = w_query.shape[1]
    width = gain.shape[0]
    heads = wide // width
    seqs = starts.shape[1]
    chunks = slots // CHUNK
    taps = taps_query.shape[0]
    smem = pl.BlockSpec(memory_space=pltpu.SMEM)
    fixed = lambda shape: pl.BlockSpec(shape, lambda n: (0,) * len(shape), pipeline_mode=pl.Buffered(1))
    piece = lambda shape: pl.BlockSpec(shape, lambda n: (chunks - 1 - n,) + (0,) * (len(shape) - 1))
    rows = lambda a: piece((CHUNK, a.shape[1]))
    outs = (
        [((slots, model), BF16)] + [((model, wide), BF16)] * 4 + [((wide, model), BF16)]
        + [((small_rows(heads, taps), model), F32), (resid.shape, BF16)]
    )
    return pl.pallas_call(
        functools.partial(backward_kernel, heads, width, seqs, chunks, count, slots // count),
        name="mixer_backward",
        grid=(chunks,),
        out_shape=[jax.ShapeDtypeStruct(s, d) for s, d in outs],
        in_specs=[smem, smem, rows(tokens), rows(grad_attended)]
        + [rows(a) for a in saved[:11]]
        + [piece((1, heads, CHUNK, CHUNK)), piece((1, heads, width, width))]
        + [fixed((model, wide))] * 4
        + [fixed(w_beta.shape), fixed((wide, model))]
        + [fixed((taps, wide))] * 3
        + [fixed((1, width)), fixed((1, model)), fixed(hidden.shape), fixed(w_down.shape), fixed(resid.shape), fixed(g_second.shape)],
        out_specs=[piece((CHUNK, model))] + [fixed(s) for s, d in outs[1:]],
        scratch_shapes=[pltpu.VMEM((model, wide), F32)] * 4
        + [pltpu.VMEM((wide, model), F32)]
        + [pltpu.VMEM((CHUNK + 8, wide), F32)] * 3
        + [pltpu.VMEM((heads, width, width), F32), ring_slots(count, slots // count, model)]
        + ring_semaphores(count),
        compiler_params=ring_params(6),
        cost_estimate=pl.CostEstimate(
            flops=2 * slots * model * wide * 10 + slots * heads * CHUNK * 2 * CHUNK * 8,
            bytes_accessed=slots * model * 6 + 10 * model * wide * 2 + slots * wide * 36,
            transcendentals=slots * wide * 8,
        ),
    )(starts, lengths, tokens, grad_attended, *saved, w_query, w_key, w_value, w_gate, w_beta, w_out, taps_query, taps_key, taps_value, gain.reshape(1, width), gain_first.reshape(1, model), hidden, w_down, resid, g_second)


def make_shards(groups, count):
    def shards(
        tokens, attn_gain, w_query, w_key, w_value, conv_query, conv_key, conv_value, w_beta, w_gate_out,
        head_gain, w_out, ffn_gain, w_gate, w_up, w_down, seq_starts, seq_lengths, cotangent,
    ):
        model = tokens.shape[1]
        heads = w_beta.shape[1]
        beta_rows = w_beta.T if heads > 1 else jnp.pad(w_beta.T, ((0, 1), (0, 0)))
        tokens_full, w_out_full = gather_tokens(tokens, w_out, count, groups)
        mixed_own, *saved = forward_mixer(
            tokens_full, w_query, w_key, w_value, w_gate_out, beta_rows,
            conv_query, conv_key, conv_value, head_gain, attn_gain, seq_starts, seq_lengths, cotangent, count,
        )
        grad_full, saved = saved[-1], saved[:-1]
        resid, ffn_full, hidden, grad_gate, grad_up = attend(
            mixed_own, w_out_full, tokens, ffn_gain, w_gate.T, w_up.T, w_down, grad_full, count
        )
        grad_resid, grad_attended, g_second, *ffn_grads = ffn_back(
            grad_gate, grad_up, hidden, w_gate.T, w_up.T, resid, cotangent, ffn_gain, ffn_full, grad_full,
            count, groups,
        )
        pulled = backward_mixer(
            tokens_full, grad_attended, saved, w_query, w_key, w_value, w_gate_out, beta_rows, w_out,
            conv_query, conv_key, conv_value, head_gain, attn_gain, seq_starts, seq_lengths,
            hidden, w_down, resid, g_second, count,
        )
        terms, gw_query, gw_key, gw_value, gw_gate_out, gw_out, small, output = pulled
        grad_tokens, total, *mixer_grads = last_step(
            terms, tokens, grad_resid, attn_gain, small,
            (gw_query, gw_key, gw_value, gw_gate_out, gw_out), count, groups,
        )
        taps, wide = conv_query.shape
        output, grad_tokens, *rest = results(
            total,
            [(output, BF16), (grad_tokens, F32)] + [(g, F32) for g in (*mixer_grads, *ffn_grads)],
            heads, taps, wide, head_gain.shape[0],
        )
        grads, (g_first, g_second, g_head, gt_query, gt_key, gt_value, g_beta) = rest[:8], rest[8:]
        return (
            output,
            grad_tokens,
            g_first[0],
            grads[0],
            grads[1],
            grads[2],
            gt_query,
            gt_key,
            gt_value,
            g_beta.T,
            grads[3],
            g_head[0],
            grads[4],
            g_second[0],
            grads[5].T,
            grads[6].T,
            grads[7],
        )

    return shards


def solution(mesh):
    placed = (
        P(("dp", "tensor"), None),
        P(),
        P(None, "tensor"),
        P(None, "tensor"),
        P(None, "tensor"),
        P(None, "tensor"),
        P(None, "tensor"),
        P(None, "tensor"),
        P(None, "tensor"),
        P(None, "tensor"),
        P(),
        P("tensor", None),
        P(),
        P(None, "tensor"),
        P(None, "tensor"),
        P("tensor", None),
        P("dp", None),
        P("dp", None),
        P(("dp", "tensor"), None),
    )
    return jax.shard_map(
        make_shards(mesh.shape["dp"], mesh.shape["tensor"]),
        mesh=mesh,
        in_specs=placed,
        out_specs=(
            P(("dp", "tensor"), None),
            P(("dp", "tensor"), None),
            P(),
            P(None, "tensor"),
            P(None, "tensor"),
            P(None, "tensor"),
            P(None, "tensor"),
            P(None, "tensor"),
            P(None, "tensor"),
            P(None, "tensor"),
            P(None, "tensor"),
            P(),
            P("tensor", None),
            P(),
            P(None, "tensor"),
            P(None, "tensor"),
            P("tensor", None),
        ),
        check_vma=False,
    )
```

```python
import functools
import jax
import jax.numpy as jnp
from jax import lax
from jax.experimental import pallas as pl
from jax.experimental.pallas import tpu as pltpu
from jax.sharding import PartitionSpec as P

CHUNK = 256
LAGS = 4
F32, BF16 = jnp.float32, jnp.bfloat16


def mm(a, b, contract=(1, 0)):
    return lax.dot_general(
        a.astype(BF16),
        b.astype(BF16),
        (((contract[0],), (contract[1],)), ((), ())),
        preferred_element_type=F32,
    )


def segment_at(places, starts, lengths, seqs):
    segment = jnp.zeros_like(places)
    for s in range(seqs):
        begin = starts[0, s]
        stop = begin + lengths[0, s]
        segment = segment + jnp.where(places >= begin, 1, 0) + jnp.where(places >= stop, 1, 0)
    return jnp.where(places < 0, -1, segment)


def chunk_masks(starts, lengths, seqs, first, size):
    rows = first + lax.broadcasted_iota(jnp.int32, (size, 1), 0)
    columns = first + lax.broadcasted_iota(jnp.int32, (1, size), 1)
    seg_rows = segment_at(rows, starts, lengths, seqs)
    seg_columns = segment_at(columns, starts, lengths, seqs)
    before = segment_at(jnp.full((1, 1), first - 1, jnp.int32), starts, lengths, seqs)
    last = segment_at(jnp.full((1, 1), first + size - 1, jnp.int32), starts, lengths, seqs)
    return rows, seg_rows, seg_columns, before, last


def inverse_unit_lower(lower, size):
    i = lax.broadcasted_iota(jnp.int32, (size, size), 0)
    j = lax.broadcasted_iota(jnp.int32, (size, size), 1)

    def corner(width):
        shift = width.bit_length() - 1
        pair = (i >> (shift + 1)) == (j >> (shift + 1))
        return pair & (((i >> shift) & 1) == 1) & (((j >> shift) & 1) == 0)

    inverse = jnp.where(i == j, 1.0, 0.0) - jnp.where(corner(1), lower, 0.0)
    width = 2
    while width < size:
        low = inverse.astype(BF16)
        if 2 * width == size:
            part = mm(mm(low[width:, width:], lower[width:, :width]), low[:width, :width])
            inverse = jnp.concatenate(
                [
                    inverse[:width],
                    jnp.concatenate([-part, inverse[width:, width:]], axis=1),
                ],
                axis=0,
            )
        else:
            between = jnp.where(corner(width), lower, 0.0)
            inverse = inverse - mm(mm(low, between), low)
        width *= 2
    return inverse


def sigmoid(v):
    return 1.0 / (1.0 + jnp.exp(-v))


def normed_rows(tokens, gain):
    value = tokens[...].astype(F32)
    unit = value * lax.rsqrt(jnp.mean(value * value, axis=1, keepdims=True) + 1e-6)
    return unit * gain[...].astype(F32).reshape(1, -1), unit


MESH = pl.DeviceIdType.MESH
SUBS = 2
PAIRS = [(sub, way) for sub in range(SUBS) for way in (0, 1)]


def ring_position(device, count):
    half, odd = device // 2, device % 2
    return half + odd * (count - 1 - 2 * half)


def ring_device(position, count):
    back = position // (count // 2)
    return (1 - back) * 2 * position + back * (2 * (count - 1 - position) + 1)


class Ring:
    def __init__(self, count):
        self.count = count
        self.me = lax.axis_index("tensor")
        self.place = ring_position(self.me, count)
        self.group = lax.axis_index("dp")

    def at(self, offset):
        return ring_device((self.place + offset + 2 * self.count) % self.count, self.count)

    def next(self, way):
        return (self.group, self.at(1 if way == 0 else -1))


class Gather:
    def __init__(self, ring, own, view, sends, recvs, rows, subs=SUBS):
        self.ring, self.own, self.view, self.sends, self.recvs, self.rows = ring, own, view, sends, recvs, rows
        self.piece = rows // (2 * subs)
        self.pairs = [(sub, way) for sub in range(subs) for way in (0, 1)]

    def origin(self, way, step):
        return self.ring.at(-step if way == 0 else step)

    def copy(self, way, sub, step, origin, first=False):
        inside = way * (self.rows // 2) + sub * self.piece
        place = self.view(origin, inside, self.piece)
        return pltpu.make_async_remote_copy(
            src_ref=self.own(inside, self.piece) if first else place,
            dst_ref=place,
            send_sem=self.sends.at[way, sub, step],
            recv_sem=self.recvs.at[way, sub, step],
            device_id=self.ring.next(way),
            device_id_type=MESH,
        )

    def begin(self):
        for sub, way in self.pairs:
            self.copy(way, sub, 0, self.ring.me, True).start()

    def arrived(self, step):
        for sub, way in self.pairs:
            self.copy(way, sub, step - 1, self.origin(way, step)).wait_recv()

    def hop(self, step):
        for sub, way in self.pairs:
            self.copy(way, sub, step - 1, self.origin(way, step)).wait_recv()
            self.copy(way, sub, step, self.origin(way, step)).start()

    def end(self):
        def drain(step, carry):
            for sub, way in self.pairs:
                self.copy(way, sub, step, self.ring.me).wait_send()
            return carry

        lax.fori_loop(0, self.ring.count - 1, drain, 0)


def row_view(ref, rows):
    return lambda origin, start, size: ref.at[pl.ds(pl.multiple_of(origin * rows + start, size), size), :]


def row_own(ref):
    return lambda start, size: ref.at[pl.ds(start, size), :]


def ring_gather(gather, between, before=None):
    count = gather.ring.count

    def run(step, carry):
        if before is not None:
            before(step)

        @pl.when(step == 0)
        def _():
            gather.begin()

        @pl.when((step > 0) & (step < count - 1))
        def _():
            gather.hop(step)

        @pl.when(step == count - 1)
        def _():
            gather.arrived(step)

        between(step)
        return carry

    lax.fori_loop(0, count, run, 0)
    gather.end()


def scatter_copy(ring, slots, sends, recvs, way, sub, step):
    return pltpu.make_async_remote_copy(
        src_ref=slots.at[way, sub, step],
        dst_ref=slots.at[way, sub, step + 1],
        send_sem=sends.at[way, sub, step],
        recv_sem=recvs.at[way, sub, step],
        device_id=ring.next(way),
        device_id_type=MESH,
    )


class Scatter:
    def __init__(self, ring, partial, slots, sends, recvs, rows, finish):
        self.ring, self.partial, self.slots, self.sends, self.recvs = ring, partial, slots, sends, recvs
        self.half, self.finish = rows // 2, finish
        self.rows, self.piece = rows, rows // (2 * SUBS)

    def terms(self, step):
        half, first, second = self.half, self.ring.at(-1 - step), self.ring.at(1 + step)
        return self.partial(
            pl.multiple_of(first * self.rows, half), pl.multiple_of(second * self.rows + half, half), step
        )

    def part(self, terms, way, sub):
        start = way * self.half + sub * self.piece
        return terms[start : start + self.piece]

    def copy(self, way, sub, step):
        return scatter_copy(self.ring, self.slots, self.sends, self.recvs, way, sub, step)

    def hop(self, step):
        terms = self.terms(step)
        for sub, way in PAIRS:
            term = self.part(terms, way, sub)

            @pl.when(step == 0)
            def _():
                self.slots[way, sub, 0] = term.astype(BF16)

            @pl.when(step > 0)
            def _():
                self.copy(way, sub, step - 1).wait_recv()
                self.slots[way, sub, step] = (self.slots[way, sub, step].astype(F32) + term).astype(BF16)

            self.copy(way, sub, step).start()

    def end(self):
        count = self.ring.count
        terms = self.terms(count - 1)
        for sub, way in PAIRS:
            self.copy(way, sub, count - 2).wait_recv()
            self.finish(
                way * self.half + sub * self.piece,
                self.piece,
                self.slots[way, sub, count - 1].astype(F32) + self.part(terms, way, sub),
            )

        def drain(step, carry):
            for sub, way in PAIRS:
                self.copy(way, sub, step).wait_send()
            return carry

        lax.fori_loop(0, count - 1, drain, 0)


def ring_scatter(scatter, between):
    def run(step, carry):
        scatter.hop(step)
        between(step)
        return carry

    lax.fori_loop(0, scatter.ring.count - 1, run, 0)
    scatter.end()


class GroupSum:
    def __init__(self, ring, groups, grads, near, far, targets, near_sems, far_sems, back_sems, keep_sems):
        self.ring, self.groups, self.grads, self.near, self.far, self.targets = ring, groups, grads, near, far, targets
        self.near_sems, self.far_sems, self.back_sems, self.keep_sems = near_sems, far_sems, back_sems, keep_sems
        self.core = ring.group % 2
        self.mate = (ring.group + 1 - 2 * self.core, ring.me)

    def peers(self):
        return [self.mate] + [
            ((self.ring.group + 2 * k) % self.groups, self.ring.me) for k in range(1, self.groups // 2)
        ]

    def half(self, i, core):
        rows = self.near[i].shape[0]
        return pl.ds(pl.multiple_of(core * rows, rows), rows)

    def near_copy(self, i):
        return pltpu.make_async_remote_copy(
            src_ref=self.grads[i].at[self.half(i, 1 - self.core), :], dst_ref=self.near[i],
            send_sem=self.near_sems.at[0, i], recv_sem=self.near_sems.at[1, i],
            device_id=self.mate, device_id_type=MESH,
        )

    def far_copy(self, i, k):
        return pltpu.make_async_remote_copy(
            src_ref=self.near[i], dst_ref=self.far[i].at[k - 1],
            send_sem=self.far_sems.at[0, i, k - 1], recv_sem=self.far_sems.at[1, i, k - 1],
            device_id=((self.ring.group + 2 * k) % self.groups, self.ring.me), device_id_type=MESH,
        )

    def back_copy(self, i):
        return pltpu.make_async_remote_copy(
            src_ref=self.far[i].at[0], dst_ref=self.targets[i].at[self.half(i, self.core), :],
            send_sem=self.back_sems.at[0, i], recv_sem=self.back_sems.at[1, i],
            device_id=self.mate, device_id_type=MESH,
        )

    def keep_copy(self, i):
        return pltpu.make_async_copy(
            self.far[i].at[0], self.targets[i].at[self.half(i, self.core), :], self.keep_sems.at[i]
        )

    def first(self, chosen):
        for i in chosen:
            self.near_copy(i).start()

    def each_block(self, i, body):
        rows = self.near[i].shape[0]
        block = next(size for size in (64, 32, 16) if rows % size == 0)

        def step(at, carry):
            start = pl.multiple_of(at * block, block)
            body(pl.ds(start, block), pl.ds(pl.multiple_of(self.core * rows + start, block), block))
            return carry

        lax.fori_loop(0, rows // block, step, 0)

    def second(self, chosen):
        for i in chosen:
            self.near_copy(i).wait_recv()

            def add(here, own, i=i):
                self.near[i][here, :] = (
                    self.near[i][here, :].astype(F32) + self.grads[i][own, :].astype(F32)
                ).astype(BF16)

            self.each_block(i, add)
            for k in range(1, self.groups // 2):
                self.far_copy(i, k).start()

    def third(self, chosen):
        for i in chosen:
            for k in range(1, self.groups // 2):
                self.far_copy(i, k).wait()

            def add(here, own, i=i):
                total = self.near[i][here, :].astype(F32)
                for k in range(self.groups // 2 - 1):
                    total = total + self.far[i][k, here, :].astype(F32)
                self.far[i][0, here, :] = total.astype(BF16)

            self.each_block(i, add)
            self.keep_copy(i).start()
            self.back_copy(i).start()

    def last(self):
        for i in range(len(self.grads)):
            self.near_copy(i).wait_send()
            self.back_copy(i).wait()
            self.keep_copy(i).wait()


def sum_scratch(shapes, groups):
    number = len(shapes)
    return (
        [pltpu.VMEM((rows // 2, columns), BF16) for rows, columns in shapes]
        + [pltpu.VMEM((groups // 2 - 1, rows // 2, columns), BF16) for rows, columns in shapes]
        + [
            pltpu.SemaphoreType.DMA((2, number)),
            pltpu.SemaphoreType.DMA((2, number, groups // 2 - 1)),
            pltpu.SemaphoreType.DMA((2, number)),
            pltpu.SemaphoreType.DMA((number,)),
        ]
    )


def greet(ring, others=()):
    barrier = pltpu.get_barrier_semaphore()
    peers = [ring.next(0), ring.next(1)] + list(others)
    for peer in peers:
        pl.semaphore_signal(barrier, inc=1, device_id=peer, device_id_type=MESH)
    pl.semaphore_wait(barrier, len(peers))


def ring_semaphores(count, subs=SUBS):
    return [pltpu.SemaphoreType.DMA((2, subs, count - 1))] * 2


def ring_slots(count, rows, columns):
    return pltpu.VMEM((2, SUBS, count, rows // (2 * SUBS), columns), BF16)


ANY = pl.BlockSpec(memory_space=pl.ANY)
VMEM = pl.BlockSpec(memory_space=pltpu.VMEM)


def ring_params(number):
    return pltpu.CompilerParams(
        collective_id=number, has_side_effects=True, vmem_limit_bytes=60 << 20
    )


WEIGHT_HOPS = 3


def gather_kernel(
    count, groups, tokens, w_out, tokens_full, w_full,
    sends, recvs, w_sends, w_recvs, local, far_sems, near_sems,
):
    ring = Ring(count)
    rows = tokens.shape[0]
    group, me = ring.group, ring.me
    part = w_out.shape[0] // groups
    across = groups // 2
    mate = (group + 1 - 2 * (group % 2), me)
    gather = Gather(ring, row_own(tokens), row_view(tokens_full, rows), sends, recvs, rows)
    own_part = lambda start, size: w_out.at[pl.ds(pl.multiple_of(group * part + start, size), size), :]
    weights = Gather(
        ring, own_part, lambda origin, start, size: w_full.at[origin, group, pl.ds(start, size), :],
        w_sends, w_recvs, part, 1,
    )
    keep = pltpu.make_async_copy(
        tokens, tokens_full.at[pl.ds(pl.multiple_of(me * rows, rows), rows), :], local.at[0]
    )
    keep_part = pltpu.make_async_copy(own_part(0, part), w_full.at[me, group], local.at[1])

    def far(k):
        return pltpu.make_async_remote_copy(
            src_ref=w_full.at[:, group], dst_ref=w_full.at[:, group],
            send_sem=far_sems.at[0, k - 1], recv_sem=far_sems.at[1, k - 1],
            device_id=((group + 2 * k) % groups, me), device_id_type=MESH,
        )

    def near(k):
        held = (group + groups - 2 * k) % groups
        return pltpu.make_async_remote_copy(
            src_ref=w_full.at[:, held], dst_ref=w_full.at[:, held],
            send_sem=near_sems.at[0, k], recv_sem=near_sems.at[1, k],
            device_id=mate, device_id_type=MESH,
        )

    greet(ring, [mate] + [((group + 2 * k) % groups, me) for k in range(1, across)])
    weights.begin()
    gather.begin()
    keep.start()
    keep_part.start()
    whole_at = -(-(count - 2) // WEIGHT_HOPS) + 1

    def forward(step, carry):
        for place in range(WEIGHT_HOPS):
            number = (step - 1) * WEIGHT_HOPS + place + 1

            @pl.when(number < count - 1)
            def _():
                weights.hop(number)

        gather.hop(step)

        @pl.when(step == whole_at)
        def _():
            weights.arrived(count - 1)
            keep_part.wait()
            for k in range(1, across):
                far(k).start()
            near(0).start()

        return carry

    lax.fori_loop(1, count - 1, forward, 0)
    for k in range(1, across):
        far(k).wait_recv()
        near(k).start()
    gather.arrived(count - 1)
    for k in range(across):
        near(k).wait()
    for k in range(1, across):
        far(k).wait_send()
    weights.end()
    gather.end()
    keep.wait()


def gather_tokens(tokens, w_out, count, groups):
    rows, model = tokens.shape
    part = w_out.shape[0] // groups
    full, w_full = pl.pallas_call(
        functools.partial(gather_kernel, count, groups),
        name="gather_tokens",
        out_shape=[
            jax.ShapeDtypeStruct((count * rows, model), tokens.dtype),
            jax.ShapeDtypeStruct((count, groups, part, model), w_out.dtype),
        ],
        in_specs=[ANY] * 2,
        out_specs=[ANY] * 2,
        scratch_shapes=ring_semaphores(count)
        + ring_semaphores(count, 1)
        + [
            pltpu.SemaphoreType.DMA((2,)),
            pltpu.SemaphoreType.DMA((2, groups // 2 - 1)),
            pltpu.SemaphoreType.DMA((2, groups // 2)),
        ],
        compiler_params=ring_params(1),
        cost_estimate=pl.CostEstimate(flops=0, bytes_accessed=300 << 20, transcendentals=0),
    )(tokens, w_out)
    return full, w_full.reshape(count * w_out.shape[0], model)


def attend_kernel(
    count, mixed, w_out, tokens, gain, w_gate, w_up, w_down, cotangents,
    resid, full, hidden, grad_gate, grad_up,
    gathered, gate_box, up_box, down_box, boxes, ahead, stages, sends, recvs, weight_sems, box_sems, out_sems, stage_sems,
):
    ring = Ring(count)
    rows = tokens.shape[0]
    half = rows // 2
    gather = Gather(
        ring, lambda start, size: row_view(gathered, rows)(ring.me, start, size), row_view(gathered, rows),
        sends, recvs, rows,
    )
    loads = [
        pltpu.make_async_copy(source, box, weight_sems.at[k])
        for k, (source, box) in enumerate(((w_gate, gate_box), (w_up, up_box), (w_down, down_box)))
    ]

    def place(way, step):
        return pl.ds(pl.multiple_of(gather.origin(way, step) * rows + way * half, half), half)

    def box_copy(way, step):
        return pltpu.make_async_copy(
            cotangents.at[place(way, step), :], boxes.at[step % 2, way], box_sems.at[step % 2, way]
        )

    def out_copy(way, step):
        at = place(way, step)
        return pltpu.make_async_copy(gathered.at[at, :], full.at[at, :], out_sems.at[way, step])

    def stage_copy(k, way, step):
        target = (hidden, grad_gate, grad_up)[k]
        return pltpu.make_async_copy(
            stages.at[step % 2, k, way], target.at[place(way, step), :], stage_sems.at[step % 2, k, way]
        )

    def settle(step):
        for k in range(3):
            for way in (0, 1):
                stage_copy(k, way, step).wait()

    for way in (0, 1):
        box_copy(way, 0).start()
    for load in loads:
        load.start()
    greet(ring)
    value = tokens[...].astype(F32) + mm(mixed[...], w_out[...])
    resid[...] = value
    scale = lax.rsqrt(jnp.mean(value * value, axis=1, keepdims=True) + 1e-6)
    gathered[pl.ds(pl.multiple_of(ring.me * rows, rows), rows), :] = (
        value * scale * gain[...].astype(F32).reshape(1, -1)
    ).astype(BF16)

    def hide(step):
        @pl.when(step == 0)
        def _():
            loads[2].wait()

        for way in (0, 1):
            box_copy(way, step).wait()

        @pl.when(step + 1 < count)
        def _():
            for way in (0, 1):
                box_copy(way, step + 1).start()

        slot = step % 2
        ahead[...] = mm(jnp.concatenate([boxes[slot, 0], boxes[slot, 1]], 0), down_box[...], (1, 1))

    def feed(step):
        @pl.when(step == 0)
        def _():
            loads[0].wait()
            loads[1].wait()

        @pl.when(step > 1)
        def _():
            settle(step - 2)

        for way in (0, 1):
            out_copy(way, step).start()
        slot = step % 2
        inputs = jnp.concatenate([gathered[place(0, step), :], gathered[place(1, step), :]], 0)
        gate = mm(inputs, gate_box[...], (1, 1))
        up = mm(inputs, up_box[...], (1, 1))
        grad = ahead[...]
        sig = sigmoid(gate)
        opened = gate * sig
        for k, result in enumerate(
            (opened * up, grad * up * sig * (1.0 + gate * (1.0 - sig)), grad * opened)
        ):
            low = result.astype(BF16)
            for way in (0, 1):
                stages[slot, k, way] = low[way * half : way * half + half]
                stage_copy(k, way, step).start()

    def before(step):
        pl.when(step > 0)(lambda: hide(step))

    def between(step):
        pl.when(step == 0)(lambda: hide(step))
        feed(step)

    ring_gather(gather, between, before)
    settle(count - 2)
    settle(count - 1)

    def drain(step, carry):
        for way in (0, 1):
            out_copy(way, step).wait()
        return carry

    lax.fori_loop(0, count, drain, 0)


def attend(mixed, w_out, tokens, gain, w_gate, w_up, w_down, cotangents, count):
    rows, model = tokens.shape
    slots, inner = count * rows, w_down.shape[0]
    return pl.pallas_call(
        functools.partial(attend_kernel, count),
        name="attend",
        out_shape=[
            jax.ShapeDtypeStruct((rows, model), F32),
            jax.ShapeDtypeStruct((slots, model), BF16),
        ]
        + [jax.ShapeDtypeStruct((slots, inner), BF16)] * 3,
        in_specs=[VMEM] * 4 + [ANY] * 4,
        out_specs=[VMEM] + [ANY] * 4,
        scratch_shapes=[pltpu.VMEM((slots, model), BF16)]
        + [pltpu.VMEM((inner, model), BF16)] * 3
        + [
            pltpu.VMEM((2, 2, rows // 2, model), BF16),
            pltpu.VMEM((rows, inner), F32),
            pltpu.VMEM((2, 3, 2, rows // 2, inner), BF16),
        ]
        + ring_semaphores(count)
        + [
            pltpu.SemaphoreType.DMA((3,)),
            pltpu.SemaphoreType.DMA((2, 2)),
            pltpu.SemaphoreType.DMA((2, count)),
            pltpu.SemaphoreType.DMA((2, 3, 2)),
        ],
        compiler_params=ring_params(2),
        cost_estimate=pl.CostEstimate(
            flops=2 * rows * model * model + 6 * slots * model * inner, bytes_accessed=300 << 20,
            transcendentals=slots * inner,
        ),
    )(mixed, w_out, tokens, gain, w_gate, w_up, w_down, cotangents)


def norm_back(inputs, scale, gain, grad_normed):
    weighted = gain * grad_normed
    inner = jnp.mean(weighted * inputs, axis=1, keepdims=True)
    unit = inputs * scale
    return scale * weighted - unit * (scale * scale * inner), grad_normed * unit


JOBS = 8


def ffn_back_kernel(
    count, groups, rows, grad_gate, grad_up, hidden_in, w_gate, w_up, resid_in, cotangent_in, gain, inputs, cotangents,
    grad_resid, full, grad_gain, sum_gate, sum_up, sum_down,
    slots, low, gw_gate, gw_up, gw_down, boxes, box_sems, hidden, resid, cotangent, load_sems, *rest,
):
    ring = Ring(count)
    sends, recvs, sends_two, recvs_two, local = rest[:5]
    sums = GroupSum(
        ring, groups, (gw_gate, gw_up, gw_down), rest[5:8], rest[8:11], (sum_gate, sum_up, sum_down), *rest[11:]
    )
    wide = boxes.shape[2]

    def box_copy(job, source):
        at = pl.multiple_of(job % (JOBS // 2) * wide, wide)
        return pltpu.make_async_copy(
            source.at[:, pl.ds(at, wide)], boxes.at[job % 2], box_sems.at[job % 2]
        )

    def fetch(job):
        @pl.when(job < JOBS // 2)
        def _():
            box_copy(job, inputs).start()

        @pl.when(job >= JOBS // 2)
        def _():
            box_copy(job, cotangents).start()

    loads = [
        pltpu.make_async_copy(source, target, load_sems.at[k])
        for k, (source, target) in enumerate(((hidden_in, hidden), (resid_in, resid), (cotangent_in, cotangent)))
    ]
    fetch(0)
    for load in loads:
        load.start()
    greet(ring, sums.peers())
    grad_gain[...] = jnp.zeros_like(grad_gain)
    half = rows // 2

    def partial(first, second, step):
        gates = jnp.concatenate([grad_gate[pl.ds(first, half), :], grad_gate[pl.ds(second, half), :]], 0)
        ups = jnp.concatenate([grad_up[pl.ds(first, half), :], grad_up[pl.ds(second, half), :]], 0)
        return mm(gates, w_gate[...]) + mm(ups, w_up[...])

    def finish(start, size, grad):
        value = resid[start : start + size, :]
        scale = lax.rsqrt(jnp.mean(value * value, axis=1, keepdims=True) + 1e-6)
        through, pieces = norm_back(value, scale, gain[...].astype(F32).reshape(1, -1), grad)
        result = cotangent[start : start + size, :].astype(F32) + through
        grad_resid[start : start + size, :] = result
        grad_gain[...] += jnp.sum(pieces, axis=0, keepdims=True)
        low[start : start + size, :] = result.astype(BF16)

    def work(job, carry):
        box_copy(job, inputs).wait()

        @pl.when(job + 1 < JOBS)
        def _():
            fetch(job + 1)

        at = pl.ds(pl.multiple_of(job % (JOBS // 2) * wide, wide), wide)

        @pl.when(job < JOBS // 2)
        def _():
            box = boxes[job % 2]
            gw_gate[:, at] = mm(grad_gate[...], box, (0, 0)).astype(BF16)
            gw_up[:, at] = mm(grad_up[...], box, (0, 0)).astype(BF16)

        @pl.when(job >= JOBS // 2)
        def _():
            gw_down[:, at] = mm(hidden[...], boxes[job % 2], (0, 0)).astype(BF16)

        return carry

    each = JOBS // 4

    def beside_scatter(step):
        @pl.when(step == 2)
        def _():
            for load in loads:
                load.wait()

        @pl.when(step == 3)
        def _():
            sums.second((0, 1))

        @pl.when(step < 4)
        def _():
            lax.fori_loop(step * each, step * each + each, work, 0)

        @pl.when(step == 1)
        def _():
            sums.first((0, 1))

        @pl.when(step == 3)
        def _():
            sums.first((2,))

        @pl.when(step == 5)
        def _():
            sums.second((2,))

    def beside_gather(step):
        @pl.when(step == count - 3)
        def _():
            sums.third((0, 1))

        @pl.when(step == count - 2)
        def _():
            sums.third((2,))

    ring_scatter(Scatter(ring, partial, slots, sends, recvs, rows, finish), beside_scatter)
    keep = pltpu.make_async_copy(low, full.at[pl.ds(pl.multiple_of(ring.me * rows, rows), rows), :], local)
    keep.start()
    ring_gather(Gather(ring, row_own(low), row_view(full, rows), sends_two, recvs_two, rows), beside_gather)
    keep.wait()
    sums.last()


def ffn_back(grad_gate, grad_up, hidden, w_gate, w_up, resid, cotangent, gain, inputs, cotangents, count, groups):
    rows, model = resid.shape
    slots, inner = grad_up.shape
    shapes = [(inner, model)] * 3
    return pl.pallas_call(
        functools.partial(ffn_back_kernel, count, groups, rows),
        name="ffn_back",
        out_shape=[
            jax.ShapeDtypeStruct((rows, model), F32),
            jax.ShapeDtypeStruct((slots, model), BF16),
            jax.ShapeDtypeStruct((1, model), F32),
        ]
        + [jax.ShapeDtypeStruct(shape, BF16) for shape in shapes],
        in_specs=[VMEM] * 2 + [ANY] + [VMEM] * 2 + [ANY] * 2 + [VMEM] + [ANY] * 2,
        out_specs=[VMEM, ANY, VMEM] + [ANY] * 3,
        scratch_shapes=[ring_slots(count, rows, model), pltpu.VMEM((rows, model), BF16)]
        + [pltpu.VMEM(shape, BF16) for shape in shapes]
        + [pltpu.VMEM((2, slots, model // (JOBS // 2)), BF16), pltpu.SemaphoreType.DMA((2,))]
        + [pltpu.VMEM((slots, inner), BF16), pltpu.VMEM((rows, model), F32), pltpu.VMEM((rows, model), BF16)]
        + [pltpu.SemaphoreType.DMA((3,))]
        + ring_semaphores(count) * 2
        + [pltpu.SemaphoreType.DMA]
        + sum_scratch(shapes, groups),
        compiler_params=ring_params(3),
        cost_estimate=pl.CostEstimate(
            flops=10 * slots * model * inner, bytes_accessed=600 << 20, transcendentals=0
        ),
    )(grad_gate, grad_up, hidden, w_gate, w_up, resid, cotangent, gain, inputs, cotangents)


def last_kernel(
    count, groups, rows, terms, tokens_in, grad_resid_in, gain, small, *rest,
):
    grads, rest = rest[:5], rest[5:]
    grad_tokens, total = rest[:2]
    targets, rest = rest[2:7], rest[7:]
    slots, first_box, second_box, second_own, boxes, box_sems, tokens, grad_resid, load_sems = rest[:9]
    sends, recvs, first_sends, first_recvs, second_sends, second_recvs = rest[9:15]
    ring = Ring(count)
    sums = GroupSum(ring, groups, grads, rest[15:20], rest[20:25], targets, *rest[25:])
    loads = [
        pltpu.make_async_copy(tokens_in, tokens, load_sems.at[0]),
        pltpu.make_async_copy(grad_resid_in, grad_resid, load_sems.at[1]),
    ]
    me, group = ring.me, ring.group
    first_peers = [(group, (me + k) % count) for k in range(1, count)]
    second_peers = [((group + k) % groups, me) for k in range(1, groups)]
    barrier = pltpu.get_barrier_semaphore()
    for peer in first_peers + second_peers:
        pl.semaphore_signal(barrier, inc=1, device_id=peer, device_id_type=MESH)
    pl.semaphore_wait(barrier, count + groups - 2)

    def first(k):
        return pltpu.make_async_remote_copy(
            src_ref=small.at[0:8], dst_ref=first_box.at[k], send_sem=first_sends.at[k],
            recv_sem=first_recvs.at[k], device_id=first_peers[k], device_id_type=MESH,
        )

    def second(k):
        return pltpu.make_async_remote_copy(
            src_ref=second_own, dst_ref=second_box.at[k], send_sem=second_sends.at[k],
            recv_sem=second_recvs.at[k], device_id=second_peers[k], device_id_type=MESH,
        )

    every = range(len(grads))
    sums.first(every)
    for k in range(count - 1):
        first(k).start()
    half = rows // 2

    def box_copy(way, start, slot):
        return pltpu.make_async_copy(
            terms.at[pl.ds(start, half), :], boxes.at[slot, way], box_sems.at[slot, way]
        )

    def fetch(step):
        for way, owner in ((0, ring.at(-1 - step)), (1, ring.at(1 + step))):
            box_copy(way, pl.multiple_of(owner * rows + way * half, half), step % 2).start()

    def partial(first, second, step):
        for way, start in ((0, first), (1, second)):
            box_copy(way, start, step % 2).wait()

        @pl.when(step + 1 < count)
        def _():
            fetch(step + 1)

        return jnp.concatenate([boxes[step % 2, 0], boxes[step % 2, 1]], 0).astype(F32)

    def finish(start, size, grad):
        value = tokens[start : start + size, :].astype(F32)
        scale = lax.rsqrt(jnp.mean(value * value, axis=1, keepdims=True) + 1e-6)
        through, pieces = norm_back(value, scale, gain[...].astype(F32).reshape(1, -1), grad)
        grad_tokens[start : start + size, :] = grad_resid[start : start + size, :] + through

    def early():
        sums.second(every)
        for k in range(count - 1):
            first(k).wait()
        mine = small[0:8]
        for k in range(count - 1):
            mine = mine + first_box[k]
        second_own[0:8] = mine
        second_own[8:] = small[8:]
        for k in range(groups - 1):
            second(k).start()

    def late():
        for k in range(groups - 1):
            second(k).wait()
        mine = second_own[...]
        for k in range(groups - 1):
            mine = mine + second_box[k]
        total[...] = mine
        for load in loads:
            load.wait()

    def beside(step):
        pl.when(step == 0)(early)
        for i in every:
            pl.when(step == count - 1 - len(every) + i)(lambda i=i: sums.third((i,)))
        pl.when(step == count - 2)(late)

    fetch(0)
    for load in loads:
        load.start()
    ring_scatter(Scatter(ring, partial, slots, sends, recvs, rows, finish), beside)
    sums.last()


def last_step(terms, tokens, grad_resid, gain, small, grads, count, groups):
    rows, model = tokens.shape
    return pl.pallas_call(
        functools.partial(last_kernel, count, groups, rows),
        name="last_step",
        out_shape=[jax.ShapeDtypeStruct((rows, model), F32), jax.ShapeDtypeStruct(small.shape, F32)]
        + [jax.ShapeDtypeStruct(g.shape, BF16) for g in grads],
        in_specs=[ANY] * 3 + [VMEM] * (2 + len(grads)),
        out_specs=[VMEM, VMEM] + [ANY] * len(grads),
        scratch_shapes=[
            ring_slots(count, rows, model),
            pltpu.VMEM((count - 1, 8, model), F32),
            pltpu.VMEM((groups - 1,) + small.shape, F32),
            pltpu.VMEM(small.shape, F32),
            pltpu.VMEM((2, 2, rows // 2, model), BF16),
            pltpu.SemaphoreType.DMA((2, 2)),
            pltpu.VMEM((rows, model), BF16),
            pltpu.VMEM((rows, model), F32),
            pltpu.SemaphoreType.DMA((2,)),
        ]
        + ring_semaphores(count)
        + [pltpu.SemaphoreType.DMA((count - 1,))] * 2
        + [pltpu.SemaphoreType.DMA((groups - 1,))] * 2
        + sum_scratch([g.shape for g in grads], groups),
        compiler_params=ring_params(4),
        cost_estimate=pl.CostEstimate(flops=0, bytes_accessed=300 << 20, transcendentals=0),
    )(terms, tokens, grad_resid, gain, small, *grads)


def results_kernel(heads, taps, wide, width, total, *refs):
    number = (len(refs) - 7) // 2
    for source, target in zip(refs[:number], refs[number : 2 * number]):
        target[...] = source[...].astype(target.dtype)
    g_first, g_second, g_head, gt_query, gt_key, gt_value, g_beta = refs[2 * number :]

    @pl.when(pl.program_id(0) == 0)
    def _():
        g_first[...] = total[0:1, :]
        g_second[...] = total[1:2, :]
        g_head[...] = total[2:3, 0:width]
        row = 8 + heads
        for place, target in enumerate((gt_query, gt_key, gt_value)):
            target[...] = total[row : row + taps, place * wide : (place + 1) * wide]
        g_beta[...] = total[8 : 8 + heads, :]


def results(total, arrays, heads, taps, wide, width):
    model = total.shape[1]
    steps = next(n for n in (2, 1) if all(a.shape[0] % (8 * n) == 0 for a, _ in arrays))
    small = [(1, model), (1, model), (1, width)] + [(taps, wide)] * 3 + [(heads, model)]
    piece = lambda a: pl.BlockSpec((a.shape[0] // steps, a.shape[1]), lambda n: (n, 0))
    whole = lambda shape: pl.BlockSpec(shape, lambda n: (0, 0))
    return pl.pallas_call(
        functools.partial(results_kernel, heads, taps, wide, width),
        name="results",
        grid=(steps,),
        out_shape=[jax.ShapeDtypeStruct(a.shape, kind) for a, kind in arrays]
        + [jax.ShapeDtypeStruct(shape, F32) for shape in small],
        in_specs=[whole(total.shape)] + [piece(a) for a, _ in arrays],
        out_specs=[piece(a) for a, _ in arrays] + [whole(shape) for shape in small],
        compiler_params=pltpu.CompilerParams(vmem_limit_bytes=56 << 20),
        cost_estimate=pl.CostEstimate(flops=0, bytes_accessed=48 << 20, transcendentals=0),
    )(total, *[a for a, _ in arrays])


def spread_hops(step, chunks, count, hop, start=0):
    each = -(-(count - 1) // (chunks - 1))
    for place in range(each):
        number = step * each + place

        @pl.when((number >= start) & (number < count - 1))
        def _():
            hop(number)


def forward_kernel(
    heads, width, seqs, count, rows_own, chunks,
    starts, lengths, tokens, w_query, w_key, w_value, w_gate, w_beta,
    taps_query, taps_key, taps_value, gain, gain_first, side,
    mixed_own, mixed, p_query, p_key, p_value, p_gate, p_beta, z_query, z_key, z_value,
    delta_out, change_out, inverse_out, state_out, side_full,
    tail_query, tail_key, tail_value, state, stage, sends, recvs, local, row_sends, row_recvs,
):
    step = pl.program_id(0)
    size = tokens.shape[0]
    first = step * size

    @pl.when(step == 0)
    def _():
        for tail in (tail_query, tail_key, tail_value):
            tail[...] = jnp.zeros_like(tail)
        state[...] = jnp.zeros_like(state)

    ring = Ring(count)
    me, group = ring.me, ring.group
    wide = heads * width
    gather = Gather(ring, row_own(side), row_view(side_full, rows_own), sends, recvs, rows_own)
    keep = pltpu.make_async_copy(
        side, side_full.at[pl.ds(pl.multiple_of(me * rows_own, rows_own), rows_own), :], local.at[0]
    )
    own_columns = pl.ds(pl.multiple_of(me * wide, wide), wide)

    def keep_rows():
        return pltpu.make_async_copy(stage.at[me], mixed_own.at[:, own_columns], local.at[1])

    def row_copy(target):
        return pltpu.make_async_remote_copy(
            src_ref=stage.at[target], dst_ref=mixed_own.at[:, own_columns],
            send_sem=row_sends.at[target], recv_sem=row_recvs.at[me],
            device_id=(group, target), device_id_type=MESH,
        )

    def row_arrival(origin):
        return pltpu.make_async_remote_copy(
            src_ref=stage.at[me], dst_ref=mixed_own.at[:, own_columns],
            send_sem=row_sends.at[origin], recv_sem=row_recvs.at[origin],
            device_id=(group, origin), device_id_type=MESH,
        )

    @pl.when(step == 0)
    def _():
        barrier = pltpu.get_barrier_semaphore()
        for k in range(1, count):
            pl.semaphore_signal(barrier, inc=1, device_id=(group, (me + k) % count), device_id_type=MESH)
        pl.semaphore_wait(barrier, count - 1)
        gather.begin()
        keep.start()

    spread_hops(step, chunks, count, gather.hop, 1)
    rows, seg_rows, seg_columns, before, last = chunk_masks(starts, lengths, seqs, first, size)
    same = seg_rows == seg_columns
    i = lax.broadcasted_iota(jnp.int32, (size, size), 0)
    j = lax.broadcasted_iota(jnp.int32, (size, size), 1)
    strict = jnp.where(same & (i > j), 1.0, 0.0)
    inclusive = jnp.where(same & (i >= j), 1.0, 0.0)
    carried = jnp.where(seg_rows == before, 1.0, 0.0)
    ending = jnp.where(seg_rows == last, 1.0, 0.0)
    kept = jnp.where(before == last, 1.0, 0.0)
    live = jnp.where(seg_rows % 2 == 1, 1.0, 0.0)
    joined = [
        jnp.where(segment_at(rows - offset, starts, lengths, seqs) == seg_rows, 1.0, 0.0)
        for offset in range(1, taps_query.shape[0])
    ]
    inputs = normed_rows(tokens, gain_first)[0].astype(BF16)

    def feature(weight, taps, tail, p_out, z_out):
        projected = jnp.dot(inputs, weight[...], preferred_element_type=F32)
        p_out[...] = projected
        tail[8:, :] = projected
        tap = taps[...].astype(F32)
        result = projected * tap[0:1]
        for offset in range(1, tap.shape[0]):
            result = result + tail[8 - offset : 8 - offset + size, :] * tap[offset : offset + 1] * joined[offset - 1]
        tail[0:8, :] = projected[size - 8 :, :]
        z_out[...] = result
        return result * sigmoid(result)

    u_query = feature(w_query, taps_query, tail_query, p_query, z_query)
    u_key = feature(w_key, taps_key, tail_key, p_key, z_key)
    u_value = feature(w_value, taps_value, tail_value, p_value, z_value)
    gate = jnp.dot(inputs, w_gate[...], preferred_element_type=F32)
    p_gate[...] = gate
    beta_pre = mm(inputs, w_beta[...], (1, 1))
    p_beta[...] = beta_pre
    strength = sigmoid(beta_pre)
    opened = gate * sigmoid(gate)
    scale = width ** (-0.5)
    head_gain = gain[...].astype(F32)
    for h in range(heads):
        cols = slice(h * width, (h + 1) * width)
        uq, uk = u_query[:, cols], u_key[:, cols]
        query = (uq * lax.rsqrt(jnp.sum(uq * uq, axis=1, keepdims=True) + 1e-6)).astype(BF16)
        key = (uk * lax.rsqrt(jnp.sum(uk * uk, axis=1, keepdims=True) + 1e-6)).astype(BF16)
        value = u_value[:, cols].astype(BF16).astype(F32)
        beta = strength[:, h : h + 1]
        memory = state[h]
        low_memory = memory.astype(BF16)
        state_out[0, h] = low_memory
        lower = mm(key, key, (1, 1)) * strict * beta
        inverse = inverse_unit_lower(lower, size).astype(BF16)
        inverse_out[0, h] = inverse
        within = mm(query, key, (1, 1)) * inclusive
        change = mm(inverse, beta * (value - carried * mm(key, low_memory)))
        low_change = change.astype(BF16)
        change_out[:, cols] = low_change
        out = scale * (carried * mm(query, low_memory) + mm(within, low_change))
        state[h] = kept * memory + mm(key, ending * change, (0, 0))
        delta_out[:, cols] = out
        normal = out * lax.rsqrt(jnp.mean(out * out, axis=1, keepdims=True) + 1e-5) * head_gain
        low_mixed = (normal * opened[:, cols] * live).astype(BF16)
        mixed[:, cols] = low_mixed
        for place in range(size // rows_own):
            stage[step * (size // rows_own) + place, :, cols] = low_mixed[place * rows_own : (place + 1) * rows_own]

    each = size // rows_own

    def send(chunk, due):
        for place in range(each):
            target = chunk * each + place

            @pl.when((chunk >= 0) & (target != me) & due((me + target) % LAGS))
            def _():
                row_copy(target).start()

    for lag in range(LAGS):
        send(step - lag, lambda own_lag, lag=lag: own_lag == lag)
    for place in range(each):
        pl.when(step * each + place == me)(lambda: keep_rows().start())

    @pl.when(step == chunks - 1)
    def _():
        for back in range(LAGS - 1):
            send(step - back, lambda own_lag, back=back: own_lag > back)

    @pl.when(step == chunks - 1)
    def _():
        gather.arrived(count - 1)
        gather.end()
        keep.wait()
        keep_rows().wait()
        for k in range(1, count):
            row_copy((me + k) % count).wait_send()
            row_arrival((me + k) % count).wait_recv()


def forward_mixer(tokens, w_query, w_key, w_value, w_gate, w_beta, taps_query, taps_key, taps_value, gain, gain_first, starts, lengths, side, count):
    slots, model = tokens.shape
    wide = w_query.shape[1]
    width = gain.shape[0]
    heads = wide // width
    seqs = starts.shape[1]
    chunks = slots // CHUNK
    taps = taps_query.shape[0]
    smem = pl.BlockSpec(memory_space=pltpu.SMEM)
    whole = lambda shape: pl.BlockSpec(shape, lambda n: (0,) * len(shape))
    piece = lambda shape: pl.BlockSpec(shape, lambda n: (n,) + (0,) * (len(shape) - 1))
    own = (slots // count, count * wide)
    outs = [
        ((slots, wide), BF16), ((slots, wide), F32), ((slots, wide), F32), ((slots, wide), F32), ((slots, wide), F32),
        ((slots, w_beta.shape[0]), F32), ((slots, wide), F32), ((slots, wide), F32), ((slots, wide), F32),
        ((slots, wide), F32), ((slots, wide), BF16),
    ]
    return pl.pallas_call(
        functools.partial(forward_kernel, heads, width, seqs, count, slots // count, chunks),
        name="mixer_forward",
        grid=(chunks,),
        out_shape=[jax.ShapeDtypeStruct(own, BF16)]
        + [jax.ShapeDtypeStruct(s, d) for s, d in outs]
        + [
            jax.ShapeDtypeStruct((chunks, heads, CHUNK, CHUNK), BF16),
            jax.ShapeDtypeStruct((chunks, heads, width, width), BF16),
            jax.ShapeDtypeStruct((slots, model), BF16),
        ],
        in_specs=[smem, smem, piece((CHUNK, model))]
        + [whole((model, wide))] * 4
        + [whole(w_beta.shape)]
        + [whole((taps, wide))] * 3
        + [whole((1, width)), VMEM, ANY],
        out_specs=[ANY]
        + [piece((CHUNK, s[1])) for s, d in outs]
        + [piece((1, heads, CHUNK, CHUNK)), piece((1, heads, width, width)), ANY],
        scratch_shapes=[pltpu.VMEM((CHUNK + 8, wide), F32)] * 3
        + [pltpu.VMEM((heads, width, width), F32), pltpu.VMEM((count, slots // count, wide), BF16)]
        + ring_semaphores(count)
        + [pltpu.SemaphoreType.DMA((2,))]
        + [pltpu.SemaphoreType.DMA((count,))] * 2,
        compiler_params=ring_params(5),
        cost_estimate=pl.CostEstimate(
            flops=2 * slots * model * wide * 4 + slots * heads * CHUNK * 2 * CHUNK * 20,
            bytes_accessed=slots * model * 2 + 4 * model * wide * 2 + slots * wide * 36,
            transcendentals=slots * wide * 4,
        ),
    )(starts, lengths, tokens, w_query, w_key, w_value, w_gate, w_beta, taps_query, taps_key, taps_value, gain.reshape(1, width), gain_first, side)


def small_rows(heads, taps):
    return -(-(8 + heads + taps) // 8) * 8


def backward_kernel(
    heads, width, seqs, chunks, count, rows_own,
    starts, lengths, tokens, grad_attended, mixed, p_query, p_key, p_value, p_gate, p_beta,
    z_query, z_key, z_value, delta_out, change_in, inverse_in, state_in,
    w_query_in, w_key_in, w_value_in, w_gate_in, w_beta, w_out, taps_query, taps_key, taps_value, gain, gain_first,
    hidden, w_down, resid_in, g_second, grad_normed, gw_query, gw_key, gw_value, gw_gate, gw_out,
    small, output,
    a_query, a_key, a_value, a_gate, a_out, head_query, head_key, head_value, flow,
    w_query, w_key, w_value, w_gate, resid, load_sems, slots, sends, recvs,
):
    step = pl.program_id(0)
    size = tokens.shape[0]
    first = (chunks - 1 - step) * size

    @pl.when(step == 0)
    def _():
        for ref in (a_query, a_key, a_value, a_gate, a_out, small, flow):
            ref[...] = jnp.zeros_like(ref)
        small[1:2, :] = g_second[...]
        for ref in (head_query, head_key, head_value):
            ref[size:, :] = jnp.zeros((8, ref.shape[1]), F32)

    half = rows_own // 2

    def partial(one, two, number):
        return mm(jnp.concatenate([hidden[pl.ds(one, half), :], hidden[pl.ds(two, half), :]], 0), w_down[...])

    def finish(start, length, down):
        output[start : start + length, :] = (resid[start : start + length, :] + down).astype(BF16)

    ring = Ring(count)
    scatter = Scatter(ring, partial, slots, sends, recvs, rows_own, finish)
    loads = [
        pltpu.make_async_copy(source, target, load_sems.at[k])
        for k, (source, target) in enumerate(
            ((w_query_in, w_query), (w_key_in, w_key), (w_value_in, w_value), (w_gate_in, w_gate), (resid_in, resid))
        )
    ]

    @pl.when(step == 0)
    def _():
        for load in loads:
            load.start()
        greet(ring)

    spread_hops(step, chunks, count, scatter.hop)
    rows, seg_rows, seg_columns, before, last = chunk_masks(starts, lengths, seqs, first, size)
    same = seg_rows == seg_columns
    i = lax.broadcasted_iota(jnp.int32, (size, size), 0)
    j = lax.broadcasted_iota(jnp.int32, (size, size), 1)
    strict = jnp.where(same & (i > j), 1.0, 0.0)
    inclusive = jnp.where(same & (i >= j), 1.0, 0.0)
    carried = jnp.where(seg_rows == before, 1.0, 0.0)
    ending = jnp.where(seg_rows == last, 1.0, 0.0)
    kept = jnp.where(before == last, 1.0, 0.0)
    live = jnp.where(seg_rows % 2 == 1, 1.0, 0.0)
    taps = taps_query.shape[0]
    joined = [
        jnp.where(segment_at(rows + offset, starts, lengths, seqs) == seg_rows, 1.0, 0.0)
        for offset in range(1, taps)
    ]
    normal_rows, unit_rows = normed_rows(tokens, gain_first)
    inputs = normal_rows.astype(BF16)
    grad_rows = grad_attended[...]
    grad_mixed = mm(grad_rows, w_out[...], (1, 1))
    a_out[...] += mm(mixed[...], grad_rows, (0, 0))
    strength = sigmoid(p_beta[...])
    scale = width ** (-0.5)
    head_gain = gain[...].astype(F32)

    grads_query, grads_key, grads_value, grads_gate, grads_beta = [], [], [], [], []
    for h in range(heads):
        cols = slice(h * width, (h + 1) * width)
        out = delta_out[:, cols]
        gate = p_gate[:, cols]
        sig_gate = sigmoid(gate)
        silu_gate = gate * sig_gate
        root = lax.rsqrt(jnp.mean(out * out, axis=1, keepdims=True) + 1e-5)
        grad = grad_mixed[:, cols] * live
        unit = out * root
        grads_gate.append(grad * unit * head_gain * (sig_gate * (1.0 + gate * (1.0 - sig_gate))))
        grad_normal = grad * silu_gate
        small[2:3, 0:width] += jnp.sum(grad_normal * unit, axis=0, keepdims=True)
        push = grad_normal * head_gain
        grad_out = scale * root * (push - unit * jnp.mean(push * unit, axis=1, keepdims=True))

        zq, zk, zv = z_query[:, cols], z_key[:, cols], z_value[:, cols]
        sq, sk, sv = sigmoid(zq), sigmoid(zk), sigmoid(zv)
        uq, uk = zq * sq, zk * sk
        nq = lax.rsqrt(jnp.sum(uq * uq, axis=1, keepdims=True) + 1e-6)
        nk = lax.rsqrt(jnp.sum(uk * uk, axis=1, keepdims=True) + 1e-6)
        unit_q, unit_k = uq * nq, uk * nk
        query, key = unit_q.astype(BF16), unit_k.astype(BF16)
        beta = strength[:, h : h + 1]
        change = change_in[:, cols]
        inverse = inverse_in[0, h]
        memory = state_in[0, h]
        flowing = flow[h]
        low_flow = flowing.astype(BF16)
        low_out = grad_out.astype(BF16)

        within = mm(query, key, (1, 1)) * inclusive
        grad_within = (mm(low_out, change, (1, 1)) * inclusive).astype(BF16)
        grad_change = mm(within, low_out, (0, 0)) + ending * mm(key, low_flow)
        grad_mid = mm(inverse, grad_change, (0, 0))
        grad_value = beta * grad_mid
        low_value = grad_value.astype(BF16)
        cross = (mm(low_value, change, (1, 1)) * strict).astype(BF16)
        grad_query = carried * mm(low_out, memory, (1, 1)) + mm(grad_within, key)
        grad_key = (
            mm(grad_within, query, (0, 0))
            + ending * mm(change, low_flow, (1, 1))
            - carried * mm(low_value, memory, (1, 1))
            - mm(cross, key)
            - mm(cross, key, (0, 0))
        )
        flow[h] = (
            kept * flowing
            + mm(query, carried * grad_out, (0, 0))
            - mm(key, carried * grad_value, (0, 0))
        )
        grads_beta.append((1.0 - beta) * jnp.sum(grad_mid * change.astype(F32), axis=1, keepdims=True))
        du_q = nq * (grad_query - unit_q * jnp.sum(grad_query * unit_q, axis=1, keepdims=True))
        du_k = nk * (grad_key - unit_k * jnp.sum(grad_key * unit_k, axis=1, keepdims=True))
        grads_query.append(du_q * sq * (1.0 + zq * (1.0 - sq)))
        grads_key.append(du_k * sk * (1.0 + zk * (1.0 - sk)))
        grads_value.append(grad_value * sv * (1.0 + zv * (1.0 - sv)))

    tap_row = 8 + heads
    wide = heads * width

    def unconv(parts, taps_ref, head, projected, place):
        lanes = slice(place * wide, (place + 1) * wide)
        grad = jnp.concatenate(parts, axis=1)
        head[0:size, :] = grad
        tap = taps_ref[...].astype(F32)
        p = projected[...]
        result = grad * tap[0:1]
        small[tap_row : tap_row + 1, lanes] += jnp.sum(p * grad, axis=0, keepdims=True)
        for offset in range(1, taps):
            moved = head[offset : offset + size, :] * joined[offset - 1]
            result = result + moved * tap[offset : offset + 1]
            row = tap_row + offset
            small[row : row + 1, lanes] += jnp.sum(p * moved, axis=0, keepdims=True)
        head[size:, :] = grad[0:8, :]
        return result.astype(BF16)

    d_query = unconv(grads_query, taps_query, head_query, p_query, 0)
    d_key = unconv(grads_key, taps_key, head_key, p_key, 1)
    d_value = unconv(grads_value, taps_value, head_value, p_value, 2)
    d_gate = jnp.concatenate(grads_gate, axis=1).astype(BF16)
    spare = [jnp.zeros((size, 1), F32)] * (w_beta.shape[0] - heads)
    d_beta = jnp.concatenate(grads_beta + spare, axis=1).astype(BF16)

    @pl.when(step == 0)
    def _():
        for load in loads:
            load.wait()

    grad_inputs = (
        mm(d_query, w_query[...], (1, 1))
        + mm(d_key, w_key[...], (1, 1))
        + mm(d_value, w_value[...], (1, 1))
        + mm(d_gate, w_gate[...], (1, 1))
        + mm(d_beta, w_beta[...])
    )
    grad_normed[...] = grad_inputs.astype(BF16)
    small[0:1, :] += jnp.sum(grad_inputs * unit_rows, axis=0, keepdims=True)
    a_query[...] += mm(inputs, d_query, (0, 0))
    a_key[...] += mm(inputs, d_key, (0, 0))
    a_value[...] += mm(inputs, d_value, (0, 0))
    a_gate[...] += mm(inputs, d_gate, (0, 0))
    small[8 : 8 + heads, :] += mm(d_beta, inputs, (0, 0))[:heads]

    @pl.when(step == chunks - 1)
    def _():
        for target, source in (
            (gw_query, a_query), (gw_key, a_key), (gw_value, a_value), (gw_gate, a_gate),
            (gw_out, a_out),
        ):
            target[...] = source[...].astype(target.dtype)
        scatter.end()


def backward_mixer(tokens, grad_attended, saved, w_query, w_key, w_value, w_gate, w_beta, w_out, taps_query, taps_key, taps_value, gain, gain_first, starts, lengths, hidden, w_down, resid, g_second, count):
    slots, model = tokens.shape
    wide = w_query.shape[1]
    width = gain.shape[0]
    heads = wide // width
    seqs = starts.shape[1]
    chunks = slots // CHUNK
    taps = taps_query.shape[0]
    smem = pl.BlockSpec(memory_space=pltpu.SMEM)
    fixed = lambda shape: pl.BlockSpec(shape, lambda n: (0,) * len(shape), pipeline_mode=pl.Buffered(1))
    piece = lambda shape: pl.BlockSpec(shape, lambda n: (chunks - 1 - n,) + (0,) * (len(shape) - 1))
    rows = lambda a: piece((CHUNK, a.shape[1]))
    outs = (
        [((slots, model), BF16)] + [((model, wide), BF16)] * 4 + [((wide, model), BF16)]
        + [((small_rows(heads, taps), model), F32), (resid.shape, BF16)]
    )
    return pl.pallas_call(
        functools.partial(backward_kernel, heads, width, seqs, chunks, count, slots // count),
        name="mixer_backward",
        grid=(chunks,),
        out_shape=[jax.ShapeDtypeStruct(s, d) for s, d in outs],
        in_specs=[smem, smem, rows(tokens), rows(grad_attended)]
        + [rows(a) for a in saved[:11]]
        + [piece((1, heads, CHUNK, CHUNK)), piece((1, heads, width, width))]
        + [ANY] * 4
        + [fixed(w_beta.shape), fixed((wide, model))]
        + [fixed((taps, wide))] * 3
        + [fixed((1, width)), VMEM, fixed(hidden.shape), fixed(w_down.shape), ANY, fixed(g_second.shape)],
        out_specs=[piece((CHUNK, model))] + [fixed(s) for s, d in outs[1:]],
        scratch_shapes=[pltpu.VMEM((model, wide), F32)] * 4
        + [pltpu.VMEM((wide, model), F32)]
        + [pltpu.VMEM((CHUNK + 8, wide), F32)] * 3
        + [pltpu.VMEM((heads, width, width), F32)]
        + [pltpu.VMEM((model, wide), BF16)] * 4
        + [pltpu.VMEM(resid.shape, F32), pltpu.SemaphoreType.DMA((5,)), ring_slots(count, slots // count, model)]
        + ring_semaphores(count),
        compiler_params=ring_params(6),
        cost_estimate=pl.CostEstimate(
            flops=2 * slots * model * wide * 10 + slots * heads * CHUNK * 2 * CHUNK * 8,
            bytes_accessed=slots * model * 6 + 10 * model * wide * 2 + slots * wide * 36,
            transcendentals=slots * wide * 8,
        ),
    )(starts, lengths, tokens, grad_attended, *saved, w_query, w_key, w_value, w_gate, w_beta, w_out, taps_query, taps_key, taps_value, gain.reshape(1, width), gain_first, hidden, w_down, resid, g_second)


def make_shards(groups, count):
    def shards(
        tokens, attn_gain, w_query, w_key, w_value, conv_query, conv_key, conv_value, w_beta, w_gate_out,
        head_gain, w_out, ffn_gain, w_gate, w_up, w_down, seq_starts, seq_lengths, cotangent,
    ):
        model = tokens.shape[1]
        heads = w_beta.shape[1]
        beta_rows = w_beta.T if heads > 1 else jnp.pad(w_beta.T, ((0, 1), (0, 0)))
        tokens_full, w_out_full = gather_tokens(tokens, w_out, count, groups)
        mixed_own, *saved = forward_mixer(
            tokens_full, w_query, w_key, w_value, w_gate_out, beta_rows,
            conv_query, conv_key, conv_value, head_gain, attn_gain, seq_starts, seq_lengths, cotangent, count,
        )
        grad_full, saved = saved[-1], saved[:-1]
        resid, ffn_full, hidden, grad_gate, grad_up = attend(
            mixed_own, w_out_full, tokens, ffn_gain, w_gate.T, w_up.T, w_down, grad_full, count
        )
        grad_resid, grad_attended, g_second, *ffn_grads = ffn_back(
            grad_gate, grad_up, hidden, w_gate.T, w_up.T, resid, cotangent, ffn_gain, ffn_full, grad_full,
            count, groups,
        )
        pulled = backward_mixer(
            tokens_full, grad_attended, saved, w_query, w_key, w_value, w_gate_out, beta_rows, w_out,
            conv_query, conv_key, conv_value, head_gain, attn_gain, seq_starts, seq_lengths,
            hidden, w_down, resid, g_second, count,
        )
        terms, gw_query, gw_key, gw_value, gw_gate_out, gw_out, small, output = pulled
        grad_tokens, total, *mixer_grads = last_step(
            terms, tokens, grad_resid, attn_gain, small,
            (gw_query, gw_key, gw_value, gw_gate_out, gw_out), count, groups,
        )
        taps, wide = conv_query.shape
        output, grad_tokens, *rest = results(
            total,
            [(output, BF16), (grad_tokens, F32)] + [(g, F32) for g in (*mixer_grads, *ffn_grads)],
            heads, taps, wide, head_gain.shape[0],
        )
        grads, (g_first, g_second, g_head, gt_query, gt_key, gt_value, g_beta) = rest[:8], rest[8:]
        return (
            output,
            grad_tokens,
            g_first[0],
            grads[0],
            grads[1],
            grads[2],
            gt_query,
            gt_key,
            gt_value,
            g_beta.T,
            grads[3],
            g_head[0],
            grads[4],
            g_second[0],
            grads[5].T,
            grads[6].T,
            grads[7],
        )

    return shards


def solution(mesh):
    placed = (
        P(("dp", "tensor"), None),
        P(),
        P(None, "tensor"),
        P(None, "tensor"),
        P(None, "tensor"),
        P(None, "tensor"),
        P(None, "tensor"),
        P(None, "tensor"),
        P(None, "tensor"),
        P(None, "tensor"),
        P(),
        P("tensor", None),
        P(),
        P(None, "tensor"),
        P(None, "tensor"),
        P("tensor", None),
        P("dp", None),
        P("dp", None),
        P(("dp", "tensor"), None),
    )
    return jax.shard_map(
        make_shards(mesh.shape["dp"], mesh.shape["tensor"]),
        mesh=mesh,
        in_specs=placed,
        out_specs=(
            P(("dp", "tensor"), None),
            P(("dp", "tensor"), None),
            P(),
            P(None, "tensor"),
            P(None, "tensor"),
            P(None, "tensor"),
            P(None, "tensor"),
            P(None, "tensor"),
            P(None, "tensor"),
            P(None, "tensor"),
            P(None, "tensor"),
            P(),
            P("tensor", None),
            P(),
            P(None, "tensor"),
            P(None, "tensor"),
            P("tensor", None),
        ),
        check_vma=False,
    )
```

```python
import functools
import jax
import jax.numpy as jnp
from jax import lax
from jax.experimental import pallas as pl
from jax.experimental.pallas import tpu as pltpu
from jax.sharding import PartitionSpec as P

CHUNK = 256
F32, BF16 = jnp.float32, jnp.bfloat16


def mm(a, b, contract=(1, 0)):
    return lax.dot_general(
        a.astype(BF16),
        b.astype(BF16),
        (((contract[0],), (contract[1],)), ((), ())),
        preferred_element_type=F32,
    )


def segment_at(places, starts, lengths, seqs):
    segment = jnp.zeros_like(places)
    for s in range(seqs):
        begin = starts[0, s]
        stop = begin + lengths[0, s]
        segment = segment + jnp.where(places >= begin, 1, 0) + jnp.where(places >= stop, 1, 0)
    return jnp.where(places < 0, -1, segment)


def chunk_masks(starts, lengths, seqs, first, size):
    rows = first + lax.broadcasted_iota(jnp.int32, (size, 1), 0)
    columns = first + lax.broadcasted_iota(jnp.int32, (1, size), 1)
    seg_rows = segment_at(rows, starts, lengths, seqs)
    seg_columns = segment_at(columns, starts, lengths, seqs)
    before = segment_at(jnp.full((1, 1), first - 1, jnp.int32), starts, lengths, seqs)
    last = segment_at(jnp.full((1, 1), first + size - 1, jnp.int32), starts, lengths, seqs)
    return rows, seg_rows, seg_columns, before, last


def inverse_unit_lower(lower, size):
    i = lax.broadcasted_iota(jnp.int32, (size, size), 0)
    j = lax.broadcasted_iota(jnp.int32, (size, size), 1)

    def corner(width):
        shift = width.bit_length() - 1
        pair = (i >> (shift + 1)) == (j >> (shift + 1))
        return pair & (((i >> shift) & 1) == 1) & (((j >> shift) & 1) == 0)

    inverse = jnp.where(i == j, 1.0, 0.0) - jnp.where(corner(1), lower, 0.0)
    width = 2
    while width < size:
        low = inverse.astype(BF16)
        if 2 * width == size:
            part = mm(mm(low[width:, width:], lower[width:, :width]), low[:width, :width])
            inverse = jnp.concatenate(
                [
                    inverse[:width],
                    jnp.concatenate([-part, inverse[width:, width:]], axis=1),
                ],
                axis=0,
            )
        else:
            between = jnp.where(corner(width), lower, 0.0)
            inverse = inverse - mm(mm(low, between), low)
        width *= 2
    return inverse


def sigmoid(v):
    return 1.0 / (1.0 + jnp.exp(-v))


def normed_rows(tokens, gain):
    value = tokens[...].astype(F32)
    unit = value * lax.rsqrt(jnp.mean(value * value, axis=1, keepdims=True) + 1e-6)
    return unit * gain[...].astype(F32).reshape(1, -1), unit


MESH = pl.DeviceIdType.MESH
SUBS = 2
PAIRS = [(sub, way) for sub in range(SUBS) for way in (0, 1)]


def ring_position(device, count):
    half, odd = device // 2, device % 2
    return half + odd * (count - 1 - 2 * half)


def ring_device(position, count):
    back = position // (count // 2)
    return (1 - back) * 2 * position + back * (2 * (count - 1 - position) + 1)


class Ring:
    def __init__(self, count):
        self.count = count
        self.me = lax.axis_index("tensor")
        self.place = ring_position(self.me, count)
        self.group = lax.axis_index("dp")

    def at(self, offset):
        return ring_device((self.place + offset + 2 * self.count) % self.count, self.count)

    def next(self, way):
        return (self.group, self.at(1 if way == 0 else -1))


class Gather:
    def __init__(self, ring, own, view, sends, recvs, rows, subs=SUBS):
        self.ring, self.own, self.view, self.sends, self.recvs, self.rows = ring, own, view, sends, recvs, rows
        self.piece = rows // (2 * subs)
        self.pairs = [(sub, way) for sub in range(subs) for way in (0, 1)]

    def origin(self, way, step):
        return self.ring.at(-step if way == 0 else step)

    def copy(self, way, sub, step, origin, first=False):
        inside = way * (self.rows // 2) + sub * self.piece
        place = self.view(origin, inside, self.piece)
        return pltpu.make_async_remote_copy(
            src_ref=self.own(inside, self.piece) if first else place,
            dst_ref=place,
            send_sem=self.sends.at[way, sub, step],
            recv_sem=self.recvs.at[way, sub, step],
            device_id=self.ring.next(way),
            device_id_type=MESH,
        )

    def begin(self):
        for sub, way in self.pairs:
            self.copy(way, sub, 0, self.ring.me, True).start()

    def arrived(self, step):
        for sub, way in self.pairs:
            self.copy(way, sub, step - 1, self.origin(way, step)).wait_recv()

    def hop(self, step):
        for sub, way in self.pairs:
            self.copy(way, sub, step - 1, self.origin(way, step)).wait_recv()
            self.copy(way, sub, step, self.origin(way, step)).start()

    def end(self):
        def drain(step, carry):
            for sub, way in self.pairs:
                self.copy(way, sub, step, self.ring.me).wait_send()
            return carry

        lax.fori_loop(0, self.ring.count - 1, drain, 0)


def row_view(ref, rows):
    return lambda origin, start, size: ref.at[pl.ds(pl.multiple_of(origin * rows + start, size), size), :]


def row_own(ref):
    return lambda start, size: ref.at[pl.ds(start, size), :]


def ring_gather(gather, between):
    count = gather.ring.count

    def run(step, carry):
        @pl.when(step == 0)
        def _():
            gather.begin()

        @pl.when((step > 0) & (step < count - 1))
        def _():
            gather.hop(step)

        @pl.when(step == count - 1)
        def _():
            gather.arrived(step)

        between(step)
        return carry

    lax.fori_loop(0, count, run, 0)
    gather.end()


def scatter_copy(ring, slots, sends, recvs, way, sub, step):
    return pltpu.make_async_remote_copy(
        src_ref=slots.at[way, sub, step],
        dst_ref=slots.at[way, sub, step + 1],
        send_sem=sends.at[way, sub, step],
        recv_sem=recvs.at[way, sub, step],
        device_id=ring.next(way),
        device_id_type=MESH,
    )


class Scatter:
    def __init__(self, ring, partial, slots, sends, recvs, rows, finish):
        self.ring, self.partial, self.slots, self.sends, self.recvs = ring, partial, slots, sends, recvs
        self.half, self.finish = rows // 2, finish
        self.rows, self.piece = rows, rows // (2 * SUBS)

    def terms(self, step):
        half, first, second = self.half, self.ring.at(-1 - step), self.ring.at(1 + step)
        return self.partial(
            pl.multiple_of(first * self.rows, half), pl.multiple_of(second * self.rows + half, half), step
        )

    def part(self, terms, way, sub):
        start = way * self.half + sub * self.piece
        return terms[start : start + self.piece]

    def copy(self, way, sub, step):
        return scatter_copy(self.ring, self.slots, self.sends, self.recvs, way, sub, step)

    def hop(self, step):
        terms = self.terms(step)
        for sub, way in PAIRS:
            term = self.part(terms, way, sub)

            @pl.when(step == 0)
            def _():
                self.slots[way, sub, 0] = term.astype(BF16)

            @pl.when(step > 0)
            def _():
                self.copy(way, sub, step - 1).wait_recv()
                self.slots[way, sub, step] = (self.slots[way, sub, step].astype(F32) + term).astype(BF16)

            self.copy(way, sub, step).start()

    def end(self):
        count = self.ring.count
        terms = self.terms(count - 1)
        for sub, way in PAIRS:
            self.copy(way, sub, count - 2).wait_recv()
            self.finish(
                way * self.half + sub * self.piece,
                self.piece,
                self.slots[way, sub, count - 1].astype(F32) + self.part(terms, way, sub),
            )

        def drain(step, carry):
            for sub, way in PAIRS:
                self.copy(way, sub, step).wait_send()
            return carry

        lax.fori_loop(0, count - 1, drain, 0)


def ring_scatter(scatter, between):
    def run(step, carry):
        scatter.hop(step)
        between(step)
        return carry

    lax.fori_loop(0, scatter.ring.count - 1, run, 0)
    scatter.end()


class GroupSum:
    def __init__(self, ring, groups, grads, near, far, targets, near_sems, far_sems, back_sems, keep_sems):
        self.ring, self.groups, self.grads, self.near, self.far, self.targets = ring, groups, grads, near, far, targets
        self.near_sems, self.far_sems, self.back_sems, self.keep_sems = near_sems, far_sems, back_sems, keep_sems
        self.core = ring.group % 2
        self.mate = (ring.group + 1 - 2 * self.core, ring.me)

    def peers(self):
        return [self.mate] + [
            ((self.ring.group + 2 * k) % self.groups, self.ring.me) for k in range(1, self.groups // 2)
        ]

    def half(self, i, core):
        rows = self.near[i].shape[0]
        return pl.ds(pl.multiple_of(core * rows, rows), rows)

    def near_copy(self, i):
        return pltpu.make_async_remote_copy(
            src_ref=self.grads[i].at[self.half(i, 1 - self.core), :], dst_ref=self.near[i],
            send_sem=self.near_sems.at[0, i], recv_sem=self.near_sems.at[1, i],
            device_id=self.mate, device_id_type=MESH,
        )

    def far_copy(self, i, k):
        return pltpu.make_async_remote_copy(
            src_ref=self.near[i], dst_ref=self.far[i].at[k - 1],
            send_sem=self.far_sems.at[0, i, k - 1], recv_sem=self.far_sems.at[1, i, k - 1],
            device_id=((self.ring.group + 2 * k) % self.groups, self.ring.me), device_id_type=MESH,
        )

    def back_copy(self, i):
        return pltpu.make_async_remote_copy(
            src_ref=self.far[i].at[0], dst_ref=self.targets[i].at[self.half(i, self.core), :],
            send_sem=self.back_sems.at[0, i], recv_sem=self.back_sems.at[1, i],
            device_id=self.mate, device_id_type=MESH,
        )

    def keep_copy(self, i):
        return pltpu.make_async_copy(
            self.far[i].at[0], self.targets[i].at[self.half(i, self.core), :], self.keep_sems.at[i]
        )

    def first(self, chosen):
        for i in chosen:
            self.near_copy(i).start()

    def each_block(self, i, body):
        rows = self.near[i].shape[0]
        block = next(size for size in (64, 32, 16) if rows % size == 0)

        def step(at, carry):
            start = pl.multiple_of(at * block, block)
            body(pl.ds(start, block), pl.ds(pl.multiple_of(self.core * rows + start, block), block))
            return carry

        lax.fori_loop(0, rows // block, step, 0)

    def second(self, chosen):
        for i in chosen:
            self.near_copy(i).wait_recv()

            def add(here, own, i=i):
                self.near[i][here, :] = (
                    self.near[i][here, :].astype(F32) + self.grads[i][own, :].astype(F32)
                ).astype(BF16)

            self.each_block(i, add)
            for k in range(1, self.groups // 2):
                self.far_copy(i, k).start()

    def third(self, chosen):
        for i in chosen:
            for k in range(1, self.groups // 2):
                self.far_copy(i, k).wait()

            def add(here, own, i=i):
                total = self.near[i][here, :].astype(F32)
                for k in range(self.groups // 2 - 1):
                    total = total + self.far[i][k, here, :].astype(F32)
                self.far[i][0, here, :] = total.astype(BF16)

            self.each_block(i, add)
            self.keep_copy(i).start()
            self.back_copy(i).start()

    def last(self):
        for i in range(len(self.grads)):
            self.near_copy(i).wait_send()
            self.back_copy(i).wait()
            self.keep_copy(i).wait()


def sum_scratch(shapes, groups):
    number = len(shapes)
    return (
        [pltpu.VMEM((rows // 2, columns), BF16) for rows, columns in shapes]
        + [pltpu.VMEM((groups // 2 - 1, rows // 2, columns), BF16) for rows, columns in shapes]
        + [
            pltpu.SemaphoreType.DMA((2, number)),
            pltpu.SemaphoreType.DMA((2, number, groups // 2 - 1)),
            pltpu.SemaphoreType.DMA((2, number)),
            pltpu.SemaphoreType.DMA((number,)),
        ]
    )


def greet(ring, others=()):
    barrier = pltpu.get_barrier_semaphore()
    peers = [ring.next(0), ring.next(1)] + list(others)
    for peer in peers:
        pl.semaphore_signal(barrier, inc=1, device_id=peer, device_id_type=MESH)
    pl.semaphore_wait(barrier, len(peers))


def ring_semaphores(count, subs=SUBS):
    return [pltpu.SemaphoreType.DMA((2, subs, count - 1))] * 2


def ring_slots(count, rows, columns):
    return pltpu.VMEM((2, SUBS, count, rows // (2 * SUBS), columns), BF16)


ANY = pl.BlockSpec(memory_space=pl.ANY)
VMEM = pl.BlockSpec(memory_space=pltpu.VMEM)


def ring_params(number):
    return pltpu.CompilerParams(
        collective_id=number, has_side_effects=True, vmem_limit_bytes=60 << 20
    )


WEIGHT_HOPS = 3


def gather_kernel(
    count, groups, tokens, w_out, tokens_full, w_full,
    sends, recvs, w_sends, w_recvs, local, far_sems, near_sems,
):
    ring = Ring(count)
    rows = tokens.shape[0]
    group, me = ring.group, ring.me
    part = w_out.shape[0] // groups
    across = groups // 2
    mate = (group + 1 - 2 * (group % 2), me)
    gather = Gather(ring, row_own(tokens), row_view(tokens_full, rows), sends, recvs, rows)
    own_part = lambda start, size: w_out.at[pl.ds(pl.multiple_of(group * part + start, size), size), :]
    weights = Gather(
        ring, own_part, lambda origin, start, size: w_full.at[origin, group, pl.ds(start, size), :],
        w_sends, w_recvs, part, 1,
    )
    keep = pltpu.make_async_copy(
        tokens, tokens_full.at[pl.ds(pl.multiple_of(me * rows, rows), rows), :], local.at[0]
    )
    keep_part = pltpu.make_async_copy(own_part(0, part), w_full.at[me, group], local.at[1])

    def far(k):
        return pltpu.make_async_remote_copy(
            src_ref=w_full.at[:, group], dst_ref=w_full.at[:, group],
            send_sem=far_sems.at[0, k - 1], recv_sem=far_sems.at[1, k - 1],
            device_id=((group + 2 * k) % groups, me), device_id_type=MESH,
        )

    def near(k):
        held = (group + groups - 2 * k) % groups
        return pltpu.make_async_remote_copy(
            src_ref=w_full.at[:, held], dst_ref=w_full.at[:, held],
            send_sem=near_sems.at[0, k], recv_sem=near_sems.at[1, k],
            device_id=mate, device_id_type=MESH,
        )

    greet(ring, [mate] + [((group + 2 * k) % groups, me) for k in range(1, across)])
    weights.begin()
    gather.begin()
    keep.start()
    keep_part.start()
    whole_at = -(-(count - 2) // WEIGHT_HOPS) + 1

    def forward(step, carry):
        for place in range(WEIGHT_HOPS):
            number = (step - 1) * WEIGHT_HOPS + place + 1

            @pl.when(number < count - 1)
            def _():
                weights.hop(number)

        gather.hop(step)

        @pl.when(step == whole_at)
        def _():
            weights.arrived(count - 1)
            keep_part.wait()
            for k in range(1, across):
                far(k).start()
            near(0).start()

        return carry

    lax.fori_loop(1, count - 1, forward, 0)
    for k in range(1, across):
        far(k).wait_recv()
        near(k).start()
    gather.arrived(count - 1)
    for k in range(across):
        near(k).wait()
    for k in range(1, across):
        far(k).wait_send()
    weights.end()
    gather.end()
    keep.wait()


def gather_tokens(tokens, w_out, count, groups):
    rows, model = tokens.shape
    part = w_out.shape[0] // groups
    full, w_full = pl.pallas_call(
        functools.partial(gather_kernel, count, groups),
        name="gather_tokens",
        out_shape=[
            jax.ShapeDtypeStruct((count * rows, model), tokens.dtype),
            jax.ShapeDtypeStruct((count, groups, part, model), w_out.dtype),
        ],
        in_specs=[ANY] * 2,
        out_specs=[ANY] * 2,
        scratch_shapes=ring_semaphores(count)
        + ring_semaphores(count, 1)
        + [
            pltpu.SemaphoreType.DMA((2,)),
            pltpu.SemaphoreType.DMA((2, groups // 2 - 1)),
            pltpu.SemaphoreType.DMA((2, groups // 2)),
        ],
        compiler_params=ring_params(1),
        cost_estimate=pl.CostEstimate(flops=0, bytes_accessed=300 << 20, transcendentals=0),
    )(tokens, w_out)
    return full, w_full.reshape(count * w_out.shape[0], model)


def attend_kernel(
    count, mixed, w_out, tokens, gain, w_gate, w_up, w_down, cotangent,
    resid, full, hidden, grad_gate, grad_up, cotangents,
    gathered, out_box, gate_box, up_box, down_box, mixed_boxes, token_boxes, normed, gates, stages,
    sends, recvs, weight_sems, keep_sem, mixed_sems, token_sems, out_sems, normed_sems, stage_sems,
):
    ring = Ring(count)
    rows = cotangent.shape[0]
    half = rows // 2
    gather = Gather(ring, row_own(cotangent), row_view(gathered, rows), sends, recvs, rows)
    keep = pltpu.make_async_copy(
        cotangent, gathered.at[pl.ds(pl.multiple_of(ring.me * rows, rows), rows), :], keep_sem
    )
    loads = [
        pltpu.make_async_copy(source, box, weight_sems.at[k])
        for k, (source, box) in enumerate(
            ((w_out, out_box), (w_gate, gate_box), (w_up, up_box), (w_down, down_box))
        )
    ]

    def place(way, step):
        return pl.ds(pl.multiple_of(gather.origin(way, step) * rows + way * half, half), half)

    def mixed_copy(way, step):
        return pltpu.make_async_copy(
            mixed.at[:, place(way, step), :], mixed_boxes.at[step % 2, way], mixed_sems.at[step % 2, way]
        )

    def token_copy(way, step):
        return pltpu.make_async_copy(
            tokens.at[place(way, step), :], token_boxes.at[step % 2, way], token_sems.at[step % 2, way]
        )

    def out_copy(way, step):
        at = place(way, step)
        return pltpu.make_async_copy(gathered.at[at, :], cotangents.at[at, :], out_sems.at[way, step])

    def normed_copy(way, step):
        return pltpu.make_async_copy(
            normed.at[step % 2, pl.ds(way * half, half), :], full.at[place(way, step), :],
            normed_sems.at[step % 2, way],
        )

    def stage_copy(k, way, step):
        target = (hidden, grad_gate, grad_up)[k]
        return pltpu.make_async_copy(
            stages.at[step % 2, k, way], target.at[place(way, step), :], stage_sems.at[step % 2, k, way]
        )

    def settle(step):
        for way in (0, 1):
            normed_copy(way, step).wait()
            for k in range(3):
                stage_copy(k, way, step).wait()

    def fetch(step):
        for way in (0, 1):
            mixed_copy(way, step).start()
            token_copy(way, step).start()

    def put(k, step, value):
        low = value.astype(BF16)
        for way in (0, 1):
            stages[step % 2, k, way] = low[way * half : way * half + half]
            stage_copy(k, way, step).start()

    def prepare(step):
        @pl.when(step > 1)
        def _():
            settle(step - 2)

        slot = step % 2
        for way in (0, 1):
            mixed_copy(way, step).wait()
            token_copy(way, step).wait()

        @pl.when(step + 1 < count)
        def _():
            fetch(step + 1)

        heads = jnp.concatenate(
            [
                jnp.concatenate([mixed_boxes[slot, way, j] for j in range(count)], 1)
                for way in (0, 1)
            ],
            0,
        )
        value = jnp.concatenate([token_boxes[slot, 0], token_boxes[slot, 1]], 0).astype(F32)
        value = value + mm(heads, out_box[...])

        @pl.when(step == 0)
        def _():
            resid[...] = value

        scale = lax.rsqrt(jnp.mean(value * value, axis=1, keepdims=True) + 1e-6)
        normed[slot] = (value * scale * gain[...].astype(F32).reshape(1, -1)).astype(BF16)
        for way in (0, 1):
            normed_copy(way, step).start()
        inputs = normed[slot]
        gate = mm(inputs, gate_box[...], (1, 1))
        up = mm(inputs, up_box[...], (1, 1))
        sig = sigmoid(gate)
        opened = gate * sig
        put(0, step, opened * up)
        gates[0] = up * sig * (1.0 + gate * (1.0 - sig))
        gates[1] = opened

    def feed(step):
        for way in (0, 1):
            out_copy(way, step).start()
        grad = mm(
            jnp.concatenate([gathered[place(0, step), :], gathered[place(1, step), :]], 0), down_box[...], (1, 1)
        )
        put(1, step, grad * gates[0])
        put(2, step, grad * gates[1])

    def run(step, carry):
        @pl.when(step == 0)
        def _():
            gather.begin()
            for load in loads:
                load.wait()

        prepare(step)

        @pl.when(step == 0)
        def _():
            keep.wait()

        @pl.when((step > 0) & (step < count - 1))
        def _():
            gather.hop(step)

        @pl.when(step == count - 1)
        def _():
            gather.arrived(step)

        feed(step)
        return carry

    keep.start()
    fetch(0)
    for load in loads:
        load.start()
    greet(ring)
    lax.fori_loop(0, count, run, 0)
    gather.end()
    settle(count - 2)
    settle(count - 1)

    def drain(step, carry):
        for way in (0, 1):
            out_copy(way, step).wait()
        return carry

    lax.fori_loop(0, count, drain, 0)


def attend(mixed, w_out, tokens, gain, w_gate, w_up, w_down, cotangent, count):
    rows, model = cotangent.shape
    slots, inner = count * rows, w_down.shape[0]
    wide = mixed.shape[2]
    return pl.pallas_call(
        functools.partial(attend_kernel, count),
        name="attend",
        out_shape=[
            jax.ShapeDtypeStruct((rows, model), F32),
            jax.ShapeDtypeStruct((slots, model), BF16),
        ]
        + [jax.ShapeDtypeStruct((slots, inner), BF16)] * 3
        + [jax.ShapeDtypeStruct((slots, model), BF16)],
        in_specs=[ANY] * 3 + [VMEM] + [ANY] * 4,
        out_specs=[VMEM] + [ANY] * 5,
        scratch_shapes=[pltpu.VMEM((slots, model), BF16), pltpu.VMEM(w_out.shape, BF16)]
        + [pltpu.VMEM((inner, model), BF16)] * 3
        + [
            pltpu.VMEM((2, 2, count, rows // 2, wide), BF16),
            pltpu.VMEM((2, 2, rows // 2, model), BF16),
            pltpu.VMEM((2, rows, model), BF16),
            pltpu.VMEM((2, rows, inner), F32),
            pltpu.VMEM((2, 3, 2, rows // 2, inner), BF16),
        ]
        + ring_semaphores(count)
        + [
            pltpu.SemaphoreType.DMA((4,)),
            pltpu.SemaphoreType.DMA,
            pltpu.SemaphoreType.DMA((2, 2)),
            pltpu.SemaphoreType.DMA((2, 2)),
            pltpu.SemaphoreType.DMA((2, count)),
            pltpu.SemaphoreType.DMA((2, 2)),
            pltpu.SemaphoreType.DMA((2, 3, 2)),
        ],
        compiler_params=ring_params(2),
        cost_estimate=pl.CostEstimate(
            flops=2 * slots * model * model + 6 * slots * model * inner, bytes_accessed=300 << 20,
            transcendentals=slots * inner,
        ),
    )(mixed, w_out, tokens, gain, w_gate, w_up, w_down, cotangent)


def norm_back(inputs, scale, gain, grad_normed):
    weighted = gain * grad_normed
    inner = jnp.mean(weighted * inputs, axis=1, keepdims=True)
    unit = inputs * scale
    return scale * weighted - unit * (scale * scale * inner), grad_normed * unit


JOBS = 8


def ffn_back_kernel(
    count, groups, rows, grad_gate, grad_up, hidden_in, w_gate, w_up, resid_in, cotangent_in, gain, inputs, cotangents,
    grad_resid, full, grad_gain, sum_gate, sum_up, sum_down,
    slots, low, gw_gate, gw_up, gw_down, boxes, box_sems, hidden, resid, cotangent, load_sems, *rest,
):
    ring = Ring(count)
    sends, recvs, sends_two, recvs_two, local = rest[:5]
    sums = GroupSum(
        ring, groups, (gw_gate, gw_up, gw_down), rest[5:8], rest[8:11], (sum_gate, sum_up, sum_down), *rest[11:]
    )
    wide = boxes.shape[2]

    def box_copy(job, source):
        at = pl.multiple_of(job % (JOBS // 2) * wide, wide)
        return pltpu.make_async_copy(
            source.at[:, pl.ds(at, wide)], boxes.at[job % 2], box_sems.at[job % 2]
        )

    def fetch(job):
        @pl.when(job < JOBS // 2)
        def _():
            box_copy(job, inputs).start()

        @pl.when(job >= JOBS // 2)
        def _():
            box_copy(job, cotangents).start()

    loads = [
        pltpu.make_async_copy(source, target, load_sems.at[k])
        for k, (source, target) in enumerate(((hidden_in, hidden), (resid_in, resid), (cotangent_in, cotangent)))
    ]
    fetch(0)
    for load in loads:
        load.start()
    greet(ring, sums.peers())
    grad_gain[...] = jnp.zeros_like(grad_gain)
    half = rows // 2

    def partial(first, second, step):
        gates = jnp.concatenate([grad_gate[pl.ds(first, half), :], grad_gate[pl.ds(second, half), :]], 0)
        ups = jnp.concatenate([grad_up[pl.ds(first, half), :], grad_up[pl.ds(second, half), :]], 0)
        return mm(gates, w_gate[...]) + mm(ups, w_up[...])

    def finish(start, size, grad):
        value = resid[start : start + size, :]
        scale = lax.rsqrt(jnp.mean(value * value, axis=1, keepdims=True) + 1e-6)
        through, pieces = norm_back(value, scale, gain[...].astype(F32).reshape(1, -1), grad)
        result = cotangent[start : start + size, :].astype(F32) + through
        grad_resid[start : start + size, :] = result
        grad_gain[...] += jnp.sum(pieces, axis=0, keepdims=True)
        low[start : start + size, :] = result.astype(BF16)

    def work(job, carry):
        box_copy(job, inputs).wait()

        @pl.when(job + 1 < JOBS)
        def _():
            fetch(job + 1)

        at = pl.ds(pl.multiple_of(job % (JOBS // 2) * wide, wide), wide)

        @pl.when(job < JOBS // 2)
        def _():
            box = boxes[job % 2]
            gw_gate[:, at] = mm(grad_gate[...], box, (0, 0)).astype(BF16)
            gw_up[:, at] = mm(grad_up[...], box, (0, 0)).astype(BF16)

        @pl.when(job >= JOBS // 2)
        def _():
            gw_down[:, at] = mm(hidden[...], boxes[job % 2], (0, 0)).astype(BF16)

        return carry

    each = JOBS // 4

    def beside_scatter(step):
        @pl.when(step == 2)
        def _():
            for load in loads:
                load.wait()

        @pl.when(step == 3)
        def _():
            sums.second((0, 1))

        @pl.when(step < 4)
        def _():
            lax.fori_loop(step * each, step * each + each, work, 0)

        @pl.when(step == 1)
        def _():
            sums.first((0, 1))

        @pl.when(step == 3)
        def _():
            sums.first((2,))

        @pl.when(step == 5)
        def _():
            sums.second((2,))

    def beside_gather(step):
        @pl.when(step == count - 3)
        def _():
            sums.third((0, 1))

        @pl.when(step == count - 2)
        def _():
            sums.third((2,))

    ring_scatter(Scatter(ring, partial, slots, sends, recvs, rows, finish), beside_scatter)
    keep = pltpu.make_async_copy(low, full.at[pl.ds(pl.multiple_of(ring.me * rows, rows), rows), :], local)
    keep.start()
    ring_gather(Gather(ring, row_own(low), row_view(full, rows), sends_two, recvs_two, rows), beside_gather)
    keep.wait()
    sums.last()


def ffn_back(grad_gate, grad_up, hidden, w_gate, w_up, resid, cotangent, gain, inputs, cotangents, count, groups):
    rows, model = resid.shape
    slots, inner = grad_up.shape
    shapes = [(inner, model)] * 3
    return pl.pallas_call(
        functools.partial(ffn_back_kernel, count, groups, rows),
        name="ffn_back",
        out_shape=[
            jax.ShapeDtypeStruct((rows, model), F32),
            jax.ShapeDtypeStruct((slots, model), BF16),
            jax.ShapeDtypeStruct((1, model), F32),
        ]
        + [jax.ShapeDtypeStruct(shape, BF16) for shape in shapes],
        in_specs=[VMEM] * 2 + [ANY] + [VMEM] * 2 + [ANY] * 2 + [VMEM] + [ANY] * 2,
        out_specs=[VMEM, ANY, VMEM] + [ANY] * 3,
        scratch_shapes=[ring_slots(count, rows, model), pltpu.VMEM((rows, model), BF16)]
        + [pltpu.VMEM(shape, BF16) for shape in shapes]
        + [pltpu.VMEM((2, slots, model // (JOBS // 2)), BF16), pltpu.SemaphoreType.DMA((2,))]
        + [pltpu.VMEM((slots, inner), BF16), pltpu.VMEM((rows, model), F32), pltpu.VMEM((rows, model), BF16)]
        + [pltpu.SemaphoreType.DMA((3,))]
        + ring_semaphores(count) * 2
        + [pltpu.SemaphoreType.DMA]
        + sum_scratch(shapes, groups),
        compiler_params=ring_params(3),
        cost_estimate=pl.CostEstimate(
            flops=10 * slots * model * inner, bytes_accessed=600 << 20, transcendentals=0
        ),
    )(grad_gate, grad_up, hidden, w_gate, w_up, resid, cotangent, gain, inputs, cotangents)


def last_kernel(
    count, groups, rows, terms, tokens_in, grad_resid_in, gain, small, *rest,
):
    grads, rest = rest[:5], rest[5:]
    grad_tokens, total = rest[:2]
    targets, rest = rest[2:7], rest[7:]
    slots, first_box, second_box, second_own, boxes, box_sems, tokens, grad_resid, load_sems = rest[:9]
    sends, recvs, first_sends, first_recvs, second_sends, second_recvs = rest[9:15]
    ring = Ring(count)
    sums = GroupSum(ring, groups, grads, rest[15:20], rest[20:25], targets, *rest[25:])
    loads = [
        pltpu.make_async_copy(tokens_in, tokens, load_sems.at[0]),
        pltpu.make_async_copy(grad_resid_in, grad_resid, load_sems.at[1]),
    ]
    me, group = ring.me, ring.group
    first_peers = [(group, (me + k) % count) for k in range(1, count)]
    second_peers = [((group + k) % groups, me) for k in range(1, groups)]
    barrier = pltpu.get_barrier_semaphore()
    for peer in first_peers + second_peers:
        pl.semaphore_signal(barrier, inc=1, device_id=peer, device_id_type=MESH)
    pl.semaphore_wait(barrier, count + groups - 2)

    def first(k):
        return pltpu.make_async_remote_copy(
            src_ref=small.at[0:8], dst_ref=first_box.at[k], send_sem=first_sends.at[k],
            recv_sem=first_recvs.at[k], device_id=first_peers[k], device_id_type=MESH,
        )

    def second(k):
        return pltpu.make_async_remote_copy(
            src_ref=second_own, dst_ref=second_box.at[k], send_sem=second_sends.at[k],
            recv_sem=second_recvs.at[k], device_id=second_peers[k], device_id_type=MESH,
        )

    every = range(len(grads))
    sums.first(every)
    for k in range(count - 1):
        first(k).start()
    half = rows // 2

    def box_copy(way, start, slot):
        return pltpu.make_async_copy(
            terms.at[pl.ds(start, half), :], boxes.at[slot, way], box_sems.at[slot, way]
        )

    def fetch(step):
        for way, owner in ((0, ring.at(-1 - step)), (1, ring.at(1 + step))):
            box_copy(way, pl.multiple_of(owner * rows + way * half, half), step % 2).start()

    def partial(first, second, step):
        for way, start in ((0, first), (1, second)):
            box_copy(way, start, step % 2).wait()

        @pl.when(step + 1 < count)
        def _():
            fetch(step + 1)

        return jnp.concatenate([boxes[step % 2, 0], boxes[step % 2, 1]], 0).astype(F32)

    def finish(start, size, grad):
        value = tokens[start : start + size, :].astype(F32)
        scale = lax.rsqrt(jnp.mean(value * value, axis=1, keepdims=True) + 1e-6)
        through, pieces = norm_back(value, scale, gain[...].astype(F32).reshape(1, -1), grad)
        grad_tokens[start : start + size, :] = grad_resid[start : start + size, :] + through

    def early():
        sums.second(every)
        for k in range(count - 1):
            first(k).wait()
        mine = small[0:8]
        for k in range(count - 1):
            mine = mine + first_box[k]
        second_own[0:8] = mine
        second_own[8:] = small[8:]
        for k in range(groups - 1):
            second(k).start()

    def late():
        for k in range(groups - 1):
            second(k).wait()
        mine = second_own[...]
        for k in range(groups - 1):
            mine = mine + second_box[k]
        total[...] = mine
        for load in loads:
            load.wait()

    def beside(step):
        pl.when(step == 0)(early)
        for i in every:
            pl.when(step == count - 1 - len(every) + i)(lambda i=i: sums.third((i,)))
        pl.when(step == count - 2)(late)

    fetch(0)
    for load in loads:
        load.start()
    ring_scatter(Scatter(ring, partial, slots, sends, recvs, rows, finish), beside)
    sums.last()


def last_step(terms, tokens, grad_resid, gain, small, grads, count, groups):
    rows, model = tokens.shape
    return pl.pallas_call(
        functools.partial(last_kernel, count, groups, rows),
        name="last_step",
        out_shape=[jax.ShapeDtypeStruct((rows, model), F32), jax.ShapeDtypeStruct(small.shape, F32)]
        + [jax.ShapeDtypeStruct(g.shape, BF16) for g in grads],
        in_specs=[ANY] * 3 + [VMEM] * (2 + len(grads)),
        out_specs=[VMEM, VMEM] + [ANY] * len(grads),
        scratch_shapes=[
            ring_slots(count, rows, model),
            pltpu.VMEM((count - 1, 8, model), F32),
            pltpu.VMEM((groups - 1,) + small.shape, F32),
            pltpu.VMEM(small.shape, F32),
            pltpu.VMEM((2, 2, rows // 2, model), BF16),
            pltpu.SemaphoreType.DMA((2, 2)),
            pltpu.VMEM((rows, model), BF16),
            pltpu.VMEM((rows, model), F32),
            pltpu.SemaphoreType.DMA((2,)),
        ]
        + ring_semaphores(count)
        + [pltpu.SemaphoreType.DMA((count - 1,))] * 2
        + [pltpu.SemaphoreType.DMA((groups - 1,))] * 2
        + sum_scratch([g.shape for g in grads], groups),
        compiler_params=ring_params(4),
        cost_estimate=pl.CostEstimate(flops=0, bytes_accessed=300 << 20, transcendentals=0),
    )(terms, tokens, grad_resid, gain, small, *grads)


def results_kernel(heads, taps, wide, width, total, *refs):
    number = (len(refs) - 7) // 2
    for source, target in zip(refs[:number], refs[number : 2 * number]):
        target[...] = source[...].astype(target.dtype)
    g_first, g_second, g_head, gt_query, gt_key, gt_value, g_beta = refs[2 * number :]

    @pl.when(pl.program_id(0) == 0)
    def _():
        g_first[...] = total[0:1, :]
        g_second[...] = total[1:2, :]
        g_head[...] = total[2:3, 0:width]
        row = 8 + heads
        for place, target in enumerate((gt_query, gt_key, gt_value)):
            target[...] = total[row : row + taps, place * wide : (place + 1) * wide]
        g_beta[...] = total[8 : 8 + heads, :]


def results(total, arrays, heads, taps, wide, width):
    model = total.shape[1]
    steps = next(n for n in (2, 1) if all(a.shape[0] % (8 * n) == 0 for a, _ in arrays))
    small = [(1, model), (1, model), (1, width)] + [(taps, wide)] * 3 + [(heads, model)]
    piece = lambda a: pl.BlockSpec((a.shape[0] // steps, a.shape[1]), lambda n: (n, 0))
    whole = lambda shape: pl.BlockSpec(shape, lambda n: (0, 0))
    return pl.pallas_call(
        functools.partial(results_kernel, heads, taps, wide, width),
        name="results",
        grid=(steps,),
        out_shape=[jax.ShapeDtypeStruct(a.shape, kind) for a, kind in arrays]
        + [jax.ShapeDtypeStruct(shape, F32) for shape in small],
        in_specs=[whole(total.shape)] + [piece(a) for a, _ in arrays],
        out_specs=[piece(a) for a, _ in arrays] + [whole(shape) for shape in small],
        compiler_params=pltpu.CompilerParams(vmem_limit_bytes=56 << 20),
        cost_estimate=pl.CostEstimate(flops=0, bytes_accessed=48 << 20, transcendentals=0),
    )(total, *[a for a, _ in arrays])


def spread_hops(step, chunks, count, hop, start=0):
    each = -(-(count - 1) // (chunks - 1))
    for place in range(each):
        number = step * each + place

        @pl.when((number >= start) & (number < count - 1))
        def _():
            hop(number)


def forward_kernel(
    heads, width, seqs, count, chunks,
    starts, lengths, tokens, w_query, w_key, w_value, w_gate, w_beta,
    taps_query, taps_key, taps_value, gain, gain_first,
    mixed_full, mixed, p_query, p_key, p_value, p_gate, p_beta, z_query, z_key, z_value,
    delta_out, change_out, inverse_out, state_out,
    tail_query, tail_key, tail_value, state, stage, sends, recvs, keeps,
):
    step = pl.program_id(0)
    size = tokens.shape[0]
    first = step * size

    @pl.when(step == 0)
    def _():
        for tail in (tail_query, tail_key, tail_value):
            tail[...] = jnp.zeros_like(tail)
        state[...] = jnp.zeros_like(state)

    ring = Ring(count)

    def chunk_gather(chunk):
        return Gather(
            ring,
            lambda start, length: stage.at[chunk, pl.ds(start, length), :],
            lambda origin, start, length: mixed_full.at[
                origin, pl.ds(pl.multiple_of(chunk * size + start, length), length), :
            ],
            sends.at[chunk], recvs.at[chunk], size, 1,
        )

    def keep(chunk):
        return pltpu.make_async_copy(
            stage.at[chunk],
            mixed_full.at[ring.me, pl.ds(pl.multiple_of(chunk * size, size), size), :],
            keeps.at[chunk],
        )

    def turn(late):
        for age in range(1, count // 2 + 1):
            number = 2 * age - 1 + late
            if number < count - 1:
                pl.when(step >= age)(lambda age=age, number=number: chunk_gather(step - age).hop(number))

    pl.when(step == 0)(lambda: greet(ring))
    turn(0)
    rows, seg_rows, seg_columns, before, last = chunk_masks(starts, lengths, seqs, first, size)
    same = seg_rows == seg_columns
    i = lax.broadcasted_iota(jnp.int32, (size, size), 0)
    j = lax.broadcasted_iota(jnp.int32, (size, size), 1)
    strict = jnp.where(same & (i > j), 1.0, 0.0)
    inclusive = jnp.where(same & (i >= j), 1.0, 0.0)
    carried = jnp.where(seg_rows == before, 1.0, 0.0)
    ending = jnp.where(seg_rows == last, 1.0, 0.0)
    kept = jnp.where(before == last, 1.0, 0.0)
    live = jnp.where(seg_rows % 2 == 1, 1.0, 0.0)
    joined = [
        jnp.where(segment_at(rows - offset, starts, lengths, seqs) == seg_rows, 1.0, 0.0)
        for offset in range(1, taps_query.shape[0])
    ]
    inputs = normed_rows(tokens, gain_first)[0].astype(BF16)

    def feature(weight, taps, tail, p_out, z_out):
        projected = jnp.dot(inputs, weight[...], preferred_element_type=F32)
        p_out[...] = projected
        tail[8:, :] = projected
        tap = taps[...].astype(F32)
        result = projected * tap[0:1]
        for offset in range(1, tap.shape[0]):
            result = result + tail[8 - offset : 8 - offset + size, :] * tap[offset : offset + 1] * joined[offset - 1]
        tail[0:8, :] = projected[size - 8 :, :]
        z_out[...] = result
        return result * sigmoid(result)

    u_query = feature(w_query, taps_query, tail_query, p_query, z_query)
    u_key = feature(w_key, taps_key, tail_key, p_key, z_key)
    u_value = feature(w_value, taps_value, tail_value, p_value, z_value)
    gate = jnp.dot(inputs, w_gate[...], preferred_element_type=F32)
    p_gate[...] = gate
    beta_pre = mm(inputs, w_beta[...], (1, 1))
    p_beta[...] = beta_pre
    strength = sigmoid(beta_pre)
    opened = gate * sigmoid(gate)
    scale = width ** (-0.5)
    head_gain = gain[...].astype(F32)
    for h in range(heads):
        if h == heads // 2:
            turn(1)
        cols = slice(h * width, (h + 1) * width)
        uq, uk = u_query[:, cols], u_key[:, cols]
        query = (uq * lax.rsqrt(jnp.sum(uq * uq, axis=1, keepdims=True) + 1e-6)).astype(BF16)
        key = (uk * lax.rsqrt(jnp.sum(uk * uk, axis=1, keepdims=True) + 1e-6)).astype(BF16)
        value = u_value[:, cols].astype(BF16).astype(F32)
        beta = strength[:, h : h + 1]
        memory = state[h]
        low_memory = memory.astype(BF16)
        state_out[0, h] = low_memory
        lower = mm(key, key, (1, 1)) * strict * beta
        inverse = inverse_unit_lower(lower, size).astype(BF16)
        inverse_out[0, h] = inverse
        within = mm(query, key, (1, 1)) * inclusive
        change = mm(inverse, beta * (value - carried * mm(key, low_memory)))
        low_change = change.astype(BF16)
        change_out[:, cols] = low_change
        out = scale * (carried * mm(query, low_memory) + mm(within, low_change))
        state[h] = kept * memory + mm(key, ending * change, (0, 0))
        delta_out[:, cols] = out
        normal = out * lax.rsqrt(jnp.mean(out * out, axis=1, keepdims=True) + 1e-5) * head_gain
        low_mixed = (normal * opened[:, cols] * live).astype(BF16)
        mixed[:, cols] = low_mixed
        stage[step, :, cols] = low_mixed

    chunk_gather(step).begin()
    keep(step).start()

    @pl.when(step == chunks - 1)
    def _():
        def finish(number, carry):
            for age in range(min(chunks, count // 2)):
                pl.when(2 * age + number < count - 1)(
                    lambda age=age: chunk_gather(chunks - 1 - age).hop(2 * age + number)
                )
            return carry

        lax.fori_loop(1, count - 1, finish, 0)

        def settle(chunk, carry):
            chunk_gather(chunk).arrived(count - 1)
            chunk_gather(chunk).end()
            keep(chunk).wait()
            return carry

        lax.fori_loop(0, chunks, settle, 0)


def forward_mixer(tokens, w_query, w_key, w_value, w_gate, w_beta, taps_query, taps_key, taps_value, gain, gain_first, starts, lengths, count):
    slots, model = tokens.shape
    wide = w_query.shape[1]
    width = gain.shape[0]
    heads = wide // width
    seqs = starts.shape[1]
    chunks = slots // CHUNK
    taps = taps_query.shape[0]
    smem = pl.BlockSpec(memory_space=pltpu.SMEM)
    whole = lambda shape: pl.BlockSpec(shape, lambda n: (0,) * len(shape))
    piece = lambda shape: pl.BlockSpec(shape, lambda n: (n,) + (0,) * (len(shape) - 1))
    outs = [
        ((slots, wide), BF16), ((slots, wide), F32), ((slots, wide), F32), ((slots, wide), F32), ((slots, wide), F32),
        ((slots, w_beta.shape[0]), F32), ((slots, wide), F32), ((slots, wide), F32), ((slots, wide), F32),
        ((slots, wide), F32), ((slots, wide), BF16),
    ]
    return pl.pallas_call(
        functools.partial(forward_kernel, heads, width, seqs, count, chunks),
        name="mixer_forward",
        grid=(chunks,),
        out_shape=[jax.ShapeDtypeStruct((count, slots, wide), BF16)]
        + [jax.ShapeDtypeStruct(s, d) for s, d in outs]
        + [
            jax.ShapeDtypeStruct((chunks, heads, CHUNK, CHUNK), BF16),
            jax.ShapeDtypeStruct((chunks, heads, width, width), BF16),
        ],
        in_specs=[smem, smem, piece((CHUNK, model))]
        + [whole((model, wide))] * 4
        + [whole(w_beta.shape)]
        + [whole((taps, wide))] * 3
        + [whole((1, width)), VMEM],
        out_specs=[ANY]
        + [piece((CHUNK, s[1])) for s, d in outs]
        + [piece((1, heads, CHUNK, CHUNK)), piece((1, heads, width, width))],
        scratch_shapes=[pltpu.VMEM((CHUNK + 8, wide), F32)] * 3
        + [pltpu.VMEM((heads, width, width), F32), pltpu.VMEM((chunks, CHUNK, wide), BF16)]
        + [pltpu.SemaphoreType.DMA((chunks, 2, 1, count - 1))] * 2
        + [pltpu.SemaphoreType.DMA((chunks,))],
        compiler_params=ring_params(5),
        cost_estimate=pl.CostEstimate(
            flops=2 * slots * model * wide * 4 + slots * heads * CHUNK * 2 * CHUNK * 20,
            bytes_accessed=slots * model * 2 + 4 * model * wide * 2 + slots * wide * 36,
            transcendentals=slots * wide * 4,
        ),
    )(starts, lengths, tokens, w_query, w_key, w_value, w_gate, w_beta, taps_query, taps_key, taps_value, gain.reshape(1, width), gain_first)


def small_rows(heads, taps):
    return -(-(8 + heads + taps) // 8) * 8


def backward_kernel(
    heads, width, seqs, chunks, count, rows_own,
    starts, lengths, tokens, grad_attended, mixed, p_query, p_key, p_value, p_gate, p_beta,
    z_query, z_key, z_value, delta_out, change_in, inverse_in, state_in,
    w_query_in, w_key_in, w_value_in, w_gate_in, w_beta, w_out, taps_query, taps_key, taps_value, gain, gain_first,
    hidden, w_down, resid_in, g_second, grad_normed, gw_query, gw_key, gw_value, gw_gate, gw_out,
    small, output,
    a_query, a_key, a_value, a_gate, a_out, head_query, head_key, head_value, flow,
    w_query, w_key, w_value, w_gate, resid, load_sems, slots, sends, recvs,
):
    step = pl.program_id(0)
    size = tokens.shape[0]
    first = (chunks - 1 - step) * size

    @pl.when(step == 0)
    def _():
        for ref in (a_query, a_key, a_value, a_gate, a_out, small, flow):
            ref[...] = jnp.zeros_like(ref)
        small[1:2, :] = g_second[...]
        for ref in (head_query, head_key, head_value):
            ref[size:, :] = jnp.zeros((8, ref.shape[1]), F32)

    half = rows_own // 2

    def partial(one, two, number):
        return mm(jnp.concatenate([hidden[pl.ds(one, half), :], hidden[pl.ds(two, half), :]], 0), w_down[...])

    def finish(start, length, down):
        output[start : start + length, :] = (resid[start : start + length, :] + down).astype(BF16)

    ring = Ring(count)
    scatter = Scatter(ring, partial, slots, sends, recvs, rows_own, finish)
    loads = [
        pltpu.make_async_copy(source, target, load_sems.at[k])
        for k, (source, target) in enumerate(
            ((w_query_in, w_query), (w_key_in, w_key), (w_value_in, w_value), (w_gate_in, w_gate), (resid_in, resid))
        )
    ]

    @pl.when(step == 0)
    def _():
        for load in loads:
            load.start()
        greet(ring)

    spread_hops(step, chunks, count, scatter.hop)
    rows, seg_rows, seg_columns, before, last = chunk_masks(starts, lengths, seqs, first, size)
    same = seg_rows == seg_columns
    i = lax.broadcasted_iota(jnp.int32, (size, size), 0)
    j = lax.broadcasted_iota(jnp.int32, (size, size), 1)
    strict = jnp.where(same & (i > j), 1.0, 0.0)
    inclusive = jnp.where(same & (i >= j), 1.0, 0.0)
    carried = jnp.where(seg_rows == before, 1.0, 0.0)
    ending = jnp.where(seg_rows == last, 1.0, 0.0)
    kept = jnp.where(before == last, 1.0, 0.0)
    live = jnp.where(seg_rows % 2 == 1, 1.0, 0.0)
    taps = taps_query.shape[0]
    joined = [
        jnp.where(segment_at(rows + offset, starts, lengths, seqs) == seg_rows, 1.0, 0.0)
        for offset in range(1, taps)
    ]
    normal_rows, unit_rows = normed_rows(tokens, gain_first)
    inputs = normal_rows.astype(BF16)
    grad_rows = grad_attended[...]
    grad_mixed = mm(grad_rows, w_out[...], (1, 1))
    a_out[...] += mm(mixed[...], grad_rows, (0, 0))
    strength = sigmoid(p_beta[...])
    scale = width ** (-0.5)
    head_gain = gain[...].astype(F32)

    grads_query, grads_key, grads_value, grads_gate, grads_beta = [], [], [], [], []
    for h in range(heads):
        cols = slice(h * width, (h + 1) * width)
        out = delta_out[:, cols]
        gate = p_gate[:, cols]
        sig_gate = sigmoid(gate)
        silu_gate = gate * sig_gate
        root = lax.rsqrt(jnp.mean(out * out, axis=1, keepdims=True) + 1e-5)
        grad = grad_mixed[:, cols] * live
        unit = out * root
        grads_gate.append(grad * unit * head_gain * (sig_gate * (1.0 + gate * (1.0 - sig_gate))))
        grad_normal = grad * silu_gate
        small[2:3, 0:width] += jnp.sum(grad_normal * unit, axis=0, keepdims=True)
        push = grad_normal * head_gain
        grad_out = scale * root * (push - unit * jnp.mean(push * unit, axis=1, keepdims=True))

        zq, zk, zv = z_query[:, cols], z_key[:, cols], z_value[:, cols]
        sq, sk, sv = sigmoid(zq), sigmoid(zk), sigmoid(zv)
        uq, uk = zq * sq, zk * sk
        nq = lax.rsqrt(jnp.sum(uq * uq, axis=1, keepdims=True) + 1e-6)
        nk = lax.rsqrt(jnp.sum(uk * uk, axis=1, keepdims=True) + 1e-6)
        unit_q, unit_k = uq * nq, uk * nk
        query, key = unit_q.astype(BF16), unit_k.astype(BF16)
        beta = strength[:, h : h + 1]
        change = change_in[:, cols]
        inverse = inverse_in[0, h]
        memory = state_in[0, h]
        flowing = flow[h]
        low_flow = flowing.astype(BF16)
        low_out = grad_out.astype(BF16)

        within = mm(query, key, (1, 1)) * inclusive
        grad_within = (mm(low_out, change, (1, 1)) * inclusive).astype(BF16)
        grad_change = mm(within, low_out, (0, 0)) + ending * mm(key, low_flow)
        grad_mid = mm(inverse, grad_change, (0, 0))
        grad_value = beta * grad_mid
        low_value = grad_value.astype(BF16)
        cross = (mm(low_value, change, (1, 1)) * strict).astype(BF16)
        grad_query = carried * mm(low_out, memory, (1, 1)) + mm(grad_within, key)
        grad_key = (
            mm(grad_within, query, (0, 0))
            + ending * mm(change, low_flow, (1, 1))
            - carried * mm(low_value, memory, (1, 1))
            - mm(cross, key)
            - mm(cross, key, (0, 0))
        )
        flow[h] = (
            kept * flowing
            + mm(query, carried * grad_out, (0, 0))
            - mm(key, carried * grad_value, (0, 0))
        )
        grads_beta.append((1.0 - beta) * jnp.sum(grad_mid * change.astype(F32), axis=1, keepdims=True))
        du_q = nq * (grad_query - unit_q * jnp.sum(grad_query * unit_q, axis=1, keepdims=True))
        du_k = nk * (grad_key - unit_k * jnp.sum(grad_key * unit_k, axis=1, keepdims=True))
        grads_query.append(du_q * sq * (1.0 + zq * (1.0 - sq)))
        grads_key.append(du_k * sk * (1.0 + zk * (1.0 - sk)))
        grads_value.append(grad_value * sv * (1.0 + zv * (1.0 - sv)))

    tap_row = 8 + heads
    wide = heads * width

    def unconv(parts, taps_ref, head, projected, place):
        lanes = slice(place * wide, (place + 1) * wide)
        grad = jnp.concatenate(parts, axis=1)
        head[0:size, :] = grad
        tap = taps_ref[...].astype(F32)
        p = projected[...]
        result = grad * tap[0:1]
        small[tap_row : tap_row + 1, lanes] += jnp.sum(p * grad, axis=0, keepdims=True)
        for offset in range(1, taps):
            moved = head[offset : offset + size, :] * joined[offset - 1]
            result = result + moved * tap[offset : offset + 1]
            row = tap_row + offset
            small[row : row + 1, lanes] += jnp.sum(p * moved, axis=0, keepdims=True)
        head[size:, :] = grad[0:8, :]
        return result.astype(BF16)

    d_query = unconv(grads_query, taps_query, head_query, p_query, 0)
    d_key = unconv(grads_key, taps_key, head_key, p_key, 1)
    d_value = unconv(grads_value, taps_value, head_value, p_value, 2)
    d_gate = jnp.concatenate(grads_gate, axis=1).astype(BF16)
    spare = [jnp.zeros((size, 1), F32)] * (w_beta.shape[0] - heads)
    d_beta = jnp.concatenate(grads_beta + spare, axis=1).astype(BF16)

    @pl.when(step == 0)
    def _():
        for load in loads:
            load.wait()

    grad_inputs = (
        mm(d_query, w_query[...], (1, 1))
        + mm(d_key, w_key[...], (1, 1))
        + mm(d_value, w_value[...], (1, 1))
        + mm(d_gate, w_gate[...], (1, 1))
        + mm(d_beta, w_beta[...])
    )
    grad_normed[...] = grad_inputs.astype(BF16)
    small[0:1, :] += jnp.sum(grad_inputs * unit_rows, axis=0, keepdims=True)
    a_query[...] += mm(inputs, d_query, (0, 0))
    a_key[...] += mm(inputs, d_key, (0, 0))
    a_value[...] += mm(inputs, d_value, (0, 0))
    a_gate[...] += mm(inputs, d_gate, (0, 0))
    small[8 : 8 + heads, :] += mm(d_beta, inputs, (0, 0))[:heads]

    @pl.when(step == chunks - 1)
    def _():
        for target, source in (
            (gw_query, a_query), (gw_key, a_key), (gw_value, a_value), (gw_gate, a_gate),
            (gw_out, a_out),
        ):
            target[...] = source[...].astype(target.dtype)
        scatter.end()


def backward_mixer(tokens, grad_attended, saved, w_query, w_key, w_value, w_gate, w_beta, w_out, taps_query, taps_key, taps_value, gain, gain_first, starts, lengths, hidden, w_down, resid, g_second, count):
    slots, model = tokens.shape
    wide = w_query.shape[1]
    width = gain.shape[0]
    heads = wide // width
    seqs = starts.shape[1]
    chunks = slots // CHUNK
    taps = taps_query.shape[0]
    smem = pl.BlockSpec(memory_space=pltpu.SMEM)
    fixed = lambda shape: pl.BlockSpec(shape, lambda n: (0,) * len(shape), pipeline_mode=pl.Buffered(1))
    piece = lambda shape: pl.BlockSpec(shape, lambda n: (chunks - 1 - n,) + (0,) * (len(shape) - 1))
    rows = lambda a: piece((CHUNK, a.shape[1]))
    outs = (
        [((slots, model), BF16)] + [((model, wide), BF16)] * 4 + [((wide, model), BF16)]
        + [((small_rows(heads, taps), model), F32), (resid.shape, BF16)]
    )
    return pl.pallas_call(
        functools.partial(backward_kernel, heads, width, seqs, chunks, count, slots // count),
        name="mixer_backward",
        grid=(chunks,),
        out_shape=[jax.ShapeDtypeStruct(s, d) for s, d in outs],
        in_specs=[smem, smem, rows(tokens), rows(grad_attended)]
        + [rows(a) for a in saved[:11]]
        + [piece((1, heads, CHUNK, CHUNK)), piece((1, heads, width, width))]
        + [ANY] * 4
        + [fixed(w_beta.shape), fixed((wide, model))]
        + [fixed((taps, wide))] * 3
        + [fixed((1, width)), VMEM, fixed(hidden.shape), fixed(w_down.shape), ANY, fixed(g_second.shape)],
        out_specs=[piece((CHUNK, model))] + [fixed(s) for s, d in outs[1:]],
        scratch_shapes=[pltpu.VMEM((model, wide), F32)] * 4
        + [pltpu.VMEM((wide, model), F32)]
        + [pltpu.VMEM((CHUNK + 8, wide), F32)] * 3
        + [pltpu.VMEM((heads, width, width), F32)]
        + [pltpu.VMEM((model, wide), BF16)] * 4
        + [pltpu.VMEM(resid.shape, F32), pltpu.SemaphoreType.DMA((5,)), ring_slots(count, slots // count, model)]
        + ring_semaphores(count),
        compiler_params=ring_params(6),
        cost_estimate=pl.CostEstimate(
            flops=2 * slots * model * wide * 10 + slots * heads * CHUNK * 2 * CHUNK * 8,
            bytes_accessed=slots * model * 6 + 10 * model * wide * 2 + slots * wide * 36,
            transcendentals=slots * wide * 8,
        ),
    )(starts, lengths, tokens, grad_attended, *saved, w_query, w_key, w_value, w_gate, w_beta, w_out, taps_query, taps_key, taps_value, gain.reshape(1, width), gain_first, hidden, w_down, resid, g_second)


def make_shards(groups, count):
    def shards(
        tokens, attn_gain, w_query, w_key, w_value, conv_query, conv_key, conv_value, w_beta, w_gate_out,
        head_gain, w_out, ffn_gain, w_gate, w_up, w_down, seq_starts, seq_lengths, cotangent,
    ):
        model = tokens.shape[1]
        heads = w_beta.shape[1]
        beta_rows = w_beta.T if heads > 1 else jnp.pad(w_beta.T, ((0, 1), (0, 0)))
        tokens_full, w_out_full = gather_tokens(tokens, w_out, count, groups)
        mixed_full, *saved = forward_mixer(
            tokens_full, w_query, w_key, w_value, w_gate_out, beta_rows,
            conv_query, conv_key, conv_value, head_gain, attn_gain, seq_starts, seq_lengths, count,
        )
        resid, ffn_full, hidden, grad_gate, grad_up, grad_full = attend(
            mixed_full, w_out_full, tokens_full, ffn_gain, w_gate.T, w_up.T, w_down, cotangent, count
        )
        grad_resid, grad_attended, g_second, *ffn_grads = ffn_back(
            grad_gate, grad_up, hidden, w_gate.T, w_up.T, resid, cotangent, ffn_gain, ffn_full, grad_full,
            count, groups,
        )
        pulled = backward_mixer(
            tokens_full, grad_attended, saved, w_query, w_key, w_value, w_gate_out, beta_rows, w_out,
            conv_query, conv_key, conv_value, head_gain, attn_gain, seq_starts, seq_lengths,
            hidden, w_down, resid, g_second, count,
        )
        terms, gw_query, gw_key, gw_value, gw_gate_out, gw_out, small, output = pulled
        grad_tokens, total, *mixer_grads = last_step(
            terms, tokens, grad_resid, attn_gain, small,
            (gw_query, gw_key, gw_value, gw_gate_out, gw_out), count, groups,
        )
        taps, wide = conv_query.shape
        output, grad_tokens, *rest = results(
            total,
            [(output, BF16), (grad_tokens, F32)] + [(g, F32) for g in (*mixer_grads, *ffn_grads)],
            heads, taps, wide, head_gain.shape[0],
        )
        grads, (g_first, g_second, g_head, gt_query, gt_key, gt_value, g_beta) = rest[:8], rest[8:]
        return (
            output,
            grad_tokens,
            g_first[0],
            grads[0],
            grads[1],
            grads[2],
            gt_query,
            gt_key,
            gt_value,
            g_beta.T,
            grads[3],
            g_head[0],
            grads[4],
            g_second[0],
            grads[5].T,
            grads[6].T,
            grads[7],
        )

    return shards


def solution(mesh):
    placed = (
        P(("dp", "tensor"), None),
        P(),
        P(None, "tensor"),
        P(None, "tensor"),
        P(None, "tensor"),
        P(None, "tensor"),
        P(None, "tensor"),
        P(None, "tensor"),
        P(None, "tensor"),
        P(None, "tensor"),
        P(),
        P("tensor", None),
        P(),
        P(None, "tensor"),
        P(None, "tensor"),
        P("tensor", None),
        P("dp", None),
        P("dp", None),
        P(("dp", "tensor"), None),
    )
    return jax.shard_map(
        make_shards(mesh.shape["dp"], mesh.shape["tensor"]),
        mesh=mesh,
        in_specs=placed,
        out_specs=(
            P(("dp", "tensor"), None),
            P(("dp", "tensor"), None),
            P(),
            P(None, "tensor"),
            P(None, "tensor"),
            P(None, "tensor"),
            P(None, "tensor"),
            P(None, "tensor"),
            P(None, "tensor"),
            P(None, "tensor"),
            P(None, "tensor"),
            P(),
            P("tensor", None),
            P(),
            P(None, "tensor"),
            P(None, "tensor"),
            P("tensor", None),
        ),
        check_vma=False,
    )
```

```python
import functools
import jax
import jax.numpy as jnp
from jax import lax
from jax.experimental import pallas as pl
from jax.experimental.pallas import tpu as pltpu
from jax.sharding import PartitionSpec as P

CHUNK = 256
F32, BF16 = jnp.float32, jnp.bfloat16


def mm(a, b, contract=(1, 0)):
    return lax.dot_general(
        a.astype(BF16),
        b.astype(BF16),
        (((contract[0],), (contract[1],)), ((), ())),
        preferred_element_type=F32,
    )


def segment_at(places, starts, lengths, seqs):
    segment = jnp.zeros_like(places)
    for s in range(seqs):
        begin = starts[0, s]
        stop = begin + lengths[0, s]
        segment = segment + jnp.where(places >= begin, 1, 0) + jnp.where(places >= stop, 1, 0)
    return jnp.where(places < 0, -1, segment)


def chunk_masks(starts, lengths, seqs, first, size):
    rows = first + lax.broadcasted_iota(jnp.int32, (size, 1), 0)
    columns = first + lax.broadcasted_iota(jnp.int32, (1, size), 1)
    seg_rows = segment_at(rows, starts, lengths, seqs)
    seg_columns = segment_at(columns, starts, lengths, seqs)
    before = segment_at(jnp.full((1, 1), first - 1, jnp.int32), starts, lengths, seqs)
    last = segment_at(jnp.full((1, 1), first + size - 1, jnp.int32), starts, lengths, seqs)
    return rows, seg_rows, seg_columns, before, last


def inverse_unit_lower(lower, size):
    i = lax.broadcasted_iota(jnp.int32, (size, size), 0)
    j = lax.broadcasted_iota(jnp.int32, (size, size), 1)

    def corner(width):
        shift = width.bit_length() - 1
        pair = (i >> (shift + 1)) == (j >> (shift + 1))
        return pair & (((i >> shift) & 1) == 1) & (((j >> shift) & 1) == 0)

    inverse = jnp.where(i == j, 1.0, 0.0) - jnp.where(corner(1), lower, 0.0)
    width = 2
    while width < size:
        low = inverse.astype(BF16)
        if 2 * width == size:
            part = mm(mm(low[width:, width:], lower[width:, :width]), low[:width, :width])
            inverse = jnp.concatenate(
                [
                    inverse[:width],
                    jnp.concatenate([-part, inverse[width:, width:]], axis=1),
                ],
                axis=0,
            )
        else:
            between = jnp.where(corner(width), lower, 0.0)
            inverse = inverse - mm(mm(low, between), low)
        width *= 2
    return inverse


def sigmoid(v):
    return 1.0 / (1.0 + jnp.exp(-v))


def normed_rows(tokens, gain):
    value = tokens[...].astype(F32)
    unit = value * lax.rsqrt(jnp.mean(value * value, axis=1, keepdims=True) + 1e-6)
    return unit * gain[...].astype(F32).reshape(1, -1), unit


MESH = pl.DeviceIdType.MESH
SUBS = 2
PAIRS = [(sub, way) for sub in range(SUBS) for way in (0, 1)]


def ring_position(device, count):
    half, odd = device // 2, device % 2
    return half + odd * (count - 1 - 2 * half)


def ring_device(position, count):
    back = position // (count // 2)
    return (1 - back) * 2 * position + back * (2 * (count - 1 - position) + 1)


class Ring:
    def __init__(self, count):
        self.count = count
        self.me = lax.axis_index("tensor")
        self.place = ring_position(self.me, count)
        self.group = lax.axis_index("dp")

    def at(self, offset):
        return ring_device((self.place + offset + 2 * self.count) % self.count, self.count)

    def next(self, way):
        return (self.group, self.at(1 if way == 0 else -1))


class Gather:
    def __init__(self, ring, own, view, sends, recvs, rows, subs=SUBS):
        self.ring, self.own, self.view, self.sends, self.recvs, self.rows = ring, own, view, sends, recvs, rows
        self.piece = rows // (2 * subs)
        self.pairs = [(sub, way) for sub in range(subs) for way in (0, 1)]

    def origin(self, way, step):
        return self.ring.at(-step if way == 0 else step)

    def copy(self, way, sub, step, origin, first=False):
        inside = way * (self.rows // 2) + sub * self.piece
        place = self.view(origin, inside, self.piece)
        return pltpu.make_async_remote_copy(
            src_ref=self.own(inside, self.piece) if first else place,
            dst_ref=place,
            send_sem=self.sends.at[way, sub, step],
            recv_sem=self.recvs.at[way, sub, step],
            device_id=self.ring.next(way),
            device_id_type=MESH,
        )

    def begin(self):
        for sub, way in self.pairs:
            self.copy(way, sub, 0, self.ring.me, True).start()

    def arrived(self, step):
        for sub, way in self.pairs:
            self.copy(way, sub, step - 1, self.origin(way, step)).wait_recv()

    def hop(self, step):
        for sub, way in self.pairs:
            self.copy(way, sub, step - 1, self.origin(way, step)).wait_recv()
            self.copy(way, sub, step, self.origin(way, step)).start()

    def end(self):
        def drain(step, carry):
            for sub, way in self.pairs:
                self.copy(way, sub, step, self.ring.me).wait_send()
            return carry

        lax.fori_loop(0, self.ring.count - 1, drain, 0)


def row_view(ref, rows):
    return lambda origin, start, size: ref.at[pl.ds(pl.multiple_of(origin * rows + start, size), size), :]


def row_own(ref):
    return lambda start, size: ref.at[pl.ds(start, size), :]


def ring_gather(gather, between):
    count = gather.ring.count

    def run(step, carry):
        @pl.when(step == 0)
        def _():
            gather.begin()

        @pl.when((step > 0) & (step < count - 1))
        def _():
            gather.hop(step)

        @pl.when(step == count - 1)
        def _():
            gather.arrived(step)

        between(step)
        return carry

    lax.fori_loop(0, count, run, 0)
    gather.end()


def scatter_copy(ring, slots, sends, recvs, way, sub, step):
    return pltpu.make_async_remote_copy(
        src_ref=slots.at[way, sub, step],
        dst_ref=slots.at[way, sub, step + 1],
        send_sem=sends.at[way, sub, step],
        recv_sem=recvs.at[way, sub, step],
        device_id=ring.next(way),
        device_id_type=MESH,
    )


class Scatter:
    def __init__(self, ring, partial, slots, sends, recvs, rows, finish):
        self.ring, self.partial, self.slots, self.sends, self.recvs = ring, partial, slots, sends, recvs
        self.half, self.finish = rows // 2, finish
        self.rows, self.piece = rows, rows // (2 * SUBS)

    def terms(self, step):
        half, first, second = self.half, self.ring.at(-1 - step), self.ring.at(1 + step)
        return self.partial(
            pl.multiple_of(first * self.rows, half), pl.multiple_of(second * self.rows + half, half), step
        )

    def part(self, terms, way, sub):
        start = way * self.half + sub * self.piece
        return terms[start : start + self.piece]

    def copy(self, way, sub, step):
        return scatter_copy(self.ring, self.slots, self.sends, self.recvs, way, sub, step)

    def hop(self, step):
        terms = self.terms(step)
        for sub, way in PAIRS:
            term = self.part(terms, way, sub)

            @pl.when(step == 0)
            def _():
                self.slots[way, sub, 0] = term.astype(BF16)

            @pl.when(step > 0)
            def _():
                self.copy(way, sub, step - 1).wait_recv()
                self.slots[way, sub, step] = (self.slots[way, sub, step].astype(F32) + term).astype(BF16)

            self.copy(way, sub, step).start()

    def end(self):
        count = self.ring.count
        terms = self.terms(count - 1)
        for sub, way in PAIRS:
            self.copy(way, sub, count - 2).wait_recv()
            self.finish(
                way * self.half + sub * self.piece,
                self.piece,
                self.slots[way, sub, count - 1].astype(F32) + self.part(terms, way, sub),
            )

        def drain(step, carry):
            for sub, way in PAIRS:
                self.copy(way, sub, step).wait_send()
            return carry

        lax.fori_loop(0, count - 1, drain, 0)


def ring_scatter(scatter, between):
    def run(step, carry):
        scatter.hop(step)
        between(step)
        return carry

    lax.fori_loop(0, scatter.ring.count - 1, run, 0)
    scatter.end()


class GroupSum:
    def __init__(self, ring, groups, grads, near, far, targets, near_sems, far_sems, back_sems, keep_sems):
        self.ring, self.groups, self.grads, self.near, self.far, self.targets = ring, groups, grads, near, far, targets
        self.near_sems, self.far_sems, self.back_sems, self.keep_sems = near_sems, far_sems, back_sems, keep_sems
        self.core = ring.group % 2
        self.mate = (ring.group + 1 - 2 * self.core, ring.me)

    def peers(self):
        return [self.mate] + [
            ((self.ring.group + 2 * k) % self.groups, self.ring.me) for k in range(1, self.groups // 2)
        ]

    def half(self, i, core):
        rows = self.near[i].shape[0]
        return pl.ds(pl.multiple_of(core * rows, rows), rows)

    def near_copy(self, i):
        return pltpu.make_async_remote_copy(
            src_ref=self.grads[i].at[self.half(i, 1 - self.core), :], dst_ref=self.near[i],
            send_sem=self.near_sems.at[0, i], recv_sem=self.near_sems.at[1, i],
            device_id=self.mate, device_id_type=MESH,
        )

    def far_copy(self, i, k):
        return pltpu.make_async_remote_copy(
            src_ref=self.near[i], dst_ref=self.far[i].at[k - 1],
            send_sem=self.far_sems.at[0, i, k - 1], recv_sem=self.far_sems.at[1, i, k - 1],
            device_id=((self.ring.group + 2 * k) % self.groups, self.ring.me), device_id_type=MESH,
        )

    def back_copy(self, i):
        return pltpu.make_async_remote_copy(
            src_ref=self.far[i].at[0], dst_ref=self.targets[i].at[self.half(i, self.core), :],
            send_sem=self.back_sems.at[0, i], recv_sem=self.back_sems.at[1, i],
            device_id=self.mate, device_id_type=MESH,
        )

    def keep_copy(self, i):
        return pltpu.make_async_copy(
            self.far[i].at[0], self.targets[i].at[self.half(i, self.core), :], self.keep_sems.at[i]
        )

    def first(self, chosen):
        for i in chosen:
            self.near_copy(i).start()

    def each_block(self, i, body):
        rows = self.near[i].shape[0]
        block = next(size for size in (64, 32, 16) if rows % size == 0)

        def step(at, carry):
            start = pl.multiple_of(at * block, block)
            body(pl.ds(start, block), pl.ds(pl.multiple_of(self.core * rows + start, block), block))
            return carry

        lax.fori_loop(0, rows // block, step, 0)

    def second(self, chosen):
        for i in chosen:
            self.near_copy(i).wait_recv()

            def add(here, own, i=i):
                self.near[i][here, :] = (
                    self.near[i][here, :].astype(F32) + self.grads[i][own, :].astype(F32)
                ).astype(BF16)

            self.each_block(i, add)
            for k in range(1, self.groups // 2):
                self.far_copy(i, k).start()

    def third(self, chosen):
        for i in chosen:
            for k in range(1, self.groups // 2):
                self.far_copy(i, k).wait()

            def add(here, own, i=i):
                total = self.near[i][here, :].astype(F32)
                for k in range(self.groups // 2 - 1):
                    total = total + self.far[i][k, here, :].astype(F32)
                self.far[i][0, here, :] = total.astype(BF16)

            self.each_block(i, add)
            self.keep_copy(i).start()
            self.back_copy(i).start()

    def last(self):
        for i in range(len(self.grads)):
            self.near_copy(i).wait_send()
            self.back_copy(i).wait()
            self.keep_copy(i).wait()


def sum_scratch(shapes, groups):
    number = len(shapes)
    return (
        [pltpu.VMEM((rows // 2, columns), BF16) for rows, columns in shapes]
        + [pltpu.VMEM((groups // 2 - 1, rows // 2, columns), BF16) for rows, columns in shapes]
        + [
            pltpu.SemaphoreType.DMA((2, number)),
            pltpu.SemaphoreType.DMA((2, number, groups // 2 - 1)),
            pltpu.SemaphoreType.DMA((2, number)),
            pltpu.SemaphoreType.DMA((number,)),
        ]
    )


def greet(ring, others=()):
    barrier = pltpu.get_barrier_semaphore()
    peers = [ring.next(0), ring.next(1)] + list(others)
    for peer in peers:
        pl.semaphore_signal(barrier, inc=1, device_id=peer, device_id_type=MESH)
    pl.semaphore_wait(barrier, len(peers))


def ring_semaphores(count, subs=SUBS):
    return [pltpu.SemaphoreType.DMA((2, subs, count - 1))] * 2


def ring_slots(count, rows, columns):
    return pltpu.VMEM((2, SUBS, count, rows // (2 * SUBS), columns), BF16)


ANY = pl.BlockSpec(memory_space=pl.ANY)
VMEM = pl.BlockSpec(memory_space=pltpu.VMEM)


def ring_params(number):
    return pltpu.CompilerParams(
        collective_id=number, has_side_effects=True, vmem_limit_bytes=60 << 20
    )


class WholeWeight:
    def __init__(self, ring, groups, weight, full, sends, recvs, keep_sem, far_sems, near_sems):
        self.ring, self.groups, self.full, self.far_sems, self.near_sems = ring, groups, full, far_sems, near_sems
        part = weight.shape[0] // groups
        group = ring.group
        own = lambda start, size: weight.at[pl.ds(pl.multiple_of(group * part + start, size), size), :]
        self.gather = Gather(
            ring, own, lambda origin, start, size: full.at[origin, group, pl.ds(start, size), :],
            sends, recvs, part, 1,
        )
        self.keep = pltpu.make_async_copy(own(0, part), full.at[ring.me, group], keep_sem)
        self.mate = (group + 1 - 2 * (group % 2), ring.me)
        self.across = groups // 2

    def peer(self, k):
        return ((self.ring.group + 2 * k) % self.groups, self.ring.me)

    def peers(self):
        return [self.mate] + [self.peer(k) for k in range(1, self.across)]

    def far(self, k):
        part = self.full.at[:, self.ring.group]
        return pltpu.make_async_remote_copy(
            src_ref=part, dst_ref=part, send_sem=self.far_sems.at[0, k - 1], recv_sem=self.far_sems.at[1, k - 1],
            device_id=self.peer(k), device_id_type=MESH,
        )

    def near(self, k):
        part = self.full.at[:, (self.ring.group + self.groups - 2 * k) % self.groups]
        return pltpu.make_async_remote_copy(
            src_ref=part, dst_ref=part, send_sem=self.near_sems.at[0, k], recv_sem=self.near_sems.at[1, k],
            device_id=self.mate, device_id_type=MESH,
        )

    def begin(self):
        self.gather.begin()
        self.keep.start()

    def exchange(self):
        self.gather.arrived(self.ring.count - 1)
        self.keep.wait()
        for k in range(1, self.across):
            self.far(k).start()
        self.near(0).start()

    def back(self):
        for k in range(1, self.across):
            self.far(k).wait_recv()
            self.near(k).start()

    def end(self):
        for k in range(self.across):
            self.near(k).wait()
        for k in range(1, self.across):
            self.far(k).wait_send()
        self.gather.end()


def gather_kernel(count, tokens, tokens_full, sends, recvs, local):
    ring = Ring(count)
    rows = tokens.shape[0]
    greet(ring)
    keep = pltpu.make_async_copy(
        tokens, tokens_full.at[pl.ds(pl.multiple_of(ring.me * rows, rows), rows), :], local
    )
    keep.start()
    ring_gather(
        Gather(ring, row_own(tokens), row_view(tokens_full, rows), sends, recvs, rows), lambda step: None
    )
    keep.wait()


def gather_tokens(tokens, count):
    rows, model = tokens.shape
    return pl.pallas_call(
        functools.partial(gather_kernel, count),
        name="gather_tokens",
        out_shape=jax.ShapeDtypeStruct((count * rows, model), tokens.dtype),
        in_specs=[ANY],
        out_specs=ANY,
        scratch_shapes=ring_semaphores(count) + [pltpu.SemaphoreType.DMA],
        compiler_params=ring_params(1),
        cost_estimate=pl.CostEstimate(flops=0, bytes_accessed=300 << 20, transcendentals=0),
    )(tokens)


def attend_kernel(
    count, mixed, w_out, tokens, gain, w_gate, w_up, w_down, cotangent,
    resid, full, hidden, grad_gate, grad_up, cotangents,
    gathered, out_box, gate_box, up_box, down_box, mixed_boxes, token_boxes, normed, gates, stages,
    sends, recvs, weight_sems, keep_sem, mixed_sems, token_sems, out_sems, normed_sems, stage_sems,
):
    ring = Ring(count)
    rows = cotangent.shape[0]
    half = rows // 2
    gather = Gather(ring, row_own(cotangent), row_view(gathered, rows), sends, recvs, rows)
    keep = pltpu.make_async_copy(
        cotangent, gathered.at[pl.ds(pl.multiple_of(ring.me * rows, rows), rows), :], keep_sem
    )
    loads = [
        pltpu.make_async_copy(source, box, weight_sems.at[k])
        for k, (source, box) in enumerate(
            ((w_out, out_box), (w_gate, gate_box), (w_up, up_box), (w_down, down_box))
        )
    ]

    def place(way, step):
        return pl.ds(pl.multiple_of(gather.origin(way, step) * rows + way * half, half), half)

    def mixed_copy(way, step):
        return pltpu.make_async_copy(
            mixed.at[:, place(way, step), :], mixed_boxes.at[step % 2, way], mixed_sems.at[step % 2, way]
        )

    def token_copy(way, step):
        return pltpu.make_async_copy(
            tokens.at[place(way, step), :], token_boxes.at[step % 2, way], token_sems.at[step % 2, way]
        )

    def out_copy(way, step):
        at = place(way, step)
        return pltpu.make_async_copy(gathered.at[at, :], cotangents.at[at, :], out_sems.at[way, step])

    def normed_copy(way, step):
        return pltpu.make_async_copy(
            normed.at[step % 2, pl.ds(way * half, half), :], full.at[place(way, step), :],
            normed_sems.at[step % 2, way],
        )

    def stage_copy(k, way, step):
        target = (hidden, grad_gate, grad_up)[k]
        return pltpu.make_async_copy(
            stages.at[step % 2, k, way], target.at[place(way, step), :], stage_sems.at[step % 2, k, way]
        )

    def settle(step):
        for way in (0, 1):
            normed_copy(way, step).wait()
            for k in range(3):
                stage_copy(k, way, step).wait()

    def fetch(step):
        for way in (0, 1):
            mixed_copy(way, step).start()
            token_copy(way, step).start()

    def put(k, step, value):
        low = value.astype(BF16)
        for way in (0, 1):
            stages[step % 2, k, way] = low[way * half : way * half + half]
            stage_copy(k, way, step).start()

    def prepare(step):
        @pl.when(step > 1)
        def _():
            settle(step - 2)

        slot = step % 2
        for way in (0, 1):
            mixed_copy(way, step).wait()
            token_copy(way, step).wait()

        @pl.when(step + 1 < count)
        def _():
            fetch(step + 1)

        heads = jnp.concatenate(
            [
                jnp.concatenate([mixed_boxes[slot, way, j] for j in range(count)], 1)
                for way in (0, 1)
            ],
            0,
        )
        value = jnp.concatenate([token_boxes[slot, 0], token_boxes[slot, 1]], 0).astype(F32)
        value = value + mm(heads, out_box[...])

        @pl.when(step == 0)
        def _():
            resid[...] = value

        scale = lax.rsqrt(jnp.mean(value * value, axis=1, keepdims=True) + 1e-6)
        normed[slot] = (value * scale * gain[...].astype(F32).reshape(1, -1)).astype(BF16)
        for way in (0, 1):
            normed_copy(way, step).start()
        inputs = normed[slot]
        gate = mm(inputs, gate_box[...], (1, 1))
        up = mm(inputs, up_box[...], (1, 1))
        sig = sigmoid(gate)
        opened = gate * sig
        put(0, step, opened * up)
        gates[0] = up * sig * (1.0 + gate * (1.0 - sig))
        gates[1] = opened

    def feed(step):
        for way in (0, 1):
            out_copy(way, step).start()
        grad = mm(
            jnp.concatenate([gathered[place(0, step), :], gathered[place(1, step), :]], 0), down_box[...], (1, 1)
        )
        put(1, step, grad * gates[0])
        put(2, step, grad * gates[1])

    def run(step, carry):
        @pl.when(step == 0)
        def _():
            gather.begin()
            for load in loads:
                load.wait()

        prepare(step)

        @pl.when(step == 0)
        def _():
            keep.wait()

        @pl.when((step > 0) & (step < count - 1))
        def _():
            gather.hop(step)

        @pl.when(step == count - 1)
        def _():
            gather.arrived(step)

        feed(step)
        return carry

    keep.start()
    fetch(0)
    for load in loads:
        load.start()
    greet(ring)
    lax.fori_loop(0, count, run, 0)
    gather.end()
    settle(count - 2)
    settle(count - 1)

    def drain(step, carry):
        for way in (0, 1):
            out_copy(way, step).wait()
        return carry

    lax.fori_loop(0, count, drain, 0)


def attend(mixed, w_out, tokens, gain, w_gate, w_up, w_down, cotangent, count):
    rows, model = cotangent.shape
    slots, inner = count * rows, w_down.shape[0]
    wide = mixed.shape[2]
    return pl.pallas_call(
        functools.partial(attend_kernel, count),
        name="attend",
        out_shape=[
            jax.ShapeDtypeStruct((rows, model), F32),
            jax.ShapeDtypeStruct((slots, model), BF16),
        ]
        + [jax.ShapeDtypeStruct((slots, inner), BF16)] * 3
        + [jax.ShapeDtypeStruct((slots, model), BF16)],
        in_specs=[ANY] * 3 + [VMEM] + [ANY] * 4,
        out_specs=[VMEM] + [ANY] * 5,
        scratch_shapes=[pltpu.VMEM((slots, model), BF16), pltpu.VMEM(w_out.shape, BF16)]
        + [pltpu.VMEM((inner, model), BF16)] * 3
        + [
            pltpu.VMEM((2, 2, count, rows // 2, wide), BF16),
            pltpu.VMEM((2, 2, rows // 2, model), BF16),
            pltpu.VMEM((2, rows, model), BF16),
            pltpu.VMEM((2, rows, inner), F32),
            pltpu.VMEM((2, 3, 2, rows // 2, inner), BF16),
        ]
        + ring_semaphores(count)
        + [
            pltpu.SemaphoreType.DMA((4,)),
            pltpu.SemaphoreType.DMA,
            pltpu.SemaphoreType.DMA((2, 2)),
            pltpu.SemaphoreType.DMA((2, 2)),
            pltpu.SemaphoreType.DMA((2, count)),
            pltpu.SemaphoreType.DMA((2, 2)),
            pltpu.SemaphoreType.DMA((2, 3, 2)),
        ],
        compiler_params=ring_params(2),
        cost_estimate=pl.CostEstimate(
            flops=2 * slots * model * model + 6 * slots * model * inner, bytes_accessed=300 << 20,
            transcendentals=slots * inner,
        ),
    )(mixed, w_out, tokens, gain, w_gate, w_up, w_down, cotangent)


def norm_back(inputs, scale, gain, grad_normed):
    weighted = gain * grad_normed
    inner = jnp.mean(weighted * inputs, axis=1, keepdims=True)
    unit = inputs * scale
    return scale * weighted - unit * (scale * scale * inner), grad_normed * unit


JOBS = 8


def ffn_back_kernel(
    count, groups, rows, grad_gate, grad_up, hidden_in, w_gate, w_up, resid_in, cotangent_in, gain, inputs, cotangents,
    grad_resid, full, grad_gain, sum_gate, sum_up, sum_down,
    slots, low, gw_gate, gw_up, gw_down, boxes, box_sems, hidden, resid, cotangent, load_sems, *rest,
):
    ring = Ring(count)
    sends, recvs, sends_two, recvs_two, local = rest[:5]
    sums = GroupSum(
        ring, groups, (gw_gate, gw_up, gw_down), rest[5:8], rest[8:11], (sum_gate, sum_up, sum_down), *rest[11:]
    )
    wide = boxes.shape[2]

    def box_copy(job, source):
        at = pl.multiple_of(job % (JOBS // 2) * wide, wide)
        return pltpu.make_async_copy(
            source.at[:, pl.ds(at, wide)], boxes.at[job % 2], box_sems.at[job % 2]
        )

    def fetch(job):
        @pl.when(job < JOBS // 2)
        def _():
            box_copy(job, inputs).start()

        @pl.when(job >= JOBS // 2)
        def _():
            box_copy(job, cotangents).start()

    loads = [
        pltpu.make_async_copy(source, target, load_sems.at[k])
        for k, (source, target) in enumerate(((hidden_in, hidden), (resid_in, resid), (cotangent_in, cotangent)))
    ]
    fetch(0)
    for load in loads:
        load.start()
    greet(ring, sums.peers())
    grad_gain[...] = jnp.zeros_like(grad_gain)
    half = rows // 2

    def partial(first, second, step):
        gates = jnp.concatenate([grad_gate[pl.ds(first, half), :], grad_gate[pl.ds(second, half), :]], 0)
        ups = jnp.concatenate([grad_up[pl.ds(first, half), :], grad_up[pl.ds(second, half), :]], 0)
        return mm(gates, w_gate[...]) + mm(ups, w_up[...])

    def finish(start, size, grad):
        value = resid[start : start + size, :]
        scale = lax.rsqrt(jnp.mean(value * value, axis=1, keepdims=True) + 1e-6)
        through, pieces = norm_back(value, scale, gain[...].astype(F32).reshape(1, -1), grad)
        result = cotangent[start : start + size, :].astype(F32) + through
        grad_resid[start : start + size, :] = result
        grad_gain[...] += jnp.sum(pieces, axis=0, keepdims=True)
        low[start : start + size, :] = result.astype(BF16)

    def work(job, carry):
        box_copy(job, inputs).wait()

        @pl.when(job + 1 < JOBS)
        def _():
            fetch(job + 1)

        at = pl.ds(pl.multiple_of(job % (JOBS // 2) * wide, wide), wide)

        @pl.when(job < JOBS // 2)
        def _():
            box = boxes[job % 2]
            gw_gate[:, at] = mm(grad_gate[...], box, (0, 0)).astype(BF16)
            gw_up[:, at] = mm(grad_up[...], box, (0, 0)).astype(BF16)

        @pl.when(job >= JOBS // 2)
        def _():
            gw_down[:, at] = mm(hidden[...], boxes[job % 2], (0, 0)).astype(BF16)

        return carry

    each = JOBS // 4

    def beside_scatter(step):
        @pl.when(step == 2)
        def _():
            for load in loads:
                load.wait()

        @pl.when(step == 3)
        def _():
            sums.second((0, 1))

        @pl.when(step < 4)
        def _():
            lax.fori_loop(step * each, step * each + each, work, 0)

        @pl.when(step == 1)
        def _():
            sums.first((0, 1))

        @pl.when(step == 3)
        def _():
            sums.first((2,))

        @pl.when(step == 5)
        def _():
            sums.second((2,))

    def beside_gather(step):
        @pl.when(step == count - 3)
        def _():
            sums.third((0, 1))

        @pl.when(step == count - 2)
        def _():
            sums.third((2,))

    ring_scatter(Scatter(ring, partial, slots, sends, recvs, rows, finish), beside_scatter)
    keep = pltpu.make_async_copy(low, full.at[pl.ds(pl.multiple_of(ring.me * rows, rows), rows), :], local)
    keep.start()
    ring_gather(Gather(ring, row_own(low), row_view(full, rows), sends_two, recvs_two, rows), beside_gather)
    keep.wait()
    sums.last()


def ffn_back(grad_gate, grad_up, hidden, w_gate, w_up, resid, cotangent, gain, inputs, cotangents, count, groups):
    rows, model = resid.shape
    slots, inner = grad_up.shape
    shapes = [(inner, model)] * 3
    return pl.pallas_call(
        functools.partial(ffn_back_kernel, count, groups, rows),
        name="ffn_back",
        out_shape=[
            jax.ShapeDtypeStruct((rows, model), F32),
            jax.ShapeDtypeStruct((slots, model), BF16),
            jax.ShapeDtypeStruct((1, model), F32),
        ]
        + [jax.ShapeDtypeStruct(shape, BF16) for shape in shapes],
        in_specs=[VMEM] * 2 + [ANY] + [VMEM] * 2 + [ANY] * 2 + [VMEM] + [ANY] * 2,
        out_specs=[VMEM, ANY, VMEM] + [ANY] * 3,
        scratch_shapes=[ring_slots(count, rows, model), pltpu.VMEM((rows, model), BF16)]
        + [pltpu.VMEM(shape, BF16) for shape in shapes]
        + [pltpu.VMEM((2, slots, model // (JOBS // 2)), BF16), pltpu.SemaphoreType.DMA((2,))]
        + [pltpu.VMEM((slots, inner), BF16), pltpu.VMEM((rows, model), F32), pltpu.VMEM((rows, model), BF16)]
        + [pltpu.SemaphoreType.DMA((3,))]
        + ring_semaphores(count) * 2
        + [pltpu.SemaphoreType.DMA]
        + sum_scratch(shapes, groups),
        compiler_params=ring_params(3),
        cost_estimate=pl.CostEstimate(
            flops=10 * slots * model * inner, bytes_accessed=600 << 20, transcendentals=0
        ),
    )(grad_gate, grad_up, hidden, w_gate, w_up, resid, cotangent, gain, inputs, cotangents)


def last_kernel(
    count, groups, rows, terms, tokens_in, grad_resid_in, gain, small, *rest,
):
    grads, rest = rest[:5], rest[5:]
    grad_tokens, total = rest[:2]
    targets, rest = rest[2:7], rest[7:]
    slots, first_box, second_box, second_own, boxes, box_sems, tokens, grad_resid, load_sems = rest[:9]
    sends, recvs, first_sends, first_recvs, second_sends, second_recvs = rest[9:15]
    ring = Ring(count)
    sums = GroupSum(ring, groups, grads, rest[15:20], rest[20:25], targets, *rest[25:])
    loads = [
        pltpu.make_async_copy(tokens_in, tokens, load_sems.at[0]),
        pltpu.make_async_copy(grad_resid_in, grad_resid, load_sems.at[1]),
    ]
    me, group = ring.me, ring.group
    first_peers = [(group, (me + k) % count) for k in range(1, count)]
    second_peers = [((group + k) % groups, me) for k in range(1, groups)]
    barrier = pltpu.get_barrier_semaphore()
    for peer in first_peers + second_peers:
        pl.semaphore_signal(barrier, inc=1, device_id=peer, device_id_type=MESH)
    pl.semaphore_wait(barrier, count + groups - 2)

    def first(k):
        return pltpu.make_async_remote_copy(
            src_ref=small.at[0:8], dst_ref=first_box.at[k], send_sem=first_sends.at[k],
            recv_sem=first_recvs.at[k], device_id=first_peers[k], device_id_type=MESH,
        )

    def second(k):
        return pltpu.make_async_remote_copy(
            src_ref=second_own, dst_ref=second_box.at[k], send_sem=second_sends.at[k],
            recv_sem=second_recvs.at[k], device_id=second_peers[k], device_id_type=MESH,
        )

    every = range(len(grads))
    sums.first(every)
    for k in range(count - 1):
        first(k).start()
    half = rows // 2

    def box_copy(way, start, slot):
        return pltpu.make_async_copy(
            terms.at[pl.ds(start, half), :], boxes.at[slot, way], box_sems.at[slot, way]
        )

    def fetch(step):
        for way, owner in ((0, ring.at(-1 - step)), (1, ring.at(1 + step))):
            box_copy(way, pl.multiple_of(owner * rows + way * half, half), step % 2).start()

    def partial(first, second, step):
        for way, start in ((0, first), (1, second)):
            box_copy(way, start, step % 2).wait()

        @pl.when(step + 1 < count)
        def _():
            fetch(step + 1)

        return jnp.concatenate([boxes[step % 2, 0], boxes[step % 2, 1]], 0).astype(F32)

    def finish(start, size, grad):
        value = tokens[start : start + size, :].astype(F32)
        scale = lax.rsqrt(jnp.mean(value * value, axis=1, keepdims=True) + 1e-6)
        through, pieces = norm_back(value, scale, gain[...].astype(F32).reshape(1, -1), grad)
        grad_tokens[start : start + size, :] = grad_resid[start : start + size, :] + through

    def early():
        sums.second(every)
        for k in range(count - 1):
            first(k).wait()
        mine = small[0:8]
        for k in range(count - 1):
            mine = mine + first_box[k]
        second_own[0:8] = mine
        second_own[8:] = small[8:]
        for k in range(groups - 1):
            second(k).start()

    def late():
        for k in range(groups - 1):
            second(k).wait()
        mine = second_own[...]
        for k in range(groups - 1):
            mine = mine + second_box[k]
        total[...] = mine
        for load in loads:
            load.wait()

    def beside(step):
        pl.when(step == 0)(early)
        for i in every:
            pl.when(step == count - 1 - len(every) + i)(lambda i=i: sums.third((i,)))
        pl.when(step == count - 2)(late)

    fetch(0)
    for load in loads:
        load.start()
    ring_scatter(Scatter(ring, partial, slots, sends, recvs, rows, finish), beside)
    sums.last()


def last_step(terms, tokens, grad_resid, gain, small, grads, count, groups):
    rows, model = tokens.shape
    return pl.pallas_call(
        functools.partial(last_kernel, count, groups, rows),
        name="last_step",
        out_shape=[jax.ShapeDtypeStruct((rows, model), F32), jax.ShapeDtypeStruct(small.shape, F32)]
        + [jax.ShapeDtypeStruct(g.shape, BF16) for g in grads],
        in_specs=[ANY] * 3 + [VMEM] * (2 + len(grads)),
        out_specs=[VMEM, VMEM] + [ANY] * len(grads),
        scratch_shapes=[
            ring_slots(count, rows, model),
            pltpu.VMEM((count - 1, 8, model), F32),
            pltpu.VMEM((groups - 1,) + small.shape, F32),
            pltpu.VMEM(small.shape, F32),
            pltpu.VMEM((2, 2, rows // 2, model), BF16),
            pltpu.SemaphoreType.DMA((2, 2)),
            pltpu.VMEM((rows, model), BF16),
            pltpu.VMEM((rows, model), F32),
            pltpu.SemaphoreType.DMA((2,)),
        ]
        + ring_semaphores(count)
        + [pltpu.SemaphoreType.DMA((count - 1,))] * 2
        + [pltpu.SemaphoreType.DMA((groups - 1,))] * 2
        + sum_scratch([g.shape for g in grads], groups),
        compiler_params=ring_params(4),
        cost_estimate=pl.CostEstimate(flops=0, bytes_accessed=300 << 20, transcendentals=0),
    )(terms, tokens, grad_resid, gain, small, *grads)


def results_kernel(heads, taps, wide, width, total, *refs):
    number = (len(refs) - 7) // 2
    for source, target in zip(refs[:number], refs[number : 2 * number]):
        target[...] = source[...].astype(target.dtype)
    g_first, g_second, g_head, gt_query, gt_key, gt_value, g_beta = refs[2 * number :]

    @pl.when(pl.program_id(0) == 0)
    def _():
        g_first[...] = total[0:1, :]
        g_second[...] = total[1:2, :]
        g_head[...] = total[2:3, 0:width]
        row = 8 + heads
        for place, target in enumerate((gt_query, gt_key, gt_value)):
            target[...] = total[row : row + taps, place * wide : (place + 1) * wide]
        g_beta[...] = total[8 : 8 + heads, :]


def results(total, arrays, heads, taps, wide, width):
    model = total.shape[1]
    steps = next(n for n in (2, 1) if all(a.shape[0] % (8 * n) == 0 for a, _ in arrays))
    small = [(1, model), (1, model), (1, width)] + [(taps, wide)] * 3 + [(heads, model)]
    piece = lambda a: pl.BlockSpec((a.shape[0] // steps, a.shape[1]), lambda n: (n, 0))
    whole = lambda shape: pl.BlockSpec(shape, lambda n: (0, 0))
    return pl.pallas_call(
        functools.partial(results_kernel, heads, taps, wide, width),
        name="results",
        grid=(steps,),
        out_shape=[jax.ShapeDtypeStruct(a.shape, kind) for a, kind in arrays]
        + [jax.ShapeDtypeStruct(shape, F32) for shape in small],
        in_specs=[whole(total.shape)] + [piece(a) for a, _ in arrays],
        out_specs=[piece(a) for a, _ in arrays] + [whole(shape) for shape in small],
        compiler_params=pltpu.CompilerParams(vmem_limit_bytes=56 << 20),
        cost_estimate=pl.CostEstimate(flops=0, bytes_accessed=48 << 20, transcendentals=0),
    )(total, *[a for a, _ in arrays])


def spread_hops(step, chunks, count, hop, start=0):
    each = -(-(count - 1) // (chunks - 1))
    for place in range(each):
        number = step * each + place

        @pl.when((number >= start) & (number < count - 1))
        def _():
            hop(number)


def plan_hops(chunks, hops, latency=1.4, segment=2.5):
    now, link, due, done, table = 0.0, 0.0, {}, {}, []

    def send(chunk):
        nonlocal link
        link = max(now, link) + 1.0
        done[chunk] = done.get(chunk, -1) + 1
        due[chunk] = link + latency

    def waiting():
        return [chunk for chunk in done if done[chunk] < hops - 1]

    for step in range(chunks):
        for half in range(2):
            ready, moves = True, []
            while ready:
                ready = sorted((due[chunk], chunk) for chunk in waiting() if due[chunk] <= now)
                if ready:
                    send(ready[0][1])
                    moves.append((ready[0][1], done[ready[0][1]]))
            table.append(moves)
            now += segment
        send(step)
    rest = []
    while waiting():
        now, chunk = max((now, 0), min((due[chunk], chunk) for chunk in waiting()))[0], min(
            (due[chunk], chunk) for chunk in waiting()
        )[1]
        send(chunk)
        rest.append((chunk, done[chunk]))
    return table, rest


def forward_kernel(
    heads, width, seqs, count, groups, chunks,
    starts, lengths, tokens, w_query, w_key, w_value, w_gate, w_beta,
    taps_query, taps_key, taps_value, gain, gain_first, w_out,
    mixed_full, w_full, mixed, p_query, p_key, p_value, p_gate, p_beta, z_query, z_key, z_value,
    delta_out, change_out, inverse_out, state_out,
    tail_query, tail_key, tail_value, state, stage, sends, recvs, keeps,
    w_sends, w_recvs, w_keep, w_far, w_near,
):
    step = pl.program_id(0)
    size = tokens.shape[0]
    first = step * size

    @pl.when(step == 0)
    def _():
        for tail in (tail_query, tail_key, tail_value):
            tail[...] = jnp.zeros_like(tail)
        state[...] = jnp.zeros_like(state)

    ring = Ring(count)

    def chunk_gather(chunk):
        return Gather(
            ring,
            lambda start, length: stage.at[chunk, pl.ds(start, length), :],
            lambda origin, start, length: mixed_full.at[
                origin, pl.ds(pl.multiple_of(chunk * size + start, length), length), :
            ],
            sends.at[chunk], recvs.at[chunk], size, 1,
        )

    def keep(chunk):
        return pltpu.make_async_copy(
            stage.at[chunk],
            mixed_full.at[ring.me, pl.ds(pl.multiple_of(chunk * size, size), size), :],
            keeps.at[chunk],
        )

    weight = WholeWeight(ring, groups, w_out, w_full, w_sends, w_recvs, w_keep, w_far, w_near)
    table, rest = plan_hops(chunks, count - 1)

    def turn(late):
        number = 2 * step + late

        @pl.when((number > 0) & (number < count - 1))
        def _():
            weight.gather.hop(number)

        if late == (count - 1) % 2:
            pl.when(number == count - 1)(weight.exchange)
        for place, moves in enumerate(table[late::2]):
            if moves:
                @pl.when(step == place)
                def _():
                    for chunk, hop in moves:
                        chunk_gather(chunk).hop(hop)

    @pl.when(step == 0)
    def _():
        greet(ring, weight.peers())
        weight.begin()

    turn(0)
    rows, seg_rows, seg_columns, before, last = chunk_masks(starts, lengths, seqs, first, size)
    same = seg_rows == seg_columns
    i = lax.broadcasted_iota(jnp.int32, (size, size), 0)
    j = lax.broadcasted_iota(jnp.int32, (size, size), 1)
    strict = jnp.where(same & (i > j), 1.0, 0.0)
    inclusive = jnp.where(same & (i >= j), 1.0, 0.0)
    carried = jnp.where(seg_rows == before, 1.0, 0.0)
    ending = jnp.where(seg_rows == last, 1.0, 0.0)
    kept = jnp.where(before == last, 1.0, 0.0)
    live = jnp.where(seg_rows % 2 == 1, 1.0, 0.0)
    joined = [
        jnp.where(segment_at(rows - offset, starts, lengths, seqs) == seg_rows, 1.0, 0.0)
        for offset in range(1, taps_query.shape[0])
    ]
    inputs = normed_rows(tokens, gain_first)[0].astype(BF16)

    def feature(weight, taps, tail, p_out, z_out):
        projected = jnp.dot(inputs, weight[...], preferred_element_type=F32)
        p_out[...] = projected
        tail[8:, :] = projected
        tap = taps[...].astype(F32)
        result = projected * tap[0:1]
        for offset in range(1, tap.shape[0]):
            result = result + tail[8 - offset : 8 - offset + size, :] * tap[offset : offset + 1] * joined[offset - 1]
        tail[0:8, :] = projected[size - 8 :, :]
        z_out[...] = result
        return result * sigmoid(result)

    u_query = feature(w_query, taps_query, tail_query, p_query, z_query)
    u_key = feature(w_key, taps_key, tail_key, p_key, z_key)
    u_value = feature(w_value, taps_value, tail_value, p_value, z_value)
    gate = jnp.dot(inputs, w_gate[...], preferred_element_type=F32)
    p_gate[...] = gate
    beta_pre = mm(inputs, w_beta[...], (1, 1))
    p_beta[...] = beta_pre
    strength = sigmoid(beta_pre)
    opened = gate * sigmoid(gate)
    scale = width ** (-0.5)
    head_gain = gain[...].astype(F32)
    for h in range(heads):
        if h == heads // 2:
            turn(1)
        cols = slice(h * width, (h + 1) * width)
        uq, uk = u_query[:, cols], u_key[:, cols]
        query = (uq * lax.rsqrt(jnp.sum(uq * uq, axis=1, keepdims=True) + 1e-6)).astype(BF16)
        key = (uk * lax.rsqrt(jnp.sum(uk * uk, axis=1, keepdims=True) + 1e-6)).astype(BF16)
        value = u_value[:, cols].astype(BF16).astype(F32)
        beta = strength[:, h : h + 1]
        memory = state[h]
        low_memory = memory.astype(BF16)
        state_out[0, h] = low_memory
        lower = mm(key, key, (1, 1)) * strict * beta
        inverse = inverse_unit_lower(lower, size).astype(BF16)
        inverse_out[0, h] = inverse
        within = mm(query, key, (1, 1)) * inclusive
        change = mm(inverse, beta * (value - carried * mm(key, low_memory)))
        low_change = change.astype(BF16)
        change_out[:, cols] = low_change
        out = scale * (carried * mm(query, low_memory) + mm(within, low_change))
        state[h] = kept * memory + mm(key, ending * change, (0, 0))
        delta_out[:, cols] = out
        normal = out * lax.rsqrt(jnp.mean(out * out, axis=1, keepdims=True) + 1e-5) * head_gain
        low_mixed = (normal * opened[:, cols] * live).astype(BF16)
        mixed[:, cols] = low_mixed
        stage[step, :, cols] = low_mixed

    chunk_gather(step).begin()
    keep(step).start()

    @pl.when(step == chunks - 1)
    def _():
        for place, (chunk, hop) in enumerate(rest):
            if place == len(rest) // 2:
                weight.back()
            chunk_gather(chunk).hop(hop)

        def settle(chunk, carry):
            chunk_gather(chunk).arrived(count - 1)
            chunk_gather(chunk).end()
            keep(chunk).wait()
            return carry

        lax.fori_loop(0, chunks, settle, 0)
        weight.end()


def forward_mixer(tokens, w_query, w_key, w_value, w_gate, w_beta, taps_query, taps_key, taps_value, gain, gain_first, starts, lengths, w_out, count, groups):
    slots, model = tokens.shape
    wide = w_query.shape[1]
    width = gain.shape[0]
    heads = wide // width
    seqs = starts.shape[1]
    chunks = slots // CHUNK
    taps = taps_query.shape[0]
    part = w_out.shape[0] // groups
    smem = pl.BlockSpec(memory_space=pltpu.SMEM)
    whole = lambda shape: pl.BlockSpec(shape, lambda n: (0,) * len(shape))
    piece = lambda shape: pl.BlockSpec(shape, lambda n: (n,) + (0,) * (len(shape) - 1))
    outs = [
        ((slots, wide), BF16), ((slots, wide), F32), ((slots, wide), F32), ((slots, wide), F32), ((slots, wide), F32),
        ((slots, w_beta.shape[0]), F32), ((slots, wide), F32), ((slots, wide), F32), ((slots, wide), F32),
        ((slots, wide), F32), ((slots, wide), BF16),
    ]
    return pl.pallas_call(
        functools.partial(forward_kernel, heads, width, seqs, count, groups, chunks),
        name="mixer_forward",
        grid=(chunks,),
        out_shape=[
            jax.ShapeDtypeStruct((count, slots, wide), BF16),
            jax.ShapeDtypeStruct((count, groups, part, model), BF16),
        ]
        + [jax.ShapeDtypeStruct(s, d) for s, d in outs]
        + [
            jax.ShapeDtypeStruct((chunks, heads, CHUNK, CHUNK), BF16),
            jax.ShapeDtypeStruct((chunks, heads, width, width), BF16),
        ],
        in_specs=[smem, smem, piece((CHUNK, model))]
        + [whole((model, wide))] * 4
        + [whole(w_beta.shape)]
        + [whole((taps, wide))] * 3
        + [whole((1, width)), VMEM, ANY],
        out_specs=[ANY, ANY]
        + [piece((CHUNK, s[1])) for s, d in outs]
        + [piece((1, heads, CHUNK, CHUNK)), piece((1, heads, width, width))],
        scratch_shapes=[pltpu.VMEM((CHUNK + 8, wide), F32)] * 3
        + [pltpu.VMEM((heads, width, width), F32), pltpu.VMEM((chunks, CHUNK, wide), BF16)]
        + [pltpu.SemaphoreType.DMA((chunks, 2, 1, count - 1))] * 2
        + [pltpu.SemaphoreType.DMA((chunks,))]
        + ring_semaphores(count, 1)
        + [
            pltpu.SemaphoreType.DMA,
            pltpu.SemaphoreType.DMA((2, groups // 2 - 1)),
            pltpu.SemaphoreType.DMA((2, groups // 2)),
        ],
        compiler_params=ring_params(5),
        cost_estimate=pl.CostEstimate(
            flops=2 * slots * model * wide * 4 + slots * heads * CHUNK * 2 * CHUNK * 20,
            bytes_accessed=slots * model * 2 + 4 * model * wide * 2 + slots * wide * 36,
            transcendentals=slots * wide * 4,
        ),
    )(starts, lengths, tokens, w_query, w_key, w_value, w_gate, w_beta, taps_query, taps_key, taps_value, gain.reshape(1, width), gain_first, w_out)


def small_rows(heads, taps):
    return -(-(8 + heads + taps) // 8) * 8


def backward_kernel(
    heads, width, seqs, chunks, count, rows_own,
    starts, lengths, tokens, grad_attended, mixed, p_query, p_key, p_value, p_gate, p_beta,
    z_query, z_key, z_value, delta_out, change_in, inverse_in, state_in,
    w_query_in, w_key_in, w_value_in, w_gate_in, w_beta, w_out, taps_query, taps_key, taps_value, gain, gain_first,
    hidden, w_down, resid_in, g_second, grad_normed, gw_query, gw_key, gw_value, gw_gate, gw_out,
    small, output,
    a_query, a_key, a_value, a_gate, a_out, head_query, head_key, head_value, flow,
    w_query, w_key, w_value, w_gate, resid, load_sems, slots, sends, recvs,
):
    step = pl.program_id(0)
    size = tokens.shape[0]
    first = (chunks - 1 - step) * size

    @pl.when(step == 0)
    def _():
        for ref in (a_query, a_key, a_value, a_gate, a_out, small, flow):
            ref[...] = jnp.zeros_like(ref)
        small[1:2, :] = g_second[...]
        for ref in (head_query, head_key, head_value):
            ref[size:, :] = jnp.zeros((8, ref.shape[1]), F32)

    half = rows_own // 2

    def partial(one, two, number):
        return mm(jnp.concatenate([hidden[pl.ds(one, half), :], hidden[pl.ds(two, half), :]], 0), w_down[...])

    def finish(start, length, down):
        output[start : start + length, :] = (resid[start : start + length, :] + down).astype(BF16)

    ring = Ring(count)
    scatter = Scatter(ring, partial, slots, sends, recvs, rows_own, finish)
    loads = [
        pltpu.make_async_copy(source, target, load_sems.at[k])
        for k, (source, target) in enumerate(
            ((w_query_in, w_query), (w_key_in, w_key), (w_value_in, w_value), (w_gate_in, w_gate), (resid_in, resid))
        )
    ]

    @pl.when(step == 0)
    def _():
        for load in loads:
            load.start()
        greet(ring)

    spread_hops(step, chunks, count, scatter.hop)
    rows, seg_rows, seg_columns, before, last = chunk_masks(starts, lengths, seqs, first, size)
    same = seg_rows == seg_columns
    i = lax.broadcasted_iota(jnp.int32, (size, size), 0)
    j = lax.broadcasted_iota(jnp.int32, (size, size), 1)
    strict = jnp.where(same & (i > j), 1.0, 0.0)
    inclusive = jnp.where(same & (i >= j), 1.0, 0.0)
    carried = jnp.where(seg_rows == before, 1.0, 0.0)
    ending = jnp.where(seg_rows == last, 1.0, 0.0)
    kept = jnp.where(before == last, 1.0, 0.0)
    live = jnp.where(seg_rows % 2 == 1, 1.0, 0.0)
    taps = taps_query.shape[0]
    joined = [
        jnp.where(segment_at(rows + offset, starts, lengths, seqs) == seg_rows, 1.0, 0.0)
        for offset in range(1, taps)
    ]
    normal_rows, unit_rows = normed_rows(tokens, gain_first)
    inputs = normal_rows.astype(BF16)
    grad_rows = grad_attended[...]
    grad_mixed = mm(grad_rows, w_out[...], (1, 1))
    a_out[...] += mm(mixed[...], grad_rows, (0, 0))
    strength = sigmoid(p_beta[...])
    scale = width ** (-0.5)
    head_gain = gain[...].astype(F32)

    grads_query, grads_key, grads_value, grads_gate, grads_beta = [], [], [], [], []
    for h in range(heads):
        cols = slice(h * width, (h + 1) * width)
        out = delta_out[:, cols]
        gate = p_gate[:, cols]
        sig_gate = sigmoid(gate)
        silu_gate = gate * sig_gate
        root = lax.rsqrt(jnp.mean(out * out, axis=1, keepdims=True) + 1e-5)
        grad = grad_mixed[:, cols] * live
        unit = out * root
        grads_gate.append(grad * unit * head_gain * (sig_gate * (1.0 + gate * (1.0 - sig_gate))))
        grad_normal = grad * silu_gate
        small[2:3, 0:width] += jnp.sum(grad_normal * unit, axis=0, keepdims=True)
        push = grad_normal * head_gain
        grad_out = scale * root * (push - unit * jnp.mean(push * unit, axis=1, keepdims=True))

        zq, zk, zv = z_query[:, cols], z_key[:, cols], z_value[:, cols]
        sq, sk, sv = sigmoid(zq), sigmoid(zk), sigmoid(zv)
        uq, uk = zq * sq, zk * sk
        nq = lax.rsqrt(jnp.sum(uq * uq, axis=1, keepdims=True) + 1e-6)
        nk = lax.rsqrt(jnp.sum(uk * uk, axis=1, keepdims=True) + 1e-6)
        unit_q, unit_k = uq * nq, uk * nk
        query, key = unit_q.astype(BF16), unit_k.astype(BF16)
        beta = strength[:, h : h + 1]
        change = change_in[:, cols]
        inverse = inverse_in[0, h]
        memory = state_in[0, h]
        flowing = flow[h]
        low_flow = flowing.astype(BF16)
        low_out = grad_out.astype(BF16)

        within = mm(query, key, (1, 1)) * inclusive
        grad_within = (mm(low_out, change, (1, 1)) * inclusive).astype(BF16)
        grad_change = mm(within, low_out, (0, 0)) + ending * mm(key, low_flow)
        grad_mid = mm(inverse, grad_change, (0, 0))
        grad_value = beta * grad_mid
        low_value = grad_value.astype(BF16)
        cross = (mm(low_value, change, (1, 1)) * strict).astype(BF16)
        grad_query = carried * mm(low_out, memory, (1, 1)) + mm(grad_within, key)
        grad_key = (
            mm(grad_within, query, (0, 0))
            + ending * mm(change, low_flow, (1, 1))
            - carried * mm(low_value, memory, (1, 1))
            - mm(cross, key)
            - mm(cross, key, (0, 0))
        )
        flow[h] = (
            kept * flowing
            + mm(query, carried * grad_out, (0, 0))
            - mm(key, carried * grad_value, (0, 0))
        )
        grads_beta.append((1.0 - beta) * jnp.sum(grad_mid * change.astype(F32), axis=1, keepdims=True))
        du_q = nq * (grad_query - unit_q * jnp.sum(grad_query * unit_q, axis=1, keepdims=True))
        du_k = nk * (grad_key - unit_k * jnp.sum(grad_key * unit_k, axis=1, keepdims=True))
        grads_query.append(du_q * sq * (1.0 + zq * (1.0 - sq)))
        grads_key.append(du_k * sk * (1.0 + zk * (1.0 - sk)))
        grads_value.append(grad_value * sv * (1.0 + zv * (1.0 - sv)))

    tap_row = 8 + heads
    wide = heads * width

    def unconv(parts, taps_ref, head, projected, place):
        lanes = slice(place * wide, (place + 1) * wide)
        grad = jnp.concatenate(parts, axis=1)
        head[0:size, :] = grad
        tap = taps_ref[...].astype(F32)
        p = projected[...]
        result = grad * tap[0:1]
        small[tap_row : tap_row + 1, lanes] += jnp.sum(p * grad, axis=0, keepdims=True)
        for offset in range(1, taps):
            moved = head[offset : offset + size, :] * joined[offset - 1]
            result = result + moved * tap[offset : offset + 1]
            row = tap_row + offset
            small[row : row + 1, lanes] += jnp.sum(p * moved, axis=0, keepdims=True)
        head[size:, :] = grad[0:8, :]
        return result.astype(BF16)

    d_query = unconv(grads_query, taps_query, head_query, p_query, 0)
    d_key = unconv(grads_key, taps_key, head_key, p_key, 1)
    d_value = unconv(grads_value, taps_value, head_value, p_value, 2)
    d_gate = jnp.concatenate(grads_gate, axis=1).astype(BF16)
    spare = [jnp.zeros((size, 1), F32)] * (w_beta.shape[0] - heads)
    d_beta = jnp.concatenate(grads_beta + spare, axis=1).astype(BF16)

    @pl.when(step == 0)
    def _():
        for load in loads:
            load.wait()

    grad_inputs = (
        mm(d_query, w_query[...], (1, 1))
        + mm(d_key, w_key[...], (1, 1))
        + mm(d_value, w_value[...], (1, 1))
        + mm(d_gate, w_gate[...], (1, 1))
        + mm(d_beta, w_beta[...])
    )
    grad_normed[...] = grad_inputs.astype(BF16)
    small[0:1, :] += jnp.sum(grad_inputs * unit_rows, axis=0, keepdims=True)
    a_query[...] += mm(inputs, d_query, (0, 0))
    a_key[...] += mm(inputs, d_key, (0, 0))
    a_value[...] += mm(inputs, d_value, (0, 0))
    a_gate[...] += mm(inputs, d_gate, (0, 0))
    small[8 : 8 + heads, :] += mm(d_beta, inputs, (0, 0))[:heads]

    @pl.when(step == chunks - 1)
    def _():
        for target, source in (
            (gw_query, a_query), (gw_key, a_key), (gw_value, a_value), (gw_gate, a_gate),
            (gw_out, a_out),
        ):
            target[...] = source[...].astype(target.dtype)
        scatter.end()


def backward_mixer(tokens, grad_attended, saved, w_query, w_key, w_value, w_gate, w_beta, w_out, taps_query, taps_key, taps_value, gain, gain_first, starts, lengths, hidden, w_down, resid, g_second, count):
    slots, model = tokens.shape
    wide = w_query.shape[1]
    width = gain.shape[0]
    heads = wide // width
    seqs = starts.shape[1]
    chunks = slots // CHUNK
    taps = taps_query.shape[0]
    smem = pl.BlockSpec(memory_space=pltpu.SMEM)
    fixed = lambda shape: pl.BlockSpec(shape, lambda n: (0,) * len(shape), pipeline_mode=pl.Buffered(1))
    piece = lambda shape: pl.BlockSpec(shape, lambda n: (chunks - 1 - n,) + (0,) * (len(shape) - 1))
    rows = lambda a: piece((CHUNK, a.shape[1]))
    outs = (
        [((slots, model), BF16)] + [((model, wide), BF16)] * 4 + [((wide, model), BF16)]
        + [((small_rows(heads, taps), model), F32), (resid.shape, BF16)]
    )
    return pl.pallas_call(
        functools.partial(backward_kernel, heads, width, seqs, chunks, count, slots // count),
        name="mixer_backward",
        grid=(chunks,),
        out_shape=[jax.ShapeDtypeStruct(s, d) for s, d in outs],
        in_specs=[smem, smem, rows(tokens), rows(grad_attended)]
        + [rows(a) for a in saved[:11]]
        + [piece((1, heads, CHUNK, CHUNK)), piece((1, heads, width, width))]
        + [ANY] * 4
        + [fixed(w_beta.shape), fixed((wide, model))]
        + [fixed((taps, wide))] * 3
        + [fixed((1, width)), VMEM, fixed(hidden.shape), fixed(w_down.shape), ANY, fixed(g_second.shape)],
        out_specs=[piece((CHUNK, model))] + [fixed(s) for s, d in outs[1:]],
        scratch_shapes=[pltpu.VMEM((model, wide), F32)] * 4
        + [pltpu.VMEM((wide, model), F32)]
        + [pltpu.VMEM((CHUNK + 8, wide), F32)] * 3
        + [pltpu.VMEM((heads, width, width), F32)]
        + [pltpu.VMEM((model, wide), BF16)] * 4
        + [pltpu.VMEM(resid.shape, F32), pltpu.SemaphoreType.DMA((5,)), ring_slots(count, slots // count, model)]
        + ring_semaphores(count),
        compiler_params=ring_params(6),
        cost_estimate=pl.CostEstimate(
            flops=2 * slots * model * wide * 10 + slots * heads * CHUNK * 2 * CHUNK * 8,
            bytes_accessed=slots * model * 6 + 10 * model * wide * 2 + slots * wide * 36,
            transcendentals=slots * wide * 8,
        ),
    )(starts, lengths, tokens, grad_attended, *saved, w_query, w_key, w_value, w_gate, w_beta, w_out, taps_query, taps_key, taps_value, gain.reshape(1, width), gain_first, hidden, w_down, resid, g_second)


def make_shards(groups, count):
    def shards(
        tokens, attn_gain, w_query, w_key, w_value, conv_query, conv_key, conv_value, w_beta, w_gate_out,
        head_gain, w_out, ffn_gain, w_gate, w_up, w_down, seq_starts, seq_lengths, cotangent,
    ):
        model = tokens.shape[1]
        heads = w_beta.shape[1]
        beta_rows = w_beta.T if heads > 1 else jnp.pad(w_beta.T, ((0, 1), (0, 0)))
        tokens_full = gather_tokens(tokens, count)
        mixed_full, w_out_full, *saved = forward_mixer(
            tokens_full, w_query, w_key, w_value, w_gate_out, beta_rows,
            conv_query, conv_key, conv_value, head_gain, attn_gain, seq_starts, seq_lengths, w_out, count, groups,
        )
        w_out_full = w_out_full.reshape(-1, tokens.shape[1])
        resid, ffn_full, hidden, grad_gate, grad_up, grad_full = attend(
            mixed_full, w_out_full, tokens_full, ffn_gain, w_gate.T, w_up.T, w_down, cotangent, count
        )
        grad_resid, grad_attended, g_second, *ffn_grads = ffn_back(
            grad_gate, grad_up, hidden, w_gate.T, w_up.T, resid, cotangent, ffn_gain, ffn_full, grad_full,
            count, groups,
        )
        pulled = backward_mixer(
            tokens_full, grad_attended, saved, w_query, w_key, w_value, w_gate_out, beta_rows, w_out,
            conv_query, conv_key, conv_value, head_gain, attn_gain, seq_starts, seq_lengths,
            hidden, w_down, resid, g_second, count,
        )
        terms, gw_query, gw_key, gw_value, gw_gate_out, gw_out, small, output = pulled
        grad_tokens, total, *mixer_grads = last_step(
            terms, tokens, grad_resid, attn_gain, small,
            (gw_query, gw_key, gw_value, gw_gate_out, gw_out), count, groups,
        )
        taps, wide = conv_query.shape
        output, grad_tokens, *rest = results(
            total,
            [(output, BF16), (grad_tokens, F32)] + [(g, F32) for g in (*mixer_grads, *ffn_grads)],
            heads, taps, wide, head_gain.shape[0],
        )
        grads, (g_first, g_second, g_head, gt_query, gt_key, gt_value, g_beta) = rest[:8], rest[8:]
        return (
            output,
            grad_tokens,
            g_first[0],
            grads[0],
            grads[1],
            grads[2],
            gt_query,
            gt_key,
            gt_value,
            g_beta.T,
            grads[3],
            g_head[0],
            grads[4],
            g_second[0],
            grads[5].T,
            grads[6].T,
            grads[7],
        )

    return shards


def solution(mesh):
    placed = (
        P(("dp", "tensor"), None),
        P(),
        P(None, "tensor"),
        P(None, "tensor"),
        P(None, "tensor"),
        P(None, "tensor"),
        P(None, "tensor"),
        P(None, "tensor"),
        P(None, "tensor"),
        P(None, "tensor"),
        P(),
        P("tensor", None),
        P(),
        P(None, "tensor"),
        P(None, "tensor"),
        P("tensor", None),
        P("dp", None),
        P("dp", None),
        P(("dp", "tensor"), None),
    )
    return jax.shard_map(
        make_shards(mesh.shape["dp"], mesh.shape["tensor"]),
        mesh=mesh,
        in_specs=placed,
        out_specs=(
            P(("dp", "tensor"), None),
            P(("dp", "tensor"), None),
            P(),
            P(None, "tensor"),
            P(None, "tensor"),
            P(None, "tensor"),
            P(None, "tensor"),
            P(None, "tensor"),
            P(None, "tensor"),
            P(None, "tensor"),
            P(None, "tensor"),
            P(),
            P("tensor", None),
            P(),
            P(None, "tensor"),
            P(None, "tensor"),
            P("tensor", None),
        ),
        check_vma=False,
    )
```

```python
import functools
import jax
import jax.numpy as jnp
from jax import lax
from jax.experimental import pallas as pl
from jax.experimental.pallas import tpu as pltpu
from jax.sharding import PartitionSpec as P

CHUNK = 256
F32, BF16 = jnp.float32, jnp.bfloat16


def mm(a, b, contract=(1, 0)):
    return lax.dot_general(
        a.astype(BF16),
        b.astype(BF16),
        (((contract[0],), (contract[1],)), ((), ())),
        preferred_element_type=F32,
    )


def segment_at(places, starts, lengths, seqs):
    segment = jnp.zeros_like(places)
    for s in range(seqs):
        begin = starts[0, s]
        stop = begin + lengths[0, s]
        segment = segment + jnp.where(places >= begin, 1, 0) + jnp.where(places >= stop, 1, 0)
    return jnp.where(places < 0, -1, segment)


def chunk_masks(starts, lengths, seqs, first, size):
    rows = first + lax.broadcasted_iota(jnp.int32, (size, 1), 0)
    columns = first + lax.broadcasted_iota(jnp.int32, (1, size), 1)
    seg_rows = segment_at(rows, starts, lengths, seqs)
    seg_columns = segment_at(columns, starts, lengths, seqs)
    before = segment_at(jnp.full((1, 1), first - 1, jnp.int32), starts, lengths, seqs)
    last = segment_at(jnp.full((1, 1), first + size - 1, jnp.int32), starts, lengths, seqs)
    return rows, seg_rows, seg_columns, before, last


def inverse_unit_lower(lower, size):
    i = lax.broadcasted_iota(jnp.int32, (size, size), 0)
    j = lax.broadcasted_iota(jnp.int32, (size, size), 1)

    def corner(width):
        shift = width.bit_length() - 1
        pair = (i >> (shift + 1)) == (j >> (shift + 1))
        return pair & (((i >> shift) & 1) == 1) & (((j >> shift) & 1) == 0)

    inverse = jnp.where(i == j, 1.0, 0.0) - jnp.where(corner(1), lower, 0.0)
    width = 2
    while width < size:
        low = inverse.astype(BF16)
        if 2 * width == size:
            part = mm(mm(low[width:, width:], lower[width:, :width]), low[:width, :width])
            inverse = jnp.concatenate(
                [
                    inverse[:width],
                    jnp.concatenate([-part, inverse[width:, width:]], axis=1),
                ],
                axis=0,
            )
        else:
            between = jnp.where(corner(width), lower, 0.0)
            inverse = inverse - mm(mm(low, between), low)
        width *= 2
    return inverse


def sigmoid(v):
    return 1.0 / (1.0 + jnp.exp(-v))


def normed_rows(tokens, gain):
    value = tokens[...].astype(F32)
    unit = value * lax.rsqrt(jnp.mean(value * value, axis=1, keepdims=True) + 1e-6)
    return unit * gain[...].astype(F32).reshape(1, -1), unit


MESH = pl.DeviceIdType.MESH
SUBS = 2
PAIRS = [(sub, way) for sub in range(SUBS) for way in (0, 1)]


def ring_position(device, count):
    half, odd = device // 2, device % 2
    return half + odd * (count - 1 - 2 * half)


def ring_device(position, count):
    back = position // (count // 2)
    return (1 - back) * 2 * position + back * (2 * (count - 1 - position) + 1)


class Ring:
    def __init__(self, count):
        self.count = count
        self.me = lax.axis_index("tensor")
        self.place = ring_position(self.me, count)
        self.group = lax.axis_index("dp")

    def at(self, offset):
        return ring_device((self.place + offset + 2 * self.count) % self.count, self.count)

    def next(self, way):
        return (self.group, self.at(1 if way == 0 else -1))


class Gather:
    def __init__(self, ring, own, view, sends, recvs, rows, subs=SUBS):
        self.ring, self.own, self.view, self.sends, self.recvs, self.rows = ring, own, view, sends, recvs, rows
        self.piece = rows // (2 * subs)
        self.pairs = [(sub, way) for sub in range(subs) for way in (0, 1)]

    def origin(self, way, step):
        return self.ring.at(-step if way == 0 else step)

    def copy(self, way, sub, step, origin, first=False):
        inside = way * (self.rows // 2) + sub * self.piece
        place = self.view(origin, inside, self.piece)
        return pltpu.make_async_remote_copy(
            src_ref=self.own(inside, self.piece) if first else place,
            dst_ref=place,
            send_sem=self.sends.at[way, sub, step],
            recv_sem=self.recvs.at[way, sub, step],
            device_id=self.ring.next(way),
            device_id_type=MESH,
        )

    def begin(self):
        for sub, way in self.pairs:
            self.copy(way, sub, 0, self.ring.me, True).start()

    def arrived(self, step):
        for sub, way in self.pairs:
            self.copy(way, sub, step - 1, self.origin(way, step)).wait_recv()

    def hop(self, step):
        for sub, way in self.pairs:
            self.copy(way, sub, step - 1, self.origin(way, step)).wait_recv()
            self.copy(way, sub, step, self.origin(way, step)).start()

    def end(self):
        def drain(step, carry):
            for sub, way in self.pairs:
                self.copy(way, sub, step, self.ring.me).wait_send()
            return carry

        lax.fori_loop(0, self.ring.count - 1, drain, 0)


def row_view(ref, rows):
    return lambda origin, start, size: ref.at[pl.ds(pl.multiple_of(origin * rows + start, size), size), :]


def row_own(ref):
    return lambda start, size: ref.at[pl.ds(start, size), :]


def ring_gather(gather, between, begun=False):
    count = gather.ring.count

    def run(step, carry):
        if not begun:
            pl.when(step == 0)(gather.begin)

        @pl.when((step > 0) & (step < count - 1))
        def _():
            gather.hop(step)

        @pl.when(step == count - 1)
        def _():
            gather.arrived(step)

        between(step)
        return carry

    lax.fori_loop(0, count, run, 0)
    gather.end()


def scatter_copy(ring, slots, sends, recvs, way, sub, step):
    return pltpu.make_async_remote_copy(
        src_ref=slots.at[way, sub, step],
        dst_ref=slots.at[way, sub, step + 1],
        send_sem=sends.at[way, sub, step],
        recv_sem=recvs.at[way, sub, step],
        device_id=ring.next(way),
        device_id_type=MESH,
    )


class Scatter:
    def __init__(self, ring, partial, slots, sends, recvs, rows, finish, after=None):
        self.after = after
        self.ring, self.partial, self.slots, self.sends, self.recvs = ring, partial, slots, sends, recvs
        self.half, self.finish = rows // 2, finish
        self.rows, self.piece = rows, rows // (2 * SUBS)

    def terms(self, step):
        half, first, second = self.half, self.ring.at(-1 - step), self.ring.at(1 + step)
        return self.partial(
            pl.multiple_of(first * self.rows, half), pl.multiple_of(second * self.rows + half, half), step
        )

    def part(self, terms, way, sub):
        start = way * self.half + sub * self.piece
        return terms[start : start + self.piece]

    def copy(self, way, sub, step):
        return scatter_copy(self.ring, self.slots, self.sends, self.recvs, way, sub, step)

    def hop(self, step):
        terms = self.terms(step)
        for sub, way in PAIRS:
            term = self.part(terms, way, sub)

            @pl.when(step == 0)
            def _():
                self.slots[way, sub, 0] = term.astype(BF16)

            @pl.when(step > 0)
            def _():
                self.copy(way, sub, step - 1).wait_recv()
                self.slots[way, sub, step] = (self.slots[way, sub, step].astype(F32) + term).astype(BF16)

            self.copy(way, sub, step).start()

    def end(self):
        count = self.ring.count
        terms = self.terms(count - 1)
        for sub, way in PAIRS:
            self.copy(way, sub, count - 2).wait_recv()
            self.finish(
                way * self.half + sub * self.piece,
                self.piece,
                self.slots[way, sub, count - 1].astype(F32) + self.part(terms, way, sub),
            )
            if self.after is not None:
                self.after(way, sub)

        def drain(step, carry):
            for sub, way in PAIRS:
                self.copy(way, sub, step).wait_send()
            return carry

        lax.fori_loop(0, count - 1, drain, 0)


def ring_scatter(scatter, between):
    def run(step, carry):
        scatter.hop(step)
        between(step)
        return carry

    lax.fori_loop(0, scatter.ring.count - 1, run, 0)
    scatter.end()


class GroupSum:
    def __init__(self, ring, groups, grads, near, far, targets, near_sems, far_sems, back_sems, keep_sems):
        self.ring, self.groups, self.grads, self.near, self.far, self.targets = ring, groups, grads, near, far, targets
        self.near_sems, self.far_sems, self.back_sems, self.keep_sems = near_sems, far_sems, back_sems, keep_sems
        self.core = ring.group % 2
        self.mate = (ring.group + 1 - 2 * self.core, ring.me)

    def peers(self):
        return [self.mate] + [
            ((self.ring.group + 2 * k) % self.groups, self.ring.me) for k in range(1, self.groups // 2)
        ]

    def half(self, i, core):
        rows = self.near[i].shape[0]
        return pl.ds(pl.multiple_of(core * rows, rows), rows)

    def near_copy(self, i):
        return pltpu.make_async_remote_copy(
            src_ref=self.grads[i].at[self.half(i, 1 - self.core), :], dst_ref=self.near[i],
            send_sem=self.near_sems.at[0, i], recv_sem=self.near_sems.at[1, i],
            device_id=self.mate, device_id_type=MESH,
        )

    def far_copy(self, i, k):
        return pltpu.make_async_remote_copy(
            src_ref=self.near[i], dst_ref=self.far[i].at[k - 1],
            send_sem=self.far_sems.at[0, i, k - 1], recv_sem=self.far_sems.at[1, i, k - 1],
            device_id=((self.ring.group + 2 * k) % self.groups, self.ring.me), device_id_type=MESH,
        )

    def back_copy(self, i):
        return pltpu.make_async_remote_copy(
            src_ref=self.far[i].at[0], dst_ref=self.targets[i].at[self.half(i, self.core), :],
            send_sem=self.back_sems.at[0, i], recv_sem=self.back_sems.at[1, i],
            device_id=self.mate, device_id_type=MESH,
        )

    def keep_copy(self, i):
        return pltpu.make_async_copy(
            self.far[i].at[0], self.targets[i].at[self.half(i, self.core), :], self.keep_sems.at[i]
        )

    def first(self, chosen):
        for i in chosen:
            self.near_copy(i).start()

    def each_block(self, i, body):
        rows = self.near[i].shape[0]
        block = next(size for size in (64, 32, 16) if rows % size == 0)

        def step(at, carry):
            start = pl.multiple_of(at * block, block)
            body(pl.ds(start, block), pl.ds(pl.multiple_of(self.core * rows + start, block), block))
            return carry

        lax.fori_loop(0, rows // block, step, 0)

    def second(self, chosen):
        for i in chosen:
            self.near_copy(i).wait_recv()

            def add(here, own, i=i):
                self.near[i][here, :] = (
                    self.near[i][here, :].astype(F32) + self.grads[i][own, :].astype(F32)
                ).astype(BF16)

            self.each_block(i, add)
            for k in range(1, self.groups // 2):
                self.far_copy(i, k).start()

    def third(self, chosen):
        for i in chosen:
            for k in range(1, self.groups // 2):
                self.far_copy(i, k).wait()

            def add(here, own, i=i):
                total = self.near[i][here, :].astype(F32)
                for k in range(self.groups // 2 - 1):
                    total = total + self.far[i][k, here, :].astype(F32)
                self.far[i][0, here, :] = total.astype(BF16)

            self.each_block(i, add)
            self.keep_copy(i).start()
            self.back_copy(i).start()

    def last(self):
        for i in range(len(self.grads)):
            self.near_copy(i).wait_send()
            self.back_copy(i).wait()
            self.keep_copy(i).wait()


def sum_scratch(shapes, groups):
    number = len(shapes)
    return (
        [pltpu.VMEM((rows // 2, columns), BF16) for rows, columns in shapes]
        + [pltpu.VMEM((groups // 2 - 1, rows // 2, columns), BF16) for rows, columns in shapes]
        + [
            pltpu.SemaphoreType.DMA((2, number)),
            pltpu.SemaphoreType.DMA((2, number, groups // 2 - 1)),
            pltpu.SemaphoreType.DMA((2, number)),
            pltpu.SemaphoreType.DMA((number,)),
        ]
    )


def greet(ring, others=()):
    barrier = pltpu.get_barrier_semaphore()
    peers = [ring.next(0), ring.next(1)] + list(others)
    for peer in peers:
        pl.semaphore_signal(barrier, inc=1, device_id=peer, device_id_type=MESH)
    pl.semaphore_wait(barrier, len(peers))


def ring_semaphores(count, subs=SUBS):
    return [pltpu.SemaphoreType.DMA((2, subs, count - 1))] * 2


def ring_slots(count, rows, columns):
    return pltpu.VMEM((2, SUBS, count, rows // (2 * SUBS), columns), BF16)


ANY = pl.BlockSpec(memory_space=pl.ANY)
VMEM = pl.BlockSpec(memory_space=pltpu.VMEM)


def ring_params(number):
    return pltpu.CompilerParams(
        collective_id=number, has_side_effects=True, vmem_limit_bytes=60 << 20
    )


class WholeWeight:
    def __init__(self, ring, groups, weight, full, sends, recvs, keep_sem, far_sems, near_sems):
        self.ring, self.groups, self.full, self.far_sems, self.near_sems = ring, groups, full, far_sems, near_sems
        part = weight.shape[0] // groups
        group = ring.group
        own = lambda start, size: weight.at[pl.ds(pl.multiple_of(group * part + start, size), size), :]
        self.gather = Gather(
            ring, own, lambda origin, start, size: full.at[origin, group, pl.ds(start, size), :],
            sends, recvs, part, 1,
        )
        self.keep = pltpu.make_async_copy(own(0, part), full.at[ring.me, group], keep_sem)
        self.mate = (group + 1 - 2 * (group % 2), ring.me)
        self.across = groups // 2

    def peer(self, k):
        return ((self.ring.group + 2 * k) % self.groups, self.ring.me)

    def peers(self):
        return [self.mate] + [self.peer(k) for k in range(1, self.across)]

    def far(self, k, way, step):
        gather = self.gather
        part = self.full.at[gather.origin(way, step), self.ring.group, pl.ds(way * gather.piece, gather.piece), :]
        return pltpu.make_async_remote_copy(
            src_ref=part, dst_ref=part,
            send_sem=self.far_sems.at[0, k - 1, way, step], recv_sem=self.far_sems.at[1, k - 1, way, step],
            device_id=self.peer(k), device_id_type=MESH,
        )

    def near(self, k):
        part = self.full.at[:, (self.ring.group + self.groups - 2 * k) % self.groups]
        return pltpu.make_async_remote_copy(
            src_ref=part, dst_ref=part, send_sem=self.near_sems.at[0, k], recv_sem=self.near_sems.at[1, k],
            device_id=self.mate, device_id_type=MESH,
        )

    def pass_on(self, step):
        for k in range(1, self.across):
            for way in (0, 1):
                self.far(k, way, step).start()

    def begin(self):
        self.gather.begin()
        self.keep.start()

    def hop(self, step):
        self.gather.hop(step)
        self.pass_on(step)

    def exchange(self):
        self.gather.arrived(self.ring.count - 1)
        self.pass_on(self.ring.count - 1)
        self.keep.wait()
        self.pass_on(0)
        self.near(0).start()

    def every_far(self, body):
        def run(step, carry):
            for k in range(1, self.across):
                for way in (0, 1):
                    body(self.far(k, way, step))
            return carry

        lax.fori_loop(0, self.ring.count, run, 0)

    def back(self):
        self.every_far(lambda copy: copy.wait_recv())
        for k in range(1, self.across):
            self.near(k).start()

    def end(self):
        for k in range(self.across):
            self.near(k).wait()
        self.every_far(lambda copy: copy.wait_send())
        self.gather.end()


def gather_kernel(count, tokens, tokens_full, sends, recvs, local):
    ring = Ring(count)
    rows = tokens.shape[0]
    greet(ring)
    keep = pltpu.make_async_copy(
        tokens, tokens_full.at[pl.ds(pl.multiple_of(ring.me * rows, rows), rows), :], local
    )
    keep.start()
    ring_gather(
        Gather(ring, row_own(tokens), row_view(tokens_full, rows), sends, recvs, rows), lambda step: None
    )
    keep.wait()


def gather_tokens(tokens, count):
    rows, model = tokens.shape
    return pl.pallas_call(
        functools.partial(gather_kernel, count),
        name="gather_tokens",
        out_shape=jax.ShapeDtypeStruct((count * rows, model), tokens.dtype),
        in_specs=[ANY],
        out_specs=ANY,
        scratch_shapes=ring_semaphores(count) + [pltpu.SemaphoreType.DMA],
        compiler_params=ring_params(1),
        cost_estimate=pl.CostEstimate(flops=0, bytes_accessed=300 << 20, transcendentals=0),
    )(tokens)


def attend_kernel(
    count, mixed, w_out, tokens, gain, w_gate, w_up, w_down, cotangent,
    resid, full, hidden, grad_gate, grad_up, cotangents,
    gathered, out_box, gate_box, up_box, down_box, mixed_boxes, token_boxes, normed, gates, stages,
    sends, recvs, weight_sems, keep_sem, mixed_sems, token_sems, out_sems, normed_sems, stage_sems,
):
    ring = Ring(count)
    rows = cotangent.shape[0]
    half = rows // 2
    gather = Gather(ring, row_own(cotangent), row_view(gathered, rows), sends, recvs, rows)
    keep = pltpu.make_async_copy(
        cotangent, gathered.at[pl.ds(pl.multiple_of(ring.me * rows, rows), rows), :], keep_sem
    )
    loads = [
        pltpu.make_async_copy(source, box, weight_sems.at[k])
        for k, (source, box) in enumerate(
            ((w_out, out_box), (w_gate, gate_box), (w_up, up_box), (w_down, down_box))
        )
    ]

    def place(way, step):
        return pl.ds(pl.multiple_of(gather.origin(way, step) * rows + way * half, half), half)

    def mixed_copy(way, step):
        return pltpu.make_async_copy(
            mixed.at[:, place(way, step), :], mixed_boxes.at[step % 2, way], mixed_sems.at[step % 2, way]
        )

    def token_copy(way, step):
        return pltpu.make_async_copy(
            tokens.at[place(way, step), :], token_boxes.at[step % 2, way], token_sems.at[step % 2, way]
        )

    def out_copy(way, step):
        at = place(way, step)
        return pltpu.make_async_copy(gathered.at[at, :], cotangents.at[at, :], out_sems.at[way, step])

    def normed_copy(way, step):
        return pltpu.make_async_copy(
            normed.at[step % 2, pl.ds(way * half, half), :], full.at[place(way, step), :],
            normed_sems.at[step % 2, way],
        )

    def stage_copy(k, way, step):
        target = (hidden, grad_gate, grad_up)[k]
        return pltpu.make_async_copy(
            stages.at[step % 2, k, way], target.at[place(way, step), :], stage_sems.at[step % 2, k, way]
        )

    def settle(step):
        for way in (0, 1):
            normed_copy(way, step).wait()
            for k in range(3):
                stage_copy(k, way, step).wait()

    def fetch(step):
        for way in (0, 1):
            mixed_copy(way, step).start()
            token_copy(way, step).start()

    def put(k, step, value):
        low = value.astype(BF16)
        for way in (0, 1):
            stages[step % 2, k, way] = low[way * half : way * half + half]
            stage_copy(k, way, step).start()

    def prepare(step):
        @pl.when(step > 1)
        def _():
            settle(step - 2)

        slot = step % 2
        for way in (0, 1):
            mixed_copy(way, step).wait()
            token_copy(way, step).wait()

        @pl.when(step + 1 < count)
        def _():
            fetch(step + 1)

        heads = jnp.concatenate(
            [
                jnp.concatenate([mixed_boxes[slot, way, j] for j in range(count)], 1)
                for way in (0, 1)
            ],
            0,
        )
        value = jnp.concatenate([token_boxes[slot, 0], token_boxes[slot, 1]], 0).astype(F32)
        value = value + mm(heads, out_box[...])

        @pl.when(step == 0)
        def _():
            resid[...] = value

        scale = lax.rsqrt(jnp.mean(value * value, axis=1, keepdims=True) + 1e-6)
        normed[slot] = (value * scale * gain[...].astype(F32).reshape(1, -1)).astype(BF16)
        for way in (0, 1):
            normed_copy(way, step).start()
        inputs = normed[slot]
        gate = mm(inputs, gate_box[...], (1, 1))
        up = mm(inputs, up_box[...], (1, 1))
        sig = sigmoid(gate)
        opened = gate * sig
        put(0, step, opened * up)
        gates[0] = up * sig * (1.0 + gate * (1.0 - sig))
        gates[1] = opened

    def feed(step):
        for way in (0, 1):
            out_copy(way, step).start()
        grad = mm(
            jnp.concatenate([gathered[place(0, step), :], gathered[place(1, step), :]], 0), down_box[...], (1, 1)
        )
        put(1, step, grad * gates[0])
        put(2, step, grad * gates[1])

    def run(step, carry):
        @pl.when(step == 0)
        def _():
            gather.begin()
            for load in loads:
                load.wait()

        prepare(step)

        @pl.when(step == 0)
        def _():
            keep.wait()

        @pl.when((step > 0) & (step < count - 1))
        def _():
            gather.hop(step)

        @pl.when(step == count - 1)
        def _():
            gather.arrived(step)

        feed(step)
        return carry

    keep.start()
    fetch(0)
    for load in loads:
        load.start()
    greet(ring)
    lax.fori_loop(0, count, run, 0)
    gather.end()
    settle(count - 2)
    settle(count - 1)

    def drain(step, carry):
        for way in (0, 1):
            out_copy(way, step).wait()
        return carry

    lax.fori_loop(0, count, drain, 0)


def attend(mixed, w_out, tokens, gain, w_gate, w_up, w_down, cotangent, count):
    rows, model = cotangent.shape
    slots, inner = count * rows, w_down.shape[0]
    wide = mixed.shape[2]
    return pl.pallas_call(
        functools.partial(attend_kernel, count),
        name="attend",
        out_shape=[
            jax.ShapeDtypeStruct((rows, model), F32),
            jax.ShapeDtypeStruct((slots, model), BF16),
        ]
        + [jax.ShapeDtypeStruct((slots, inner), BF16)] * 3
        + [jax.ShapeDtypeStruct((slots, model), BF16)],
        in_specs=[ANY] * 3 + [VMEM] + [ANY] * 4,
        out_specs=[VMEM] + [ANY] * 5,
        scratch_shapes=[pltpu.VMEM((slots, model), BF16), pltpu.VMEM(w_out.shape, BF16)]
        + [pltpu.VMEM((inner, model), BF16)] * 3
        + [
            pltpu.VMEM((2, 2, count, rows // 2, wide), BF16),
            pltpu.VMEM((2, 2, rows // 2, model), BF16),
            pltpu.VMEM((2, rows, model), BF16),
            pltpu.VMEM((2, rows, inner), F32),
            pltpu.VMEM((2, 3, 2, rows // 2, inner), BF16),
        ]
        + ring_semaphores(count)
        + [
            pltpu.SemaphoreType.DMA((4,)),
            pltpu.SemaphoreType.DMA,
            pltpu.SemaphoreType.DMA((2, 2)),
            pltpu.SemaphoreType.DMA((2, 2)),
            pltpu.SemaphoreType.DMA((2, count)),
            pltpu.SemaphoreType.DMA((2, 2)),
            pltpu.SemaphoreType.DMA((2, 3, 2)),
        ],
        compiler_params=ring_params(2),
        cost_estimate=pl.CostEstimate(
            flops=2 * slots * model * model + 6 * slots * model * inner, bytes_accessed=300 << 20,
            transcendentals=slots * inner,
        ),
    )(mixed, w_out, tokens, gain, w_gate, w_up, w_down, cotangent)


def norm_back(inputs, scale, gain, grad_normed):
    weighted = gain * grad_normed
    inner = jnp.mean(weighted * inputs, axis=1, keepdims=True)
    unit = inputs * scale
    return scale * weighted - unit * (scale * scale * inner), grad_normed * unit


JOBS = 8


def ffn_back_kernel(
    count, groups, rows, grad_gate, grad_up, hidden_in, w_gate, w_up, resid_in, cotangent_in, gain, inputs, cotangents,
    grad_resid, full, grad_gain, sum_gate, sum_up, sum_down,
    slots, low, gw_gate, gw_up, gw_down, boxes, box_sems, hidden, resid, cotangent, load_sems, *rest,
):
    ring = Ring(count)
    sends, recvs, sends_two, recvs_two, local = rest[:5]
    sums = GroupSum(
        ring, groups, (gw_gate, gw_up, gw_down), rest[5:8], rest[8:11], (sum_gate, sum_up, sum_down), *rest[11:]
    )
    wide = boxes.shape[2]

    def box_copy(job, source):
        at = pl.multiple_of(job % (JOBS // 2) * wide, wide)
        return pltpu.make_async_copy(
            source.at[:, pl.ds(at, wide)], boxes.at[job % 2], box_sems.at[job % 2]
        )

    def fetch(job):
        @pl.when(job < JOBS // 2)
        def _():
            box_copy(job, inputs).start()

        @pl.when(job >= JOBS // 2)
        def _():
            box_copy(job, cotangents).start()

    loads = [
        pltpu.make_async_copy(source, target, load_sems.at[k])
        for k, (source, target) in enumerate(((hidden_in, hidden), (resid_in, resid), (cotangent_in, cotangent)))
    ]
    fetch(0)
    for load in loads:
        load.start()
    greet(ring, sums.peers())
    grad_gain[...] = jnp.zeros_like(grad_gain)
    half = rows // 2

    def partial(first, second, step):
        gates = jnp.concatenate([grad_gate[pl.ds(first, half), :], grad_gate[pl.ds(second, half), :]], 0)
        ups = jnp.concatenate([grad_up[pl.ds(first, half), :], grad_up[pl.ds(second, half), :]], 0)
        return mm(gates, w_gate[...]) + mm(ups, w_up[...])

    def finish(start, size, grad):
        value = resid[start : start + size, :]
        scale = lax.rsqrt(jnp.mean(value * value, axis=1, keepdims=True) + 1e-6)
        through, pieces = norm_back(value, scale, gain[...].astype(F32).reshape(1, -1), grad)
        result = cotangent[start : start + size, :].astype(F32) + through
        grad_resid[start : start + size, :] = result
        grad_gain[...] += jnp.sum(pieces, axis=0, keepdims=True)
        low[start : start + size, :] = result.astype(BF16)

    def work(job, carry):
        box_copy(job, inputs).wait()

        @pl.when(job + 1 < JOBS)
        def _():
            fetch(job + 1)

        at = pl.ds(pl.multiple_of(job % (JOBS // 2) * wide, wide), wide)

        @pl.when(job < JOBS // 2)
        def _():
            box = boxes[job % 2]
            gw_gate[:, at] = mm(grad_gate[...], box, (0, 0)).astype(BF16)
            gw_up[:, at] = mm(grad_up[...], box, (0, 0)).astype(BF16)

        @pl.when(job >= JOBS // 2)
        def _():
            gw_down[:, at] = mm(hidden[...], boxes[job % 2], (0, 0)).astype(BF16)

        return carry

    each = JOBS // 4

    def beside_scatter(step):
        @pl.when(step == 2)
        def _():
            for load in loads:
                load.wait()

        @pl.when(step == 3)
        def _():
            sums.second((0, 1))

        @pl.when(step < 4)
        def _():
            lax.fori_loop(step * each, step * each + each, work, 0)

        @pl.when(step == 1)
        def _():
            sums.first((0, 1))

        @pl.when(step == 3)
        def _():
            sums.first((2,))

        @pl.when(step == 5)
        def _():
            sums.second((2,))

    def beside_gather(step):
        @pl.when(step == count - 3)
        def _():
            sums.third((0, 1))

        @pl.when(step == count - 2)
        def _():
            sums.third((2,))

    gather = Gather(ring, row_own(low), row_view(full, rows), sends_two, recvs_two, rows)
    start = lambda way, sub: gather.copy(way, sub, 0, ring.me, True).start()
    ring_scatter(Scatter(ring, partial, slots, sends, recvs, rows, finish, start), beside_scatter)
    keep = pltpu.make_async_copy(low, full.at[pl.ds(pl.multiple_of(ring.me * rows, rows), rows), :], local)
    keep.start()
    ring_gather(gather, beside_gather, True)
    keep.wait()
    sums.last()


def ffn_back(grad_gate, grad_up, hidden, w_gate, w_up, resid, cotangent, gain, inputs, cotangents, count, groups):
    rows, model = resid.shape
    slots, inner = grad_up.shape
    shapes = [(inner, model)] * 3
    return pl.pallas_call(
        functools.partial(ffn_back_kernel, count, groups, rows),
        name="ffn_back",
        out_shape=[
            jax.ShapeDtypeStruct((rows, model), F32),
            jax.ShapeDtypeStruct((slots, model), BF16),
            jax.ShapeDtypeStruct((1, model), F32),
        ]
        + [jax.ShapeDtypeStruct(shape, BF16) for shape in shapes],
        in_specs=[VMEM] * 2 + [ANY] + [VMEM] * 2 + [ANY] * 2 + [VMEM] + [ANY] * 2,
        out_specs=[VMEM, ANY, VMEM] + [ANY] * 3,
        scratch_shapes=[ring_slots(count, rows, model), pltpu.VMEM((rows, model), BF16)]
        + [pltpu.VMEM(shape, BF16) for shape in shapes]
        + [pltpu.VMEM((2, slots, model // (JOBS // 2)), BF16), pltpu.SemaphoreType.DMA((2,))]
        + [pltpu.VMEM((slots, inner), BF16), pltpu.VMEM((rows, model), F32), pltpu.VMEM((rows, model), BF16)]
        + [pltpu.SemaphoreType.DMA((3,))]
        + ring_semaphores(count) * 2
        + [pltpu.SemaphoreType.DMA]
        + sum_scratch(shapes, groups),
        compiler_params=ring_params(3),
        cost_estimate=pl.CostEstimate(
            flops=10 * slots * model * inner, bytes_accessed=600 << 20, transcendentals=0
        ),
    )(grad_gate, grad_up, hidden, w_gate, w_up, resid, cotangent, gain, inputs, cotangents)


def last_kernel(
    count, groups, rows, terms, tokens_in, grad_resid_in, gain, small, *rest,
):
    grads, rest = rest[:5], rest[5:]
    grad_tokens, total = rest[:2]
    targets, rest = rest[2:7], rest[7:]
    slots, first_box, second_box, second_own, boxes, box_sems, tokens, grad_resid, load_sems = rest[:9]
    sends, recvs, first_sends, first_recvs, second_sends, second_recvs = rest[9:15]
    ring = Ring(count)
    sums = GroupSum(ring, groups, grads, rest[15:20], rest[20:25], targets, *rest[25:])
    loads = [
        pltpu.make_async_copy(tokens_in, tokens, load_sems.at[0]),
        pltpu.make_async_copy(grad_resid_in, grad_resid, load_sems.at[1]),
    ]
    me, group = ring.me, ring.group
    first_peers = [(group, (me + k) % count) for k in range(1, count)]
    second_peers = [((group + k) % groups, me) for k in range(1, groups)]
    barrier = pltpu.get_barrier_semaphore()
    for peer in first_peers + second_peers:
        pl.semaphore_signal(barrier, inc=1, device_id=peer, device_id_type=MESH)
    pl.semaphore_wait(barrier, count + groups - 2)

    def first(k):
        return pltpu.make_async_remote_copy(
            src_ref=small.at[0:8], dst_ref=first_box.at[k], send_sem=first_sends.at[k],
            recv_sem=first_recvs.at[k], device_id=first_peers[k], device_id_type=MESH,
        )

    def second(k):
        return pltpu.make_async_remote_copy(
            src_ref=second_own, dst_ref=second_box.at[k], send_sem=second_sends.at[k],
            recv_sem=second_recvs.at[k], device_id=second_peers[k], device_id_type=MESH,
        )

    every = range(len(grads))
    sums.first(every)
    for k in range(count - 1):
        first(k).start()
    half = rows // 2

    def box_copy(way, start, slot):
        return pltpu.make_async_copy(
            terms.at[pl.ds(start, half), :], boxes.at[slot, way], box_sems.at[slot, way]
        )

    def fetch(step):
        for way, owner in ((0, ring.at(-1 - step)), (1, ring.at(1 + step))):
            box_copy(way, pl.multiple_of(owner * rows + way * half, half), step % 2).start()

    def partial(first, second, step):
        for way, start in ((0, first), (1, second)):
            box_copy(way, start, step % 2).wait()

        @pl.when(step + 1 < count)
        def _():
            fetch(step + 1)

        return jnp.concatenate([boxes[step % 2, 0], boxes[step % 2, 1]], 0).astype(F32)

    def finish(start, size, grad):
        value = tokens[start : start + size, :].astype(F32)
        scale = lax.rsqrt(jnp.mean(value * value, axis=1, keepdims=True) + 1e-6)
        through, pieces = norm_back(value, scale, gain[...].astype(F32).reshape(1, -1), grad)
        grad_tokens[start : start + size, :] = grad_resid[start : start + size, :] + through

    def early():
        sums.second(every)
        for k in range(count - 1):
            first(k).wait()
        mine = small[0:8]
        for k in range(count - 1):
            mine = mine + first_box[k]
        second_own[0:8] = mine
        second_own[8:] = small[8:]
        for k in range(groups - 1):
            second(k).start()

    def late():
        for k in range(groups - 1):
            second(k).wait()
        mine = second_own[...]
        for k in range(groups - 1):
            mine = mine + second_box[k]
        total[...] = mine
        for load in loads:
            load.wait()

    def beside(step):
        pl.when(step == 0)(early)
        for i in every:
            pl.when(step == count - 1 - len(every) + i)(lambda i=i: sums.third((i,)))
        pl.when(step == count - 2)(late)

    fetch(0)
    for load in loads:
        load.start()
    ring_scatter(Scatter(ring, partial, slots, sends, recvs, rows, finish), beside)
    sums.last()


def last_step(terms, tokens, grad_resid, gain, small, grads, count, groups):
    rows, model = tokens.shape
    return pl.pallas_call(
        functools.partial(last_kernel, count, groups, rows),
        name="last_step",
        out_shape=[jax.ShapeDtypeStruct((rows, model), F32), jax.ShapeDtypeStruct(small.shape, F32)]
        + [jax.ShapeDtypeStruct(g.shape, BF16) for g in grads],
        in_specs=[ANY] * 3 + [VMEM] * (2 + len(grads)),
        out_specs=[VMEM, VMEM] + [ANY] * len(grads),
        scratch_shapes=[
            ring_slots(count, rows, model),
            pltpu.VMEM((count - 1, 8, model), F32),
            pltpu.VMEM((groups - 1,) + small.shape, F32),
            pltpu.VMEM(small.shape, F32),
            pltpu.VMEM((2, 2, rows // 2, model), BF16),
            pltpu.SemaphoreType.DMA((2, 2)),
            pltpu.VMEM((rows, model), BF16),
            pltpu.VMEM((rows, model), F32),
            pltpu.SemaphoreType.DMA((2,)),
        ]
        + ring_semaphores(count)
        + [pltpu.SemaphoreType.DMA((count - 1,))] * 2
        + [pltpu.SemaphoreType.DMA((groups - 1,))] * 2
        + sum_scratch([g.shape for g in grads], groups),
        compiler_params=ring_params(4),
        cost_estimate=pl.CostEstimate(flops=0, bytes_accessed=300 << 20, transcendentals=0),
    )(terms, tokens, grad_resid, gain, small, *grads)


def results_kernel(heads, taps, wide, width, total, *refs):
    number = (len(refs) - 7) // 2
    for source, target in zip(refs[:number], refs[number : 2 * number]):
        target[...] = source[...].astype(target.dtype)
    g_first, g_second, g_head, gt_query, gt_key, gt_value, g_beta = refs[2 * number :]

    @pl.when(pl.program_id(0) == 0)
    def _():
        g_first[...] = total[0:1, :]
        g_second[...] = total[1:2, :]
        g_head[...] = total[2:3, 0:width]
        row = 8 + heads
        for place, target in enumerate((gt_query, gt_key, gt_value)):
            target[...] = total[row : row + taps, place * wide : (place + 1) * wide]
        g_beta[...] = total[8 : 8 + heads, :]


def results(total, arrays, heads, taps, wide, width):
    model = total.shape[1]
    steps = next(n for n in (2, 1) if all(a.shape[0] % (8 * n) == 0 for a, _ in arrays))
    small = [(1, model), (1, model), (1, width)] + [(taps, wide)] * 3 + [(heads, model)]
    piece = lambda a: pl.BlockSpec((a.shape[0] // steps, a.shape[1]), lambda n: (n, 0))
    whole = lambda shape: pl.BlockSpec(shape, lambda n: (0, 0))
    return pl.pallas_call(
        functools.partial(results_kernel, heads, taps, wide, width),
        name="results",
        grid=(steps,),
        out_shape=[jax.ShapeDtypeStruct(a.shape, kind) for a, kind in arrays]
        + [jax.ShapeDtypeStruct(shape, F32) for shape in small],
        in_specs=[whole(total.shape)] + [piece(a) for a, _ in arrays],
        out_specs=[piece(a) for a, _ in arrays] + [whole(shape) for shape in small],
        compiler_params=pltpu.CompilerParams(vmem_limit_bytes=56 << 20),
        cost_estimate=pl.CostEstimate(flops=0, bytes_accessed=48 << 20, transcendentals=0),
    )(total, *[a for a, _ in arrays])


def spread_hops(step, chunks, count, hop, start=0):
    each = -(-(count - 1) // (chunks - 1))
    for place in range(each):
        number = step * each + place

        @pl.when((number >= start) & (number < count - 1))
        def _():
            hop(number)


def forward_kernel(
    heads, width, seqs, count, groups, chunks,
    starts, lengths, tokens, w_query, w_key, w_value, w_gate, w_beta,
    taps_query, taps_key, taps_value, gain, gain_first, w_out,
    mixed_full, w_full, mixed, p_query, p_key, p_value, p_gate, p_beta, z_query, z_key, z_value,
    delta_out, change_out, inverse_out, state_out,
    tail_query, tail_key, tail_value, state, stage, sends, recvs, keeps,
    w_sends, w_recvs, w_keep, w_far, w_near,
):
    step = pl.program_id(0)
    size = tokens.shape[0]
    first = step * size

    @pl.when(step == 0)
    def _():
        for tail in (tail_query, tail_key, tail_value):
            tail[...] = jnp.zeros_like(tail)
        state[...] = jnp.zeros_like(state)

    ring = Ring(count)

    def chunk_gather(chunk):
        return Gather(
            ring,
            lambda start, length: stage.at[chunk, pl.ds(start, length), :],
            lambda origin, start, length: mixed_full.at[
                origin, pl.ds(pl.multiple_of(chunk * size + start, length), length), :
            ],
            sends.at[chunk], recvs.at[chunk], size, 1,
        )

    def keep(chunk):
        return pltpu.make_async_copy(
            stage.at[chunk],
            mixed_full.at[ring.me, pl.ds(pl.multiple_of(chunk * size, size), size), :],
            keeps.at[chunk],
        )

    weight = WholeWeight(ring, groups, w_out, w_full, w_sends, w_recvs, w_keep, w_far, w_near)
    each = -(-(count - 1) // (chunks - 1))

    def weight_hops():
        for place in range(each):
            number = step * each + place
            pl.when((number > 0) & (number < count - 1))(lambda: weight.hop(number))
            pl.when(number == count - 1)(weight.exchange)

    def chunk_hops():
        for age in range(1, min(count - 1, chunks)):
            pl.when(step >= age)(lambda age=age: chunk_gather(step - age).hop(age))

    @pl.when(step == 0)
    def _():
        greet(ring, weight.peers())
        weight.begin()

    weight_hops()
    rows, seg_rows, seg_columns, before, last = chunk_masks(starts, lengths, seqs, first, size)
    same = seg_rows == seg_columns
    i = lax.broadcasted_iota(jnp.int32, (size, size), 0)
    j = lax.broadcasted_iota(jnp.int32, (size, size), 1)
    strict = jnp.where(same & (i > j), 1.0, 0.0)
    inclusive = jnp.where(same & (i >= j), 1.0, 0.0)
    carried = jnp.where(seg_rows == before, 1.0, 0.0)
    ending = jnp.where(seg_rows == last, 1.0, 0.0)
    kept = jnp.where(before == last, 1.0, 0.0)
    live = jnp.where(seg_rows % 2 == 1, 1.0, 0.0)
    joined = [
        jnp.where(segment_at(rows - offset, starts, lengths, seqs) == seg_rows, 1.0, 0.0)
        for offset in range(1, taps_query.shape[0])
    ]
    inputs = normed_rows(tokens, gain_first)[0].astype(BF16)

    def feature(weight, taps, tail, p_out, z_out):
        projected = jnp.dot(inputs, weight[...], preferred_element_type=F32)
        p_out[...] = projected
        tail[8:, :] = projected
        tap = taps[...].astype(F32)
        result = projected * tap[0:1]
        for offset in range(1, tap.shape[0]):
            result = result + tail[8 - offset : 8 - offset + size, :] * tap[offset : offset + 1] * joined[offset - 1]
        tail[0:8, :] = projected[size - 8 :, :]
        z_out[...] = result
        return result * sigmoid(result)

    u_query = feature(w_query, taps_query, tail_query, p_query, z_query)
    u_key = feature(w_key, taps_key, tail_key, p_key, z_key)
    u_value = feature(w_value, taps_value, tail_value, p_value, z_value)
    gate = jnp.dot(inputs, w_gate[...], preferred_element_type=F32)
    p_gate[...] = gate
    beta_pre = mm(inputs, w_beta[...], (1, 1))
    p_beta[...] = beta_pre
    strength = sigmoid(beta_pre)
    opened = gate * sigmoid(gate)
    scale = width ** (-0.5)
    head_gain = gain[...].astype(F32)
    for h in range(heads):
        if h == heads // 2:
            chunk_hops()
        cols = slice(h * width, (h + 1) * width)
        uq, uk = u_query[:, cols], u_key[:, cols]
        query = (uq * lax.rsqrt(jnp.sum(uq * uq, axis=1, keepdims=True) + 1e-6)).astype(BF16)
        key = (uk * lax.rsqrt(jnp.sum(uk * uk, axis=1, keepdims=True) + 1e-6)).astype(BF16)
        value = u_value[:, cols].astype(BF16).astype(F32)
        beta = strength[:, h : h + 1]
        memory = state[h]
        low_memory = memory.astype(BF16)
        state_out[0, h] = low_memory
        lower = mm(key, key, (1, 1)) * strict * beta
        inverse = inverse_unit_lower(lower, size).astype(BF16)
        inverse_out[0, h] = inverse
        within = mm(query, key, (1, 1)) * inclusive
        change = mm(inverse, beta * (value - carried * mm(key, low_memory)))
        low_change = change.astype(BF16)
        change_out[:, cols] = low_change
        out = scale * (carried * mm(query, low_memory) + mm(within, low_change))
        state[h] = kept * memory + mm(key, ending * change, (0, 0))
        delta_out[:, cols] = out
        normal = out * lax.rsqrt(jnp.mean(out * out, axis=1, keepdims=True) + 1e-5) * head_gain
        low_mixed = (normal * opened[:, cols] * live).astype(BF16)
        mixed[:, cols] = low_mixed
        stage[step, :, cols] = low_mixed

    chunk_gather(step).begin()
    keep(step).start()

    @pl.when(step == chunks - 1)
    def _():
        def finish(number, carry):
            pl.when(number == (count - 1) // 2)(weight.back)
            for age in range(min(count - 1, chunks) - 1, -1, -1):
                pl.when(age + number < count - 1)(
                    lambda age=age: chunk_gather(chunks - 1 - age).hop(age + number)
                )
            return carry

        lax.fori_loop(1, count - 1, finish, 0)

        def settle(chunk, carry):
            chunk_gather(chunk).arrived(count - 1)
            chunk_gather(chunk).end()
            keep(chunk).wait()
            return carry

        lax.fori_loop(0, chunks, settle, 0)
        weight.end()


def forward_mixer(tokens, w_query, w_key, w_value, w_gate, w_beta, taps_query, taps_key, taps_value, gain, gain_first, starts, lengths, w_out, count, groups):
    slots, model = tokens.shape
    wide = w_query.shape[1]
    width = gain.shape[0]
    heads = wide // width
    seqs = starts.shape[1]
    chunks = slots // CHUNK
    taps = taps_query.shape[0]
    part = w_out.shape[0] // groups
    smem = pl.BlockSpec(memory_space=pltpu.SMEM)
    whole = lambda shape: pl.BlockSpec(shape, lambda n: (0,) * len(shape))
    piece = lambda shape: pl.BlockSpec(shape, lambda n: (n,) + (0,) * (len(shape) - 1))
    outs = [
        ((slots, wide), BF16), ((slots, wide), F32), ((slots, wide), F32), ((slots, wide), F32), ((slots, wide), F32),
        ((slots, w_beta.shape[0]), F32), ((slots, wide), F32), ((slots, wide), F32), ((slots, wide), F32),
        ((slots, wide), F32), ((slots, wide), BF16),
    ]
    return pl.pallas_call(
        functools.partial(forward_kernel, heads, width, seqs, count, groups, chunks),
        name="mixer_forward",
        grid=(chunks,),
        out_shape=[
            jax.ShapeDtypeStruct((count, slots, wide), BF16),
            jax.ShapeDtypeStruct((count, groups, part, model), BF16),
        ]
        + [jax.ShapeDtypeStruct(s, d) for s, d in outs]
        + [
            jax.ShapeDtypeStruct((chunks, heads, CHUNK, CHUNK), BF16),
            jax.ShapeDtypeStruct((chunks, heads, width, width), BF16),
        ],
        in_specs=[smem, smem, piece((CHUNK, model))]
        + [whole((model, wide))] * 4
        + [whole(w_beta.shape)]
        + [whole((taps, wide))] * 3
        + [whole((1, width)), VMEM, ANY],
        out_specs=[ANY, ANY]
        + [piece((CHUNK, s[1])) for s, d in outs]
        + [piece((1, heads, CHUNK, CHUNK)), piece((1, heads, width, width))],
        scratch_shapes=[pltpu.VMEM((CHUNK + 8, wide), F32)] * 3
        + [pltpu.VMEM((heads, width, width), F32), pltpu.VMEM((chunks, CHUNK, wide), BF16)]
        + [pltpu.SemaphoreType.DMA((chunks, 2, 1, count - 1))] * 2
        + [pltpu.SemaphoreType.DMA((chunks,))]
        + ring_semaphores(count, 1)
        + [
            pltpu.SemaphoreType.DMA,
            pltpu.SemaphoreType.DMA((2, groups // 2 - 1, 2, count)),
            pltpu.SemaphoreType.DMA((2, groups // 2)),
        ],
        compiler_params=ring_params(5),
        cost_estimate=pl.CostEstimate(
            flops=2 * slots * model * wide * 4 + slots * heads * CHUNK * 2 * CHUNK * 20,
            bytes_accessed=slots * model * 2 + 4 * model * wide * 2 + slots * wide * 36,
            transcendentals=slots * wide * 4,
        ),
    )(starts, lengths, tokens, w_query, w_key, w_value, w_gate, w_beta, taps_query, taps_key, taps_value, gain.reshape(1, width), gain_first, w_out)


def small_rows(heads, taps):
    return -(-(8 + heads + taps) // 8) * 8


def backward_kernel(
    heads, width, seqs, chunks, count, rows_own,
    starts, lengths, tokens, grad_attended, mixed, p_query, p_key, p_value, p_gate, p_beta,
    z_query, z_key, z_value, delta_out, change_in, inverse_in, state_in,
    w_query_in, w_key_in, w_value_in, w_gate_in, w_beta, w_out, taps_query, taps_key, taps_value, gain, gain_first,
    hidden, w_down, resid_in, g_second, grad_normed, gw_query, gw_key, gw_value, gw_gate, gw_out,
    small, output,
    a_query, a_key, a_value, a_gate, a_out, head_query, head_key, head_value, flow,
    w_query, w_key, w_value, w_gate, resid, load_sems, slots, sends, recvs,
):
    step = pl.program_id(0)
    size = tokens.shape[0]
    first = (chunks - 1 - step) * size

    @pl.when(step == 0)
    def _():
        for ref in (a_query, a_key, a_value, a_gate, a_out, small, flow):
            ref[...] = jnp.zeros_like(ref)
        small[1:2, :] = g_second[...]
        for ref in (head_query, head_key, head_value):
            ref[size:, :] = jnp.zeros((8, ref.shape[1]), F32)

    half = rows_own // 2

    def partial(one, two, number):
        return mm(jnp.concatenate([hidden[pl.ds(one, half), :], hidden[pl.ds(two, half), :]], 0), w_down[...])

    def finish(start, length, down):
        output[start : start + length, :] = (resid[start : start + length, :] + down).astype(BF16)

    ring = Ring(count)
    scatter = Scatter(ring, partial, slots, sends, recvs, rows_own, finish)
    loads = [
        pltpu.make_async_copy(source, target, load_sems.at[k])
        for k, (source, target) in enumerate(
            ((w_query_in, w_query), (w_key_in, w_key), (w_value_in, w_value), (w_gate_in, w_gate), (resid_in, resid))
        )
    ]

    @pl.when(step == 0)
    def _():
        for load in loads:
            load.start()
        greet(ring)

    spread_hops(step, chunks, count, scatter.hop)
    rows, seg_rows, seg_columns, before, last = chunk_masks(starts, lengths, seqs, first, size)
    same = seg_rows == seg_columns
    i = lax.broadcasted_iota(jnp.int32, (size, size), 0)
    j = lax.broadcasted_iota(jnp.int32, (size, size), 1)
    strict = jnp.where(same & (i > j), 1.0, 0.0)
    inclusive = jnp.where(same & (i >= j), 1.0, 0.0)
    carried = jnp.where(seg_rows == before, 1.0, 0.0)
    ending = jnp.where(seg_rows == last, 1.0, 0.0)
    kept = jnp.where(before == last, 1.0, 0.0)
    live = jnp.where(seg_rows % 2 == 1, 1.0, 0.0)
    taps = taps_query.shape[0]
    joined = [
        jnp.where(segment_at(rows + offset, starts, lengths, seqs) == seg_rows, 1.0, 0.0)
        for offset in range(1, taps)
    ]
    normal_rows, unit_rows = normed_rows(tokens, gain_first)
    inputs = normal_rows.astype(BF16)
    grad_rows = grad_attended[...]
    grad_mixed = mm(grad_rows, w_out[...], (1, 1))
    a_out[...] += mm(mixed[...], grad_rows, (0, 0))
    strength = sigmoid(p_beta[...])
    scale = width ** (-0.5)
    head_gain = gain[...].astype(F32)

    grads_query, grads_key, grads_value, grads_gate, grads_beta = [], [], [], [], []
    for h in range(heads):
        cols = slice(h * width, (h + 1) * width)
        out = delta_out[:, cols]
        gate = p_gate[:, cols]
        sig_gate = sigmoid(gate)
        silu_gate = gate * sig_gate
        root = lax.rsqrt(jnp.mean(out * out, axis=1, keepdims=True) + 1e-5)
        grad = grad_mixed[:, cols] * live
        unit = out * root
        grads_gate.append(grad * unit * head_gain * (sig_gate * (1.0 + gate * (1.0 - sig_gate))))
        grad_normal = grad * silu_gate
        small[2:3, 0:width] += jnp.sum(grad_normal * unit, axis=0, keepdims=True)
        push = grad_normal * head_gain
        grad_out = scale * root * (push - unit * jnp.mean(push * unit, axis=1, keepdims=True))

        zq, zk, zv = z_query[:, cols], z_key[:, cols], z_value[:, cols]
        sq, sk, sv = sigmoid(zq), sigmoid(zk), sigmoid(zv)
        uq, uk = zq * sq, zk * sk
        nq = lax.rsqrt(jnp.sum(uq * uq, axis=1, keepdims=True) + 1e-6)
        nk = lax.rsqrt(jnp.sum(uk * uk, axis=1, keepdims=True) + 1e-6)
        unit_q, unit_k = uq * nq, uk * nk
        query, key = unit_q.astype(BF16), unit_k.astype(BF16)
        beta = strength[:, h : h + 1]
        change = change_in[:, cols]
        inverse = inverse_in[0, h]
        memory = state_in[0, h]
        flowing = flow[h]
        low_flow = flowing.astype(BF16)
        low_out = grad_out.astype(BF16)

        within = mm(query, key, (1, 1)) * inclusive
        grad_within = (mm(low_out, change, (1, 1)) * inclusive).astype(BF16)
        grad_change = mm(within, low_out, (0, 0)) + ending * mm(key, low_flow)
        grad_mid = mm(inverse, grad_change, (0, 0))
        grad_value = beta * grad_mid
        low_value = grad_value.astype(BF16)
        cross = (mm(low_value, change, (1, 1)) * strict).astype(BF16)
        grad_query = carried * mm(low_out, memory, (1, 1)) + mm(grad_within, key)
        grad_key = (
            mm(grad_within, query, (0, 0))
            + ending * mm(change, low_flow, (1, 1))
            - carried * mm(low_value, memory, (1, 1))
            - mm(cross, key)
            - mm(cross, key, (0, 0))
        )
        flow[h] = (
            kept * flowing
            + mm(query, carried * grad_out, (0, 0))
            - mm(key, carried * grad_value, (0, 0))
        )
        grads_beta.append((1.0 - beta) * jnp.sum(grad_mid * change.astype(F32), axis=1, keepdims=True))
        du_q = nq * (grad_query - unit_q * jnp.sum(grad_query * unit_q, axis=1, keepdims=True))
        du_k = nk * (grad_key - unit_k * jnp.sum(grad_key * unit_k, axis=1, keepdims=True))
        grads_query.append(du_q * sq * (1.0 + zq * (1.0 - sq)))
        grads_key.append(du_k * sk * (1.0 + zk * (1.0 - sk)))
        grads_value.append(grad_value * sv * (1.0 + zv * (1.0 - sv)))

    tap_row = 8 + heads
    wide = heads * width

    def unconv(parts, taps_ref, head, projected, place):
        lanes = slice(place * wide, (place + 1) * wide)
        grad = jnp.concatenate(parts, axis=1)
        head[0:size, :] = grad
        tap = taps_ref[...].astype(F32)
        p = projected[...]
        result = grad * tap[0:1]
        small[tap_row : tap_row + 1, lanes] += jnp.sum(p * grad, axis=0, keepdims=True)
        for offset in range(1, taps):
            moved = head[offset : offset + size, :] * joined[offset - 1]
            result = result + moved * tap[offset : offset + 1]
            row = tap_row + offset
            small[row : row + 1, lanes] += jnp.sum(p * moved, axis=0, keepdims=True)
        head[size:, :] = grad[0:8, :]
        return result.astype(BF16)

    d_query = unconv(grads_query, taps_query, head_query, p_query, 0)
    d_key = unconv(grads_key, taps_key, head_key, p_key, 1)
    d_value = unconv(grads_value, taps_value, head_value, p_value, 2)
    d_gate = jnp.concatenate(grads_gate, axis=1).astype(BF16)
    spare = [jnp.zeros((size, 1), F32)] * (w_beta.shape[0] - heads)
    d_beta = jnp.concatenate(grads_beta + spare, axis=1).astype(BF16)

    @pl.when(step == 0)
    def _():
        for load in loads:
            load.wait()

    grad_inputs = (
        mm(d_query, w_query[...], (1, 1))
        + mm(d_key, w_key[...], (1, 1))
        + mm(d_value, w_value[...], (1, 1))
        + mm(d_gate, w_gate[...], (1, 1))
        + mm(d_beta, w_beta[...])
    )
    grad_normed[...] = grad_inputs.astype(BF16)
    small[0:1, :] += jnp.sum(grad_inputs * unit_rows, axis=0, keepdims=True)
    a_query[...] += mm(inputs, d_query, (0, 0))
    a_key[...] += mm(inputs, d_key, (0, 0))
    a_value[...] += mm(inputs, d_value, (0, 0))
    a_gate[...] += mm(inputs, d_gate, (0, 0))
    small[8 : 8 + heads, :] += mm(d_beta, inputs, (0, 0))[:heads]

    @pl.when(step == chunks - 1)
    def _():
        for target, source in (
            (gw_query, a_query), (gw_key, a_key), (gw_value, a_value), (gw_gate, a_gate),
            (gw_out, a_out),
        ):
            target[...] = source[...].astype(target.dtype)
        scatter.end()


def backward_mixer(tokens, grad_attended, saved, w_query, w_key, w_value, w_gate, w_beta, w_out, taps_query, taps_key, taps_value, gain, gain_first, starts, lengths, hidden, w_down, resid, g_second, count):
    slots, model = tokens.shape
    wide = w_query.shape[1]
    width = gain.shape[0]
    heads = wide // width
    seqs = starts.shape[1]
    chunks = slots // CHUNK
    taps = taps_query.shape[0]
    smem = pl.BlockSpec(memory_space=pltpu.SMEM)
    fixed = lambda shape: pl.BlockSpec(shape, lambda n: (0,) * len(shape), pipeline_mode=pl.Buffered(1))
    piece = lambda shape: pl.BlockSpec(shape, lambda n: (chunks - 1 - n,) + (0,) * (len(shape) - 1))
    rows = lambda a: piece((CHUNK, a.shape[1]))
    outs = (
        [((slots, model), BF16)] + [((model, wide), BF16)] * 4 + [((wide, model), BF16)]
        + [((small_rows(heads, taps), model), F32), (resid.shape, BF16)]
    )
    return pl.pallas_call(
        functools.partial(backward_kernel, heads, width, seqs, chunks, count, slots // count),
        name="mixer_backward",
        grid=(chunks,),
        out_shape=[jax.ShapeDtypeStruct(s, d) for s, d in outs],
        in_specs=[smem, smem, rows(tokens), rows(grad_attended)]
        + [rows(a) for a in saved[:11]]
        + [piece((1, heads, CHUNK, CHUNK)), piece((1, heads, width, width))]
        + [ANY] * 4
        + [fixed(w_beta.shape), fixed((wide, model))]
        + [fixed((taps, wide))] * 3
        + [fixed((1, width)), VMEM, fixed(hidden.shape), fixed(w_down.shape), ANY, fixed(g_second.shape)],
        out_specs=[piece((CHUNK, model))] + [fixed(s) for s, d in outs[1:]],
        scratch_shapes=[pltpu.VMEM((model, wide), F32)] * 4
        + [pltpu.VMEM((wide, model), F32)]
        + [pltpu.VMEM((CHUNK + 8, wide), F32)] * 3
        + [pltpu.VMEM((heads, width, width), F32)]
        + [pltpu.VMEM((model, wide), BF16)] * 4
        + [pltpu.VMEM(resid.shape, F32), pltpu.SemaphoreType.DMA((5,)), ring_slots(count, slots // count, model)]
        + ring_semaphores(count),
        compiler_params=ring_params(6),
        cost_estimate=pl.CostEstimate(
            flops=2 * slots * model * wide * 10 + slots * heads * CHUNK * 2 * CHUNK * 8,
            bytes_accessed=slots * model * 6 + 10 * model * wide * 2 + slots * wide * 36,
            transcendentals=slots * wide * 8,
        ),
    )(starts, lengths, tokens, grad_attended, *saved, w_query, w_key, w_value, w_gate, w_beta, w_out, taps_query, taps_key, taps_value, gain.reshape(1, width), gain_first, hidden, w_down, resid, g_second)


def make_shards(groups, count):
    def shards(
        tokens, attn_gain, w_query, w_key, w_value, conv_query, conv_key, conv_value, w_beta, w_gate_out,
        head_gain, w_out, ffn_gain, w_gate, w_up, w_down, seq_starts, seq_lengths, cotangent,
    ):
        model = tokens.shape[1]
        heads = w_beta.shape[1]
        beta_rows = w_beta.T if heads > 1 else jnp.pad(w_beta.T, ((0, 1), (0, 0)))
        tokens_full = gather_tokens(tokens, count)
        mixed_full, w_out_full, *saved = forward_mixer(
            tokens_full, w_query, w_key, w_value, w_gate_out, beta_rows,
            conv_query, conv_key, conv_value, head_gain, attn_gain, seq_starts, seq_lengths, w_out, count, groups,
        )
        w_out_full = w_out_full.reshape(-1, tokens.shape[1])
        resid, ffn_full, hidden, grad_gate, grad_up, grad_full = attend(
            mixed_full, w_out_full, tokens_full, ffn_gain, w_gate.T, w_up.T, w_down, cotangent, count
        )
        grad_resid, grad_attended, g_second, *ffn_grads = ffn_back(
            grad_gate, grad_up, hidden, w_gate.T, w_up.T, resid, cotangent, ffn_gain, ffn_full, grad_full,
            count, groups,
        )
        pulled = backward_mixer(
            tokens_full, grad_attended, saved, w_query, w_key, w_value, w_gate_out, beta_rows, w_out,
            conv_query, conv_key, conv_value, head_gain, attn_gain, seq_starts, seq_lengths,
            hidden, w_down, resid, g_second, count,
        )
        terms, gw_query, gw_key, gw_value, gw_gate_out, gw_out, small, output = pulled
        grad_tokens, total, *mixer_grads = last_step(
            terms, tokens, grad_resid, attn_gain, small,
            (gw_query, gw_key, gw_value, gw_gate_out, gw_out), count, groups,
        )
        taps, wide = conv_query.shape
        output, grad_tokens, *rest = results(
            total,
            [(output, BF16), (grad_tokens, F32)] + [(g, F32) for g in (*mixer_grads, *ffn_grads)],
            heads, taps, wide, head_gain.shape[0],
        )
        grads, (g_first, g_second, g_head, gt_query, gt_key, gt_value, g_beta) = rest[:8], rest[8:]
        return (
            output,
            grad_tokens,
            g_first[0],
            grads[0],
            grads[1],
            grads[2],
            gt_query,
            gt_key,
            gt_value,
            g_beta.T,
            grads[3],
            g_head[0],
            grads[4],
            g_second[0],
            grads[5].T,
            grads[6].T,
            grads[7],
        )

    return shards


def solution(mesh):
    placed = (
        P(("dp", "tensor"), None),
        P(),
        P(None, "tensor"),
        P(None, "tensor"),
        P(None, "tensor"),
        P(None, "tensor"),
        P(None, "tensor"),
        P(None, "tensor"),
        P(None, "tensor"),
        P(None, "tensor"),
        P(),
        P("tensor", None),
        P(),
        P(None, "tensor"),
        P(None, "tensor"),
        P("tensor", None),
        P("dp", None),
        P("dp", None),
        P(("dp", "tensor"), None),
    )
    return jax.shard_map(
        make_shards(mesh.shape["dp"], mesh.shape["tensor"]),
        mesh=mesh,
        in_specs=placed,
        out_specs=(
            P(("dp", "tensor"), None),
            P(("dp", "tensor"), None),
            P(),
            P(None, "tensor"),
            P(None, "tensor"),
            P(None, "tensor"),
            P(None, "tensor"),
            P(None, "tensor"),
            P(None, "tensor"),
            P(None, "tensor"),
            P(None, "tensor"),
            P(),
            P("tensor", None),
            P(),
            P(None, "tensor"),
            P(None, "tensor"),
            P("tensor", None),
        ),
        check_vma=False,
    )
```

```python
import functools
import jax
import jax.numpy as jnp
from jax import lax
from jax.experimental import pallas as pl
from jax.experimental.pallas import tpu as pltpu
from jax.sharding import PartitionSpec as P

CHUNK = 256
F32, BF16 = jnp.float32, jnp.bfloat16


def mm(a, b, contract=(1, 0)):
    return lax.dot_general(
        a.astype(BF16),
        b.astype(BF16),
        (((contract[0],), (contract[1],)), ((), ())),
        preferred_element_type=F32,
    )


def segment_at(places, starts, lengths, seqs):
    segment = jnp.zeros_like(places)
    for s in range(seqs):
        begin = starts[0, s]
        stop = begin + lengths[0, s]
        segment = segment + jnp.where(places >= begin, 1, 0) + jnp.where(places >= stop, 1, 0)
    return jnp.where(places < 0, -1, segment)


def chunk_masks(starts, lengths, seqs, first, size):
    rows = first + lax.broadcasted_iota(jnp.int32, (size, 1), 0)
    columns = first + lax.broadcasted_iota(jnp.int32, (1, size), 1)
    seg_rows = segment_at(rows, starts, lengths, seqs)
    seg_columns = segment_at(columns, starts, lengths, seqs)
    before = segment_at(jnp.full((1, 1), first - 1, jnp.int32), starts, lengths, seqs)
    last = segment_at(jnp.full((1, 1), first + size - 1, jnp.int32), starts, lengths, seqs)
    return rows, seg_rows, seg_columns, before, last


def inverse_unit_lower(lower, size):
    i = lax.broadcasted_iota(jnp.int32, (size, size), 0)
    j = lax.broadcasted_iota(jnp.int32, (size, size), 1)

    def corner(width):
        shift = width.bit_length() - 1
        pair = (i >> (shift + 1)) == (j >> (shift + 1))
        return pair & (((i >> shift) & 1) == 1) & (((j >> shift) & 1) == 0)

    inverse = jnp.where(i == j, 1.0, 0.0) - jnp.where(corner(1), lower, 0.0)
    width = 2
    while width < size:
        low = inverse.astype(BF16)
        if 2 * width == size:
            part = mm(mm(low[width:, width:], lower[width:, :width]), low[:width, :width])
            inverse = jnp.concatenate(
                [
                    inverse[:width],
                    jnp.concatenate([-part, inverse[width:, width:]], axis=1),
                ],
                axis=0,
            )
        else:
            between = jnp.where(corner(width), lower, 0.0)
            inverse = inverse - mm(mm(low, between), low)
        width *= 2
    return inverse


def sigmoid(v):
    return 1.0 / (1.0 + jnp.exp(-v))


def normed_rows(tokens, gain):
    value = tokens[...].astype(F32)
    unit = value * lax.rsqrt(jnp.mean(value * value, axis=1, keepdims=True) + 1e-6)
    return unit * gain[...].astype(F32).reshape(1, -1), unit


MESH = pl.DeviceIdType.MESH
SUBS = 2
PAIRS = [(sub, way) for sub in range(SUBS) for way in (0, 1)]


def ring_position(device, count):
    half, odd = device // 2, device % 2
    return half + odd * (count - 1 - 2 * half)


def ring_device(position, count):
    back = position // (count // 2)
    return (1 - back) * 2 * position + back * (2 * (count - 1 - position) + 1)


class Ring:
    def __init__(self, count):
        self.count = count
        self.me = lax.axis_index("tensor")
        self.place = ring_position(self.me, count)
        self.group = lax.axis_index("dp")

    def at(self, offset):
        return ring_device((self.place + offset + 2 * self.count) % self.count, self.count)

    def next(self, way):
        return (self.group, self.at(1 if way == 0 else -1))


class Gather:
    def __init__(self, ring, own, view, sends, recvs, rows, subs=SUBS):
        self.ring, self.own, self.view, self.sends, self.recvs, self.rows = ring, own, view, sends, recvs, rows
        self.piece = rows // (2 * subs)
        self.pairs = [(sub, way) for sub in range(subs) for way in (0, 1)]

    def origin(self, way, step):
        return self.ring.at(-step if way == 0 else step)

    def copy(self, way, sub, step, origin, first=False):
        inside = way * (self.rows // 2) + sub * self.piece
        place = self.view(origin, inside, self.piece)
        return pltpu.make_async_remote_copy(
            src_ref=self.own(inside, self.piece) if first else place,
            dst_ref=place,
            send_sem=self.sends.at[way, sub, step],
            recv_sem=self.recvs.at[way, sub, step],
            device_id=self.ring.next(way),
            device_id_type=MESH,
        )

    def begin(self):
        for sub, way in self.pairs:
            self.copy(way, sub, 0, self.ring.me, True).start()

    def arrived(self, step):
        for sub, way in self.pairs:
            self.copy(way, sub, step - 1, self.origin(way, step)).wait_recv()

    def hop(self, step):
        for sub, way in self.pairs:
            self.copy(way, sub, step - 1, self.origin(way, step)).wait_recv()
            self.copy(way, sub, step, self.origin(way, step)).start()

    def end(self):
        def drain(step, carry):
            for sub, way in self.pairs:
                self.copy(way, sub, step, self.ring.me).wait_send()
            return carry

        lax.fori_loop(0, self.ring.count - 1, drain, 0)


def row_view(ref, rows):
    return lambda origin, start, size: ref.at[pl.ds(pl.multiple_of(origin * rows + start, size), size), :]


def row_own(ref):
    return lambda start, size: ref.at[pl.ds(start, size), :]


def ring_gather(gather, between, begun=False):
    count = gather.ring.count

    def run(step, carry):
        if not begun:
            pl.when(step == 0)(gather.begin)

        @pl.when((step > 0) & (step < count - 1))
        def _():
            gather.hop(step)

        @pl.when(step == count - 1)
        def _():
            gather.arrived(step)

        between(step)
        return carry

    lax.fori_loop(0, count, run, 0)
    gather.end()


def scatter_copy(ring, slots, sends, recvs, way, sub, step):
    return pltpu.make_async_remote_copy(
        src_ref=slots.at[way, sub, step],
        dst_ref=slots.at[way, sub, step + 1],
        send_sem=sends.at[way, sub, step],
        recv_sem=recvs.at[way, sub, step],
        device_id=ring.next(way),
        device_id_type=MESH,
    )


class Scatter:
    def __init__(self, ring, partial, slots, sends, recvs, rows, finish, after=None):
        self.after = after
        self.ring, self.partial, self.slots, self.sends, self.recvs = ring, partial, slots, sends, recvs
        self.half, self.finish = rows // 2, finish
        self.rows, self.piece = rows, rows // (2 * SUBS)

    def terms(self, step):
        half, first, second = self.half, self.ring.at(-1 - step), self.ring.at(1 + step)
        return self.partial(
            pl.multiple_of(first * self.rows, half), pl.multiple_of(second * self.rows + half, half), step
        )

    def part(self, terms, way, sub):
        start = way * self.half + sub * self.piece
        return terms[start : start + self.piece]

    def copy(self, way, sub, step):
        return scatter_copy(self.ring, self.slots, self.sends, self.recvs, way, sub, step)

    def hop(self, step):
        self.pass_on(step, self.terms(step))

    def pass_on(self, step, terms):
        for sub, way in PAIRS:
            term = self.part(terms, way, sub)

            @pl.when(step == 0)
            def _():
                self.slots[way, sub, 0] = term.astype(BF16)

            @pl.when(step > 0)
            def _():
                self.copy(way, sub, step - 1).wait_recv()
                self.slots[way, sub, step] = (self.slots[way, sub, step].astype(F32) + term).astype(BF16)

            self.copy(way, sub, step).start()

    def end(self):
        self.take(self.terms(self.ring.count - 1))
        self.drain()

    def take(self, terms):
        count = self.ring.count
        for sub, way in PAIRS:
            self.copy(way, sub, count - 2).wait_recv()
            self.finish(
                way * self.half + sub * self.piece,
                self.piece,
                self.slots[way, sub, count - 1].astype(F32) + self.part(terms, way, sub),
            )
            if self.after is not None:
                self.after(way, sub)

    def drain(self):
        def run(step, carry):
            for sub, way in PAIRS:
                self.copy(way, sub, step).wait_send()
            return carry

        lax.fori_loop(0, self.ring.count - 1, run, 0)


def ring_scatter(scatter, between):
    count = scatter.ring.count

    def run(step, carry):
        terms = scatter.terms(step)
        pl.when(step < count - 1)(lambda: scatter.pass_on(step, terms))
        pl.when(step == count - 1)(lambda: scatter.take(terms))
        between(step)
        return carry

    lax.fori_loop(0, count, run, 0)
    scatter.drain()


class GroupSum:
    def __init__(self, ring, groups, grads, near, far, targets, near_sems, far_sems, back_sems, keep_sems):
        self.ring, self.groups, self.grads, self.near, self.far, self.targets = ring, groups, grads, near, far, targets
        self.near_sems, self.far_sems, self.back_sems, self.keep_sems = near_sems, far_sems, back_sems, keep_sems
        self.core = ring.group % 2
        self.mate = (ring.group + 1 - 2 * self.core, ring.me)

    def peers(self):
        return [self.mate] + [
            ((self.ring.group + 2 * k) % self.groups, self.ring.me) for k in range(1, self.groups // 2)
        ]

    def half(self, i, core):
        rows = self.near[i].shape[0]
        return pl.ds(pl.multiple_of(core * rows, rows), rows)

    def near_copy(self, i):
        return pltpu.make_async_remote_copy(
            src_ref=self.grads[i].at[self.half(i, 1 - self.core), :], dst_ref=self.near[i],
            send_sem=self.near_sems.at[0, i], recv_sem=self.near_sems.at[1, i],
            device_id=self.mate, device_id_type=MESH,
        )

    def far_copy(self, i, k):
        return pltpu.make_async_remote_copy(
            src_ref=self.near[i], dst_ref=self.far[i].at[k - 1],
            send_sem=self.far_sems.at[0, i, k - 1], recv_sem=self.far_sems.at[1, i, k - 1],
            device_id=((self.ring.group + 2 * k) % self.groups, self.ring.me), device_id_type=MESH,
        )

    def back_copy(self, i):
        return pltpu.make_async_remote_copy(
            src_ref=self.far[i].at[0], dst_ref=self.targets[i].at[self.half(i, self.core), :],
            send_sem=self.back_sems.at[0, i], recv_sem=self.back_sems.at[1, i],
            device_id=self.mate, device_id_type=MESH,
        )

    def keep_copy(self, i):
        return pltpu.make_async_copy(
            self.far[i].at[0], self.targets[i].at[self.half(i, self.core), :], self.keep_sems.at[i]
        )

    def first(self, chosen):
        for i in chosen:
            self.near_copy(i).start()

    def each_block(self, i, body):
        rows = self.near[i].shape[0]
        block = next(size for size in (64, 32, 16) if rows % size == 0)

        def step(at, carry):
            start = pl.multiple_of(at * block, block)
            body(pl.ds(start, block), pl.ds(pl.multiple_of(self.core * rows + start, block), block))
            return carry

        lax.fori_loop(0, rows // block, step, 0)

    def second(self, chosen):
        for i in chosen:
            self.near_copy(i).wait_recv()

            def add(here, own, i=i):
                self.near[i][here, :] = (
                    self.near[i][here, :].astype(F32) + self.grads[i][own, :].astype(F32)
                ).astype(BF16)

            self.each_block(i, add)
            for k in range(1, self.groups // 2):
                self.far_copy(i, k).start()

    def third(self, chosen):
        for i in chosen:
            for k in range(1, self.groups // 2):
                self.far_copy(i, k).wait()

            def add(here, own, i=i):
                total = self.near[i][here, :].astype(F32)
                for k in range(self.groups // 2 - 1):
                    total = total + self.far[i][k, here, :].astype(F32)
                self.far[i][0, here, :] = total.astype(BF16)

            self.each_block(i, add)
            self.keep_copy(i).start()
            self.back_copy(i).start()

    def last(self):
        for i in range(len(self.grads)):
            self.near_copy(i).wait_send()
            self.back_copy(i).wait()
            self.keep_copy(i).wait()


def sum_scratch(shapes, groups):
    number = len(shapes)
    return (
        [pltpu.VMEM((rows // 2, columns), BF16) for rows, columns in shapes]
        + [pltpu.VMEM((groups // 2 - 1, rows // 2, columns), BF16) for rows, columns in shapes]
        + [
            pltpu.SemaphoreType.DMA((2, number)),
            pltpu.SemaphoreType.DMA((2, number, groups // 2 - 1)),
            pltpu.SemaphoreType.DMA((2, number)),
            pltpu.SemaphoreType.DMA((number,)),
        ]
    )


def greet(ring, others=()):
    barrier = pltpu.get_barrier_semaphore()
    peers = [ring.next(0), ring.next(1)] + list(others)
    for peer in peers:
        pl.semaphore_signal(barrier, inc=1, device_id=peer, device_id_type=MESH)
    pl.semaphore_wait(barrier, len(peers))


def ring_semaphores(count, subs=SUBS):
    return [pltpu.SemaphoreType.DMA((2, subs, count - 1))] * 2


def ring_slots(count, rows, columns):
    return pltpu.VMEM((2, SUBS, count, rows // (2 * SUBS), columns), BF16)


ANY = pl.BlockSpec(memory_space=pl.ANY)
VMEM = pl.BlockSpec(memory_space=pltpu.VMEM)


def ring_params(number):
    return pltpu.CompilerParams(
        collective_id=number, has_side_effects=True, vmem_limit_bytes=60 << 20
    )


class WholeWeight:
    def __init__(self, ring, groups, weight, full, sends, recvs, keep_sem, far_sems, near_sems):
        self.ring, self.groups, self.full, self.far_sems, self.near_sems = ring, groups, full, far_sems, near_sems
        part = weight.shape[0] // groups
        group = ring.group
        own = lambda start, size: weight.at[pl.ds(pl.multiple_of(group * part + start, size), size), :]
        self.gather = Gather(
            ring, own, lambda origin, start, size: full.at[origin, group, pl.ds(start, size), :],
            sends, recvs, part, 1,
        )
        self.keep = pltpu.make_async_copy(own(0, part), full.at[ring.me, group], keep_sem)
        self.mate = (group + 1 - 2 * (group % 2), ring.me)
        self.across = groups // 2

    def peer(self, k):
        return ((self.ring.group + 2 * k) % self.groups, self.ring.me)

    def peers(self):
        return [self.mate] + [self.peer(k) for k in range(1, self.across)]

    def far(self, k, way, step):
        gather = self.gather
        part = self.full.at[gather.origin(way, step), self.ring.group, pl.ds(way * gather.piece, gather.piece), :]
        return pltpu.make_async_remote_copy(
            src_ref=part, dst_ref=part,
            send_sem=self.far_sems.at[0, k - 1, way, step], recv_sem=self.far_sems.at[1, k - 1, way, step],
            device_id=self.peer(k), device_id_type=MESH,
        )

    def near(self, k):
        part = self.full.at[:, (self.ring.group + self.groups - 2 * k) % self.groups]
        return pltpu.make_async_remote_copy(
            src_ref=part, dst_ref=part, send_sem=self.near_sems.at[0, k], recv_sem=self.near_sems.at[1, k],
            device_id=self.mate, device_id_type=MESH,
        )

    def pass_on(self, step):
        for k in range(1, self.across):
            for way in (0, 1):
                self.far(k, way, step).start()

    def begin(self):
        self.gather.begin()
        self.keep.start()

    def hop(self, step):
        self.gather.hop(step)
        self.pass_on(step)

    def exchange(self):
        self.gather.arrived(self.ring.count - 1)
        self.pass_on(self.ring.count - 1)
        self.keep.wait()
        self.pass_on(0)
        self.near(0).start()

    def every_far(self, body):
        def run(step, carry):
            for k in range(1, self.across):
                for way in (0, 1):
                    body(self.far(k, way, step))
            return carry

        lax.fori_loop(0, self.ring.count, run, 0)

    def back(self):
        self.every_far(lambda copy: copy.wait_recv())
        for k in range(1, self.across):
            self.near(k).start()

    def end(self):
        for k in range(self.across):
            self.near(k).wait()
        self.every_far(lambda copy: copy.wait_send())
        self.gather.end()


def gather_kernel(count, tokens, tokens_full, sends, recvs, local):
    ring = Ring(count)
    rows = tokens.shape[0]
    greet(ring)
    keep = pltpu.make_async_copy(
        tokens, tokens_full.at[pl.ds(pl.multiple_of(ring.me * rows, rows), rows), :], local
    )
    keep.start()
    ring_gather(
        Gather(ring, row_own(tokens), row_view(tokens_full, rows), sends, recvs, rows), lambda step: None
    )
    keep.wait()


def gather_tokens(tokens, count):
    rows, model = tokens.shape
    return pl.pallas_call(
        functools.partial(gather_kernel, count),
        name="gather_tokens",
        out_shape=jax.ShapeDtypeStruct((count * rows, model), tokens.dtype),
        in_specs=[ANY],
        out_specs=ANY,
        scratch_shapes=ring_semaphores(count) + [pltpu.SemaphoreType.DMA],
        compiler_params=ring_params(1),
        cost_estimate=pl.CostEstimate(flops=0, bytes_accessed=300 << 20, transcendentals=0),
    )(tokens)


def attend_kernel(
    count, mixed, w_out, tokens, gain, w_gate, w_up, w_down, cotangent,
    resid, full, hidden, grad_gate, grad_up, cotangents,
    gathered, out_box, gate_box, up_box, down_box, mixed_boxes, token_boxes, normed, gates, stages,
    sends, recvs, weight_sems, keep_sem, mixed_sems, token_sems, out_sems, normed_sems, stage_sems,
):
    ring = Ring(count)
    rows = cotangent.shape[0]
    half = rows // 2
    gather = Gather(ring, row_own(cotangent), row_view(gathered, rows), sends, recvs, rows)
    keep = pltpu.make_async_copy(
        cotangent, gathered.at[pl.ds(pl.multiple_of(ring.me * rows, rows), rows), :], keep_sem
    )
    loads = [
        pltpu.make_async_copy(source, box, weight_sems.at[k])
        for k, (source, box) in enumerate(
            ((w_out, out_box), (w_gate, gate_box), (w_up, up_box), (w_down, down_box))
        )
    ]

    def place(way, step):
        return pl.ds(pl.multiple_of(gather.origin(way, step) * rows + way * half, half), half)

    def mixed_copy(way, step):
        return pltpu.make_async_copy(
            mixed.at[:, place(way, step), :], mixed_boxes.at[step % 2, way], mixed_sems.at[step % 2, way]
        )

    def token_copy(way, step):
        return pltpu.make_async_copy(
            tokens.at[place(way, step), :], token_boxes.at[step % 2, way], token_sems.at[step % 2, way]
        )

    def out_copy(way, step):
        at = place(way, step)
        return pltpu.make_async_copy(gathered.at[at, :], cotangents.at[at, :], out_sems.at[way, step])

    def normed_copy(way, step):
        return pltpu.make_async_copy(
            normed.at[step % 2, pl.ds(way * half, half), :], full.at[place(way, step), :],
            normed_sems.at[step % 2, way],
        )

    def stage_copy(k, way, step):
        target = (hidden, grad_gate, grad_up)[k]
        return pltpu.make_async_copy(
            stages.at[step % 2, k, way], target.at[place(way, step), :], stage_sems.at[step % 2, k, way]
        )

    def settle(step):
        for way in (0, 1):
            normed_copy(way, step).wait()
            for k in range(3):
                stage_copy(k, way, step).wait()

    def fetch(step):
        for way in (0, 1):
            mixed_copy(way, step).start()
            token_copy(way, step).start()

    def put(k, step, value):
        low = value.astype(BF16)
        for way in (0, 1):
            stages[step % 2, k, way] = low[way * half : way * half + half]
            stage_copy(k, way, step).start()

    def prepare(step):
        @pl.when(step > 1)
        def _():
            settle(step - 2)

        slot = step % 2
        for way in (0, 1):
            mixed_copy(way, step).wait()
            token_copy(way, step).wait()

        @pl.when(step + 1 < count)
        def _():
            fetch(step + 1)

        heads = jnp.concatenate(
            [
                jnp.concatenate([mixed_boxes[slot, way, j] for j in range(count)], 1)
                for way in (0, 1)
            ],
            0,
        )
        value = jnp.concatenate([token_boxes[slot, 0], token_boxes[slot, 1]], 0).astype(F32)
        value = value + mm(heads, out_box[...])

        @pl.when(step == 0)
        def _():
            resid[...] = value

        scale = lax.rsqrt(jnp.mean(value * value, axis=1, keepdims=True) + 1e-6)
        normed[slot] = (value * scale * gain[...].astype(F32).reshape(1, -1)).astype(BF16)
        for way in (0, 1):
            normed_copy(way, step).start()
        inputs = normed[slot]
        gate = mm(inputs, gate_box[...], (1, 1))
        up = mm(inputs, up_box[...], (1, 1))
        sig = sigmoid(gate)
        opened = gate * sig
        put(0, step, opened * up)
        gates[0] = up * sig * (1.0 + gate * (1.0 - sig))
        gates[1] = opened

    def feed(step):
        for way in (0, 1):
            out_copy(way, step).start()
        grad = mm(
            jnp.concatenate([gathered[place(0, step), :], gathered[place(1, step), :]], 0), down_box[...], (1, 1)
        )
        put(1, step, grad * gates[0])
        put(2, step, grad * gates[1])

    def run(step, carry):
        @pl.when(step == 0)
        def _():
            gather.begin()
            for load in loads:
                load.wait()

        prepare(step)

        @pl.when(step == 0)
        def _():
            keep.wait()

        @pl.when((step > 0) & (step < count - 1))
        def _():
            gather.hop(step)

        @pl.when(step == count - 1)
        def _():
            gather.arrived(step)

        feed(step)
        return carry

    keep.start()
    fetch(0)
    for load in loads:
        load.start()
    greet(ring)
    lax.fori_loop(0, count, run, 0)
    gather.end()
    settle(count - 2)
    settle(count - 1)

    def drain(step, carry):
        for way in (0, 1):
            out_copy(way, step).wait()
        return carry

    lax.fori_loop(0, count, drain, 0)


def attend(mixed, w_out, tokens, gain, w_gate, w_up, w_down, cotangent, count):
    rows, model = cotangent.shape
    slots, inner = count * rows, w_down.shape[0]
    wide = mixed.shape[2]
    return pl.pallas_call(
        functools.partial(attend_kernel, count),
        name="attend",
        out_shape=[
            jax.ShapeDtypeStruct((rows, model), F32),
            jax.ShapeDtypeStruct((slots, model), BF16),
        ]
        + [jax.ShapeDtypeStruct((slots, inner), BF16)] * 3
        + [jax.ShapeDtypeStruct((slots, model), BF16)],
        in_specs=[ANY] * 3 + [VMEM] + [ANY] * 4,
        out_specs=[VMEM] + [ANY] * 5,
        scratch_shapes=[pltpu.VMEM((slots, model), BF16), pltpu.VMEM(w_out.shape, BF16)]
        + [pltpu.VMEM((inner, model), BF16)] * 3
        + [
            pltpu.VMEM((2, 2, count, rows // 2, wide), BF16),
            pltpu.VMEM((2, 2, rows // 2, model), BF16),
            pltpu.VMEM((2, rows, model), BF16),
            pltpu.VMEM((2, rows, inner), F32),
            pltpu.VMEM((2, 3, 2, rows // 2, inner), BF16),
        ]
        + ring_semaphores(count)
        + [
            pltpu.SemaphoreType.DMA((4,)),
            pltpu.SemaphoreType.DMA,
            pltpu.SemaphoreType.DMA((2, 2)),
            pltpu.SemaphoreType.DMA((2, 2)),
            pltpu.SemaphoreType.DMA((2, count)),
            pltpu.SemaphoreType.DMA((2, 2)),
            pltpu.SemaphoreType.DMA((2, 3, 2)),
        ],
        compiler_params=ring_params(2),
        cost_estimate=pl.CostEstimate(
            flops=2 * slots * model * model + 6 * slots * model * inner, bytes_accessed=300 << 20,
            transcendentals=slots * inner,
        ),
    )(mixed, w_out, tokens, gain, w_gate, w_up, w_down, cotangent)


def norm_back(inputs, scale, gain, grad_normed):
    weighted = gain * grad_normed
    inner = jnp.mean(weighted * inputs, axis=1, keepdims=True)
    unit = inputs * scale
    return scale * weighted - unit * (scale * scale * inner), grad_normed * unit


JOBS = 8


def ffn_back_kernel(
    count, groups, rows, grad_gate, grad_up, hidden_in, w_gate, w_up, resid_in, cotangent_in, gain, inputs, cotangents,
    grad_resid, full, grad_gain, sum_gate, sum_up, sum_down,
    slots, low, gw_gate, gw_up, gw_down, boxes, box_sems, hidden, resid, cotangent, load_sems, *rest,
):
    ring = Ring(count)
    sends, recvs, sends_two, recvs_two, local = rest[:5]
    sums = GroupSum(
        ring, groups, (gw_gate, gw_up, gw_down), rest[5:8], rest[8:11], (sum_gate, sum_up, sum_down), *rest[11:]
    )
    wide = boxes.shape[2]

    def box_copy(job, source):
        at = pl.multiple_of(job % (JOBS // 2) * wide, wide)
        return pltpu.make_async_copy(
            source.at[:, pl.ds(at, wide)], boxes.at[job % 2], box_sems.at[job % 2]
        )

    def fetch(job):
        @pl.when(job < JOBS // 2)
        def _():
            box_copy(job, inputs).start()

        @pl.when(job >= JOBS // 2)
        def _():
            box_copy(job, cotangents).start()

    loads = [
        pltpu.make_async_copy(source, target, load_sems.at[k])
        for k, (source, target) in enumerate(((hidden_in, hidden), (resid_in, resid), (cotangent_in, cotangent)))
    ]
    fetch(0)
    for load in loads:
        load.start()
    greet(ring, sums.peers())
    grad_gain[...] = jnp.zeros_like(grad_gain)
    half = rows // 2

    def partial(first, second, step):
        gates = jnp.concatenate([grad_gate[pl.ds(first, half), :], grad_gate[pl.ds(second, half), :]], 0)
        ups = jnp.concatenate([grad_up[pl.ds(first, half), :], grad_up[pl.ds(second, half), :]], 0)
        return mm(gates, w_gate[...]) + mm(ups, w_up[...])

    def finish(start, size, grad):
        value = resid[start : start + size, :]
        scale = lax.rsqrt(jnp.mean(value * value, axis=1, keepdims=True) + 1e-6)
        through, pieces = norm_back(value, scale, gain[...].astype(F32).reshape(1, -1), grad)
        result = cotangent[start : start + size, :].astype(F32) + through
        grad_resid[start : start + size, :] = result
        grad_gain[...] += jnp.sum(pieces, axis=0, keepdims=True)
        low[start : start + size, :] = result.astype(BF16)

    def work(job, carry):
        box_copy(job, inputs).wait()

        @pl.when(job + 1 < JOBS)
        def _():
            fetch(job + 1)

        at = pl.ds(pl.multiple_of(job % (JOBS // 2) * wide, wide), wide)

        @pl.when(job < JOBS // 2)
        def _():
            box = boxes[job % 2]
            gw_gate[:, at] = mm(grad_gate[...], box, (0, 0)).astype(BF16)
            gw_up[:, at] = mm(grad_up[...], box, (0, 0)).astype(BF16)

        @pl.when(job >= JOBS // 2)
        def _():
            gw_down[:, at] = mm(hidden[...], boxes[job % 2], (0, 0)).astype(BF16)

        return carry

    each = JOBS // 4

    def beside_scatter(step):
        @pl.when(step == 2)
        def _():
            for load in loads:
                load.wait()

        @pl.when(step == 3)
        def _():
            sums.second((0, 1))

        @pl.when(step < 4)
        def _():
            lax.fori_loop(step * each, step * each + each, work, 0)

        @pl.when(step == 1)
        def _():
            sums.first((0, 1))

        @pl.when(step == 3)
        def _():
            sums.first((2,))

        @pl.when(step == 5)
        def _():
            sums.second((2,))

    def beside_gather(step):
        @pl.when(step == count - 3)
        def _():
            sums.third((0, 1))

        @pl.when(step == count - 2)
        def _():
            sums.third((2,))

    gather = Gather(ring, row_own(low), row_view(full, rows), sends_two, recvs_two, rows)
    start = lambda way, sub: gather.copy(way, sub, 0, ring.me, True).start()
    ring_scatter(Scatter(ring, partial, slots, sends, recvs, rows, finish, start), beside_scatter)
    keep = pltpu.make_async_copy(low, full.at[pl.ds(pl.multiple_of(ring.me * rows, rows), rows), :], local)
    keep.start()
    ring_gather(gather, beside_gather, True)
    keep.wait()
    sums.last()


def ffn_back(grad_gate, grad_up, hidden, w_gate, w_up, resid, cotangent, gain, inputs, cotangents, count, groups):
    rows, model = resid.shape
    slots, inner = grad_up.shape
    shapes = [(inner, model)] * 3
    return pl.pallas_call(
        functools.partial(ffn_back_kernel, count, groups, rows),
        name="ffn_back",
        out_shape=[
            jax.ShapeDtypeStruct((rows, model), F32),
            jax.ShapeDtypeStruct((slots, model), BF16),
            jax.ShapeDtypeStruct((1, model), F32),
        ]
        + [jax.ShapeDtypeStruct(shape, BF16) for shape in shapes],
        in_specs=[VMEM] * 2 + [ANY] + [VMEM] * 2 + [ANY] * 2 + [VMEM] + [ANY] * 2,
        out_specs=[VMEM, ANY, VMEM] + [ANY] * 3,
        scratch_shapes=[ring_slots(count, rows, model), pltpu.VMEM((rows, model), BF16)]
        + [pltpu.VMEM(shape, BF16) for shape in shapes]
        + [pltpu.VMEM((2, slots, model // (JOBS // 2)), BF16), pltpu.SemaphoreType.DMA((2,))]
        + [pltpu.VMEM((slots, inner), BF16), pltpu.VMEM((rows, model), F32), pltpu.VMEM((rows, model), BF16)]
        + [pltpu.SemaphoreType.DMA((3,))]
        + ring_semaphores(count) * 2
        + [pltpu.SemaphoreType.DMA]
        + sum_scratch(shapes, groups),
        compiler_params=ring_params(3),
        cost_estimate=pl.CostEstimate(
            flops=10 * slots * model * inner, bytes_accessed=600 << 20, transcendentals=0
        ),
    )(grad_gate, grad_up, hidden, w_gate, w_up, resid, cotangent, gain, inputs, cotangents)


def last_kernel(
    count, groups, rows, terms, tokens_in, grad_resid_in, gain, small, *rest,
):
    grads, rest = rest[:5], rest[5:]
    grad_tokens, total = rest[:2]
    targets, rest = rest[2:7], rest[7:]
    slots, first_box, second_box, second_own, boxes, box_sems, tokens, grad_resid, load_sems = rest[:9]
    sends, recvs, first_sends, first_recvs, second_sends, second_recvs = rest[9:15]
    ring = Ring(count)
    sums = GroupSum(ring, groups, grads, rest[15:20], rest[20:25], targets, *rest[25:])
    loads = [
        pltpu.make_async_copy(tokens_in, tokens, load_sems.at[0]),
        pltpu.make_async_copy(grad_resid_in, grad_resid, load_sems.at[1]),
    ]
    me, group = ring.me, ring.group
    first_peers = [(group, (me + k) % count) for k in range(1, count)]
    second_peers = [((group + k) % groups, me) for k in range(1, groups)]
    barrier = pltpu.get_barrier_semaphore()
    for peer in first_peers + second_peers:
        pl.semaphore_signal(barrier, inc=1, device_id=peer, device_id_type=MESH)
    pl.semaphore_wait(barrier, count + groups - 2)

    def first(k):
        return pltpu.make_async_remote_copy(
            src_ref=small.at[0:8], dst_ref=first_box.at[k], send_sem=first_sends.at[k],
            recv_sem=first_recvs.at[k], device_id=first_peers[k], device_id_type=MESH,
        )

    def second(k):
        return pltpu.make_async_remote_copy(
            src_ref=second_own, dst_ref=second_box.at[k], send_sem=second_sends.at[k],
            recv_sem=second_recvs.at[k], device_id=second_peers[k], device_id_type=MESH,
        )

    every = range(len(grads))
    sums.first(every)
    for k in range(count - 1):
        first(k).start()
    half = rows // 2

    def box_copy(way, start, slot):
        return pltpu.make_async_copy(
            terms.at[pl.ds(start, half), :], boxes.at[slot, way], box_sems.at[slot, way]
        )

    def fetch(step):
        for way, owner in ((0, ring.at(-1 - step)), (1, ring.at(1 + step))):
            box_copy(way, pl.multiple_of(owner * rows + way * half, half), step % 2).start()

    def partial(first, second, step):
        for way, start in ((0, first), (1, second)):
            box_copy(way, start, step % 2).wait()

        @pl.when(step + 1 < count)
        def _():
            fetch(step + 1)

        return jnp.concatenate([boxes[step % 2, 0], boxes[step % 2, 1]], 0).astype(F32)

    def finish(start, size, grad):
        value = tokens[start : start + size, :].astype(F32)
        scale = lax.rsqrt(jnp.mean(value * value, axis=1, keepdims=True) + 1e-6)
        through, pieces = norm_back(value, scale, gain[...].astype(F32).reshape(1, -1), grad)
        grad_tokens[start : start + size, :] = grad_resid[start : start + size, :] + through

    def early():
        sums.second(every)
        for k in range(count - 1):
            first(k).wait()
        mine = small[0:8]
        for k in range(count - 1):
            mine = mine + first_box[k]
        second_own[0:8] = mine
        second_own[8:] = small[8:]
        for k in range(groups - 1):
            second(k).start()

    def late():
        for k in range(groups - 1):
            second(k).wait()
        mine = second_own[...]
        for k in range(groups - 1):
            mine = mine + second_box[k]
        total[...] = mine
        for load in loads:
            load.wait()

    def beside(step):
        pl.when(step == 0)(early)
        for i in every:
            pl.when(step == count - 1 - len(every) + i)(lambda i=i: sums.third((i,)))
        pl.when(step == count - 2)(late)

    fetch(0)
    for load in loads:
        load.start()
    ring_scatter(Scatter(ring, partial, slots, sends, recvs, rows, finish), beside)
    sums.last()


def last_step(terms, tokens, grad_resid, gain, small, grads, count, groups):
    rows, model = tokens.shape
    return pl.pallas_call(
        functools.partial(last_kernel, count, groups, rows),
        name="last_step",
        out_shape=[jax.ShapeDtypeStruct((rows, model), F32), jax.ShapeDtypeStruct(small.shape, F32)]
        + [jax.ShapeDtypeStruct(g.shape, BF16) for g in grads],
        in_specs=[ANY] * 3 + [VMEM] * (2 + len(grads)),
        out_specs=[VMEM, VMEM] + [ANY] * len(grads),
        scratch_shapes=[
            ring_slots(count, rows, model),
            pltpu.VMEM((count - 1, 8, model), F32),
            pltpu.VMEM((groups - 1,) + small.shape, F32),
            pltpu.VMEM(small.shape, F32),
            pltpu.VMEM((2, 2, rows // 2, model), BF16),
            pltpu.SemaphoreType.DMA((2, 2)),
            pltpu.VMEM((rows, model), BF16),
            pltpu.VMEM((rows, model), F32),
            pltpu.SemaphoreType.DMA((2,)),
        ]
        + ring_semaphores(count)
        + [pltpu.SemaphoreType.DMA((count - 1,))] * 2
        + [pltpu.SemaphoreType.DMA((groups - 1,))] * 2
        + sum_scratch([g.shape for g in grads], groups),
        compiler_params=ring_params(4),
        cost_estimate=pl.CostEstimate(flops=0, bytes_accessed=300 << 20, transcendentals=0),
    )(terms, tokens, grad_resid, gain, small, *grads)


def results_kernel(heads, taps, wide, width, total, *refs):
    number = (len(refs) - 7) // 2
    for source, target in zip(refs[:number], refs[number : 2 * number]):
        target[...] = source[...].astype(target.dtype)
    g_first, g_second, g_head, gt_query, gt_key, gt_value, g_beta = refs[2 * number :]

    @pl.when(pl.program_id(0) == 0)
    def _():
        g_first[...] = total[0:1, :]
        g_second[...] = total[1:2, :]
        g_head[...] = total[2:3, 0:width]
        row = 8 + heads
        for place, target in enumerate((gt_query, gt_key, gt_value)):
            target[...] = total[row : row + taps, place * wide : (place + 1) * wide]
        g_beta[...] = total[8 : 8 + heads, :]


def results(total, arrays, heads, taps, wide, width):
    model = total.shape[1]
    steps = next(n for n in (2, 1) if all(a.shape[0] % (8 * n) == 0 for a, _ in arrays))
    small = [(1, model), (1, model), (1, width)] + [(taps, wide)] * 3 + [(heads, model)]
    piece = lambda a: pl.BlockSpec((a.shape[0] // steps, a.shape[1]), lambda n: (n, 0))
    whole = lambda shape: pl.BlockSpec(shape, lambda n: (0, 0))
    return pl.pallas_call(
        functools.partial(results_kernel, heads, taps, wide, width),
        name="results",
        grid=(steps,),
        out_shape=[jax.ShapeDtypeStruct(a.shape, kind) for a, kind in arrays]
        + [jax.ShapeDtypeStruct(shape, F32) for shape in small],
        in_specs=[whole(total.shape)] + [piece(a) for a, _ in arrays],
        out_specs=[piece(a) for a, _ in arrays] + [whole(shape) for shape in small],
        compiler_params=pltpu.CompilerParams(vmem_limit_bytes=56 << 20),
        cost_estimate=pl.CostEstimate(flops=0, bytes_accessed=48 << 20, transcendentals=0),
    )(total, *[a for a, _ in arrays])


def spread_hops(step, chunks, count, hop, start=0):
    each = -(-(count - 1) // (chunks - 1))
    for place in range(each):
        number = step * each + place

        @pl.when((number >= start) & (number < count - 1))
        def _():
            hop(number)


def plan_hops(chunks, hops, latency=0.8, segment=2.5):
    now, link, due, done, table = 0.0, 0.0, {}, {}, []

    def send(chunk):
        nonlocal link
        link = max(now, link) + 1.0
        done[chunk] = done.get(chunk, -1) + 1
        due[chunk] = link + latency

    for step in range(chunks):
        for half in range(2):
            ready, moves = True, []
            while ready:
                ready = sorted((due[c], c) for c in due if due[c] <= now and done[c] < hops - 1)
                if ready:
                    send(ready[0][1])
                    moves.append((ready[0][1], done[ready[0][1]]))
            table.append(moves)
            now += segment
        send(step)
    return table, [done[chunk] for chunk in range(chunks)]


def forward_kernel(
    heads, width, seqs, count, groups, chunks,
    starts, lengths, tokens, w_query, w_key, w_value, w_gate, w_beta,
    taps_query, taps_key, taps_value, gain, gain_first, w_out,
    mixed_full, w_full, mixed, p_query, p_key, p_value, p_gate, p_beta, z_query, z_key, z_value,
    delta_out, change_out, inverse_out, state_out,
    tail_query, tail_key, tail_value, state, stage, sends, recvs, keeps,
    w_sends, w_recvs, w_keep, w_far, w_near,
):
    step = pl.program_id(0)
    size = tokens.shape[0]
    first = step * size

    @pl.when(step == 0)
    def _():
        for tail in (tail_query, tail_key, tail_value):
            tail[...] = jnp.zeros_like(tail)
        state[...] = jnp.zeros_like(state)

    ring = Ring(count)

    def chunk_gather(chunk):
        return Gather(
            ring,
            lambda start, length: stage.at[chunk, pl.ds(start, length), :],
            lambda origin, start, length: mixed_full.at[
                origin, pl.ds(pl.multiple_of(chunk * size + start, length), length), :
            ],
            sends.at[chunk], recvs.at[chunk], size, 1,
        )

    def keep(chunk):
        return pltpu.make_async_copy(
            stage.at[chunk],
            mixed_full.at[ring.me, pl.ds(pl.multiple_of(chunk * size, size), size), :],
            keeps.at[chunk],
        )

    weight = WholeWeight(ring, groups, w_out, w_full, w_sends, w_recvs, w_keep, w_far, w_near)
    each = -(-(count - 1) // (chunks - 1))

    def weight_hops(late=0):
        for place in range(each):
            number = (2 * step + late) * each + place
            pl.when((number > 0) & (number < count - 1))(lambda: weight.hop(number))
            pl.when(number == count - 1)(weight.exchange)

    table, done = plan_hops(chunks, count - 1)

    def chunk_hops(half):
        for place, moves in enumerate(table[half::2]):
            if moves:
                @pl.when(step == place)
                def _():
                    for chunk, hop in moves:
                        chunk_gather(chunk).hop(hop)

    @pl.when(step == 0)
    def _():
        greet(ring, weight.peers())
        weight.begin()

    weight_hops()
    chunk_hops(0)
    rows, seg_rows, seg_columns, before, last = chunk_masks(starts, lengths, seqs, first, size)
    same = seg_rows == seg_columns
    i = lax.broadcasted_iota(jnp.int32, (size, size), 0)
    j = lax.broadcasted_iota(jnp.int32, (size, size), 1)
    strict = jnp.where(same & (i > j), 1.0, 0.0)
    inclusive = jnp.where(same & (i >= j), 1.0, 0.0)
    carried = jnp.where(seg_rows == before, 1.0, 0.0)
    ending = jnp.where(seg_rows == last, 1.0, 0.0)
    kept = jnp.where(before == last, 1.0, 0.0)
    live = jnp.where(seg_rows % 2 == 1, 1.0, 0.0)
    joined = [
        jnp.where(segment_at(rows - offset, starts, lengths, seqs) == seg_rows, 1.0, 0.0)
        for offset in range(1, taps_query.shape[0])
    ]
    inputs = normed_rows(tokens, gain_first)[0].astype(BF16)

    def feature(weight, taps, tail, p_out, z_out):
        projected = jnp.dot(inputs, weight[...], preferred_element_type=F32)
        p_out[...] = projected
        tail[8:, :] = projected
        tap = taps[...].astype(F32)
        result = projected * tap[0:1]
        for offset in range(1, tap.shape[0]):
            result = result + tail[8 - offset : 8 - offset + size, :] * tap[offset : offset + 1] * joined[offset - 1]
        tail[0:8, :] = projected[size - 8 :, :]
        z_out[...] = result
        return result * sigmoid(result)

    u_query = feature(w_query, taps_query, tail_query, p_query, z_query)
    u_key = feature(w_key, taps_key, tail_key, p_key, z_key)
    u_value = feature(w_value, taps_value, tail_value, p_value, z_value)
    gate = jnp.dot(inputs, w_gate[...], preferred_element_type=F32)
    p_gate[...] = gate
    beta_pre = mm(inputs, w_beta[...], (1, 1))
    p_beta[...] = beta_pre
    strength = sigmoid(beta_pre)
    opened = gate * sigmoid(gate)
    scale = width ** (-0.5)
    head_gain = gain[...].astype(F32)
    for h in range(heads):
        if h == heads // 2:
            weight_hops(1)
            chunk_hops(1)
        cols = slice(h * width, (h + 1) * width)
        uq, uk = u_query[:, cols], u_key[:, cols]
        query = (uq * lax.rsqrt(jnp.sum(uq * uq, axis=1, keepdims=True) + 1e-6)).astype(BF16)
        key = (uk * lax.rsqrt(jnp.sum(uk * uk, axis=1, keepdims=True) + 1e-6)).astype(BF16)
        value = u_value[:, cols].astype(BF16).astype(F32)
        beta = strength[:, h : h + 1]
        memory = state[h]
        low_memory = memory.astype(BF16)
        state_out[0, h] = low_memory
        lower = mm(key, key, (1, 1)) * strict * beta
        inverse = inverse_unit_lower(lower, size).astype(BF16)
        inverse_out[0, h] = inverse
        within = mm(query, key, (1, 1)) * inclusive
        change = mm(inverse, beta * (value - carried * mm(key, low_memory)))
        low_change = change.astype(BF16)
        change_out[:, cols] = low_change
        out = scale * (carried * mm(query, low_memory) + mm(within, low_change))
        state[h] = kept * memory + mm(key, ending * change, (0, 0))
        delta_out[:, cols] = out
        normal = out * lax.rsqrt(jnp.mean(out * out, axis=1, keepdims=True) + 1e-5) * head_gain
        low_mixed = (normal * opened[:, cols] * live).astype(BF16)
        mixed[:, cols] = low_mixed
        stage[step, :, cols] = low_mixed

    chunk_gather(step).begin()
    keep(step).start()

    @pl.when(step == chunks - 1)
    def _():
        def finish(number, carry):
            pl.when(number == (count - 1) // 2)(weight.back)
            for chunk in range(chunks):
                if done[chunk] < count - 2:
                    pl.when(done[chunk] + number < count - 1)(
                        lambda chunk=chunk: chunk_gather(chunk).hop(done[chunk] + number)
                    )
            return carry

        lax.fori_loop(1, count - 1, finish, 0)

        def settle(chunk, carry):
            chunk_gather(chunk).arrived(count - 1)
            chunk_gather(chunk).end()
            keep(chunk).wait()
            return carry

        lax.fori_loop(0, chunks, settle, 0)
        weight.end()


def forward_mixer(tokens, w_query, w_key, w_value, w_gate, w_beta, taps_query, taps_key, taps_value, gain, gain_first, starts, lengths, w_out, count, groups):
    slots, model = tokens.shape
    wide = w_query.shape[1]
    width = gain.shape[0]
    heads = wide // width
    seqs = starts.shape[1]
    chunks = slots // CHUNK
    taps = taps_query.shape[0]
    part = w_out.shape[0] // groups
    smem = pl.BlockSpec(memory_space=pltpu.SMEM)
    whole = lambda shape: pl.BlockSpec(shape, lambda n: (0,) * len(shape))
    piece = lambda shape: pl.BlockSpec(shape, lambda n: (n,) + (0,) * (len(shape) - 1))
    outs = [
        ((slots, wide), BF16), ((slots, wide), F32), ((slots, wide), F32), ((slots, wide), F32), ((slots, wide), F32),
        ((slots, w_beta.shape[0]), F32), ((slots, wide), F32), ((slots, wide), F32), ((slots, wide), F32),
        ((slots, wide), F32), ((slots, wide), BF16),
    ]
    return pl.pallas_call(
        functools.partial(forward_kernel, heads, width, seqs, count, groups, chunks),
        name="mixer_forward",
        grid=(chunks,),
        out_shape=[
            jax.ShapeDtypeStruct((count, slots, wide), BF16),
            jax.ShapeDtypeStruct((count, groups, part, model), BF16),
        ]
        + [jax.ShapeDtypeStruct(s, d) for s, d in outs]
        + [
            jax.ShapeDtypeStruct((chunks, heads, CHUNK, CHUNK), BF16),
            jax.ShapeDtypeStruct((chunks, heads, width, width), BF16),
        ],
        in_specs=[smem, smem, piece((CHUNK, model))]
        + [whole((model, wide))] * 4
        + [whole(w_beta.shape)]
        + [whole((taps, wide))] * 3
        + [whole((1, width)), VMEM, ANY],
        out_specs=[ANY, ANY]
        + [piece((CHUNK, s[1])) for s, d in outs]
        + [piece((1, heads, CHUNK, CHUNK)), piece((1, heads, width, width))],
        scratch_shapes=[pltpu.VMEM((CHUNK + 8, wide), F32)] * 3
        + [pltpu.VMEM((heads, width, width), F32), pltpu.VMEM((chunks, CHUNK, wide), BF16)]
        + [pltpu.SemaphoreType.DMA((chunks, 2, 1, count - 1))] * 2
        + [pltpu.SemaphoreType.DMA((chunks,))]
        + ring_semaphores(count, 1)
        + [
            pltpu.SemaphoreType.DMA,
            pltpu.SemaphoreType.DMA((2, groups // 2 - 1, 2, count)),
            pltpu.SemaphoreType.DMA((2, groups // 2)),
        ],
        compiler_params=ring_params(5),
        cost_estimate=pl.CostEstimate(
            flops=2 * slots * model * wide * 4 + slots * heads * CHUNK * 2 * CHUNK * 20,
            bytes_accessed=slots * model * 2 + 4 * model * wide * 2 + slots * wide * 36,
            transcendentals=slots * wide * 4,
        ),
    )(starts, lengths, tokens, w_query, w_key, w_value, w_gate, w_beta, taps_query, taps_key, taps_value, gain.reshape(1, width), gain_first, w_out)


def small_rows(heads, taps):
    return -(-(8 + heads + taps) // 8) * 8


def backward_kernel(
    heads, width, seqs, chunks, count, rows_own,
    starts, lengths, tokens, grad_attended, mixed, p_query, p_key, p_value, p_gate, p_beta,
    z_query, z_key, z_value, delta_out, change_in, inverse_in, state_in,
    w_query_in, w_key_in, w_value_in, w_gate_in, w_beta, w_out, taps_query, taps_key, taps_value, gain, gain_first,
    hidden, w_down, resid_in, g_second, grad_normed, gw_query, gw_key, gw_value, gw_gate, gw_out,
    small, output,
    a_query, a_key, a_value, a_gate, a_out, head_query, head_key, head_value, flow,
    w_query, w_key, w_value, w_gate, resid, load_sems, slots, sends, recvs,
):
    step = pl.program_id(0)
    size = tokens.shape[0]
    first = (chunks - 1 - step) * size

    @pl.when(step == 0)
    def _():
        for ref in (a_query, a_key, a_value, a_gate, a_out, small, flow):
            ref[...] = jnp.zeros_like(ref)
        small[1:2, :] = g_second[...]
        for ref in (head_query, head_key, head_value):
            ref[size:, :] = jnp.zeros((8, ref.shape[1]), F32)

    half = rows_own // 2

    def partial(one, two, number):
        return mm(jnp.concatenate([hidden[pl.ds(one, half), :], hidden[pl.ds(two, half), :]], 0), w_down[...])

    def finish(start, length, down):
        output[start : start + length, :] = (resid[start : start + length, :] + down).astype(BF16)

    ring = Ring(count)
    scatter = Scatter(ring, partial, slots, sends, recvs, rows_own, finish)
    loads = [
        pltpu.make_async_copy(source, target, load_sems.at[k])
        for k, (source, target) in enumerate(
            ((w_query_in, w_query), (w_key_in, w_key), (w_value_in, w_value), (w_gate_in, w_gate), (resid_in, resid))
        )
    ]

    @pl.when(step == 0)
    def _():
        for load in loads:
            load.start()
        greet(ring)

    spread_hops(step, chunks, count, scatter.hop)
    rows, seg_rows, seg_columns, before, last = chunk_masks(starts, lengths, seqs, first, size)
    same = seg_rows == seg_columns
    i = lax.broadcasted_iota(jnp.int32, (size, size), 0)
    j = lax.broadcasted_iota(jnp.int32, (size, size), 1)
    strict = jnp.where(same & (i > j), 1.0, 0.0)
    inclusive = jnp.where(same & (i >= j), 1.0, 0.0)
    carried = jnp.where(seg_rows == before, 1.0, 0.0)
    ending = jnp.where(seg_rows == last, 1.0, 0.0)
    kept = jnp.where(before == last, 1.0, 0.0)
    live = jnp.where(seg_rows % 2 == 1, 1.0, 0.0)
    taps = taps_query.shape[0]
    joined = [
        jnp.where(segment_at(rows + offset, starts, lengths, seqs) == seg_rows, 1.0, 0.0)
        for offset in range(1, taps)
    ]
    normal_rows, unit_rows = normed_rows(tokens, gain_first)
    inputs = normal_rows.astype(BF16)
    grad_rows = grad_attended[...]
    grad_mixed = mm(grad_rows, w_out[...], (1, 1))
    a_out[...] += mm(mixed[...], grad_rows, (0, 0))
    strength = sigmoid(p_beta[...])
    scale = width ** (-0.5)
    head_gain = gain[...].astype(F32)

    grads_query, grads_key, grads_value, grads_gate, grads_beta = [], [], [], [], []
    for h in range(heads):
        cols = slice(h * width, (h + 1) * width)
        out = delta_out[:, cols]
        gate = p_gate[:, cols]
        sig_gate = sigmoid(gate)
        silu_gate = gate * sig_gate
        root = lax.rsqrt(jnp.mean(out * out, axis=1, keepdims=True) + 1e-5)
        grad = grad_mixed[:, cols] * live
        unit = out * root
        grads_gate.append(grad * unit * head_gain * (sig_gate * (1.0 + gate * (1.0 - sig_gate))))
        grad_normal = grad * silu_gate
        small[2:3, 0:width] += jnp.sum(grad_normal * unit, axis=0, keepdims=True)
        push = grad_normal * head_gain
        grad_out = scale * root * (push - unit * jnp.mean(push * unit, axis=1, keepdims=True))

        zq, zk, zv = z_query[:, cols], z_key[:, cols], z_value[:, cols]
        sq, sk, sv = sigmoid(zq), sigmoid(zk), sigmoid(zv)
        uq, uk = zq * sq, zk * sk
        nq = lax.rsqrt(jnp.sum(uq * uq, axis=1, keepdims=True) + 1e-6)
        nk = lax.rsqrt(jnp.sum(uk * uk, axis=1, keepdims=True) + 1e-6)
        unit_q, unit_k = uq * nq, uk * nk
        query, key = unit_q.astype(BF16), unit_k.astype(BF16)
        beta = strength[:, h : h + 1]
        change = change_in[:, cols]
        inverse = inverse_in[0, h]
        memory = state_in[0, h]
        flowing = flow[h]
        low_flow = flowing.astype(BF16)
        low_out = grad_out.astype(BF16)

        within = mm(query, key, (1, 1)) * inclusive
        grad_within = (mm(low_out, change, (1, 1)) * inclusive).astype(BF16)
        grad_change = mm(within, low_out, (0, 0)) + ending * mm(key, low_flow)
        grad_mid = mm(inverse, grad_change, (0, 0))
        grad_value = beta * grad_mid
        low_value = grad_value.astype(BF16)
        cross = (mm(low_value, change, (1, 1)) * strict).astype(BF16)
        grad_query = carried * mm(low_out, memory, (1, 1)) + mm(grad_within, key)
        grad_key = (
            mm(grad_within, query, (0, 0))
            + ending * mm(change, low_flow, (1, 1))
            - carried * mm(low_value, memory, (1, 1))
            - mm(cross, key)
            - mm(cross, key, (0, 0))
        )
        flow[h] = (
            kept * flowing
            + mm(query, carried * grad_out, (0, 0))
            - mm(key, carried * grad_value, (0, 0))
        )
        grads_beta.append((1.0 - beta) * jnp.sum(grad_mid * change.astype(F32), axis=1, keepdims=True))
        du_q = nq * (grad_query - unit_q * jnp.sum(grad_query * unit_q, axis=1, keepdims=True))
        du_k = nk * (grad_key - unit_k * jnp.sum(grad_key * unit_k, axis=1, keepdims=True))
        grads_query.append(du_q * sq * (1.0 + zq * (1.0 - sq)))
        grads_key.append(du_k * sk * (1.0 + zk * (1.0 - sk)))
        grads_value.append(grad_value * sv * (1.0 + zv * (1.0 - sv)))

    tap_row = 8 + heads
    wide = heads * width

    def unconv(parts, taps_ref, head, projected, place):
        lanes = slice(place * wide, (place + 1) * wide)
        grad = jnp.concatenate(parts, axis=1)
        head[0:size, :] = grad
        tap = taps_ref[...].astype(F32)
        p = projected[...]
        result = grad * tap[0:1]
        small[tap_row : tap_row + 1, lanes] += jnp.sum(p * grad, axis=0, keepdims=True)
        for offset in range(1, taps):
            moved = head[offset : offset + size, :] * joined[offset - 1]
            result = result + moved * tap[offset : offset + 1]
            row = tap_row + offset
            small[row : row + 1, lanes] += jnp.sum(p * moved, axis=0, keepdims=True)
        head[size:, :] = grad[0:8, :]
        return result.astype(BF16)

    d_query = unconv(grads_query, taps_query, head_query, p_query, 0)
    d_key = unconv(grads_key, taps_key, head_key, p_key, 1)
    d_value = unconv(grads_value, taps_value, head_value, p_value, 2)
    d_gate = jnp.concatenate(grads_gate, axis=1).astype(BF16)
    spare = [jnp.zeros((size, 1), F32)] * (w_beta.shape[0] - heads)
    d_beta = jnp.concatenate(grads_beta + spare, axis=1).astype(BF16)

    @pl.when(step == 0)
    def _():
        for load in loads:
            load.wait()

    grad_inputs = (
        mm(d_query, w_query[...], (1, 1))
        + mm(d_key, w_key[...], (1, 1))
        + mm(d_value, w_value[...], (1, 1))
        + mm(d_gate, w_gate[...], (1, 1))
        + mm(d_beta, w_beta[...])
    )
    grad_normed[...] = grad_inputs.astype(BF16)
    small[0:1, :] += jnp.sum(grad_inputs * unit_rows, axis=0, keepdims=True)
    a_query[...] += mm(inputs, d_query, (0, 0))
    a_key[...] += mm(inputs, d_key, (0, 0))
    a_value[...] += mm(inputs, d_value, (0, 0))
    a_gate[...] += mm(inputs, d_gate, (0, 0))
    small[8 : 8 + heads, :] += mm(d_beta, inputs, (0, 0))[:heads]

    @pl.when(step == chunks - 1)
    def _():
        for target, source in (
            (gw_query, a_query), (gw_key, a_key), (gw_value, a_value), (gw_gate, a_gate),
            (gw_out, a_out),
        ):
            target[...] = source[...].astype(target.dtype)
        scatter.end()


def backward_mixer(tokens, grad_attended, saved, w_query, w_key, w_value, w_gate, w_beta, w_out, taps_query, taps_key, taps_value, gain, gain_first, starts, lengths, hidden, w_down, resid, g_second, count):
    slots, model = tokens.shape
    wide = w_query.shape[1]
    width = gain.shape[0]
    heads = wide // width
    seqs = starts.shape[1]
    chunks = slots // CHUNK
    taps = taps_query.shape[0]
    smem = pl.BlockSpec(memory_space=pltpu.SMEM)
    fixed = lambda shape: pl.BlockSpec(shape, lambda n: (0,) * len(shape), pipeline_mode=pl.Buffered(1))
    piece = lambda shape: pl.BlockSpec(shape, lambda n: (chunks - 1 - n,) + (0,) * (len(shape) - 1))
    rows = lambda a: piece((CHUNK, a.shape[1]))
    outs = (
        [((slots, model), BF16)] + [((model, wide), BF16)] * 4 + [((wide, model), BF16)]
        + [((small_rows(heads, taps), model), F32), (resid.shape, BF16)]
    )
    return pl.pallas_call(
        functools.partial(backward_kernel, heads, width, seqs, chunks, count, slots // count),
        name="mixer_backward",
        grid=(chunks,),
        out_shape=[jax.ShapeDtypeStruct(s, d) for s, d in outs],
        in_specs=[smem, smem, rows(tokens), rows(grad_attended)]
        + [rows(a) for a in saved[:11]]
        + [piece((1, heads, CHUNK, CHUNK)), piece((1, heads, width, width))]
        + [ANY] * 4
        + [fixed(w_beta.shape), fixed((wide, model))]
        + [fixed((taps, wide))] * 3
        + [fixed((1, width)), VMEM, fixed(hidden.shape), fixed(w_down.shape), ANY, fixed(g_second.shape)],
        out_specs=[piece((CHUNK, model))] + [fixed(s) for s, d in outs[1:]],
        scratch_shapes=[pltpu.VMEM((model, wide), F32)] * 4
        + [pltpu.VMEM((wide, model), F32)]
        + [pltpu.VMEM((CHUNK + 8, wide), F32)] * 3
        + [pltpu.VMEM((heads, width, width), F32)]
        + [pltpu.VMEM((model, wide), BF16)] * 4
        + [pltpu.VMEM(resid.shape, F32), pltpu.SemaphoreType.DMA((5,)), ring_slots(count, slots // count, model)]
        + ring_semaphores(count),
        compiler_params=ring_params(6),
        cost_estimate=pl.CostEstimate(
            flops=2 * slots * model * wide * 10 + slots * heads * CHUNK * 2 * CHUNK * 8,
            bytes_accessed=slots * model * 6 + 10 * model * wide * 2 + slots * wide * 36,
            transcendentals=slots * wide * 8,
        ),
    )(starts, lengths, tokens, grad_attended, *saved, w_query, w_key, w_value, w_gate, w_beta, w_out, taps_query, taps_key, taps_value, gain.reshape(1, width), gain_first, hidden, w_down, resid, g_second)


def make_shards(groups, count):
    def shards(
        tokens, attn_gain, w_query, w_key, w_value, conv_query, conv_key, conv_value, w_beta, w_gate_out,
        head_gain, w_out, ffn_gain, w_gate, w_up, w_down, seq_starts, seq_lengths, cotangent,
    ):
        model = tokens.shape[1]
        heads = w_beta.shape[1]
        beta_rows = w_beta.T if heads > 1 else jnp.pad(w_beta.T, ((0, 1), (0, 0)))
        tokens_full = gather_tokens(tokens, count)
        mixed_full, w_out_full, *saved = forward_mixer(
            tokens_full, w_query, w_key, w_value, w_gate_out, beta_rows,
            conv_query, conv_key, conv_value, head_gain, attn_gain, seq_starts, seq_lengths, w_out, count, groups,
        )
        w_out_full = w_out_full.reshape(-1, tokens.shape[1])
        resid, ffn_full, hidden, grad_gate, grad_up, grad_full = attend(
            mixed_full, w_out_full, tokens_full, ffn_gain, w_gate.T, w_up.T, w_down, cotangent, count
        )
        grad_resid, grad_attended, g_second, *ffn_grads = ffn_back(
            grad_gate, grad_up, hidden, w_gate.T, w_up.T, resid, cotangent, ffn_gain, ffn_full, grad_full,
            count, groups,
        )
        pulled = backward_mixer(
            tokens_full, grad_attended, saved, w_query, w_key, w_value, w_gate_out, beta_rows, w_out,
            conv_query, conv_key, conv_value, head_gain, attn_gain, seq_starts, seq_lengths,
            hidden, w_down, resid, g_second, count,
        )
        terms, gw_query, gw_key, gw_value, gw_gate_out, gw_out, small, output = pulled
        grad_tokens, total, *mixer_grads = last_step(
            terms, tokens, grad_resid, attn_gain, small,
            (gw_query, gw_key, gw_value, gw_gate_out, gw_out), count, groups,
        )
        taps, wide = conv_query.shape
        output, grad_tokens, *rest = results(
            total,
            [(output, BF16), (grad_tokens, F32)] + [(g, F32) for g in (*mixer_grads, *ffn_grads)],
            heads, taps, wide, head_gain.shape[0],
        )
        grads, (g_first, g_second, g_head, gt_query, gt_key, gt_value, g_beta) = rest[:8], rest[8:]
        return (
            output,
            grad_tokens,
            g_first[0],
            grads[0],
            grads[1],
            grads[2],
            gt_query,
            gt_key,
            gt_value,
            g_beta.T,
            grads[3],
            g_head[0],
            grads[4],
            g_second[0],
            grads[5].T,
            grads[6].T,
            grads[7],
        )

    return shards


def solution(mesh):
    placed = (
        P(("dp", "tensor"), None),
        P(),
        P(None, "tensor"),
        P(None, "tensor"),
        P(None, "tensor"),
        P(None, "tensor"),
        P(None, "tensor"),
        P(None, "tensor"),
        P(None, "tensor"),
        P(None, "tensor"),
        P(),
        P("tensor", None),
        P(),
        P(None, "tensor"),
        P(None, "tensor"),
        P("tensor", None),
        P("dp", None),
        P("dp", None),
        P(("dp", "tensor"), None),
    )
    return jax.shard_map(
        make_shards(mesh.shape["dp"], mesh.shape["tensor"]),
        mesh=mesh,
        in_specs=placed,
        out_specs=(
            P(("dp", "tensor"), None),
            P(("dp", "tensor"), None),
            P(),
            P(None, "tensor"),
            P(None, "tensor"),
            P(None, "tensor"),
            P(None, "tensor"),
            P(None, "tensor"),
            P(None, "tensor"),
            P(None, "tensor"),
            P(None, "tensor"),
            P(),
            P("tensor", None),
            P(),
            P(None, "tensor"),
            P(None, "tensor"),
            P("tensor", None),
        ),
        check_vma=False,
    )
```

```python
import functools
import jax
import jax.numpy as jnp
from jax import lax
from jax.experimental import pallas as pl
from jax.experimental.pallas import tpu as pltpu
from jax.sharding import PartitionSpec as P

CHUNK = 256
F32, BF16 = jnp.float32, jnp.bfloat16


def mm(a, b, contract=(1, 0)):
    return lax.dot_general(
        a.astype(BF16),
        b.astype(BF16),
        (((contract[0],), (contract[1],)), ((), ())),
        preferred_element_type=F32,
    )


def segment_at(places, starts, lengths, seqs):
    segment = jnp.zeros_like(places)
    for s in range(seqs):
        begin = starts[0, s]
        stop = begin + lengths[0, s]
        segment = segment + jnp.where(places >= begin, 1, 0) + jnp.where(places >= stop, 1, 0)
    return jnp.where(places < 0, -1, segment)


def chunk_masks(starts, lengths, seqs, first, size):
    rows = first + lax.broadcasted_iota(jnp.int32, (size, 1), 0)
    columns = first + lax.broadcasted_iota(jnp.int32, (1, size), 1)
    seg_rows = segment_at(rows, starts, lengths, seqs)
    seg_columns = segment_at(columns, starts, lengths, seqs)
    before = segment_at(jnp.full((1, 1), first - 1, jnp.int32), starts, lengths, seqs)
    last = segment_at(jnp.full((1, 1), first + size - 1, jnp.int32), starts, lengths, seqs)
    return rows, seg_rows, seg_columns, before, last


def inverse_unit_lower(lower, size):
    i = lax.broadcasted_iota(jnp.int32, (size, size), 0)
    j = lax.broadcasted_iota(jnp.int32, (size, size), 1)

    def corner(width):
        shift = width.bit_length() - 1
        pair = (i >> (shift + 1)) == (j >> (shift + 1))
        return pair & (((i >> shift) & 1) == 1) & (((j >> shift) & 1) == 0)

    inverse = jnp.where(i == j, 1.0, 0.0) - jnp.where(corner(1), lower, 0.0)
    width = 2
    while width < size:
        low = inverse.astype(BF16)
        if 2 * width == size:
            part = mm(mm(low[width:, width:], lower[width:, :width]), low[:width, :width])
            inverse = jnp.concatenate(
                [
                    inverse[:width],
                    jnp.concatenate([-part, inverse[width:, width:]], axis=1),
                ],
                axis=0,
            )
        else:
            between = jnp.where(corner(width), lower, 0.0)
            inverse = inverse - mm(mm(low, between), low)
        width *= 2
    return inverse


def sigmoid(v):
    return 1.0 / (1.0 + jnp.exp(-v))


def normed_rows(tokens, gain):
    value = tokens[...].astype(F32)
    unit = value * lax.rsqrt(jnp.mean(value * value, axis=1, keepdims=True) + 1e-6)
    return unit * gain[...].astype(F32).reshape(1, -1), unit


MESH = pl.DeviceIdType.MESH
SUBS = 2
PAIRS = [(sub, way) for sub in range(SUBS) for way in (0, 1)]


def ring_position(device, count):
    half, odd = device // 2, device % 2
    return half + odd * (count - 1 - 2 * half)


def ring_device(position, count):
    back = position // (count // 2)
    return (1 - back) * 2 * position + back * (2 * (count - 1 - position) + 1)


class Ring:
    def __init__(self, count):
        self.count = count
        self.me = lax.axis_index("tensor")
        self.place = ring_position(self.me, count)
        self.group = lax.axis_index("dp")

    def at(self, offset):
        return ring_device((self.place + offset + 2 * self.count) % self.count, self.count)

    def next(self, way):
        return (self.group, self.at(1 if way == 0 else -1))


class Gather:
    def __init__(self, ring, own, view, sends, recvs, rows, subs=SUBS):
        self.ring, self.own, self.view, self.sends, self.recvs, self.rows = ring, own, view, sends, recvs, rows
        self.piece = rows // (2 * subs)
        self.pairs = [(sub, way) for sub in range(subs) for way in (0, 1)]

    def origin(self, way, step):
        return self.ring.at(-step if way == 0 else step)

    def copy(self, way, sub, step, origin, first=False):
        inside = way * (self.rows // 2) + sub * self.piece
        place = self.view(origin, inside, self.piece)
        return pltpu.make_async_remote_copy(
            src_ref=self.own(inside, self.piece) if first else place,
            dst_ref=place,
            send_sem=self.sends.at[way, sub, step],
            recv_sem=self.recvs.at[way, sub, step],
            device_id=self.ring.next(way),
            device_id_type=MESH,
        )

    def begin(self):
        for sub, way in self.pairs:
            self.copy(way, sub, 0, self.ring.me, True).start()

    def arrived(self, step):
        for sub, way in self.pairs:
            self.copy(way, sub, step - 1, self.origin(way, step)).wait_recv()

    def hop(self, step):
        for sub, way in self.pairs:
            self.copy(way, sub, step - 1, self.origin(way, step)).wait_recv()
            self.copy(way, sub, step, self.origin(way, step)).start()

    def end(self):
        def drain(step, carry):
            for sub, way in self.pairs:
                self.copy(way, sub, step, self.ring.me).wait_send()
            return carry

        lax.fori_loop(0, self.ring.count - 1, drain, 0)


def row_view(ref, rows):
    return lambda origin, start, size: ref.at[pl.ds(pl.multiple_of(origin * rows + start, size), size), :]


def row_own(ref):
    return lambda start, size: ref.at[pl.ds(start, size), :]


def ring_gather(gather, between, begun=False):
    count = gather.ring.count

    def run(step, carry):
        if not begun:
            pl.when(step == 0)(gather.begin)

        @pl.when((step > 0) & (step < count - 1))
        def _():
            gather.hop(step)

        @pl.when(step == count - 1)
        def _():
            gather.arrived(step)

        between(step)
        return carry

    lax.fori_loop(0, count, run, 0)
    gather.end()


def scatter_copy(ring, slots, sends, recvs, way, sub, step):
    return pltpu.make_async_remote_copy(
        src_ref=slots.at[way, sub, step],
        dst_ref=slots.at[way, sub, step + 1],
        send_sem=sends.at[way, sub, step],
        recv_sem=recvs.at[way, sub, step],
        device_id=ring.next(way),
        device_id_type=MESH,
    )


class Scatter:
    def __init__(self, ring, partial, slots, sends, recvs, rows, finish, after=None):
        self.after = after
        self.ring, self.partial, self.slots, self.sends, self.recvs = ring, partial, slots, sends, recvs
        self.half, self.finish = rows // 2, finish
        self.rows, self.piece = rows, rows // (2 * SUBS)

    def terms(self, step):
        half, first, second = self.half, self.ring.at(-1 - step), self.ring.at(1 + step)
        return self.partial(
            pl.multiple_of(first * self.rows, half), pl.multiple_of(second * self.rows + half, half), step
        )

    def part(self, terms, way, sub):
        start = way * self.half + sub * self.piece
        return terms[start : start + self.piece]

    def copy(self, way, sub, step):
        return scatter_copy(self.ring, self.slots, self.sends, self.recvs, way, sub, step)

    def hop(self, step):
        self.pass_on(step, self.terms(step))

    def pass_on(self, step, terms):
        for sub, way in PAIRS:
            term = self.part(terms, way, sub)

            @pl.when(step == 0)
            def _():
                self.slots[way, sub, 0] = term.astype(BF16)

            @pl.when(step > 0)
            def _():
                self.copy(way, sub, step - 1).wait_recv()
                self.slots[way, sub, step] = (self.slots[way, sub, step].astype(F32) + term).astype(BF16)

            self.copy(way, sub, step).start()

    def end(self):
        self.take(self.terms(self.ring.count - 1))
        self.drain()

    def take(self, terms):
        count = self.ring.count
        for sub, way in PAIRS:
            self.copy(way, sub, count - 2).wait_recv()
            self.finish(
                way * self.half + sub * self.piece,
                self.piece,
                self.slots[way, sub, count - 1].astype(F32) + self.part(terms, way, sub),
            )
            if self.after is not None:
                self.after(way, sub)

    def drain(self):
        def run(step, carry):
            for sub, way in PAIRS:
                self.copy(way, sub, step).wait_send()
            return carry

        lax.fori_loop(0, self.ring.count - 1, run, 0)


def ring_scatter(scatter, between):
    count = scatter.ring.count

    def run(step, carry):
        terms = scatter.terms(step)
        pl.when(step < count - 1)(lambda: scatter.pass_on(step, terms))
        pl.when(step == count - 1)(lambda: scatter.take(terms))
        between(step)
        return carry

    lax.fori_loop(0, count, run, 0)
    scatter.drain()


class GroupSum:
    def __init__(self, ring, groups, grads, near, far, targets, near_sems, far_sems, back_sems, keep_sems):
        self.ring, self.groups, self.grads, self.near, self.far, self.targets = ring, groups, grads, near, far, targets
        self.near_sems, self.far_sems, self.back_sems, self.keep_sems = near_sems, far_sems, back_sems, keep_sems
        self.core = ring.group % 2
        self.mate = (ring.group + 1 - 2 * self.core, ring.me)

    def peers(self):
        return [self.mate] + [
            ((self.ring.group + 2 * k) % self.groups, self.ring.me) for k in range(1, self.groups // 2)
        ]

    def half(self, i, core):
        rows = self.near[i].shape[0]
        return pl.ds(pl.multiple_of(core * rows, rows), rows)

    def near_copy(self, i):
        return pltpu.make_async_remote_copy(
            src_ref=self.grads[i].at[self.half(i, 1 - self.core), :], dst_ref=self.near[i],
            send_sem=self.near_sems.at[0, i], recv_sem=self.near_sems.at[1, i],
            device_id=self.mate, device_id_type=MESH,
        )

    def far_copy(self, i, k):
        return pltpu.make_async_remote_copy(
            src_ref=self.near[i], dst_ref=self.far[i].at[k - 1],
            send_sem=self.far_sems.at[0, i, k - 1], recv_sem=self.far_sems.at[1, i, k - 1],
            device_id=((self.ring.group + 2 * k) % self.groups, self.ring.me), device_id_type=MESH,
        )

    def back_copy(self, i):
        return pltpu.make_async_remote_copy(
            src_ref=self.far[i].at[0], dst_ref=self.targets[i].at[self.half(i, self.core), :],
            send_sem=self.back_sems.at[0, i], recv_sem=self.back_sems.at[1, i],
            device_id=self.mate, device_id_type=MESH,
        )

    def keep_copy(self, i):
        return pltpu.make_async_copy(
            self.far[i].at[0], self.targets[i].at[self.half(i, self.core), :], self.keep_sems.at[i]
        )

    def first(self, chosen):
        for i in chosen:
            self.near_copy(i).start()

    def each_block(self, i, body):
        rows = self.near[i].shape[0]
        block = next(size for size in (64, 32, 16) if rows % size == 0)

        def step(at, carry):
            start = pl.multiple_of(at * block, block)
            body(pl.ds(start, block), pl.ds(pl.multiple_of(self.core * rows + start, block), block))
            return carry

        lax.fori_loop(0, rows // block, step, 0)

    def second(self, chosen):
        for i in chosen:
            self.near_copy(i).wait_recv()

            def add(here, own, i=i):
                self.near[i][here, :] = (
                    self.near[i][here, :].astype(F32) + self.grads[i][own, :].astype(F32)
                ).astype(BF16)

            self.each_block(i, add)
            for k in range(1, self.groups // 2):
                self.far_copy(i, k).start()

    def third(self, chosen):
        for i in chosen:
            for k in range(1, self.groups // 2):
                self.far_copy(i, k).wait()

            def add(here, own, i=i):
                total = self.near[i][here, :].astype(F32)
                for k in range(self.groups // 2 - 1):
                    total = total + self.far[i][k, here, :].astype(F32)
                self.far[i][0, here, :] = total.astype(BF16)

            self.each_block(i, add)
            self.keep_copy(i).start()
            self.back_copy(i).start()

    def last(self):
        for i in range(len(self.grads)):
            self.near_copy(i).wait_send()
            self.back_copy(i).wait()
            self.keep_copy(i).wait()


def sum_scratch(shapes, groups):
    number = len(shapes)
    return (
        [pltpu.VMEM((rows // 2, columns), BF16) for rows, columns in shapes]
        + [pltpu.VMEM((groups // 2 - 1, rows // 2, columns), BF16) for rows, columns in shapes]
        + [
            pltpu.SemaphoreType.DMA((2, number)),
            pltpu.SemaphoreType.DMA((2, number, groups // 2 - 1)),
            pltpu.SemaphoreType.DMA((2, number)),
            pltpu.SemaphoreType.DMA((number,)),
        ]
    )


def greet(ring, others=()):
    barrier = pltpu.get_barrier_semaphore()
    peers = [ring.next(0), ring.next(1)] + list(others)
    for peer in peers:
        pl.semaphore_signal(barrier, inc=1, device_id=peer, device_id_type=MESH)
    pl.semaphore_wait(barrier, len(peers))


def ring_semaphores(count, subs=SUBS):
    return [pltpu.SemaphoreType.DMA((2, subs, count - 1))] * 2


def ring_slots(count, rows, columns):
    return pltpu.VMEM((2, SUBS, count, rows // (2 * SUBS), columns), BF16)


ANY = pl.BlockSpec(memory_space=pl.ANY)
VMEM = pl.BlockSpec(memory_space=pltpu.VMEM)


def ring_params(number):
    return pltpu.CompilerParams(
        collective_id=number, has_side_effects=True, vmem_limit_bytes=60 << 20
    )


class WholeWeight:
    def __init__(self, ring, groups, weight, full, sends, recvs, keep_sem, far_sems, near_sems):
        self.ring, self.groups, self.full, self.far_sems, self.near_sems = ring, groups, full, far_sems, near_sems
        part = weight.shape[0] // groups
        group = ring.group
        own = lambda start, size: weight.at[pl.ds(pl.multiple_of(group * part + start, size), size), :]
        self.gather = Gather(
            ring, own, lambda origin, start, size: full.at[origin, group, pl.ds(start, size), :],
            sends, recvs, part, 1,
        )
        self.keep = pltpu.make_async_copy(own(0, part), full.at[ring.me, group], keep_sem)
        self.mate = (group + 1 - 2 * (group % 2), ring.me)
        self.across = groups // 2

    def peer(self, k):
        return ((self.ring.group + 2 * k) % self.groups, self.ring.me)

    def peers(self):
        return [self.mate] + [self.peer(k) for k in range(1, self.across)]

    def far(self, k, way, step):
        gather = self.gather
        part = self.full.at[gather.origin(way, step), self.ring.group, pl.ds(way * gather.piece, gather.piece), :]
        return pltpu.make_async_remote_copy(
            src_ref=part, dst_ref=part,
            send_sem=self.far_sems.at[0, k - 1, way, step], recv_sem=self.far_sems.at[1, k - 1, way, step],
            device_id=self.peer(k), device_id_type=MESH,
        )

    def near(self, k):
        part = self.full.at[:, (self.ring.group + self.groups - 2 * k) % self.groups]
        return pltpu.make_async_remote_copy(
            src_ref=part, dst_ref=part, send_sem=self.near_sems.at[0, k], recv_sem=self.near_sems.at[1, k],
            device_id=self.mate, device_id_type=MESH,
        )

    def pass_on(self, step):
        for k in range(1, self.across):
            for way in (0, 1):
                self.far(k, way, step).start()

    def begin(self):
        self.gather.begin()
        self.keep.start()

    def hop(self, step):
        self.gather.hop(step)
        self.pass_on(step)

    def exchange(self):
        self.gather.arrived(self.ring.count - 1)
        self.pass_on(self.ring.count - 1)
        self.keep.wait()
        self.pass_on(0)
        self.near(0).start()

    def every_far(self, body):
        def run(step, carry):
            for k in range(1, self.across):
                for way in (0, 1):
                    body(self.far(k, way, step))
            return carry

        lax.fori_loop(0, self.ring.count, run, 0)

    def back(self):
        self.every_far(lambda copy: copy.wait_recv())
        for k in range(1, self.across):
            self.near(k).start()

    def end(self):
        for k in range(self.across):
            self.near(k).wait()
        self.every_far(lambda copy: copy.wait_send())
        self.gather.end()


def gather_kernel(count, tokens, tokens_full, sends, recvs, local):
    ring = Ring(count)
    rows = tokens.shape[0]
    greet(ring)
    keep = pltpu.make_async_copy(
        tokens, tokens_full.at[pl.ds(pl.multiple_of(ring.me * rows, rows), rows), :], local
    )
    keep.start()
    ring_gather(
        Gather(ring, row_own(tokens), row_view(tokens_full, rows), sends, recvs, rows), lambda step: None
    )
    keep.wait()


def gather_tokens(tokens, count):
    rows, model = tokens.shape
    return pl.pallas_call(
        functools.partial(gather_kernel, count),
        name="gather_tokens",
        out_shape=jax.ShapeDtypeStruct((count * rows, model), tokens.dtype),
        in_specs=[ANY],
        out_specs=ANY,
        scratch_shapes=ring_semaphores(count) + [pltpu.SemaphoreType.DMA],
        compiler_params=ring_params(1),
        cost_estimate=pl.CostEstimate(flops=0, bytes_accessed=300 << 20, transcendentals=0),
    )(tokens)


def attend_kernel(
    count, mixed, w_out, tokens, gain, w_gate, w_up, w_down, cotangent,
    resid, full, hidden, grad_gate, grad_up, cotangents,
    gathered, out_box, gate_box, up_box, down_box, mixed_boxes, token_boxes, normed, gates, stages,
    sends, recvs, weight_sems, keep_sem, mixed_sems, token_sems, out_sems, normed_sems, stage_sems,
):
    ring = Ring(count)
    rows = cotangent.shape[0]
    half = rows // 2
    gather = Gather(ring, row_own(cotangent), row_view(gathered, rows), sends, recvs, rows)
    keep = pltpu.make_async_copy(
        cotangent, gathered.at[pl.ds(pl.multiple_of(ring.me * rows, rows), rows), :], keep_sem
    )
    loads = [
        pltpu.make_async_copy(source, box, weight_sems.at[k])
        for k, (source, box) in enumerate(
            ((w_out, out_box), (w_gate, gate_box), (w_up, up_box), (w_down, down_box))
        )
    ]

    def place(way, step):
        return pl.ds(pl.multiple_of(gather.origin(way, step) * rows + way * half, half), half)

    def mixed_copy(way, step):
        return pltpu.make_async_copy(
            mixed.at[:, place(way, step), :], mixed_boxes.at[step % 2, way], mixed_sems.at[step % 2, way]
        )

    def token_copy(way, step):
        return pltpu.make_async_copy(
            tokens.at[place(way, step), :], token_boxes.at[step % 2, way], token_sems.at[step % 2, way]
        )

    def out_copy(way, step):
        at = place(way, step)
        return pltpu.make_async_copy(gathered.at[at, :], cotangents.at[at, :], out_sems.at[way, step])

    def normed_copy(way, step):
        return pltpu.make_async_copy(
            normed.at[step % 2, pl.ds(way * half, half), :], full.at[place(way, step), :],
            normed_sems.at[step % 2, way],
        )

    def stage_copy(k, way, step):
        target = (hidden, grad_gate, grad_up)[k]
        return pltpu.make_async_copy(
            stages.at[step % 2, k, way], target.at[place(way, step), :], stage_sems.at[step % 2, k, way]
        )

    def settle(step):
        for way in (0, 1):
            normed_copy(way, step).wait()
            for k in range(3):
                stage_copy(k, way, step).wait()

    def fetch(step):
        for way in (0, 1):
            mixed_copy(way, step).start()
            token_copy(way, step).start()

    def put(k, step, value):
        low = value.astype(BF16)
        for way in (0, 1):
            stages[step % 2, k, way] = low[way * half : way * half + half]
            stage_copy(k, way, step).start()

    def prepare(step):
        @pl.when(step > 1)
        def _():
            settle(step - 2)

        slot = step % 2
        for way in (0, 1):
            mixed_copy(way, step).wait()
            token_copy(way, step).wait()

        @pl.when(step + 1 < count)
        def _():
            fetch(step + 1)

        heads = jnp.concatenate(
            [
                jnp.concatenate([mixed_boxes[slot, way, j] for j in range(count)], 1)
                for way in (0, 1)
            ],
            0,
        )
        value = jnp.concatenate([token_boxes[slot, 0], token_boxes[slot, 1]], 0).astype(F32)
        value = value + mm(heads, out_box[...])

        @pl.when(step == 0)
        def _():
            resid[...] = value

        scale = lax.rsqrt(jnp.mean(value * value, axis=1, keepdims=True) + 1e-6)
        normed[slot] = (value * scale * gain[...].astype(F32).reshape(1, -1)).astype(BF16)
        for way in (0, 1):
            normed_copy(way, step).start()
        inputs = normed[slot]
        gate = mm(inputs, gate_box[...], (1, 1))
        up = mm(inputs, up_box[...], (1, 1))
        sig = sigmoid(gate)
        opened = gate * sig
        put(0, step, opened * up)
        gates[0] = up * sig * (1.0 + gate * (1.0 - sig))
        gates[1] = opened

    def feed(step):
        for way in (0, 1):
            out_copy(way, step).start()
        grad = mm(
            jnp.concatenate([gathered[place(0, step), :], gathered[place(1, step), :]], 0), down_box[...], (1, 1)
        )
        put(1, step, grad * gates[0])
        put(2, step, grad * gates[1])

    def run(step, carry):
        @pl.when(step == 0)
        def _():
            gather.begin()
            for load in loads:
                load.wait()

        prepare(step)

        @pl.when(step == 0)
        def _():
            keep.wait()

        @pl.when((step > 0) & (step < count - 1))
        def _():
            gather.hop(step)

        @pl.when(step == count - 1)
        def _():
            gather.arrived(step)

        feed(step)
        return carry

    keep.start()
    fetch(0)
    for load in loads:
        load.start()
    greet(ring)
    lax.fori_loop(0, count, run, 0)
    gather.end()
    settle(count - 2)
    settle(count - 1)

    def drain(step, carry):
        for way in (0, 1):
            out_copy(way, step).wait()
        return carry

    lax.fori_loop(0, count, drain, 0)


def attend(mixed, w_out, tokens, gain, w_gate, w_up, w_down, cotangent, count):
    rows, model = cotangent.shape
    slots, inner = count * rows, w_down.shape[0]
    wide = mixed.shape[2]
    return pl.pallas_call(
        functools.partial(attend_kernel, count),
        name="attend",
        out_shape=[
            jax.ShapeDtypeStruct((rows, model), F32),
            jax.ShapeDtypeStruct((slots, model), BF16),
        ]
        + [jax.ShapeDtypeStruct((slots, inner), BF16)] * 3
        + [jax.ShapeDtypeStruct((slots, model), BF16)],
        in_specs=[ANY] * 3 + [VMEM] + [ANY] * 4,
        out_specs=[VMEM] + [ANY] * 5,
        scratch_shapes=[pltpu.VMEM((slots, model), BF16), pltpu.VMEM(w_out.shape, BF16)]
        + [pltpu.VMEM((inner, model), BF16)] * 3
        + [
            pltpu.VMEM((2, 2, count, rows // 2, wide), BF16),
            pltpu.VMEM((2, 2, rows // 2, model), BF16),
            pltpu.VMEM((2, rows, model), BF16),
            pltpu.VMEM((2, rows, inner), F32),
            pltpu.VMEM((2, 3, 2, rows // 2, inner), BF16),
        ]
        + ring_semaphores(count)
        + [
            pltpu.SemaphoreType.DMA((4,)),
            pltpu.SemaphoreType.DMA,
            pltpu.SemaphoreType.DMA((2, 2)),
            pltpu.SemaphoreType.DMA((2, 2)),
            pltpu.SemaphoreType.DMA((2, count)),
            pltpu.SemaphoreType.DMA((2, 2)),
            pltpu.SemaphoreType.DMA((2, 3, 2)),
        ],
        compiler_params=ring_params(2),
        cost_estimate=pl.CostEstimate(
            flops=2 * slots * model * model + 6 * slots * model * inner, bytes_accessed=300 << 20,
            transcendentals=slots * inner,
        ),
    )(mixed, w_out, tokens, gain, w_gate, w_up, w_down, cotangent)


def norm_back(inputs, scale, gain, grad_normed):
    weighted = gain * grad_normed
    inner = jnp.mean(weighted * inputs, axis=1, keepdims=True)
    unit = inputs * scale
    return scale * weighted - unit * (scale * scale * inner), grad_normed * unit


JOBS = 8


def ffn_back_kernel(
    count, groups, rows, grad_gate, grad_up, hidden_in, w_gate, w_up, resid_in, cotangent_in, gain, inputs, cotangents,
    grad_resid, full, grad_gain, sum_gate, sum_up, sum_down,
    slots, low, gw_gate, gw_up, gw_down, boxes, box_sems, hidden, resid, cotangent, load_sems, *rest,
):
    ring = Ring(count)
    sends, recvs, sends_two, recvs_two, local = rest[:5]
    sums = GroupSum(
        ring, groups, (gw_gate, gw_up, gw_down), rest[5:8], rest[8:11], (sum_gate, sum_up, sum_down), *rest[11:]
    )
    wide = boxes.shape[2]

    def box_copy(job, source):
        at = pl.multiple_of(job % (JOBS // 2) * wide, wide)
        return pltpu.make_async_copy(
            source.at[:, pl.ds(at, wide)], boxes.at[job % 2], box_sems.at[job % 2]
        )

    def fetch(job):
        @pl.when(job < JOBS // 2)
        def _():
            box_copy(job, inputs).start()

        @pl.when(job >= JOBS // 2)
        def _():
            box_copy(job, cotangents).start()

    loads = [
        pltpu.make_async_copy(source, target, load_sems.at[k])
        for k, (source, target) in enumerate(((hidden_in, hidden), (resid_in, resid), (cotangent_in, cotangent)))
    ]
    fetch(0)
    for load in loads:
        load.start()
    greet(ring, sums.peers())
    grad_gain[...] = jnp.zeros_like(grad_gain)
    half = rows // 2

    def partial(first, second, step):
        gates = jnp.concatenate([grad_gate[pl.ds(first, half), :], grad_gate[pl.ds(second, half), :]], 0)
        ups = jnp.concatenate([grad_up[pl.ds(first, half), :], grad_up[pl.ds(second, half), :]], 0)
        return mm(gates, w_gate[...]) + mm(ups, w_up[...])

    def finish(start, size, grad):
        value = resid[start : start + size, :]
        scale = lax.rsqrt(jnp.mean(value * value, axis=1, keepdims=True) + 1e-6)
        through, pieces = norm_back(value, scale, gain[...].astype(F32).reshape(1, -1), grad)
        result = cotangent[start : start + size, :].astype(F32) + through
        grad_resid[start : start + size, :] = result
        grad_gain[...] += jnp.sum(pieces, axis=0, keepdims=True)
        low[start : start + size, :] = result.astype(BF16)

    def work(job, carry):
        box_copy(job, inputs).wait()

        @pl.when(job + 1 < JOBS)
        def _():
            fetch(job + 1)

        at = pl.ds(pl.multiple_of(job % (JOBS // 2) * wide, wide), wide)

        @pl.when(job < JOBS // 2)
        def _():
            box = boxes[job % 2]
            gw_gate[:, at] = mm(grad_gate[...], box, (0, 0)).astype(BF16)
            gw_up[:, at] = mm(grad_up[...], box, (0, 0)).astype(BF16)

        @pl.when(job >= JOBS // 2)
        def _():
            gw_down[:, at] = mm(hidden[...], boxes[job % 2], (0, 0)).astype(BF16)

        return carry

    each = JOBS // 4

    def beside_scatter(step):
        @pl.when(step == 2)
        def _():
            for load in loads:
                load.wait()

        @pl.when(step == 3)
        def _():
            sums.second((0, 1))

        @pl.when(step < 4)
        def _():
            lax.fori_loop(step * each, step * each + each, work, 0)

        @pl.when(step == 1)
        def _():
            sums.first((0, 1))

        @pl.when(step == 3)
        def _():
            sums.first((2,))

        @pl.when(step == 5)
        def _():
            sums.second((2,))

    def beside_gather(step):
        @pl.when(step == count - 3)
        def _():
            sums.third((0, 1))

        @pl.when(step == count - 2)
        def _():
            sums.third((2,))

    gather = Gather(ring, row_own(low), row_view(full, rows), sends_two, recvs_two, rows)
    start = lambda way, sub: gather.copy(way, sub, 0, ring.me, True).start()
    ring_scatter(Scatter(ring, partial, slots, sends, recvs, rows, finish, start), beside_scatter)
    keep = pltpu.make_async_copy(low, full.at[pl.ds(pl.multiple_of(ring.me * rows, rows), rows), :], local)
    keep.start()
    ring_gather(gather, beside_gather, True)
    keep.wait()
    sums.last()


def ffn_back(grad_gate, grad_up, hidden, w_gate, w_up, resid, cotangent, gain, inputs, cotangents, count, groups):
    rows, model = resid.shape
    slots, inner = grad_up.shape
    shapes = [(inner, model)] * 3
    return pl.pallas_call(
        functools.partial(ffn_back_kernel, count, groups, rows),
        name="ffn_back",
        out_shape=[
            jax.ShapeDtypeStruct((rows, model), F32),
            jax.ShapeDtypeStruct((slots, model), BF16),
            jax.ShapeDtypeStruct((1, model), F32),
        ]
        + [jax.ShapeDtypeStruct(shape, BF16) for shape in shapes],
        in_specs=[VMEM] * 2 + [ANY] + [VMEM] * 2 + [ANY] * 2 + [VMEM] + [ANY] * 2,
        out_specs=[VMEM, ANY, VMEM] + [ANY] * 3,
        scratch_shapes=[ring_slots(count, rows, model), pltpu.VMEM((rows, model), BF16)]
        + [pltpu.VMEM(shape, BF16) for shape in shapes]
        + [pltpu.VMEM((2, slots, model // (JOBS // 2)), BF16), pltpu.SemaphoreType.DMA((2,))]
        + [pltpu.VMEM((slots, inner), BF16), pltpu.VMEM((rows, model), F32), pltpu.VMEM((rows, model), BF16)]
        + [pltpu.SemaphoreType.DMA((3,))]
        + ring_semaphores(count) * 2
        + [pltpu.SemaphoreType.DMA]
        + sum_scratch(shapes, groups),
        compiler_params=ring_params(3),
        cost_estimate=pl.CostEstimate(
            flops=10 * slots * model * inner, bytes_accessed=600 << 20, transcendentals=0
        ),
    )(grad_gate, grad_up, hidden, w_gate, w_up, resid, cotangent, gain, inputs, cotangents)


def last_kernel(
    count, groups, rows, terms, tokens_in, grad_resid_in, gain, small, *rest,
):
    grads, rest = rest[:5], rest[5:]
    grad_tokens, total = rest[:2]
    targets, rest = rest[2:7], rest[7:]
    slots, first_box, slice_own, spread, second_box, second_own, boxes, box_sems, tokens, grad_resid, load_sems = rest[:11]
    sends, recvs, first_sends, first_recvs, spread_sends, spread_recvs, second_sends, second_recvs = rest[11:19]
    ring = Ring(count)
    sums = GroupSum(ring, groups, grads, rest[19:24], rest[24:29], targets, *rest[29:])
    loads = [
        pltpu.make_async_copy(tokens_in, tokens, load_sems.at[0]),
        pltpu.make_async_copy(grad_resid_in, grad_resid, load_sems.at[1]),
    ]
    me, group = ring.me, ring.group
    first_peers = [(group, (me + k) % count) for k in range(1, count)]
    second_peers = [((group + k) % groups, me) for k in range(1, groups)]
    barrier = pltpu.get_barrier_semaphore()
    for peer in first_peers + second_peers:
        pl.semaphore_signal(barrier, inc=1, device_id=peer, device_id_type=MESH)
    pl.semaphore_wait(barrier, count + groups - 2)

    lanes = small.shape[1] // count

    def lanes_of(device):
        return pl.ds(pl.multiple_of(device * lanes, lanes), lanes)

    def first(k):
        peer = first_peers[k]
        return pltpu.make_async_remote_copy(
            src_ref=small.at[0:8, lanes_of(peer[1])], dst_ref=first_box.at[k], send_sem=first_sends.at[k],
            recv_sem=first_recvs.at[k], device_id=peer, device_id_type=MESH,
        )

    def share(k):
        return pltpu.make_async_remote_copy(
            src_ref=slice_own, dst_ref=spread.at[:, lanes_of(me)], send_sem=spread_sends.at[k],
            recv_sem=spread_recvs.at[k], device_id=first_peers[k], device_id_type=MESH,
        )

    def second(k):
        return pltpu.make_async_remote_copy(
            src_ref=second_own, dst_ref=second_box.at[k], send_sem=second_sends.at[k],
            recv_sem=second_recvs.at[k], device_id=second_peers[k], device_id_type=MESH,
        )

    every = range(len(grads))
    sums.first(every)
    for k in range(count - 1):
        first(k).start()
    half = rows // 2

    def box_copy(way, start, slot):
        return pltpu.make_async_copy(
            terms.at[pl.ds(start, half), :], boxes.at[slot, way], box_sems.at[slot, way]
        )

    def fetch(step):
        for way, owner in ((0, ring.at(-1 - step)), (1, ring.at(1 + step))):
            box_copy(way, pl.multiple_of(owner * rows + way * half, half), step % 2).start()

    def partial(first, second, step):
        for way, start in ((0, first), (1, second)):
            box_copy(way, start, step % 2).wait()

        @pl.when(step + 1 < count)
        def _():
            fetch(step + 1)

        return jnp.concatenate([boxes[step % 2, 0], boxes[step % 2, 1]], 0).astype(F32)

    def finish(start, size, grad):
        value = tokens[start : start + size, :].astype(F32)
        scale = lax.rsqrt(jnp.mean(value * value, axis=1, keepdims=True) + 1e-6)
        through, pieces = norm_back(value, scale, gain[...].astype(F32).reshape(1, -1), grad)
        grad_tokens[start : start + size, :] = grad_resid[start : start + size, :] + through

    def early():
        sums.second(every)
        for k in range(count - 1):
            first(k).wait()
        mine = small[0:8, lanes_of(me)]
        for k in range(count - 1):
            mine = mine + first_box[k]
        slice_own[...] = mine
        spread[:, lanes_of(me)] = mine
        for k in range(count - 1):
            share(k).start()

    def soon():
        for k in range(count - 1):
            share(k).wait()
        second_own[0:8] = spread[...]
        second_own[8:] = small[8:]
        for k in range(groups - 1):
            second(k).start()

    def late():
        for k in range(groups - 1):
            second(k).wait()
        mine = second_own[...]
        for k in range(groups - 1):
            mine = mine + second_box[k]
        total[...] = mine
        for load in loads:
            load.wait()

    def beside(step):
        pl.when(step == 0)(early)
        pl.when(step == 1)(soon)
        for i in every:
            pl.when(step == count - 1 - len(every) + i)(lambda i=i: sums.third((i,)))
        pl.when(step == count - 2)(late)

    fetch(0)
    for load in loads:
        load.start()
    ring_scatter(Scatter(ring, partial, slots, sends, recvs, rows, finish), beside)
    sums.last()


def last_step(terms, tokens, grad_resid, gain, small, grads, count, groups):
    rows, model = tokens.shape
    return pl.pallas_call(
        functools.partial(last_kernel, count, groups, rows),
        name="last_step",
        out_shape=[jax.ShapeDtypeStruct((rows, model), F32), jax.ShapeDtypeStruct(small.shape, F32)]
        + [jax.ShapeDtypeStruct(g.shape, BF16) for g in grads],
        in_specs=[ANY] * 3 + [VMEM] * (2 + len(grads)),
        out_specs=[VMEM, VMEM] + [ANY] * len(grads),
        scratch_shapes=[
            ring_slots(count, rows, model),
            pltpu.VMEM((count - 1, 8, model // count), F32),
            pltpu.VMEM((8, model // count), F32),
            pltpu.VMEM((8, model), F32),
            pltpu.VMEM((groups - 1,) + small.shape, F32),
            pltpu.VMEM(small.shape, F32),
            pltpu.VMEM((2, 2, rows // 2, model), BF16),
            pltpu.SemaphoreType.DMA((2, 2)),
            pltpu.VMEM((rows, model), BF16),
            pltpu.VMEM((rows, model), F32),
            pltpu.SemaphoreType.DMA((2,)),
        ]
        + ring_semaphores(count)
        + [pltpu.SemaphoreType.DMA((count - 1,))] * 4
        + [pltpu.SemaphoreType.DMA((groups - 1,))] * 2
        + sum_scratch([g.shape for g in grads], groups),
        compiler_params=ring_params(4),
        cost_estimate=pl.CostEstimate(flops=0, bytes_accessed=300 << 20, transcendentals=0),
    )(terms, tokens, grad_resid, gain, small, *grads)


def results_kernel(heads, taps, wide, width, total, *refs):
    number = (len(refs) - 7) // 2
    for source, target in zip(refs[:number], refs[number : 2 * number]):
        target[...] = source[...].astype(target.dtype)
    g_first, g_second, g_head, gt_query, gt_key, gt_value, g_beta = refs[2 * number :]

    @pl.when(pl.program_id(0) == 0)
    def _():
        g_first[...] = total[0:1, :]
        g_second[...] = total[1:2, :]
        g_head[...] = total[2:3, 0:width]
        row = 8 + heads
        for place, target in enumerate((gt_query, gt_key, gt_value)):
            target[...] = total[row : row + taps, place * wide : (place + 1) * wide]
        g_beta[...] = total[8 : 8 + heads, :]


def results(total, arrays, heads, taps, wide, width):
    model = total.shape[1]
    steps = next(n for n in (2, 1) if all(a.shape[0] % (8 * n) == 0 for a, _ in arrays))
    small = [(1, model), (1, model), (1, width)] + [(taps, wide)] * 3 + [(heads, model)]
    piece = lambda a: pl.BlockSpec((a.shape[0] // steps, a.shape[1]), lambda n: (n, 0))
    whole = lambda shape: pl.BlockSpec(shape, lambda n: (0, 0))
    return pl.pallas_call(
        functools.partial(results_kernel, heads, taps, wide, width),
        name="results",
        grid=(steps,),
        out_shape=[jax.ShapeDtypeStruct(a.shape, kind) for a, kind in arrays]
        + [jax.ShapeDtypeStruct(shape, F32) for shape in small],
        in_specs=[whole(total.shape)] + [piece(a) for a, _ in arrays],
        out_specs=[piece(a) for a, _ in arrays] + [whole(shape) for shape in small],
        compiler_params=pltpu.CompilerParams(vmem_limit_bytes=56 << 20),
        cost_estimate=pl.CostEstimate(flops=0, bytes_accessed=48 << 20, transcendentals=0),
    )(total, *[a for a, _ in arrays])


def spread_hops(step, chunks, count, hop, start=0):
    each = -(-(count - 1) // (chunks - 1))
    for place in range(each):
        number = step * each + place

        @pl.when((number >= start) & (number < count - 1))
        def _():
            hop(number)


def plan_hops(chunks, hops, latency=0.8, segment=2.5):
    now, link, due, done, table = 0.0, 0.0, {}, {}, []

    def send(chunk):
        nonlocal link
        link = max(now, link) + 1.0
        done[chunk] = done.get(chunk, -1) + 1
        due[chunk] = link + latency

    for step in range(chunks):
        for half in range(2):
            ready, moves = True, []
            while ready:
                ready = sorted((due[c], c) for c in due if due[c] <= now and done[c] < hops - 1)
                if ready:
                    send(ready[0][1])
                    moves.append((ready[0][1], done[ready[0][1]]))
            table.append(moves)
            now += segment
        send(step)
    return table, [done[chunk] for chunk in range(chunks)]


def forward_kernel(
    heads, width, seqs, count, groups, chunks,
    starts, lengths, tokens, w_query, w_key, w_value, w_gate, w_beta,
    taps_query, taps_key, taps_value, gain, gain_first, w_out,
    mixed_full, w_full, mixed, p_query, p_key, p_value, p_gate, p_beta, z_query, z_key, z_value,
    delta_out, change_out, inverse_out, state_out,
    tail_query, tail_key, tail_value, state, stage, sends, recvs, keeps,
    w_sends, w_recvs, w_keep, w_far, w_near,
):
    step = pl.program_id(0)
    size = tokens.shape[0]
    first = step * size

    @pl.when(step == 0)
    def _():
        for tail in (tail_query, tail_key, tail_value):
            tail[...] = jnp.zeros_like(tail)
        state[...] = jnp.zeros_like(state)

    ring = Ring(count)

    def chunk_gather(chunk):
        return Gather(
            ring,
            lambda start, length: stage.at[chunk, pl.ds(start, length), :],
            lambda origin, start, length: mixed_full.at[
                origin, pl.ds(pl.multiple_of(chunk * size + start, length), length), :
            ],
            sends.at[chunk], recvs.at[chunk], size, 1,
        )

    def keep(chunk):
        return pltpu.make_async_copy(
            stage.at[chunk],
            mixed_full.at[ring.me, pl.ds(pl.multiple_of(chunk * size, size), size), :],
            keeps.at[chunk],
        )

    weight = WholeWeight(ring, groups, w_out, w_full, w_sends, w_recvs, w_keep, w_far, w_near)
    each = -(-(count - 1) // (chunks - 1))

    def weight_hops(late=0):
        for place in range(each):
            number = (2 * step + late) * each + place
            pl.when((number > 0) & (number < count - 1))(lambda: weight.hop(number))
            pl.when(number == count - 1)(weight.exchange)

    table, done = plan_hops(chunks, count - 1)

    def chunk_hops(half):
        for place, moves in enumerate(table[half::2]):
            if moves:
                @pl.when(step == place)
                def _():
                    for chunk, hop in moves:
                        chunk_gather(chunk).hop(hop)

    @pl.when(step == 0)
    def _():
        greet(ring, weight.peers())
        weight.begin()

    weight_hops()
    chunk_hops(0)
    rows, seg_rows, seg_columns, before, last = chunk_masks(starts, lengths, seqs, first, size)
    same = seg_rows == seg_columns
    i = lax.broadcasted_iota(jnp.int32, (size, size), 0)
    j = lax.broadcasted_iota(jnp.int32, (size, size), 1)
    strict = jnp.where(same & (i > j), 1.0, 0.0)
    inclusive = jnp.where(same & (i >= j), 1.0, 0.0)
    carried = jnp.where(seg_rows == before, 1.0, 0.0)
    ending = jnp.where(seg_rows == last, 1.0, 0.0)
    kept = jnp.where(before == last, 1.0, 0.0)
    live = jnp.where(seg_rows % 2 == 1, 1.0, 0.0)
    joined = [
        jnp.where(segment_at(rows - offset, starts, lengths, seqs) == seg_rows, 1.0, 0.0)
        for offset in range(1, taps_query.shape[0])
    ]
    inputs = normed_rows(tokens, gain_first)[0].astype(BF16)

    def feature(weight, taps, tail, p_out, z_out):
        projected = jnp.dot(inputs, weight[...], preferred_element_type=F32)
        p_out[...] = projected
        tail[8:, :] = projected
        tap = taps[...].astype(F32)
        result = projected * tap[0:1]
        for offset in range(1, tap.shape[0]):
            result = result + tail[8 - offset : 8 - offset + size, :] * tap[offset : offset + 1] * joined[offset - 1]
        tail[0:8, :] = projected[size - 8 :, :]
        z_out[...] = result
        return result * sigmoid(result)

    u_query = feature(w_query, taps_query, tail_query, p_query, z_query)
    u_key = feature(w_key, taps_key, tail_key, p_key, z_key)
    u_value = feature(w_value, taps_value, tail_value, p_value, z_value)
    gate = jnp.dot(inputs, w_gate[...], preferred_element_type=F32)
    p_gate[...] = gate
    beta_pre = mm(inputs, w_beta[...], (1, 1))
    p_beta[...] = beta_pre
    strength = sigmoid(beta_pre)
    opened = gate * sigmoid(gate)
    scale = width ** (-0.5)
    head_gain = gain[...].astype(F32)
    for h in range(heads):
        if h == heads // 2:
            weight_hops(1)
            chunk_hops(1)
        cols = slice(h * width, (h + 1) * width)
        uq, uk = u_query[:, cols], u_key[:, cols]
        query = (uq * lax.rsqrt(jnp.sum(uq * uq, axis=1, keepdims=True) + 1e-6)).astype(BF16)
        key = (uk * lax.rsqrt(jnp.sum(uk * uk, axis=1, keepdims=True) + 1e-6)).astype(BF16)
        value = u_value[:, cols].astype(BF16).astype(F32)
        beta = strength[:, h : h + 1]
        memory = state[h]
        low_memory = memory.astype(BF16)
        state_out[0, h] = low_memory
        lower = mm(key, key, (1, 1)) * strict * beta
        inverse = inverse_unit_lower(lower, size).astype(BF16)
        inverse_out[0, h] = inverse
        within = mm(query, key, (1, 1)) * inclusive
        change = mm(inverse, beta * (value - carried * mm(key, low_memory)))
        low_change = change.astype(BF16)
        change_out[:, cols] = low_change
        out = scale * (carried * mm(query, low_memory) + mm(within, low_change))
        state[h] = kept * memory + mm(key, ending * change, (0, 0))
        delta_out[:, cols] = out
        normal = out * lax.rsqrt(jnp.mean(out * out, axis=1, keepdims=True) + 1e-5) * head_gain
        low_mixed = (normal * opened[:, cols] * live).astype(BF16)
        mixed[:, cols] = low_mixed
        stage[step, :, cols] = low_mixed

    chunk_gather(step).begin()
    keep(step).start()

    @pl.when(step == chunks - 1)
    def _():
        def finish(number, carry):
            pl.when(number == (count - 1) // 2)(weight.back)
            for chunk in range(chunks):
                if done[chunk] < count - 2:
                    pl.when(done[chunk] + number < count - 1)(
                        lambda chunk=chunk: chunk_gather(chunk).hop(done[chunk] + number)
                    )
            return carry

        lax.fori_loop(1, count - 1, finish, 0)

        def settle(chunk, carry):
            chunk_gather(chunk).arrived(count - 1)
            chunk_gather(chunk).end()
            keep(chunk).wait()
            return carry

        lax.fori_loop(0, chunks, settle, 0)
        weight.end()


def forward_mixer(tokens, w_query, w_key, w_value, w_gate, w_beta, taps_query, taps_key, taps_value, gain, gain_first, starts, lengths, w_out, count, groups):
    slots, model = tokens.shape
    wide = w_query.shape[1]
    width = gain.shape[0]
    heads = wide // width
    seqs = starts.shape[1]
    chunks = slots // CHUNK
    taps = taps_query.shape[0]
    part = w_out.shape[0] // groups
    smem = pl.BlockSpec(memory_space=pltpu.SMEM)
    whole = lambda shape: pl.BlockSpec(shape, lambda n: (0,) * len(shape))
    piece = lambda shape: pl.BlockSpec(shape, lambda n: (n,) + (0,) * (len(shape) - 1))
    outs = [
        ((slots, wide), BF16), ((slots, wide), F32), ((slots, wide), F32), ((slots, wide), F32), ((slots, wide), F32),
        ((slots, w_beta.shape[0]), F32), ((slots, wide), F32), ((slots, wide), F32), ((slots, wide), F32),
        ((slots, wide), F32), ((slots, wide), BF16),
    ]
    return pl.pallas_call(
        functools.partial(forward_kernel, heads, width, seqs, count, groups, chunks),
        name="mixer_forward",
        grid=(chunks,),
        out_shape=[
            jax.ShapeDtypeStruct((count, slots, wide), BF16),
            jax.ShapeDtypeStruct((count, groups, part, model), BF16),
        ]
        + [jax.ShapeDtypeStruct(s, d) for s, d in outs]
        + [
            jax.ShapeDtypeStruct((chunks, heads, CHUNK, CHUNK), BF16),
            jax.ShapeDtypeStruct((chunks, heads, width, width), BF16),
        ],
        in_specs=[smem, smem, piece((CHUNK, model))]
        + [whole((model, wide))] * 4
        + [whole(w_beta.shape)]
        + [whole((taps, wide))] * 3
        + [whole((1, width)), VMEM, ANY],
        out_specs=[ANY, ANY]
        + [piece((CHUNK, s[1])) for s, d in outs]
        + [piece((1, heads, CHUNK, CHUNK)), piece((1, heads, width, width))],
        scratch_shapes=[pltpu.VMEM((CHUNK + 8, wide), F32)] * 3
        + [pltpu.VMEM((heads, width, width), F32), pltpu.VMEM((chunks, CHUNK, wide), BF16)]
        + [pltpu.SemaphoreType.DMA((chunks, 2, 1, count - 1))] * 2
        + [pltpu.SemaphoreType.DMA((chunks,))]
        + ring_semaphores(count, 1)
        + [
            pltpu.SemaphoreType.DMA,
            pltpu.SemaphoreType.DMA((2, groups // 2 - 1, 2, count)),
            pltpu.SemaphoreType.DMA((2, groups // 2)),
        ],
        compiler_params=ring_params(5),
        cost_estimate=pl.CostEstimate(
            flops=2 * slots * model * wide * 4 + slots * heads * CHUNK * 2 * CHUNK * 20,
            bytes_accessed=slots * model * 2 + 4 * model * wide * 2 + slots * wide * 36,
            transcendentals=slots * wide * 4,
        ),
    )(starts, lengths, tokens, w_query, w_key, w_value, w_gate, w_beta, taps_query, taps_key, taps_value, gain.reshape(1, width), gain_first, w_out)


def small_rows(heads, taps):
    return -(-(8 + heads + taps) // 8) * 8


def backward_kernel(
    heads, width, seqs, chunks, count, rows_own,
    starts, lengths, tokens, grad_attended, mixed, p_query, p_key, p_value, p_gate, p_beta,
    z_query, z_key, z_value, delta_out, change_in, inverse_in, state_in,
    w_query_in, w_key_in, w_value_in, w_gate_in, w_beta, w_out, taps_query, taps_key, taps_value, gain, gain_first,
    hidden, w_down, resid_in, g_second, grad_normed, gw_query, gw_key, gw_value, gw_gate, gw_out,
    small, output,
    a_query, a_key, a_value, a_gate, a_out, head_query, head_key, head_value, flow,
    w_query, w_key, w_value, w_gate, resid, load_sems, slots, sends, recvs,
):
    step = pl.program_id(0)
    size = tokens.shape[0]
    first = (chunks - 1 - step) * size

    @pl.when(step == 0)
    def _():
        for ref in (a_query, a_key, a_value, a_gate, a_out, small, flow):
            ref[...] = jnp.zeros_like(ref)
        small[1:2, :] = g_second[...]
        for ref in (head_query, head_key, head_value):
            ref[size:, :] = jnp.zeros((8, ref.shape[1]), F32)

    half = rows_own // 2

    def partial(one, two, number):
        return mm(jnp.concatenate([hidden[pl.ds(one, half), :], hidden[pl.ds(two, half), :]], 0), w_down[...])

    def finish(start, length, down):
        output[start : start + length, :] = (resid[start : start + length, :] + down).astype(BF16)

    ring = Ring(count)
    scatter = Scatter(ring, partial, slots, sends, recvs, rows_own, finish)
    loads = [
        pltpu.make_async_copy(source, target, load_sems.at[k])
        for k, (source, target) in enumerate(
            ((w_query_in, w_query), (w_key_in, w_key), (w_value_in, w_value), (w_gate_in, w_gate), (resid_in, resid))
        )
    ]

    @pl.when(step == 0)
    def _():
        for load in loads:
            load.start()
        greet(ring)

    spread_hops(step, chunks, count, scatter.hop)
    rows, seg_rows, seg_columns, before, last = chunk_masks(starts, lengths, seqs, first, size)
    same = seg_rows == seg_columns
    i = lax.broadcasted_iota(jnp.int32, (size, size), 0)
    j = lax.broadcasted_iota(jnp.int32, (size, size), 1)
    strict = jnp.where(same & (i > j), 1.0, 0.0)
    inclusive = jnp.where(same & (i >= j), 1.0, 0.0)
    carried = jnp.where(seg_rows == before, 1.0, 0.0)
    ending = jnp.where(seg_rows == last, 1.0, 0.0)
    kept = jnp.where(before == last, 1.0, 0.0)
    live = jnp.where(seg_rows % 2 == 1, 1.0, 0.0)
    taps = taps_query.shape[0]
    joined = [
        jnp.where(segment_at(rows + offset, starts, lengths, seqs) == seg_rows, 1.0, 0.0)
        for offset in range(1, taps)
    ]
    normal_rows, unit_rows = normed_rows(tokens, gain_first)
    inputs = normal_rows.astype(BF16)
    grad_rows = grad_attended[...]
    grad_mixed = mm(grad_rows, w_out[...], (1, 1))
    a_out[...] += mm(mixed[...], grad_rows, (0, 0))
    strength = sigmoid(p_beta[...])
    scale = width ** (-0.5)
    head_gain = gain[...].astype(F32)

    grads_query, grads_key, grads_value, grads_gate, grads_beta = [], [], [], [], []
    for h in range(heads):
        cols = slice(h * width, (h + 1) * width)
        out = delta_out[:, cols]
        gate = p_gate[:, cols]
        sig_gate = sigmoid(gate)
        silu_gate = gate * sig_gate
        root = lax.rsqrt(jnp.mean(out * out, axis=1, keepdims=True) + 1e-5)
        grad = grad_mixed[:, cols] * live
        unit = out * root
        grads_gate.append(grad * unit * head_gain * (sig_gate * (1.0 + gate * (1.0 - sig_gate))))
        grad_normal = grad * silu_gate
        small[2:3, 0:width] += jnp.sum(grad_normal * unit, axis=0, keepdims=True)
        push = grad_normal * head_gain
        grad_out = scale * root * (push - unit * jnp.mean(push * unit, axis=1, keepdims=True))

        zq, zk, zv = z_query[:, cols], z_key[:, cols], z_value[:, cols]
        sq, sk, sv = sigmoid(zq), sigmoid(zk), sigmoid(zv)
        uq, uk = zq * sq, zk * sk
        nq = lax.rsqrt(jnp.sum(uq * uq, axis=1, keepdims=True) + 1e-6)
        nk = lax.rsqrt(jnp.sum(uk * uk, axis=1, keepdims=True) + 1e-6)
        unit_q, unit_k = uq * nq, uk * nk
        query, key = unit_q.astype(BF16), unit_k.astype(BF16)
        beta = strength[:, h : h + 1]
        change = change_in[:, cols]
        inverse = inverse_in[0, h]
        memory = state_in[0, h]
        flowing = flow[h]
        low_flow = flowing.astype(BF16)
        low_out = grad_out.astype(BF16)

        within = mm(query, key, (1, 1)) * inclusive
        grad_within = (mm(low_out, change, (1, 1)) * inclusive).astype(BF16)
        grad_change = mm(within, low_out, (0, 0)) + ending * mm(key, low_flow)
        grad_mid = mm(inverse, grad_change, (0, 0))
        grad_value = beta * grad_mid
        low_value = grad_value.astype(BF16)
        cross = (mm(low_value, change, (1, 1)) * strict).astype(BF16)
        grad_query = carried * mm(low_out, memory, (1, 1)) + mm(grad_within, key)
        grad_key = (
            mm(grad_within, query, (0, 0))
            + ending * mm(change, low_flow, (1, 1))
            - carried * mm(low_value, memory, (1, 1))
            - mm(cross, key)
            - mm(cross, key, (0, 0))
        )
        flow[h] = (
            kept * flowing
            + mm(query, carried * grad_out, (0, 0))
            - mm(key, carried * grad_value, (0, 0))
        )
        grads_beta.append((1.0 - beta) * jnp.sum(grad_mid * change.astype(F32), axis=1, keepdims=True))
        du_q = nq * (grad_query - unit_q * jnp.sum(grad_query * unit_q, axis=1, keepdims=True))
        du_k = nk * (grad_key - unit_k * jnp.sum(grad_key * unit_k, axis=1, keepdims=True))
        grads_query.append(du_q * sq * (1.0 + zq * (1.0 - sq)))
        grads_key.append(du_k * sk * (1.0 + zk * (1.0 - sk)))
        grads_value.append(grad_value * sv * (1.0 + zv * (1.0 - sv)))

    tap_row = 8 + heads
    wide = heads * width

    def unconv(parts, taps_ref, head, projected, place):
        lanes = slice(place * wide, (place + 1) * wide)
        grad = jnp.concatenate(parts, axis=1)
        head[0:size, :] = grad
        tap = taps_ref[...].astype(F32)
        p = projected[...]
        result = grad * tap[0:1]
        small[tap_row : tap_row + 1, lanes] += jnp.sum(p * grad, axis=0, keepdims=True)
        for offset in range(1, taps):
            moved = head[offset : offset + size, :] * joined[offset - 1]
            result = result + moved * tap[offset : offset + 1]
            row = tap_row + offset
            small[row : row + 1, lanes] += jnp.sum(p * moved, axis=0, keepdims=True)
        head[size:, :] = grad[0:8, :]
        return result.astype(BF16)

    d_query = unconv(grads_query, taps_query, head_query, p_query, 0)
    d_key = unconv(grads_key, taps_key, head_key, p_key, 1)
    d_value = unconv(grads_value, taps_value, head_value, p_value, 2)
    d_gate = jnp.concatenate(grads_gate, axis=1).astype(BF16)
    spare = [jnp.zeros((size, 1), F32)] * (w_beta.shape[0] - heads)
    d_beta = jnp.concatenate(grads_beta + spare, axis=1).astype(BF16)

    @pl.when(step == 0)
    def _():
        for load in loads:
            load.wait()

    grad_inputs = (
        mm(d_query, w_query[...], (1, 1))
        + mm(d_key, w_key[...], (1, 1))
        + mm(d_value, w_value[...], (1, 1))
        + mm(d_gate, w_gate[...], (1, 1))
        + mm(d_beta, w_beta[...])
    )
    grad_normed[...] = grad_inputs.astype(BF16)
    small[0:1, :] += jnp.sum(grad_inputs * unit_rows, axis=0, keepdims=True)
    a_query[...] += mm(inputs, d_query, (0, 0))
    a_key[...] += mm(inputs, d_key, (0, 0))
    a_value[...] += mm(inputs, d_value, (0, 0))
    a_gate[...] += mm(inputs, d_gate, (0, 0))
    small[8 : 8 + heads, :] += mm(d_beta, inputs, (0, 0))[:heads]

    @pl.when(step == chunks - 1)
    def _():
        for target, source in (
            (gw_query, a_query), (gw_key, a_key), (gw_value, a_value), (gw_gate, a_gate),
            (gw_out, a_out),
        ):
            target[...] = source[...].astype(target.dtype)
        scatter.end()


def backward_mixer(tokens, grad_attended, saved, w_query, w_key, w_value, w_gate, w_beta, w_out, taps_query, taps_key, taps_value, gain, gain_first, starts, lengths, hidden, w_down, resid, g_second, count):
    slots, model = tokens.shape
    wide = w_query.shape[1]
    width = gain.shape[0]
    heads = wide // width
    seqs = starts.shape[1]
    chunks = slots // CHUNK
    taps = taps_query.shape[0]
    smem = pl.BlockSpec(memory_space=pltpu.SMEM)
    fixed = lambda shape: pl.BlockSpec(shape, lambda n: (0,) * len(shape), pipeline_mode=pl.Buffered(1))
    piece = lambda shape: pl.BlockSpec(shape, lambda n: (chunks - 1 - n,) + (0,) * (len(shape) - 1))
    rows = lambda a: piece((CHUNK, a.shape[1]))
    outs = (
        [((slots, model), BF16)] + [((model, wide), BF16)] * 4 + [((wide, model), BF16)]
        + [((small_rows(heads, taps), model), F32), (resid.shape, BF16)]
    )
    return pl.pallas_call(
        functools.partial(backward_kernel, heads, width, seqs, chunks, count, slots // count),
        name="mixer_backward",
        grid=(chunks,),
        out_shape=[jax.ShapeDtypeStruct(s, d) for s, d in outs],
        in_specs=[smem, smem, rows(tokens), rows(grad_attended)]
        + [rows(a) for a in saved[:11]]
        + [piece((1, heads, CHUNK, CHUNK)), piece((1, heads, width, width))]
        + [ANY] * 4
        + [fixed(w_beta.shape), fixed((wide, model))]
        + [fixed((taps, wide))] * 3
        + [fixed((1, width)), VMEM, fixed(hidden.shape), fixed(w_down.shape), ANY, fixed(g_second.shape)],
        out_specs=[piece((CHUNK, model))] + [fixed(s) for s, d in outs[1:]],
        scratch_shapes=[pltpu.VMEM((model, wide), F32)] * 4
        + [pltpu.VMEM((wide, model), F32)]
        + [pltpu.VMEM((CHUNK + 8, wide), F32)] * 3
        + [pltpu.VMEM((heads, width, width), F32)]
        + [pltpu.VMEM((model, wide), BF16)] * 4
        + [pltpu.VMEM(resid.shape, F32), pltpu.SemaphoreType.DMA((5,)), ring_slots(count, slots // count, model)]
        + ring_semaphores(count),
        compiler_params=ring_params(6),
        cost_estimate=pl.CostEstimate(
            flops=2 * slots * model * wide * 10 + slots * heads * CHUNK * 2 * CHUNK * 8,
            bytes_accessed=slots * model * 6 + 10 * model * wide * 2 + slots * wide * 36,
            transcendentals=slots * wide * 8,
        ),
    )(starts, lengths, tokens, grad_attended, *saved, w_query, w_key, w_value, w_gate, w_beta, w_out, taps_query, taps_key, taps_value, gain.reshape(1, width), gain_first, hidden, w_down, resid, g_second)


def make_shards(groups, count):
    def shards(
        tokens, attn_gain, w_query, w_key, w_value, conv_query, conv_key, conv_value, w_beta, w_gate_out,
        head_gain, w_out, ffn_gain, w_gate, w_up, w_down, seq_starts, seq_lengths, cotangent,
    ):
        model = tokens.shape[1]
        heads = w_beta.shape[1]
        beta_rows = w_beta.T if heads > 1 else jnp.pad(w_beta.T, ((0, 1), (0, 0)))
        tokens_full = gather_tokens(tokens, count)
        mixed_full, w_out_full, *saved = forward_mixer(
            tokens_full, w_query, w_key, w_value, w_gate_out, beta_rows,
            conv_query, conv_key, conv_value, head_gain, attn_gain, seq_starts, seq_lengths, w_out, count, groups,
        )
        w_out_full = w_out_full.reshape(-1, tokens.shape[1])
        resid, ffn_full, hidden, grad_gate, grad_up, grad_full = attend(
            mixed_full, w_out_full, tokens_full, ffn_gain, w_gate.T, w_up.T, w_down, cotangent, count
        )
        grad_resid, grad_attended, g_second, *ffn_grads = ffn_back(
            grad_gate, grad_up, hidden, w_gate.T, w_up.T, resid, cotangent, ffn_gain, ffn_full, grad_full,
            count, groups,
        )
        pulled = backward_mixer(
            tokens_full, grad_attended, saved, w_query, w_key, w_value, w_gate_out, beta_rows, w_out,
            conv_query, conv_key, conv_value, head_gain, attn_gain, seq_starts, seq_lengths,
            hidden, w_down, resid, g_second, count,
        )
        terms, gw_query, gw_key, gw_value, gw_gate_out, gw_out, small, output = pulled
        grad_tokens, total, *mixer_grads = last_step(
            terms, tokens, grad_resid, attn_gain, small,
            (gw_query, gw_key, gw_value, gw_gate_out, gw_out), count, groups,
        )
        taps, wide = conv_query.shape
        output, grad_tokens, *rest = results(
            total,
            [(output, BF16), (grad_tokens, F32)] + [(g, F32) for g in (*mixer_grads, *ffn_grads)],
            heads, taps, wide, head_gain.shape[0],
        )
        grads, (g_first, g_second, g_head, gt_query, gt_key, gt_value, g_beta) = rest[:8], rest[8:]
        return (
            output,
            grad_tokens,
            g_first[0],
            grads[0],
            grads[1],
            grads[2],
            gt_query,
            gt_key,
            gt_value,
            g_beta.T,
            grads[3],
            g_head[0],
            grads[4],
            g_second[0],
            grads[5].T,
            grads[6].T,
            grads[7],
        )

    return shards


def solution(mesh):
    placed = (
        P(("dp", "tensor"), None),
        P(),
        P(None, "tensor"),
        P(None, "tensor"),
        P(None, "tensor"),
        P(None, "tensor"),
        P(None, "tensor"),
        P(None, "tensor"),
        P(None, "tensor"),
        P(None, "tensor"),
        P(),
        P("tensor", None),
        P(),
        P(None, "tensor"),
        P(None, "tensor"),
        P("tensor", None),
        P("dp", None),
        P("dp", None),
        P(("dp", "tensor"), None),
    )
    return jax.shard_map(
        make_shards(mesh.shape["dp"], mesh.shape["tensor"]),
        mesh=mesh,
        in_specs=placed,
        out_specs=(
            P(("dp", "tensor"), None),
            P(("dp", "tensor"), None),
            P(),
            P(None, "tensor"),
            P(None, "tensor"),
            P(None, "tensor"),
            P(None, "tensor"),
            P(None, "tensor"),
            P(None, "tensor"),
            P(None, "tensor"),
            P(None, "tensor"),
            P(),
            P("tensor", None),
            P(),
            P(None, "tensor"),
            P(None, "tensor"),
            P("tensor", None),
        ),
        check_vma=False,
    )
```

```python
import functools
import jax
import jax.numpy as jnp
from jax import lax
from jax.experimental import pallas as pl
from jax.experimental.pallas import tpu as pltpu
from jax.sharding import PartitionSpec as P

CHUNK = 256
F32, BF16 = jnp.float32, jnp.bfloat16


def mm(a, b, contract=(1, 0)):
    return lax.dot_general(
        a.astype(BF16),
        b.astype(BF16),
        (((contract[0],), (contract[1],)), ((), ())),
        preferred_element_type=F32,
    )


def segment_at(places, starts, lengths, seqs):
    segment = jnp.zeros_like(places)
    for s in range(seqs):
        begin = starts[0, s]
        stop = begin + lengths[0, s]
        segment = segment + jnp.where(places >= begin, 1, 0) + jnp.where(places >= stop, 1, 0)
    return jnp.where(places < 0, -1, segment)


def chunk_masks(starts, lengths, seqs, first, size):
    rows = first + lax.broadcasted_iota(jnp.int32, (size, 1), 0)
    columns = first + lax.broadcasted_iota(jnp.int32, (1, size), 1)
    seg_rows = segment_at(rows, starts, lengths, seqs)
    seg_columns = segment_at(columns, starts, lengths, seqs)
    before = segment_at(jnp.full((1, 1), first - 1, jnp.int32), starts, lengths, seqs)
    last = segment_at(jnp.full((1, 1), first + size - 1, jnp.int32), starts, lengths, seqs)
    return rows, seg_rows, seg_columns, before, last


def inverse_unit_lower(lower, size):
    i = lax.broadcasted_iota(jnp.int32, (size, size), 0)
    j = lax.broadcasted_iota(jnp.int32, (size, size), 1)

    def corner(width):
        shift = width.bit_length() - 1
        pair = (i >> (shift + 1)) == (j >> (shift + 1))
        return pair & (((i >> shift) & 1) == 1) & (((j >> shift) & 1) == 0)

    inverse = jnp.where(i == j, 1.0, 0.0) - jnp.where(corner(1), lower, 0.0)
    width = 2
    while width < size:
        low = inverse.astype(BF16)
        if 2 * width == size:
            part = mm(mm(low[width:, width:], lower[width:, :width]), low[:width, :width])
            inverse = jnp.concatenate(
                [
                    inverse[:width],
                    jnp.concatenate([-part, inverse[width:, width:]], axis=1),
                ],
                axis=0,
            )
        else:
            between = jnp.where(corner(width), lower, 0.0)
            inverse = inverse - mm(mm(low, between), low)
        width *= 2
    return inverse


def sigmoid(v):
    return 1.0 / (1.0 + jnp.exp(-v))


def normed_rows(tokens, gain):
    value = tokens[...].astype(F32)
    unit = value * lax.rsqrt(jnp.mean(value * value, axis=1, keepdims=True) + 1e-6)
    return unit * gain[...].astype(F32).reshape(1, -1), unit


MESH = pl.DeviceIdType.MESH
SUBS = 2
PAIRS = [(sub, way) for sub in range(SUBS) for way in (0, 1)]


def ring_position(device, count):
    half, odd = device // 2, device % 2
    return half + odd * (count - 1 - 2 * half)


def ring_device(position, count):
    back = position // (count // 2)
    return (1 - back) * 2 * position + back * (2 * (count - 1 - position) + 1)


class Ring:
    def __init__(self, count):
        self.count = count
        self.me = lax.axis_index("tensor")
        self.place = ring_position(self.me, count)
        self.group = lax.axis_index("dp")

    def at(self, offset):
        return ring_device((self.place + offset + 2 * self.count) % self.count, self.count)

    def next(self, way):
        return (self.group, self.at(1 if way == 0 else -1))


class Gather:
    def __init__(self, ring, own, view, sends, recvs, rows, subs=SUBS):
        self.ring, self.own, self.view, self.sends, self.recvs, self.rows = ring, own, view, sends, recvs, rows
        self.piece = rows // (2 * subs)
        self.pairs = [(sub, way) for sub in range(subs) for way in (0, 1)]

    def origin(self, way, step):
        return self.ring.at(-step if way == 0 else step)

    def copy(self, way, sub, step, origin, first=False):
        inside = way * (self.rows // 2) + sub * self.piece
        place = self.view(origin, inside, self.piece)
        return pltpu.make_async_remote_copy(
            src_ref=self.own(inside, self.piece) if first else place,
            dst_ref=place,
            send_sem=self.sends.at[way, sub, step],
            recv_sem=self.recvs.at[way, sub, step],
            device_id=self.ring.next(way),
            device_id_type=MESH,
        )

    def begin(self):
        for sub, way in self.pairs:
            self.copy(way, sub, 0, self.ring.me, True).start()

    def arrived(self, step):
        for sub, way in self.pairs:
            self.copy(way, sub, step - 1, self.origin(way, step)).wait_recv()

    def hop(self, step):
        for sub, way in self.pairs:
            self.copy(way, sub, step - 1, self.origin(way, step)).wait_recv()
            self.copy(way, sub, step, self.origin(way, step)).start()

    def end(self):
        def drain(step, carry):
            for sub, way in self.pairs:
                self.copy(way, sub, step, self.ring.me).wait_send()
            return carry

        lax.fori_loop(0, self.ring.count - 1, drain, 0)


def row_view(ref, rows):
    return lambda origin, start, size: ref.at[pl.ds(pl.multiple_of(origin * rows + start, size), size), :]


def row_own(ref):
    return lambda start, size: ref.at[pl.ds(start, size), :]


def ring_gather(gather, between, begun=False):
    count = gather.ring.count

    def run(step, carry):
        if not begun:
            pl.when(step == 0)(gather.begin)

        @pl.when((step > 0) & (step < count - 1))
        def _():
            gather.hop(step)

        @pl.when(step == count - 1)
        def _():
            gather.arrived(step)

        between(step)
        return carry

    lax.fori_loop(0, count, run, 0)
    gather.end()


def scatter_copy(ring, slots, sends, recvs, way, sub, step):
    return pltpu.make_async_remote_copy(
        src_ref=slots.at[way, sub, step],
        dst_ref=slots.at[way, sub, step + 1],
        send_sem=sends.at[way, sub, step],
        recv_sem=recvs.at[way, sub, step],
        device_id=ring.next(way),
        device_id_type=MESH,
    )


class Scatter:
    def __init__(self, ring, partial, slots, sends, recvs, rows, finish, after=None):
        self.after = after
        self.ring, self.partial, self.slots, self.sends, self.recvs = ring, partial, slots, sends, recvs
        self.half, self.finish = rows // 2, finish
        self.rows, self.piece = rows, rows // (2 * SUBS)

    def terms(self, step):
        half, first, second = self.half, self.ring.at(-1 - step), self.ring.at(1 + step)
        return self.partial(
            pl.multiple_of(first * self.rows, half), pl.multiple_of(second * self.rows + half, half), step
        )

    def part(self, terms, way, sub):
        start = way * self.half + sub * self.piece
        return terms[start : start + self.piece]

    def copy(self, way, sub, step):
        return scatter_copy(self.ring, self.slots, self.sends, self.recvs, way, sub, step)

    def hop(self, step):
        self.pass_on(step, self.terms(step))

    def pass_on(self, step, terms):
        for sub, way in PAIRS:
            term = self.part(terms, way, sub)

            @pl.when(step == 0)
            def _():
                self.slots[way, sub, 0] = term.astype(BF16)

            @pl.when(step > 0)
            def _():
                self.copy(way, sub, step - 1).wait_recv()
                self.slots[way, sub, step] = (self.slots[way, sub, step].astype(F32) + term).astype(BF16)

            self.copy(way, sub, step).start()

    def end(self):
        self.take(self.terms(self.ring.count - 1))
        self.drain()

    def take(self, terms):
        count = self.ring.count
        for sub, way in PAIRS:
            self.copy(way, sub, count - 2).wait_recv()
            self.finish(
                way * self.half + sub * self.piece,
                self.piece,
                self.slots[way, sub, count - 1].astype(F32) + self.part(terms, way, sub),
            )
            if self.after is not None:
                self.after(way, sub)

    def drain(self):
        def run(step, carry):
            for sub, way in PAIRS:
                self.copy(way, sub, step).wait_send()
            return carry

        lax.fori_loop(0, self.ring.count - 1, run, 0)


def ring_scatter(scatter, between):
    count = scatter.ring.count

    def run(step, carry):
        terms = scatter.terms(step)
        pl.when(step < count - 1)(lambda: scatter.pass_on(step, terms))
        pl.when(step == count - 1)(lambda: scatter.take(terms))
        between(step)
        return carry

    lax.fori_loop(0, count, run, 0)
    scatter.drain()


class GroupSum:
    def __init__(self, ring, groups, grads, near, far, targets, near_sems, far_sems, back_sems, keep_sems):
        self.ring, self.groups, self.grads, self.near, self.far, self.targets = ring, groups, grads, near, far, targets
        self.near_sems, self.far_sems, self.back_sems, self.keep_sems = near_sems, far_sems, back_sems, keep_sems
        self.core = ring.group % 2
        self.mate = (ring.group + 1 - 2 * self.core, ring.me)

    def peers(self):
        return [self.mate] + [
            ((self.ring.group + 2 * k) % self.groups, self.ring.me) for k in range(1, self.groups // 2)
        ]

    def half(self, i, core):
        rows = self.near[i].shape[0]
        return pl.ds(pl.multiple_of(core * rows, rows), rows)

    def near_copy(self, i):
        return pltpu.make_async_remote_copy(
            src_ref=self.grads[i].at[self.half(i, 1 - self.core), :], dst_ref=self.near[i],
            send_sem=self.near_sems.at[0, i], recv_sem=self.near_sems.at[1, i],
            device_id=self.mate, device_id_type=MESH,
        )

    def far_copy(self, i, k):
        return pltpu.make_async_remote_copy(
            src_ref=self.near[i], dst_ref=self.far[i].at[k - 1],
            send_sem=self.far_sems.at[0, i, k - 1], recv_sem=self.far_sems.at[1, i, k - 1],
            device_id=((self.ring.group + 2 * k) % self.groups, self.ring.me), device_id_type=MESH,
        )

    def back_copy(self, i):
        return pltpu.make_async_remote_copy(
            src_ref=self.far[i].at[0], dst_ref=self.targets[i].at[self.half(i, self.core), :],
            send_sem=self.back_sems.at[0, i], recv_sem=self.back_sems.at[1, i],
            device_id=self.mate, device_id_type=MESH,
        )

    def keep_copy(self, i):
        return pltpu.make_async_copy(
            self.far[i].at[0], self.targets[i].at[self.half(i, self.core), :], self.keep_sems.at[i]
        )

    def first(self, chosen):
        for i in chosen:
            self.near_copy(i).start()

    def each_block(self, i, body):
        rows = self.near[i].shape[0]
        block = next(size for size in (64, 32, 16) if rows % size == 0)

        def step(at, carry):
            start = pl.multiple_of(at * block, block)
            body(pl.ds(start, block), pl.ds(pl.multiple_of(self.core * rows + start, block), block))
            return carry

        lax.fori_loop(0, rows // block, step, 0)

    def second(self, chosen):
        for i in chosen:
            self.near_copy(i).wait_recv()

            def add(here, own, i=i):
                self.near[i][here, :] = (
                    self.near[i][here, :].astype(F32) + self.grads[i][own, :].astype(F32)
                ).astype(BF16)

            self.each_block(i, add)
            for k in range(1, self.groups // 2):
                self.far_copy(i, k).start()

    def third(self, chosen):
        for i in chosen:
            for k in range(1, self.groups // 2):
                self.far_copy(i, k).wait()

            def add(here, own, i=i):
                total = self.near[i][here, :].astype(F32)
                for k in range(self.groups // 2 - 1):
                    total = total + self.far[i][k, here, :].astype(F32)
                self.far[i][0, here, :] = total.astype(BF16)

            self.each_block(i, add)
            self.keep_copy(i).start()
            self.back_copy(i).start()

    def last(self):
        for i in range(len(self.grads)):
            self.near_copy(i).wait_send()
            self.back_copy(i).wait()
            self.keep_copy(i).wait()


def sum_scratch(shapes, groups):
    number = len(shapes)
    return (
        [pltpu.VMEM((rows // 2, columns), BF16) for rows, columns in shapes]
        + [pltpu.VMEM((groups // 2 - 1, rows // 2, columns), BF16) for rows, columns in shapes]
        + [
            pltpu.SemaphoreType.DMA((2, number)),
            pltpu.SemaphoreType.DMA((2, number, groups // 2 - 1)),
            pltpu.SemaphoreType.DMA((2, number)),
            pltpu.SemaphoreType.DMA((number,)),
        ]
    )


def greet(ring, others=()):
    barrier = pltpu.get_barrier_semaphore()
    peers = [ring.next(0), ring.next(1)] + list(others)
    for peer in peers:
        pl.semaphore_signal(barrier, inc=1, device_id=peer, device_id_type=MESH)
    pl.semaphore_wait(barrier, len(peers))


def ring_semaphores(count, subs=SUBS):
    return [pltpu.SemaphoreType.DMA((2, subs, count - 1))] * 2


def ring_slots(count, rows, columns):
    return pltpu.VMEM((2, SUBS, count, rows // (2 * SUBS), columns), BF16)


ANY = pl.BlockSpec(memory_space=pl.ANY)
VMEM = pl.BlockSpec(memory_space=pltpu.VMEM)


def ring_params(number):
    return pltpu.CompilerParams(
        collective_id=number, has_side_effects=True, vmem_limit_bytes=60 << 20
    )


class WholeWeight:
    def __init__(self, ring, groups, weight, full, sends, recvs, keep_sem, far_sems, near_sems):
        self.ring, self.groups, self.full, self.far_sems, self.near_sems = ring, groups, full, far_sems, near_sems
        part = weight.shape[0] // groups
        group = ring.group
        own = lambda start, size: weight.at[pl.ds(pl.multiple_of(group * part + start, size), size), :]
        self.gather = Gather(
            ring, own, lambda origin, start, size: full.at[origin, group, pl.ds(start, size), :],
            sends, recvs, part, 1,
        )
        self.keep = pltpu.make_async_copy(own(0, part), full.at[ring.me, group], keep_sem)
        self.mate = (group + 1 - 2 * (group % 2), ring.me)
        self.across = groups // 2

    def peer(self, k):
        return ((self.ring.group + 2 * k) % self.groups, self.ring.me)

    def peers(self):
        return [self.mate] + [self.peer(k) for k in range(1, self.across)]

    def far(self, k, way, step):
        gather = self.gather
        part = self.full.at[gather.origin(way, step), self.ring.group, pl.ds(way * gather.piece, gather.piece), :]
        return pltpu.make_async_remote_copy(
            src_ref=part, dst_ref=part,
            send_sem=self.far_sems.at[0, k - 1, way, step], recv_sem=self.far_sems.at[1, k - 1, way, step],
            device_id=self.peer(k), device_id_type=MESH,
        )

    def near(self, k):
        part = self.full.at[:, (self.ring.group + self.groups - 2 * k) % self.groups]
        return pltpu.make_async_remote_copy(
            src_ref=part, dst_ref=part, send_sem=self.near_sems.at[0, k], recv_sem=self.near_sems.at[1, k],
            device_id=self.mate, device_id_type=MESH,
        )

    def pass_on(self, step):
        for k in range(1, self.across):
            for way in (0, 1):
                self.far(k, way, step).start()

    def begin(self):
        self.gather.begin()
        self.keep.start()

    def hop(self, step):
        self.gather.hop(step)
        self.pass_on(step)

    def exchange(self):
        self.gather.arrived(self.ring.count - 1)
        self.pass_on(self.ring.count - 1)
        self.keep.wait()
        self.pass_on(0)
        self.near(0).start()

    def every_far(self, body):
        def run(step, carry):
            for k in range(1, self.across):
                for way in (0, 1):
                    body(self.far(k, way, step))
            return carry

        lax.fori_loop(0, self.ring.count, run, 0)

    def back(self):
        self.every_far(lambda copy: copy.wait_recv())
        for k in range(1, self.across):
            self.near(k).start()

    def end(self):
        for k in range(self.across):
            self.near(k).wait()
        self.every_far(lambda copy: copy.wait_send())
        self.gather.end()


def gather_kernel(count, tokens, tokens_full, sends, recvs, local):
    ring = Ring(count)
    rows = tokens.shape[0]
    greet(ring)
    keep = pltpu.make_async_copy(
        tokens, tokens_full.at[pl.ds(pl.multiple_of(ring.me * rows, rows), rows), :], local
    )
    keep.start()
    ring_gather(
        Gather(ring, row_own(tokens), row_view(tokens_full, rows), sends, recvs, rows), lambda step: None
    )
    keep.wait()


def gather_tokens(tokens, count):
    rows, model = tokens.shape
    return pl.pallas_call(
        functools.partial(gather_kernel, count),
        name="gather_tokens",
        out_shape=jax.ShapeDtypeStruct((count * rows, model), tokens.dtype),
        in_specs=[ANY],
        out_specs=ANY,
        scratch_shapes=ring_semaphores(count) + [pltpu.SemaphoreType.DMA],
        compiler_params=ring_params(1),
        cost_estimate=pl.CostEstimate(flops=0, bytes_accessed=300 << 20, transcendentals=0),
    )(tokens)


def attend_kernel(
    count, mixed, w_out, tokens, gain, w_gate, w_up, w_down, cotangent,
    resid, full, hidden, grad_gate, grad_up, cotangents,
    gathered, out_box, gate_box, up_box, down_box, mixed_boxes, token_boxes, normed, gates, stages,
    sends, recvs, weight_sems, keep_sem, mixed_sems, token_sems, out_sems, normed_sems, stage_sems,
):
    ring = Ring(count)
    rows = cotangent.shape[0]
    half = rows // 2
    gather = Gather(ring, row_own(cotangent), row_view(gathered, rows), sends, recvs, rows)
    keep = pltpu.make_async_copy(
        cotangent, gathered.at[pl.ds(pl.multiple_of(ring.me * rows, rows), rows), :], keep_sem
    )
    loads = [
        pltpu.make_async_copy(source, box, weight_sems.at[k])
        for k, (source, box) in enumerate(
            ((w_out, out_box), (w_gate, gate_box), (w_up, up_box), (w_down, down_box))
        )
    ]

    def place(way, step):
        return pl.ds(pl.multiple_of(gather.origin(way, step) * rows + way * half, half), half)

    def mixed_copy(way, step):
        return pltpu.make_async_copy(
            mixed.at[:, place(way, step), :], mixed_boxes.at[step % 2, way], mixed_sems.at[step % 2, way]
        )

    def token_copy(way, step):
        return pltpu.make_async_copy(
            tokens.at[place(way, step), :], token_boxes.at[step % 2, way], token_sems.at[step % 2, way]
        )

    def out_copy(way, step):
        at = place(way, step)
        return pltpu.make_async_copy(gathered.at[at, :], cotangents.at[at, :], out_sems.at[way, step])

    def normed_copy(way, step):
        return pltpu.make_async_copy(
            normed.at[step % 2, pl.ds(way * half, half), :], full.at[place(way, step), :],
            normed_sems.at[step % 2, way],
        )

    def stage_copy(k, way, step):
        target = (hidden, grad_gate, grad_up)[k]
        return pltpu.make_async_copy(
            stages.at[step % 2, k, way], target.at[place(way, step), :], stage_sems.at[step % 2, k, way]
        )

    def settle(step):
        for way in (0, 1):
            normed_copy(way, step).wait()
            for k in range(3):
                stage_copy(k, way, step).wait()

    def fetch(step):
        for way in (0, 1):
            mixed_copy(way, step).start()
            token_copy(way, step).start()

    def put(k, step, value):
        low = value.astype(BF16)
        for way in (0, 1):
            stages[step % 2, k, way] = low[way * half : way * half + half]
            stage_copy(k, way, step).start()

    def prepare(step):
        @pl.when(step > 1)
        def _():
            settle(step - 2)

        slot = step % 2
        for way in (0, 1):
            mixed_copy(way, step).wait()
            token_copy(way, step).wait()

        @pl.when(step + 1 < count)
        def _():
            fetch(step + 1)

        heads = jnp.concatenate(
            [
                jnp.concatenate([mixed_boxes[slot, way, j] for j in range(count)], 1)
                for way in (0, 1)
            ],
            0,
        )
        value = jnp.concatenate([token_boxes[slot, 0], token_boxes[slot, 1]], 0).astype(F32)
        value = value + mm(heads, out_box[...])

        @pl.when(step == 0)
        def _():
            resid[...] = value

        scale = lax.rsqrt(jnp.mean(value * value, axis=1, keepdims=True) + 1e-6)
        normed[slot] = (value * scale * gain[...].astype(F32).reshape(1, -1)).astype(BF16)
        for way in (0, 1):
            normed_copy(way, step).start()
        inputs = normed[slot]
        gate = mm(inputs, gate_box[...], (1, 1))
        up = mm(inputs, up_box[...], (1, 1))
        sig = sigmoid(gate)
        opened = gate * sig
        put(0, step, opened * up)
        gates[0] = up * sig * (1.0 + gate * (1.0 - sig))
        gates[1] = opened

    def feed(step):
        for way in (0, 1):
            out_copy(way, step).start()
        grad = mm(
            jnp.concatenate([gathered[place(0, step), :], gathered[place(1, step), :]], 0), down_box[...], (1, 1)
        )
        put(1, step, grad * gates[0])
        put(2, step, grad * gates[1])

    def run(step, carry):
        @pl.when(step == 0)
        def _():
            gather.begin()
            for load in loads:
                load.wait()

        prepare(step)

        @pl.when(step == 0)
        def _():
            keep.wait()

        @pl.when((step > 0) & (step < count - 1))
        def _():
            gather.hop(step)

        @pl.when(step == count - 1)
        def _():
            gather.arrived(step)

        feed(step)
        return carry

    keep.start()
    fetch(0)
    for load in loads:
        load.start()
    greet(ring)
    lax.fori_loop(0, count, run, 0)
    gather.end()
    settle(count - 2)
    settle(count - 1)

    def drain(step, carry):
        for way in (0, 1):
            out_copy(way, step).wait()
        return carry

    lax.fori_loop(0, count, drain, 0)


def attend(mixed, w_out, tokens, gain, w_gate, w_up, w_down, cotangent, count):
    rows, model = cotangent.shape
    slots, inner = count * rows, w_down.shape[0]
    wide = mixed.shape[2]
    return pl.pallas_call(
        functools.partial(attend_kernel, count),
        name="attend",
        out_shape=[
            jax.ShapeDtypeStruct((rows, model), F32),
            jax.ShapeDtypeStruct((slots, model), BF16),
        ]
        + [jax.ShapeDtypeStruct((slots, inner), BF16)] * 3
        + [jax.ShapeDtypeStruct((slots, model), BF16)],
        in_specs=[ANY] * 3 + [VMEM] + [ANY] * 4,
        out_specs=[VMEM] + [ANY] * 5,
        scratch_shapes=[pltpu.VMEM((slots, model), BF16), pltpu.VMEM(w_out.shape, BF16)]
        + [pltpu.VMEM((inner, model), BF16)] * 3
        + [
            pltpu.VMEM((2, 2, count, rows // 2, wide), BF16),
            pltpu.VMEM((2, 2, rows // 2, model), BF16),
            pltpu.VMEM((2, rows, model), BF16),
            pltpu.VMEM((2, rows, inner), F32),
            pltpu.VMEM((2, 3, 2, rows // 2, inner), BF16),
        ]
        + ring_semaphores(count)
        + [
            pltpu.SemaphoreType.DMA((4,)),
            pltpu.SemaphoreType.DMA,
            pltpu.SemaphoreType.DMA((2, 2)),
            pltpu.SemaphoreType.DMA((2, 2)),
            pltpu.SemaphoreType.DMA((2, count)),
            pltpu.SemaphoreType.DMA((2, 2)),
            pltpu.SemaphoreType.DMA((2, 3, 2)),
        ],
        compiler_params=ring_params(2),
        cost_estimate=pl.CostEstimate(
            flops=2 * slots * model * model + 6 * slots * model * inner, bytes_accessed=300 << 20,
            transcendentals=slots * inner,
        ),
    )(mixed, w_out, tokens, gain, w_gate, w_up, w_down, cotangent)


def norm_back(inputs, scale, gain, grad_normed):
    weighted = gain * grad_normed
    inner = jnp.mean(weighted * inputs, axis=1, keepdims=True)
    unit = inputs * scale
    return scale * weighted - unit * (scale * scale * inner), grad_normed * unit


JOBS = 8


def ffn_back_kernel(
    count, groups, rows, grad_gate_in, grad_up_in, hidden_in, w_gate_in, w_up_in, resid_in, cotangent_in, gain, inputs, cotangents,
    grad_resid, full, grad_gain, sum_gate, sum_up, sum_down,
    slots, low, gw_gate, gw_up, gw_down, boxes, box_sems, hidden, resid, cotangent, grad_gate, grad_up, w_gate, w_up, load_sems, *rest,
):
    ring = Ring(count)
    sends, recvs, sends_two, recvs_two, local = rest[:5]
    sums = GroupSum(
        ring, groups, (gw_gate, gw_up, gw_down), rest[5:8], rest[8:11], (sum_gate, sum_up, sum_down), *rest[11:]
    )
    wide = boxes.shape[2]

    def box_copy(job, source):
        at = pl.multiple_of(job % (JOBS // 2) * wide, wide)
        return pltpu.make_async_copy(
            source.at[:, pl.ds(at, wide)], boxes.at[job % 2], box_sems.at[job % 2]
        )

    def fetch(job):
        @pl.when(job < JOBS // 2)
        def _():
            box_copy(job, inputs).start()

        @pl.when(job >= JOBS // 2)
        def _():
            box_copy(job, cotangents).start()

    loads = [
        pltpu.make_async_copy(source, target, load_sems.at[k])
        for k, (source, target) in enumerate(
            (
                (w_gate_in, w_gate), (w_up_in, w_up), (grad_gate_in, grad_gate), (grad_up_in, grad_up),
                (hidden_in, hidden), (resid_in, resid), (cotangent_in, cotangent),
            )
        )
    ]
    for load in loads[:4]:
        load.start()
    fetch(0)
    for load in loads[4:]:
        load.start()
    greet(ring, sums.peers())
    for load in loads[:4]:
        load.wait()
    grad_gain[...] = jnp.zeros_like(grad_gain)
    half = rows // 2

    def partial(first, second, step):
        gates = jnp.concatenate([grad_gate[pl.ds(first, half), :], grad_gate[pl.ds(second, half), :]], 0)
        ups = jnp.concatenate([grad_up[pl.ds(first, half), :], grad_up[pl.ds(second, half), :]], 0)
        return mm(gates, w_gate[...]) + mm(ups, w_up[...])

    def finish(start, size, grad):
        value = resid[start : start + size, :]
        scale = lax.rsqrt(jnp.mean(value * value, axis=1, keepdims=True) + 1e-6)
        through, pieces = norm_back(value, scale, gain[...].astype(F32).reshape(1, -1), grad)
        result = cotangent[start : start + size, :].astype(F32) + through
        grad_resid[start : start + size, :] = result
        grad_gain[...] += jnp.sum(pieces, axis=0, keepdims=True)
        low[start : start + size, :] = result.astype(BF16)

    def work(job, carry):
        box_copy(job, inputs).wait()

        @pl.when(job + 1 < JOBS)
        def _():
            fetch(job + 1)

        at = pl.ds(pl.multiple_of(job % (JOBS // 2) * wide, wide), wide)

        @pl.when(job < JOBS // 2)
        def _():
            box = boxes[job % 2]
            gw_gate[:, at] = mm(grad_gate[...], box, (0, 0)).astype(BF16)
            gw_up[:, at] = mm(grad_up[...], box, (0, 0)).astype(BF16)

        @pl.when(job >= JOBS // 2)
        def _():
            gw_down[:, at] = mm(hidden[...], boxes[job % 2], (0, 0)).astype(BF16)

        return carry

    each = JOBS // 4

    def beside_scatter(step):
        @pl.when(step == 2)
        def _():
            for load in loads[4:]:
                load.wait()

        @pl.when(step == 3)
        def _():
            sums.second((0, 1))

        @pl.when(step < 4)
        def _():
            lax.fori_loop(step * each, step * each + each, work, 0)

        @pl.when(step == 1)
        def _():
            sums.first((0, 1))

        @pl.when(step == 3)
        def _():
            sums.first((2,))

        @pl.when(step == 5)
        def _():
            sums.second((2,))

    def beside_gather(step):
        @pl.when(step == count - 3)
        def _():
            sums.third((0, 1))

        @pl.when(step == count - 2)
        def _():
            sums.third((2,))

    gather = Gather(ring, row_own(low), row_view(full, rows), sends_two, recvs_two, rows)
    start = lambda way, sub: gather.copy(way, sub, 0, ring.me, True).start()
    ring_scatter(Scatter(ring, partial, slots, sends, recvs, rows, finish, start), beside_scatter)
    keep = pltpu.make_async_copy(low, full.at[pl.ds(pl.multiple_of(ring.me * rows, rows), rows), :], local)
    keep.start()
    ring_gather(gather, beside_gather, True)
    keep.wait()
    sums.last()


def ffn_back(grad_gate, grad_up, hidden, w_gate, w_up, resid, cotangent, gain, inputs, cotangents, count, groups):
    rows, model = resid.shape
    slots, inner = grad_up.shape
    shapes = [(inner, model)] * 3
    return pl.pallas_call(
        functools.partial(ffn_back_kernel, count, groups, rows),
        name="ffn_back",
        out_shape=[
            jax.ShapeDtypeStruct((rows, model), F32),
            jax.ShapeDtypeStruct((slots, model), BF16),
            jax.ShapeDtypeStruct((1, model), F32),
        ]
        + [jax.ShapeDtypeStruct(shape, BF16) for shape in shapes],
        in_specs=[ANY] * 7 + [VMEM] + [ANY] * 2,
        out_specs=[VMEM, ANY, VMEM] + [ANY] * 3,
        scratch_shapes=[ring_slots(count, rows, model), pltpu.VMEM((rows, model), BF16)]
        + [pltpu.VMEM(shape, BF16) for shape in shapes]
        + [pltpu.VMEM((2, slots, model // (JOBS // 2)), BF16), pltpu.SemaphoreType.DMA((2,))]
        + [pltpu.VMEM((slots, inner), BF16), pltpu.VMEM((rows, model), F32), pltpu.VMEM((rows, model), BF16)]
        + [pltpu.VMEM((slots, inner), BF16)] * 2
        + [pltpu.VMEM((inner, model), BF16)] * 2
        + [pltpu.SemaphoreType.DMA((7,))]
        + ring_semaphores(count) * 2
        + [pltpu.SemaphoreType.DMA]
        + sum_scratch(shapes, groups),
        compiler_params=ring_params(3),
        cost_estimate=pl.CostEstimate(
            flops=10 * slots * model * inner, bytes_accessed=600 << 20, transcendentals=0
        ),
    )(grad_gate, grad_up, hidden, w_gate, w_up, resid, cotangent, gain, inputs, cotangents)


def last_kernel(
    count, groups, rows, terms, tokens_in, grad_resid_in, gain, small, *rest,
):
    grads_in, rest = rest[:5], rest[5:]
    grad_tokens, total = rest[:2]
    targets, rest = rest[2:7], rest[7:]
    slots, first_box, slice_own, spread, second_box, second_own, boxes, box_sems, tokens, grad_resid, load_sems = rest[:11]
    sends, recvs, first_sends, first_recvs, spread_sends, spread_recvs, second_sends, second_recvs = rest[11:19]
    ring = Ring(count)
    grads, grad_sems = rest[33:38], rest[38]
    sums = GroupSum(ring, groups, grads, rest[19:24], rest[24:29], targets, *rest[29:33])
    loads = [
        pltpu.make_async_copy(tokens_in, tokens, load_sems.at[0]),
        pltpu.make_async_copy(grad_resid_in, grad_resid, load_sems.at[1]),
    ]
    fills = [
        pltpu.make_async_copy(source, target, grad_sems.at[k])
        for k, (source, target) in enumerate(zip(grads_in, grads))
    ]
    for fill in fills:
        fill.start()
    me, group = ring.me, ring.group
    first_peers = [(group, (me + k) % count) for k in range(1, count)]
    second_peers = [((group + k) % groups, me) for k in range(1, groups)]
    barrier = pltpu.get_barrier_semaphore()
    for peer in first_peers + second_peers:
        pl.semaphore_signal(barrier, inc=1, device_id=peer, device_id_type=MESH)
    pl.semaphore_wait(barrier, count + groups - 2)

    lanes = small.shape[1] // count

    def lanes_of(device):
        return pl.ds(pl.multiple_of(device * lanes, lanes), lanes)

    def first(k):
        peer = first_peers[k]
        return pltpu.make_async_remote_copy(
            src_ref=small.at[0:8, lanes_of(peer[1])], dst_ref=first_box.at[k], send_sem=first_sends.at[k],
            recv_sem=first_recvs.at[k], device_id=peer, device_id_type=MESH,
        )

    def share(k):
        return pltpu.make_async_remote_copy(
            src_ref=slice_own, dst_ref=spread.at[:, lanes_of(me)], send_sem=spread_sends.at[k],
            recv_sem=spread_recvs.at[k], device_id=first_peers[k], device_id_type=MESH,
        )

    def second(k):
        return pltpu.make_async_remote_copy(
            src_ref=second_own, dst_ref=second_box.at[k], send_sem=second_sends.at[k],
            recv_sem=second_recvs.at[k], device_id=second_peers[k], device_id_type=MESH,
        )

    every = range(len(grads))
    for fill in fills:
        fill.wait()
    sums.first(every)
    for k in range(count - 1):
        first(k).start()
    half = rows // 2

    def box_copy(way, start, slot):
        return pltpu.make_async_copy(
            terms.at[pl.ds(start, half), :], boxes.at[slot, way], box_sems.at[slot, way]
        )

    def fetch(step):
        for way, owner in ((0, ring.at(-1 - step)), (1, ring.at(1 + step))):
            box_copy(way, pl.multiple_of(owner * rows + way * half, half), step % 2).start()

    def partial(first, second, step):
        for way, start in ((0, first), (1, second)):
            box_copy(way, start, step % 2).wait()

        @pl.when(step + 1 < count)
        def _():
            fetch(step + 1)

        return jnp.concatenate([boxes[step % 2, 0], boxes[step % 2, 1]], 0).astype(F32)

    def finish(start, size, grad):
        value = tokens[start : start + size, :].astype(F32)
        scale = lax.rsqrt(jnp.mean(value * value, axis=1, keepdims=True) + 1e-6)
        through, pieces = norm_back(value, scale, gain[...].astype(F32).reshape(1, -1), grad)
        grad_tokens[start : start + size, :] = grad_resid[start : start + size, :] + through

    def early():
        sums.second(every)
        for k in range(count - 1):
            first(k).wait()
        mine = small[0:8, lanes_of(me)]
        for k in range(count - 1):
            mine = mine + first_box[k]
        slice_own[...] = mine
        spread[:, lanes_of(me)] = mine
        for k in range(count - 1):
            share(k).start()

    def soon():
        for k in range(count - 1):
            share(k).wait()
        second_own[0:8] = spread[...]
        second_own[8:] = small[8:]
        for k in range(groups - 1):
            second(k).start()

    def late():
        for k in range(groups - 1):
            second(k).wait()
        mine = second_own[...]
        for k in range(groups - 1):
            mine = mine + second_box[k]
        total[...] = mine
        for load in loads:
            load.wait()

    def beside(step):
        pl.when(step == 0)(early)
        pl.when(step == 1)(soon)
        for i in every:
            pl.when(step == count - 1 - len(every) + i)(lambda i=i: sums.third((i,)))
        pl.when(step == count - 2)(late)

    fetch(0)
    for load in loads:
        load.start()
    ring_scatter(Scatter(ring, partial, slots, sends, recvs, rows, finish), beside)
    sums.last()


def last_step(terms, tokens, grad_resid, gain, small, grads, count, groups):
    rows, model = tokens.shape
    return pl.pallas_call(
        functools.partial(last_kernel, count, groups, rows),
        name="last_step",
        out_shape=[jax.ShapeDtypeStruct((rows, model), F32), jax.ShapeDtypeStruct(small.shape, F32)]
        + [jax.ShapeDtypeStruct(g.shape, BF16) for g in grads],
        in_specs=[ANY] * 3 + [VMEM] * 2 + [ANY] * len(grads),
        out_specs=[VMEM, VMEM] + [ANY] * len(grads),
        scratch_shapes=[
            ring_slots(count, rows, model),
            pltpu.VMEM((count - 1, 8, model // count), F32),
            pltpu.VMEM((8, model // count), F32),
            pltpu.VMEM((8, model), F32),
            pltpu.VMEM((groups - 1,) + small.shape, F32),
            pltpu.VMEM(small.shape, F32),
            pltpu.VMEM((2, 2, rows // 2, model), BF16),
            pltpu.SemaphoreType.DMA((2, 2)),
            pltpu.VMEM((rows, model), BF16),
            pltpu.VMEM((rows, model), F32),
            pltpu.SemaphoreType.DMA((2,)),
        ]
        + ring_semaphores(count)
        + [pltpu.SemaphoreType.DMA((count - 1,))] * 4
        + [pltpu.SemaphoreType.DMA((groups - 1,))] * 2
        + sum_scratch([g.shape for g in grads], groups)
        + [pltpu.VMEM(g.shape, BF16) for g in grads]
        + [pltpu.SemaphoreType.DMA((len(grads),))],
        compiler_params=ring_params(4),
        cost_estimate=pl.CostEstimate(flops=0, bytes_accessed=300 << 20, transcendentals=0),
    )(terms, tokens, grad_resid, gain, small, *grads)


def results_kernel(heads, taps, wide, width, total, *refs):
    number = (len(refs) - 7) // 2
    for source, target in zip(refs[:number], refs[number : 2 * number]):
        target[...] = source[...].astype(target.dtype)
    g_first, g_second, g_head, gt_query, gt_key, gt_value, g_beta = refs[2 * number :]

    @pl.when(pl.program_id(0) == 0)
    def _():
        g_first[...] = total[0:1, :]
        g_second[...] = total[1:2, :]
        g_head[...] = total[2:3, 0:width]
        row = 8 + heads
        for place, target in enumerate((gt_query, gt_key, gt_value)):
            target[...] = total[row : row + taps, place * wide : (place + 1) * wide]
        g_beta[...] = total[8 : 8 + heads, :]


def results(total, arrays, heads, taps, wide, width):
    model = total.shape[1]
    steps = next(n for n in (2, 1) if all(a.shape[0] % (8 * n) == 0 for a, _ in arrays))
    small = [(1, model), (1, model), (1, width)] + [(taps, wide)] * 3 + [(heads, model)]
    piece = lambda a: pl.BlockSpec((a.shape[0] // steps, a.shape[1]), lambda n: (n, 0))
    whole = lambda shape: pl.BlockSpec(shape, lambda n: (0, 0))
    return pl.pallas_call(
        functools.partial(results_kernel, heads, taps, wide, width),
        name="results",
        grid=(steps,),
        out_shape=[jax.ShapeDtypeStruct(a.shape, kind) for a, kind in arrays]
        + [jax.ShapeDtypeStruct(shape, F32) for shape in small],
        in_specs=[whole(total.shape)] + [piece(a) for a, _ in arrays],
        out_specs=[piece(a) for a, _ in arrays] + [whole(shape) for shape in small],
        compiler_params=pltpu.CompilerParams(vmem_limit_bytes=56 << 20),
        cost_estimate=pl.CostEstimate(flops=0, bytes_accessed=48 << 20, transcendentals=0),
    )(total, *[a for a, _ in arrays])


def spread_hops(step, chunks, count, hop, start=0):
    each = -(-(count - 1) // (chunks - 1))
    for place in range(each):
        number = step * each + place

        @pl.when((number >= start) & (number < count - 1))
        def _():
            hop(number)


def plan_hops(chunks, hops, latency=0.8, segment=2.5):
    now, link, due, done, table = 0.0, 0.0, {}, {}, []

    def send(chunk):
        nonlocal link
        link = max(now, link) + 1.0
        done[chunk] = done.get(chunk, -1) + 1
        due[chunk] = link + latency

    for step in range(chunks):
        for half in range(2):
            ready, moves = True, []
            while ready:
                ready = sorted((due[c], c) for c in due if due[c] <= now and done[c] < hops - 1)
                if ready:
                    send(ready[0][1])
                    moves.append((ready[0][1], done[ready[0][1]]))
            table.append(moves)
            now += segment
        send(step)
    return table, [done[chunk] for chunk in range(chunks)]


def forward_kernel(
    heads, width, seqs, count, groups, chunks,
    starts, lengths, tokens, w_query_in, w_key_in, w_value_in, w_gate_in, w_beta,
    taps_query, taps_key, taps_value, gain, gain_first, w_out,
    mixed_full, w_full, mixed, p_query, p_key, p_value, p_gate, p_beta, z_query, z_key, z_value,
    delta_out, change_out, inverse_out, state_out,
    tail_query, tail_key, tail_value, state, stage, sends, recvs, keeps,
    w_sends, w_recvs, w_keep, w_far, w_near, w_query, w_key, w_value, w_gate, load_sems,
):
    step = pl.program_id(0)
    size = tokens.shape[0]
    first = step * size

    @pl.when(step == 0)
    def _():
        for tail in (tail_query, tail_key, tail_value):
            tail[...] = jnp.zeros_like(tail)
        state[...] = jnp.zeros_like(state)

    ring = Ring(count)

    def chunk_gather(chunk):
        return Gather(
            ring,
            lambda start, length: stage.at[chunk, pl.ds(start, length), :],
            lambda origin, start, length: mixed_full.at[
                origin, pl.ds(pl.multiple_of(chunk * size + start, length), length), :
            ],
            sends.at[chunk], recvs.at[chunk], size, 1,
        )

    def keep(chunk):
        return pltpu.make_async_copy(
            stage.at[chunk],
            mixed_full.at[ring.me, pl.ds(pl.multiple_of(chunk * size, size), size), :],
            keeps.at[chunk],
        )

    weight = WholeWeight(ring, groups, w_out, w_full, w_sends, w_recvs, w_keep, w_far, w_near)
    each = -(-(count - 1) // (chunks - 1))

    def weight_hops(late=0):
        for place in range(each):
            number = (2 * step + late) * each + place
            pl.when((number > 0) & (number < count - 1))(lambda: weight.hop(number))
            pl.when(number == count - 1)(weight.exchange)

    table, done = plan_hops(chunks, count - 1)

    def chunk_hops(half):
        for place, moves in enumerate(table[half::2]):
            if moves:
                @pl.when(step == place)
                def _():
                    for chunk, hop in moves:
                        chunk_gather(chunk).hop(hop)

    @pl.when(step == 0)
    def _():
        loads = [
            pltpu.make_async_copy(source, target, load_sems.at[k])
            for k, (source, target) in enumerate(
                ((w_query_in, w_query), (w_key_in, w_key), (w_value_in, w_value), (w_gate_in, w_gate))
            )
        ]
        for load in loads:
            load.start()
        greet(ring, weight.peers())
        weight.begin()
        for load in loads:
            load.wait()

    weight_hops()
    chunk_hops(0)
    rows, seg_rows, seg_columns, before, last = chunk_masks(starts, lengths, seqs, first, size)
    same = seg_rows == seg_columns
    i = lax.broadcasted_iota(jnp.int32, (size, size), 0)
    j = lax.broadcasted_iota(jnp.int32, (size, size), 1)
    strict = jnp.where(same & (i > j), 1.0, 0.0)
    inclusive = jnp.where(same & (i >= j), 1.0, 0.0)
    carried = jnp.where(seg_rows == before, 1.0, 0.0)
    ending = jnp.where(seg_rows == last, 1.0, 0.0)
    kept = jnp.where(before == last, 1.0, 0.0)
    live = jnp.where(seg_rows % 2 == 1, 1.0, 0.0)
    joined = [
        jnp.where(segment_at(rows - offset, starts, lengths, seqs) == seg_rows, 1.0, 0.0)
        for offset in range(1, taps_query.shape[0])
    ]
    inputs = normed_rows(tokens, gain_first)[0].astype(BF16)

    def feature(weight, taps, tail, p_out, z_out):
        projected = jnp.dot(inputs, weight[...], preferred_element_type=F32)
        p_out[...] = projected
        tail[8:, :] = projected
        tap = taps[...].astype(F32)
        result = projected * tap[0:1]
        for offset in range(1, tap.shape[0]):
            result = result + tail[8 - offset : 8 - offset + size, :] * tap[offset : offset + 1] * joined[offset - 1]
        tail[0:8, :] = projected[size - 8 :, :]
        z_out[...] = result
        return result * sigmoid(result)

    u_query = feature(w_query, taps_query, tail_query, p_query, z_query)
    u_key = feature(w_key, taps_key, tail_key, p_key, z_key)
    u_value = feature(w_value, taps_value, tail_value, p_value, z_value)
    gate = jnp.dot(inputs, w_gate[...], preferred_element_type=F32)
    p_gate[...] = gate
    beta_pre = mm(inputs, w_beta[...], (1, 1))
    p_beta[...] = beta_pre
    strength = sigmoid(beta_pre)
    opened = gate * sigmoid(gate)
    scale = width ** (-0.5)
    head_gain = gain[...].astype(F32)
    for h in range(heads):
        if h == heads // 2:
            weight_hops(1)
            chunk_hops(1)
        cols = slice(h * width, (h + 1) * width)
        uq, uk = u_query[:, cols], u_key[:, cols]
        query = (uq * lax.rsqrt(jnp.sum(uq * uq, axis=1, keepdims=True) + 1e-6)).astype(BF16)
        key = (uk * lax.rsqrt(jnp.sum(uk * uk, axis=1, keepdims=True) + 1e-6)).astype(BF16)
        value = u_value[:, cols].astype(BF16).astype(F32)
        beta = strength[:, h : h + 1]
        memory = state[h]
        low_memory = memory.astype(BF16)
        state_out[0, h] = low_memory
        lower = mm(key, key, (1, 1)) * strict * beta
        inverse = inverse_unit_lower(lower, size).astype(BF16)
        inverse_out[0, h] = inverse
        within = mm(query, key, (1, 1)) * inclusive
        change = mm(inverse, beta * (value - carried * mm(key, low_memory)))
        low_change = change.astype(BF16)
        change_out[:, cols] = low_change
        out = scale * (carried * mm(query, low_memory) + mm(within, low_change))
        state[h] = kept * memory + mm(key, ending * change, (0, 0))
        delta_out[:, cols] = out
        normal = out * lax.rsqrt(jnp.mean(out * out, axis=1, keepdims=True) + 1e-5) * head_gain
        low_mixed = (normal * opened[:, cols] * live).astype(BF16)
        mixed[:, cols] = low_mixed
        stage[step, :, cols] = low_mixed

    chunk_gather(step).begin()
    keep(step).start()

    @pl.when(step == chunks - 1)
    def _():
        def finish(number, carry):
            pl.when(number == (count - 1) // 2)(weight.back)
            for chunk in range(chunks):
                if done[chunk] < count - 2:
                    pl.when(done[chunk] + number < count - 1)(
                        lambda chunk=chunk: chunk_gather(chunk).hop(done[chunk] + number)
                    )
            return carry

        lax.fori_loop(1, count - 1, finish, 0)

        def settle(chunk, carry):
            chunk_gather(chunk).arrived(count - 1)
            chunk_gather(chunk).end()
            keep(chunk).wait()
            return carry

        lax.fori_loop(0, chunks, settle, 0)
        weight.end()


def forward_mixer(tokens, w_query, w_key, w_value, w_gate, w_beta, taps_query, taps_key, taps_value, gain, gain_first, starts, lengths, w_out, count, groups):
    slots, model = tokens.shape
    wide = w_query.shape[1]
    width = gain.shape[0]
    heads = wide // width
    seqs = starts.shape[1]
    chunks = slots // CHUNK
    taps = taps_query.shape[0]
    part = w_out.shape[0] // groups
    smem = pl.BlockSpec(memory_space=pltpu.SMEM)
    whole = lambda shape: pl.BlockSpec(shape, lambda n: (0,) * len(shape))
    piece = lambda shape: pl.BlockSpec(shape, lambda n: (n,) + (0,) * (len(shape) - 1))
    outs = [
        ((slots, wide), BF16), ((slots, wide), F32), ((slots, wide), F32), ((slots, wide), F32), ((slots, wide), F32),
        ((slots, w_beta.shape[0]), F32), ((slots, wide), F32), ((slots, wide), F32), ((slots, wide), F32),
        ((slots, wide), F32), ((slots, wide), BF16),
    ]
    return pl.pallas_call(
        functools.partial(forward_kernel, heads, width, seqs, count, groups, chunks),
        name="mixer_forward",
        grid=(chunks,),
        out_shape=[
            jax.ShapeDtypeStruct((count, slots, wide), BF16),
            jax.ShapeDtypeStruct((count, groups, part, model), BF16),
        ]
        + [jax.ShapeDtypeStruct(s, d) for s, d in outs]
        + [
            jax.ShapeDtypeStruct((chunks, heads, CHUNK, CHUNK), BF16),
            jax.ShapeDtypeStruct((chunks, heads, width, width), BF16),
        ],
        in_specs=[smem, smem, piece((CHUNK, model))]
        + [ANY] * 4
        + [whole(w_beta.shape)]
        + [whole((taps, wide))] * 3
        + [whole((1, width)), VMEM, ANY],
        out_specs=[ANY, ANY]
        + [piece((CHUNK, s[1])) for s, d in outs]
        + [piece((1, heads, CHUNK, CHUNK)), piece((1, heads, width, width))],
        scratch_shapes=[pltpu.VMEM((CHUNK + 8, wide), F32)] * 3
        + [pltpu.VMEM((heads, width, width), F32), pltpu.VMEM((chunks, CHUNK, wide), BF16)]
        + [pltpu.SemaphoreType.DMA((chunks, 2, 1, count - 1))] * 2
        + [pltpu.SemaphoreType.DMA((chunks,))]
        + ring_semaphores(count, 1)
        + [
            pltpu.SemaphoreType.DMA,
            pltpu.SemaphoreType.DMA((2, groups // 2 - 1, 2, count)),
            pltpu.SemaphoreType.DMA((2, groups // 2)),
        ]
        + [pltpu.VMEM((model, wide), BF16)] * 4
        + [pltpu.SemaphoreType.DMA((4,))],
        compiler_params=ring_params(5),
        cost_estimate=pl.CostEstimate(
            flops=2 * slots * model * wide * 4 + slots * heads * CHUNK * 2 * CHUNK * 20,
            bytes_accessed=slots * model * 2 + 4 * model * wide * 2 + slots * wide * 36,
            transcendentals=slots * wide * 4,
        ),
    )(starts, lengths, tokens, w_query, w_key, w_value, w_gate, w_beta, taps_query, taps_key, taps_value, gain.reshape(1, width), gain_first, w_out)


def small_rows(heads, taps):
    return -(-(8 + heads + taps) // 8) * 8


def backward_kernel(
    heads, width, seqs, chunks, count, rows_own,
    starts, lengths, tokens, grad_attended, mixed, p_query, p_key, p_value, p_gate, p_beta,
    z_query, z_key, z_value, delta_out, change_in, inverse_in, state_in,
    w_query_in, w_key_in, w_value_in, w_gate_in, w_beta, w_out_in, taps_query, taps_key, taps_value, gain, gain_first,
    hidden_in, w_down_in, resid_in, g_second, grad_normed, gw_query, gw_key, gw_value, gw_gate, gw_out,
    small, output,
    a_query, a_key, a_value, a_gate, a_out, head_query, head_key, head_value, flow,
    w_query, w_key, w_value, w_gate, resid, w_out, hidden, w_down, load_sems, slots, sends, recvs,
):
    step = pl.program_id(0)
    size = tokens.shape[0]
    first = (chunks - 1 - step) * size

    @pl.when(step == 0)
    def _():
        for ref in (a_query, a_key, a_value, a_gate, a_out, small, flow):
            ref[...] = jnp.zeros_like(ref)
        small[1:2, :] = g_second[...]
        for ref in (head_query, head_key, head_value):
            ref[size:, :] = jnp.zeros((8, ref.shape[1]), F32)

    half = rows_own // 2

    def partial(one, two, number):
        return mm(jnp.concatenate([hidden[pl.ds(one, half), :], hidden[pl.ds(two, half), :]], 0), w_down[...])

    def finish(start, length, down):
        output[start : start + length, :] = (resid[start : start + length, :] + down).astype(BF16)

    ring = Ring(count)
    scatter = Scatter(ring, partial, slots, sends, recvs, rows_own, finish)
    loads = [
        pltpu.make_async_copy(source, target, load_sems.at[k])
        for k, (source, target) in enumerate(
            ((w_query_in, w_query), (w_key_in, w_key), (w_value_in, w_value), (w_gate_in, w_gate), (resid_in, resid),
             (w_out_in, w_out), (hidden_in, hidden), (w_down_in, w_down))
        )
    ]

    @pl.when(step == 0)
    def _():
        for load in reversed(loads):
            load.start()
        greet(ring)
        for load in loads[6:]:
            load.wait()

    spread_hops(step, chunks, count, scatter.hop)

    @pl.when(step == 0)
    def _():
        loads[5].wait()

    rows, seg_rows, seg_columns, before, last = chunk_masks(starts, lengths, seqs, first, size)
    same = seg_rows == seg_columns
    i = lax.broadcasted_iota(jnp.int32, (size, size), 0)
    j = lax.broadcasted_iota(jnp.int32, (size, size), 1)
    strict = jnp.where(same & (i > j), 1.0, 0.0)
    inclusive = jnp.where(same & (i >= j), 1.0, 0.0)
    carried = jnp.where(seg_rows == before, 1.0, 0.0)
    ending = jnp.where(seg_rows == last, 1.0, 0.0)
    kept = jnp.where(before == last, 1.0, 0.0)
    live = jnp.where(seg_rows % 2 == 1, 1.0, 0.0)
    taps = taps_query.shape[0]
    joined = [
        jnp.where(segment_at(rows + offset, starts, lengths, seqs) == seg_rows, 1.0, 0.0)
        for offset in range(1, taps)
    ]
    normal_rows, unit_rows = normed_rows(tokens, gain_first)
    inputs = normal_rows.astype(BF16)
    grad_rows = grad_attended[...]
    grad_mixed = mm(grad_rows, w_out[...], (1, 1))
    a_out[...] += mm(mixed[...], grad_rows, (0, 0))
    strength = sigmoid(p_beta[...])
    scale = width ** (-0.5)
    head_gain = gain[...].astype(F32)

    grads_query, grads_key, grads_value, grads_gate, grads_beta = [], [], [], [], []
    for h in range(heads):
        cols = slice(h * width, (h + 1) * width)
        out = delta_out[:, cols]
        gate = p_gate[:, cols]
        sig_gate = sigmoid(gate)
        silu_gate = gate * sig_gate
        root = lax.rsqrt(jnp.mean(out * out, axis=1, keepdims=True) + 1e-5)
        grad = grad_mixed[:, cols] * live
        unit = out * root
        grads_gate.append(grad * unit * head_gain * (sig_gate * (1.0 + gate * (1.0 - sig_gate))))
        grad_normal = grad * silu_gate
        small[2:3, 0:width] += jnp.sum(grad_normal * unit, axis=0, keepdims=True)
        push = grad_normal * head_gain
        grad_out = scale * root * (push - unit * jnp.mean(push * unit, axis=1, keepdims=True))

        zq, zk, zv = z_query[:, cols], z_key[:, cols], z_value[:, cols]
        sq, sk, sv = sigmoid(zq), sigmoid(zk), sigmoid(zv)
        uq, uk = zq * sq, zk * sk
        nq = lax.rsqrt(jnp.sum(uq * uq, axis=1, keepdims=True) + 1e-6)
        nk = lax.rsqrt(jnp.sum(uk * uk, axis=1, keepdims=True) + 1e-6)
        unit_q, unit_k = uq * nq, uk * nk
        query, key = unit_q.astype(BF16), unit_k.astype(BF16)
        beta = strength[:, h : h + 1]
        change = change_in[:, cols]
        inverse = inverse_in[0, h]
        memory = state_in[0, h]
        flowing = flow[h]
        low_flow = flowing.astype(BF16)
        low_out = grad_out.astype(BF16)

        within = mm(query, key, (1, 1)) * inclusive
        grad_within = (mm(low_out, change, (1, 1)) * inclusive).astype(BF16)
        grad_change = mm(within, low_out, (0, 0)) + ending * mm(key, low_flow)
        grad_mid = mm(inverse, grad_change, (0, 0))
        grad_value = beta * grad_mid
        low_value = grad_value.astype(BF16)
        cross = (mm(low_value, change, (1, 1)) * strict).astype(BF16)
        grad_query = carried * mm(low_out, memory, (1, 1)) + mm(grad_within, key)
        grad_key = (
            mm(grad_within, query, (0, 0))
            + ending * mm(change, low_flow, (1, 1))
            - carried * mm(low_value, memory, (1, 1))
            - mm(cross, key)
            - mm(cross, key, (0, 0))
        )
        flow[h] = (
            kept * flowing
            + mm(query, carried * grad_out, (0, 0))
            - mm(key, carried * grad_value, (0, 0))
        )
        grads_beta.append((1.0 - beta) * jnp.sum(grad_mid * change.astype(F32), axis=1, keepdims=True))
        du_q = nq * (grad_query - unit_q * jnp.sum(grad_query * unit_q, axis=1, keepdims=True))
        du_k = nk * (grad_key - unit_k * jnp.sum(grad_key * unit_k, axis=1, keepdims=True))
        grads_query.append(du_q * sq * (1.0 + zq * (1.0 - sq)))
        grads_key.append(du_k * sk * (1.0 + zk * (1.0 - sk)))
        grads_value.append(grad_value * sv * (1.0 + zv * (1.0 - sv)))

    tap_row = 8 + heads
    wide = heads * width

    def unconv(parts, taps_ref, head, projected, place):
        lanes = slice(place * wide, (place + 1) * wide)
        grad = jnp.concatenate(parts, axis=1)
        head[0:size, :] = grad
        tap = taps_ref[...].astype(F32)
        p = projected[...]
        result = grad * tap[0:1]
        small[tap_row : tap_row + 1, lanes] += jnp.sum(p * grad, axis=0, keepdims=True)
        for offset in range(1, taps):
            moved = head[offset : offset + size, :] * joined[offset - 1]
            result = result + moved * tap[offset : offset + 1]
            row = tap_row + offset
            small[row : row + 1, lanes] += jnp.sum(p * moved, axis=0, keepdims=True)
        head[size:, :] = grad[0:8, :]
        return result.astype(BF16)

    d_query = unconv(grads_query, taps_query, head_query, p_query, 0)
    d_key = unconv(grads_key, taps_key, head_key, p_key, 1)
    d_value = unconv(grads_value, taps_value, head_value, p_value, 2)
    d_gate = jnp.concatenate(grads_gate, axis=1).astype(BF16)
    spare = [jnp.zeros((size, 1), F32)] * (w_beta.shape[0] - heads)
    d_beta = jnp.concatenate(grads_beta + spare, axis=1).astype(BF16)

    @pl.when(step == 0)
    def _():
        for load in loads[:5]:
            load.wait()

    grad_inputs = (
        mm(d_query, w_query[...], (1, 1))
        + mm(d_key, w_key[...], (1, 1))
        + mm(d_value, w_value[...], (1, 1))
        + mm(d_gate, w_gate[...], (1, 1))
        + mm(d_beta, w_beta[...])
    )
    grad_normed[...] = grad_inputs.astype(BF16)
    small[0:1, :] += jnp.sum(grad_inputs * unit_rows, axis=0, keepdims=True)
    a_query[...] += mm(inputs, d_query, (0, 0))
    a_key[...] += mm(inputs, d_key, (0, 0))
    a_value[...] += mm(inputs, d_value, (0, 0))
    a_gate[...] += mm(inputs, d_gate, (0, 0))
    small[8 : 8 + heads, :] += mm(d_beta, inputs, (0, 0))[:heads]

    @pl.when(step == chunks - 1)
    def _():
        for target, source in (
            (gw_query, a_query), (gw_key, a_key), (gw_value, a_value), (gw_gate, a_gate),
            (gw_out, a_out),
        ):
            target[...] = source[...].astype(target.dtype)
        scatter.end()


def backward_mixer(tokens, grad_attended, saved, w_query, w_key, w_value, w_gate, w_beta, w_out, taps_query, taps_key, taps_value, gain, gain_first, starts, lengths, hidden, w_down, resid, g_second, count):
    slots, model = tokens.shape
    wide = w_query.shape[1]
    width = gain.shape[0]
    heads = wide // width
    seqs = starts.shape[1]
    chunks = slots // CHUNK
    taps = taps_query.shape[0]
    smem = pl.BlockSpec(memory_space=pltpu.SMEM)
    fixed = lambda shape: pl.BlockSpec(shape, lambda n: (0,) * len(shape), pipeline_mode=pl.Buffered(1))
    piece = lambda shape: pl.BlockSpec(shape, lambda n: (chunks - 1 - n,) + (0,) * (len(shape) - 1))
    rows = lambda a: piece((CHUNK, a.shape[1]))
    outs = (
        [((slots, model), BF16)] + [((model, wide), BF16)] * 4 + [((wide, model), BF16)]
        + [((small_rows(heads, taps), model), F32), (resid.shape, BF16)]
    )
    return pl.pallas_call(
        functools.partial(backward_kernel, heads, width, seqs, chunks, count, slots // count),
        name="mixer_backward",
        grid=(chunks,),
        out_shape=[jax.ShapeDtypeStruct(s, d) for s, d in outs],
        in_specs=[smem, smem, rows(tokens), rows(grad_attended)]
        + [rows(a) for a in saved[:11]]
        + [piece((1, heads, CHUNK, CHUNK)), piece((1, heads, width, width))]
        + [ANY] * 4
        + [fixed(w_beta.shape), ANY]
        + [fixed((taps, wide))] * 3
        + [fixed((1, width)), VMEM, ANY, ANY, ANY, fixed(g_second.shape)],
        out_specs=[piece((CHUNK, model))] + [fixed(s) for s, d in outs[1:]],
        scratch_shapes=[pltpu.VMEM((model, wide), F32)] * 4
        + [pltpu.VMEM((wide, model), F32)]
        + [pltpu.VMEM((CHUNK + 8, wide), F32)] * 3
        + [pltpu.VMEM((heads, width, width), F32)]
        + [pltpu.VMEM((model, wide), BF16)] * 4
        + [pltpu.VMEM(resid.shape, F32)]
        + [pltpu.VMEM(a.shape, BF16) for a in (w_out, hidden, w_down)]
        + [pltpu.SemaphoreType.DMA((8,)), ring_slots(count, slots // count, model)]
        + ring_semaphores(count),
        compiler_params=ring_params(6),
        cost_estimate=pl.CostEstimate(
            flops=2 * slots * model * wide * 10 + slots * heads * CHUNK * 2 * CHUNK * 8,
            bytes_accessed=slots * model * 6 + 10 * model * wide * 2 + slots * wide * 36,
            transcendentals=slots * wide * 8,
        ),
    )(starts, lengths, tokens, grad_attended, *saved, w_query, w_key, w_value, w_gate, w_beta, w_out, taps_query, taps_key, taps_value, gain.reshape(1, width), gain_first, hidden, w_down, resid, g_second)


def make_shards(groups, count):
    def shards(
        tokens, attn_gain, w_query, w_key, w_value, conv_query, conv_key, conv_value, w_beta, w_gate_out,
        head_gain, w_out, ffn_gain, w_gate, w_up, w_down, seq_starts, seq_lengths, cotangent,
    ):
        model = tokens.shape[1]
        heads = w_beta.shape[1]
        beta_rows = w_beta.T if heads > 1 else jnp.pad(w_beta.T, ((0, 1), (0, 0)))
        tokens_full = gather_tokens(tokens, count)
        mixed_full, w_out_full, *saved = forward_mixer(
            tokens_full, w_query, w_key, w_value, w_gate_out, beta_rows,
            conv_query, conv_key, conv_value, head_gain, attn_gain, seq_starts, seq_lengths, w_out, count, groups,
        )
        w_out_full = w_out_full.reshape(-1, tokens.shape[1])
        resid, ffn_full, hidden, grad_gate, grad_up, grad_full = attend(
            mixed_full, w_out_full, tokens_full, ffn_gain, w_gate.T, w_up.T, w_down, cotangent, count
        )
        grad_resid, grad_attended, g_second, *ffn_grads = ffn_back(
            grad_gate, grad_up, hidden, w_gate.T, w_up.T, resid, cotangent, ffn_gain, ffn_full, grad_full,
            count, groups,
        )
        pulled = backward_mixer(
            tokens_full, grad_attended, saved, w_query, w_key, w_value, w_gate_out, beta_rows, w_out,
            conv_query, conv_key, conv_value, head_gain, attn_gain, seq_starts, seq_lengths,
            hidden, w_down, resid, g_second, count,
        )
        terms, gw_query, gw_key, gw_value, gw_gate_out, gw_out, small, output = pulled
        grad_tokens, total, *mixer_grads = last_step(
            terms, tokens, grad_resid, attn_gain, small,
            (gw_query, gw_key, gw_value, gw_gate_out, gw_out), count, groups,
        )
        taps, wide = conv_query.shape
        output, grad_tokens, *rest = results(
            total,
            [(output, BF16), (grad_tokens, F32)] + [(g, F32) for g in (*mixer_grads, *ffn_grads)],
            heads, taps, wide, head_gain.shape[0],
        )
        grads, (g_first, g_second, g_head, gt_query, gt_key, gt_value, g_beta) = rest[:8], rest[8:]
        return (
            output,
            grad_tokens,
            g_first[0],
            grads[0],
            grads[1],
            grads[2],
            gt_query,
            gt_key,
            gt_value,
            g_beta.T,
            grads[3],
            g_head[0],
            grads[4],
            g_second[0],
            grads[5].T,
            grads[6].T,
            grads[7],
        )

    return shards


def solution(mesh):
    placed = (
        P(("dp", "tensor"), None),
        P(),
        P(None, "tensor"),
        P(None, "tensor"),
        P(None, "tensor"),
        P(None, "tensor"),
        P(None, "tensor"),
        P(None, "tensor"),
        P(None, "tensor"),
        P(None, "tensor"),
        P(),
        P("tensor", None),
        P(),
        P(None, "tensor"),
        P(None, "tensor"),
        P("tensor", None),
        P("dp", None),
        P("dp", None),
        P(("dp", "tensor"), None),
    )
    return jax.shard_map(
        make_shards(mesh.shape["dp"], mesh.shape["tensor"]),
        mesh=mesh,
        in_specs=placed,
        out_specs=(
            P(("dp", "tensor"), None),
            P(("dp", "tensor"), None),
            P(),
            P(None, "tensor"),
            P(None, "tensor"),
            P(None, "tensor"),
            P(None, "tensor"),
            P(None, "tensor"),
            P(None, "tensor"),
            P(None, "tensor"),
            P(None, "tensor"),
            P(),
            P("tensor", None),
            P(),
            P(None, "tensor"),
            P(None, "tensor"),
            P("tensor", None),
        ),
        check_vma=False,
    )
```

```python
import functools
import jax
import jax.numpy as jnp
from jax import lax
from jax.experimental import pallas as pl
from jax.experimental.pallas import tpu as pltpu
from jax.sharding import PartitionSpec as P

CHUNK = 256
F32, BF16 = jnp.float32, jnp.bfloat16


def mm(a, b, contract=(1, 0)):
    return lax.dot_general(
        a.astype(BF16),
        b.astype(BF16),
        (((contract[0],), (contract[1],)), ((), ())),
        preferred_element_type=F32,
    )


def segment_at(places, starts, lengths, seqs):
    segment = jnp.zeros_like(places)
    for s in range(seqs):
        begin = starts[0, s]
        stop = begin + lengths[0, s]
        segment = segment + jnp.where(places >= begin, 1, 0) + jnp.where(places >= stop, 1, 0)
    return jnp.where(places < 0, -1, segment)


def chunk_masks(starts, lengths, seqs, first, size):
    rows = first + lax.broadcasted_iota(jnp.int32, (size, 1), 0)
    columns = first + lax.broadcasted_iota(jnp.int32, (1, size), 1)
    seg_rows = segment_at(rows, starts, lengths, seqs)
    seg_columns = segment_at(columns, starts, lengths, seqs)
    before = segment_at(jnp.full((1, 1), first - 1, jnp.int32), starts, lengths, seqs)
    last = segment_at(jnp.full((1, 1), first + size - 1, jnp.int32), starts, lengths, seqs)
    return rows, seg_rows, seg_columns, before, last


def inverse_unit_lower(lower, size):
    i = lax.broadcasted_iota(jnp.int32, (size, size), 0)
    j = lax.broadcasted_iota(jnp.int32, (size, size), 1)

    def corner(width):
        shift = width.bit_length() - 1
        pair = (i >> (shift + 1)) == (j >> (shift + 1))
        return pair & (((i >> shift) & 1) == 1) & (((j >> shift) & 1) == 0)

    inverse = jnp.where(i == j, 1.0, 0.0) - jnp.where(corner(1), lower, 0.0)
    width = 2
    while width < size:
        low = inverse.astype(BF16)
        if 2 * width == size:
            part = mm(mm(low[width:, width:], lower[width:, :width]), low[:width, :width])
            inverse = jnp.concatenate(
                [
                    inverse[:width],
                    jnp.concatenate([-part, inverse[width:, width:]], axis=1),
                ],
                axis=0,
            )
        else:
            between = jnp.where(corner(width), lower, 0.0)
            inverse = inverse - mm(mm(low, between), low)
        width *= 2
    return inverse


def sigmoid(v):
    return 1.0 / (1.0 + jnp.exp(-v))


def normed_rows(tokens, gain):
    value = tokens[...].astype(F32)
    unit = value * lax.rsqrt(jnp.mean(value * value, axis=1, keepdims=True) + 1e-6)
    return unit * gain[...].astype(F32).reshape(1, -1), unit


MESH = pl.DeviceIdType.MESH
SUBS = 2
PAIRS = [(sub, way) for sub in range(SUBS) for way in (0, 1)]


def ring_position(device, count):
    half, odd = device // 2, device % 2
    return half + odd * (count - 1 - 2 * half)


def ring_device(position, count):
    back = position // (count // 2)
    return (1 - back) * 2 * position + back * (2 * (count - 1 - position) + 1)


class Ring:
    def __init__(self, count):
        self.count = count
        self.me = lax.axis_index("tensor")
        self.place = ring_position(self.me, count)
        self.group = lax.axis_index("dp")

    def at(self, offset):
        return ring_device((self.place + offset + 2 * self.count) % self.count, self.count)

    def next(self, way):
        return (self.group, self.at(1 if way == 0 else -1))


class Gather:
    def __init__(self, ring, own, view, sends, recvs, rows, subs=SUBS):
        self.ring, self.own, self.view, self.sends, self.recvs, self.rows = ring, own, view, sends, recvs, rows
        self.piece = rows // (2 * subs)
        self.pairs = [(sub, way) for sub in range(subs) for way in (0, 1)]

    def origin(self, way, step):
        return self.ring.at(-step if way == 0 else step)

    def copy(self, way, sub, step, origin, first=False):
        inside = way * (self.rows // 2) + sub * self.piece
        place = self.view(origin, inside, self.piece)
        return pltpu.make_async_remote_copy(
            src_ref=self.own(inside, self.piece) if first else place,
            dst_ref=place,
            send_sem=self.sends.at[way, sub, step],
            recv_sem=self.recvs.at[way, sub, step],
            device_id=self.ring.next(way),
            device_id_type=MESH,
        )

    def begin(self):
        for sub, way in self.pairs:
            self.copy(way, sub, 0, self.ring.me, True).start()

    def arrived(self, step):
        for sub, way in self.pairs:
            self.copy(way, sub, step - 1, self.origin(way, step)).wait_recv()

    def hop(self, step):
        for sub, way in self.pairs:
            self.copy(way, sub, step - 1, self.origin(way, step)).wait_recv()
            self.copy(way, sub, step, self.origin(way, step)).start()

    def end(self):
        def drain(step, carry):
            for sub, way in self.pairs:
                self.copy(way, sub, step, self.ring.me).wait_send()
            return carry

        lax.fori_loop(0, self.ring.count - 1, drain, 0)


def row_view(ref, rows):
    return lambda origin, start, size: ref.at[pl.ds(pl.multiple_of(origin * rows + start, size), size), :]


def row_own(ref):
    return lambda start, size: ref.at[pl.ds(start, size), :]


def ring_gather(gather, between, begun=False):
    count = gather.ring.count

    def run(step, carry):
        if not begun:
            pl.when(step == 0)(gather.begin)

        @pl.when((step > 0) & (step < count - 1))
        def _():
            gather.hop(step)

        @pl.when(step == count - 1)
        def _():
            gather.arrived(step)

        between(step)
        return carry

    lax.fori_loop(0, count, run, 0)
    gather.end()


def scatter_copy(ring, slots, sends, recvs, way, sub, step):
    return pltpu.make_async_remote_copy(
        src_ref=slots.at[way, sub, step],
        dst_ref=slots.at[way, sub, step + 1],
        send_sem=sends.at[way, sub, step],
        recv_sem=recvs.at[way, sub, step],
        device_id=ring.next(way),
        device_id_type=MESH,
    )


class Scatter:
    def __init__(self, ring, partial, slots, sends, recvs, rows, finish, after=None):
        self.after = after
        self.ring, self.partial, self.slots, self.sends, self.recvs = ring, partial, slots, sends, recvs
        self.half, self.finish = rows // 2, finish
        self.rows, self.piece = rows, rows // (2 * SUBS)

    def terms(self, step):
        half, first, second = self.half, self.ring.at(-1 - step), self.ring.at(1 + step)
        return self.partial(
            pl.multiple_of(first * self.rows, half), pl.multiple_of(second * self.rows + half, half), step
        )

    def part(self, terms, way, sub):
        start = way * self.half + sub * self.piece
        return terms[start : start + self.piece]

    def copy(self, way, sub, step):
        return scatter_copy(self.ring, self.slots, self.sends, self.recvs, way, sub, step)

    def hop(self, step):
        self.pass_on(step, self.terms(step))

    def pass_on(self, step, terms):
        for sub, way in PAIRS:
            term = self.part(terms, way, sub)

            @pl.when(step == 0)
            def _():
                self.slots[way, sub, 0] = term.astype(BF16)

            @pl.when(step > 0)
            def _():
                self.copy(way, sub, step - 1).wait_recv()
                self.slots[way, sub, step] = (self.slots[way, sub, step].astype(F32) + term).astype(BF16)

            self.copy(way, sub, step).start()

    def end(self):
        self.take(self.terms(self.ring.count - 1))
        self.drain()

    def take(self, terms):
        count = self.ring.count
        for sub, way in PAIRS:
            self.copy(way, sub, count - 2).wait_recv()
            self.finish(
                way * self.half + sub * self.piece,
                self.piece,
                self.slots[way, sub, count - 1].astype(F32) + self.part(terms, way, sub),
            )
            if self.after is not None:
                self.after(way, sub)

    def drain(self):
        def run(step, carry):
            for sub, way in PAIRS:
                self.copy(way, sub, step).wait_send()
            return carry

        lax.fori_loop(0, self.ring.count - 1, run, 0)


def ring_scatter(scatter, between):
    count = scatter.ring.count

    def run(step, carry):
        terms = scatter.terms(step)
        pl.when(step < count - 1)(lambda: scatter.pass_on(step, terms))
        pl.when(step == count - 1)(lambda: scatter.take(terms))
        between(step)
        return carry

    lax.fori_loop(0, count, run, 0)
    scatter.drain()


class GroupSum:
    def __init__(self, ring, groups, grads, near, far, targets, near_sems, far_sems, back_sems, keep_sems):
        self.ring, self.groups, self.grads, self.near, self.far, self.targets = ring, groups, grads, near, far, targets
        self.near_sems, self.far_sems, self.back_sems, self.keep_sems = near_sems, far_sems, back_sems, keep_sems
        self.core = ring.group % 2
        self.mate = (ring.group + 1 - 2 * self.core, ring.me)

    def peers(self):
        return [self.mate] + [
            ((self.ring.group + 2 * k) % self.groups, self.ring.me) for k in range(1, self.groups // 2)
        ]

    def half(self, i, core):
        rows = self.near[i].shape[0]
        return pl.ds(pl.multiple_of(core * rows, rows), rows)

    def near_copy(self, i):
        return pltpu.make_async_remote_copy(
            src_ref=self.grads[i].at[self.half(i, 1 - self.core), :], dst_ref=self.near[i],
            send_sem=self.near_sems.at[0, i], recv_sem=self.near_sems.at[1, i],
            device_id=self.mate, device_id_type=MESH,
        )

    def far_copy(self, i, k):
        return pltpu.make_async_remote_copy(
            src_ref=self.near[i], dst_ref=self.far[i].at[k - 1],
            send_sem=self.far_sems.at[0, i, k - 1], recv_sem=self.far_sems.at[1, i, k - 1],
            device_id=((self.ring.group + 2 * k) % self.groups, self.ring.me), device_id_type=MESH,
        )

    def back_copy(self, i):
        return pltpu.make_async_remote_copy(
            src_ref=self.far[i].at[0], dst_ref=self.targets[i].at[self.half(i, self.core), :],
            send_sem=self.back_sems.at[0, i], recv_sem=self.back_sems.at[1, i],
            device_id=self.mate, device_id_type=MESH,
        )

    def keep_copy(self, i):
        return pltpu.make_async_copy(
            self.far[i].at[0], self.targets[i].at[self.half(i, self.core), :], self.keep_sems.at[i]
        )

    def first(self, chosen):
        for i in chosen:
            self.near_copy(i).start()

    def each_block(self, i, body):
        rows = self.near[i].shape[0]
        block = next(size for size in (64, 32, 16) if rows % size == 0)

        def step(at, carry):
            start = pl.multiple_of(at * block, block)
            body(pl.ds(start, block), pl.ds(pl.multiple_of(self.core * rows + start, block), block))
            return carry

        lax.fori_loop(0, rows // block, step, 0)

    def second(self, chosen):
        for i in chosen:
            self.near_copy(i).wait_recv()

            def add(here, own, i=i):
                self.near[i][here, :] = (
                    self.near[i][here, :].astype(F32) + self.grads[i][own, :].astype(F32)
                ).astype(BF16)

            self.each_block(i, add)
            for k in range(1, self.groups // 2):
                self.far_copy(i, k).start()

    def third(self, chosen):
        for i in chosen:
            for k in range(1, self.groups // 2):
                self.far_copy(i, k).wait()

            def add(here, own, i=i):
                total = self.near[i][here, :].astype(F32)
                for k in range(self.groups // 2 - 1):
                    total = total + self.far[i][k, here, :].astype(F32)
                self.far[i][0, here, :] = total.astype(BF16)

            self.each_block(i, add)
            self.keep_copy(i).start()
            self.back_copy(i).start()

    def last(self):
        for i in range(len(self.grads)):
            self.near_copy(i).wait_send()
            self.back_copy(i).wait()
            self.keep_copy(i).wait()


def sum_scratch(shapes, groups):
    number = len(shapes)
    return (
        [pltpu.VMEM((rows // 2, columns), BF16) for rows, columns in shapes]
        + [pltpu.VMEM((groups // 2 - 1, rows // 2, columns), BF16) for rows, columns in shapes]
        + [
            pltpu.SemaphoreType.DMA((2, number)),
            pltpu.SemaphoreType.DMA((2, number, groups // 2 - 1)),
            pltpu.SemaphoreType.DMA((2, number)),
            pltpu.SemaphoreType.DMA((number,)),
        ]
    )


def greet(ring, others=()):
    barrier = pltpu.get_barrier_semaphore()
    peers = [ring.next(0), ring.next(1)] + list(others)
    for peer in peers:
        pl.semaphore_signal(barrier, inc=1, device_id=peer, device_id_type=MESH)
    pl.semaphore_wait(barrier, len(peers))


def ring_semaphores(count, subs=SUBS):
    return [pltpu.SemaphoreType.DMA((2, subs, count - 1))] * 2


def ring_slots(count, rows, columns):
    return pltpu.VMEM((2, SUBS, count, rows // (2 * SUBS), columns), BF16)


ANY = pl.BlockSpec(memory_space=pl.ANY)
VMEM = pl.BlockSpec(memory_space=pltpu.VMEM)


def ring_params(number):
    return pltpu.CompilerParams(
        collective_id=number, has_side_effects=True, vmem_limit_bytes=60 << 20
    )


class WholeWeight:
    def __init__(self, ring, groups, weight, full, sends, recvs, keep_sem, far_sems, near_sems):
        self.ring, self.groups, self.full, self.far_sems, self.near_sems = ring, groups, full, far_sems, near_sems
        part = weight.shape[0] // groups
        group = ring.group
        own = lambda start, size: weight.at[pl.ds(pl.multiple_of(group * part + start, size), size), :]
        self.gather = Gather(
            ring, own, lambda origin, start, size: full.at[origin, group, pl.ds(start, size), :],
            sends, recvs, part, 1,
        )
        self.keep = pltpu.make_async_copy(own(0, part), full.at[ring.me, group], keep_sem)
        self.mate = (group + 1 - 2 * (group % 2), ring.me)
        self.across = groups // 2

    def peer(self, k):
        return ((self.ring.group + 2 * k) % self.groups, self.ring.me)

    def peers(self):
        return [self.mate] + [self.peer(k) for k in range(1, self.across)]

    def far(self, k, way, step):
        gather = self.gather
        part = self.full.at[gather.origin(way, step), self.ring.group, pl.ds(way * gather.piece, gather.piece), :]
        return pltpu.make_async_remote_copy(
            src_ref=part, dst_ref=part,
            send_sem=self.far_sems.at[0, k - 1, way, step], recv_sem=self.far_sems.at[1, k - 1, way, step],
            device_id=self.peer(k), device_id_type=MESH,
        )

    def near(self, k):
        part = self.full.at[:, (self.ring.group + self.groups - 2 * k) % self.groups]
        return pltpu.make_async_remote_copy(
            src_ref=part, dst_ref=part, send_sem=self.near_sems.at[0, k], recv_sem=self.near_sems.at[1, k],
            device_id=self.mate, device_id_type=MESH,
        )

    def pass_on(self, step):
        for k in range(1, self.across):
            for way in (0, 1):
                self.far(k, way, step).start()

    def begin(self):
        self.gather.begin()
        self.keep.start()

    def hop(self, step):
        self.gather.hop(step)
        self.pass_on(step)

    def exchange(self):
        self.gather.arrived(self.ring.count - 1)
        self.pass_on(self.ring.count - 1)
        self.keep.wait()
        self.pass_on(0)
        self.near(0).start()

    def every_far(self, body):
        def run(step, carry):
            for k in range(1, self.across):
                for way in (0, 1):
                    body(self.far(k, way, step))
            return carry

        lax.fori_loop(0, self.ring.count, run, 0)

    def back(self):
        self.every_far(lambda copy: copy.wait_recv())
        for k in range(1, self.across):
            self.near(k).start()

    def end(self):
        for k in range(self.across):
            self.near(k).wait()
        self.every_far(lambda copy: copy.wait_send())
        self.gather.end()


def gather_kernel(count, tokens, tokens_full, sends, recvs, local):
    ring = Ring(count)
    rows = tokens.shape[0]
    greet(ring)
    keep = pltpu.make_async_copy(
        tokens, tokens_full.at[pl.ds(pl.multiple_of(ring.me * rows, rows), rows), :], local
    )
    keep.start()
    ring_gather(
        Gather(ring, row_own(tokens), row_view(tokens_full, rows), sends, recvs, rows), lambda step: None
    )
    keep.wait()


def gather_tokens(tokens, count):
    rows, model = tokens.shape
    return pl.pallas_call(
        functools.partial(gather_kernel, count),
        name="gather_tokens",
        out_shape=jax.ShapeDtypeStruct((count * rows, model), tokens.dtype),
        in_specs=[ANY],
        out_specs=ANY,
        scratch_shapes=ring_semaphores(count) + [pltpu.SemaphoreType.DMA],
        compiler_params=ring_params(1),
        cost_estimate=pl.CostEstimate(flops=0, bytes_accessed=300 << 20, transcendentals=0),
    )(tokens)


def attend_kernel(
    count, mixed, w_out, tokens, gain, w_gate, w_up, w_down, cotangent,
    resid, full, hidden, grad_gate, grad_up, cotangents,
    gathered, out_box, gate_box, up_box, down_box, mixed_boxes, token_boxes, normed, gates, stages,
    sends, recvs, weight_sems, keep_sem, mixed_sems, token_sems, out_sems, normed_sems, stage_sems,
):
    ring = Ring(count)
    rows = cotangent.shape[0]
    half = rows // 2
    gather = Gather(ring, row_own(cotangent), row_view(gathered, rows), sends, recvs, rows)
    keep = pltpu.make_async_copy(
        cotangent, gathered.at[pl.ds(pl.multiple_of(ring.me * rows, rows), rows), :], keep_sem
    )
    loads = [
        pltpu.make_async_copy(source, box, weight_sems.at[k])
        for k, (source, box) in enumerate(
            ((w_out, out_box), (w_gate, gate_box), (w_up, up_box), (w_down, down_box))
        )
    ]

    def place(way, step):
        return pl.ds(pl.multiple_of(gather.origin(way, step) * rows + way * half, half), half)

    def mixed_copy(way, step):
        return pltpu.make_async_copy(
            mixed.at[:, place(way, step), :], mixed_boxes.at[step % 2, way], mixed_sems.at[step % 2, way]
        )

    def token_copy(way, step):
        return pltpu.make_async_copy(
            tokens.at[place(way, step), :], token_boxes.at[step % 2, way], token_sems.at[step % 2, way]
        )

    def out_copy(way, step):
        at = place(way, step)
        return pltpu.make_async_copy(gathered.at[at, :], cotangents.at[at, :], out_sems.at[way, step])

    def normed_copy(way, step):
        return pltpu.make_async_copy(
            normed.at[step % 2, pl.ds(way * half, half), :], full.at[place(way, step), :],
            normed_sems.at[step % 2, way],
        )

    def stage_copy(k, way, step):
        target = (hidden, grad_gate, grad_up)[k]
        return pltpu.make_async_copy(
            stages.at[step % 2, k, way], target.at[place(way, step), :], stage_sems.at[step % 2, k, way]
        )

    def settle(step):
        for way in (0, 1):
            normed_copy(way, step).wait()
            for k in range(3):
                stage_copy(k, way, step).wait()

    def fetch(step):
        for way in (0, 1):
            mixed_copy(way, step).start()
            token_copy(way, step).start()

    def put(k, step, value):
        low = value.astype(BF16)
        for way in (0, 1):
            stages[step % 2, k, way] = low[way * half : way * half + half]
            stage_copy(k, way, step).start()

    def prepare(step):
        @pl.when(step > 1)
        def _():
            settle(step - 2)

        slot = step % 2
        for way in (0, 1):
            mixed_copy(way, step).wait()
            token_copy(way, step).wait()

        @pl.when(step + 1 < count)
        def _():
            fetch(step + 1)

        heads = jnp.concatenate(
            [
                jnp.concatenate([mixed_boxes[slot, way, j] for j in range(count)], 1)
                for way in (0, 1)
            ],
            0,
        )
        value = jnp.concatenate([token_boxes[slot, 0], token_boxes[slot, 1]], 0).astype(F32)
        value = value + mm(heads, out_box[...])

        @pl.when(step == 0)
        def _():
            resid[...] = value

        scale = lax.rsqrt(jnp.mean(value * value, axis=1, keepdims=True) + 1e-6)
        normed[slot] = (value * scale * gain[...].astype(F32).reshape(1, -1)).astype(BF16)
        for way in (0, 1):
            normed_copy(way, step).start()
        inputs = normed[slot]
        gate = mm(inputs, gate_box[...], (1, 1))
        up = mm(inputs, up_box[...], (1, 1))
        sig = sigmoid(gate)
        opened = gate * sig
        put(0, step, opened * up)
        gates[0] = up * sig * (1.0 + gate * (1.0 - sig))
        gates[1] = opened

    def feed(step):
        for way in (0, 1):
            out_copy(way, step).start()
        grad = mm(
            jnp.concatenate([gathered[place(0, step), :], gathered[place(1, step), :]], 0), down_box[...], (1, 1)
        )
        put(1, step, grad * gates[0])
        put(2, step, grad * gates[1])

    def run(step, carry):
        @pl.when(step == 0)
        def _():
            gather.begin()
            for load in loads:
                load.wait()

        prepare(step)

        @pl.when(step == 0)
        def _():
            keep.wait()

        @pl.when((step > 0) & (step < count - 1))
        def _():
            gather.hop(step)

        @pl.when(step == count - 1)
        def _():
            gather.arrived(step)

        feed(step)
        return carry

    keep.start()
    fetch(0)
    for load in loads:
        load.start()
    greet(ring)
    lax.fori_loop(0, count, run, 0)
    gather.end()
    settle(count - 2)
    settle(count - 1)

    def drain(step, carry):
        for way in (0, 1):
            out_copy(way, step).wait()
        return carry

    lax.fori_loop(0, count, drain, 0)


def attend(mixed, w_out, tokens, gain, w_gate, w_up, w_down, cotangent, count):
    rows, model = cotangent.shape
    slots, inner = count * rows, w_down.shape[0]
    wide = mixed.shape[2]
    return pl.pallas_call(
        functools.partial(attend_kernel, count),
        name="attend",
        out_shape=[
            jax.ShapeDtypeStruct((rows, model), F32),
            jax.ShapeDtypeStruct((slots, model), BF16),
        ]
        + [jax.ShapeDtypeStruct((slots, inner), BF16)] * 3
        + [jax.ShapeDtypeStruct((slots, model), BF16)],
        in_specs=[ANY] * 3 + [VMEM] + [ANY] * 4,
        out_specs=[VMEM] + [ANY] * 5,
        scratch_shapes=[pltpu.VMEM((slots, model), BF16), pltpu.VMEM(w_out.shape, BF16)]
        + [pltpu.VMEM((inner, model), BF16)] * 3
        + [
            pltpu.VMEM((2, 2, count, rows // 2, wide), BF16),
            pltpu.VMEM((2, 2, rows // 2, model), BF16),
            pltpu.VMEM((2, rows, model), BF16),
            pltpu.VMEM((2, rows, inner), F32),
            pltpu.VMEM((2, 3, 2, rows // 2, inner), BF16),
        ]
        + ring_semaphores(count)
        + [
            pltpu.SemaphoreType.DMA((4,)),
            pltpu.SemaphoreType.DMA,
            pltpu.SemaphoreType.DMA((2, 2)),
            pltpu.SemaphoreType.DMA((2, 2)),
            pltpu.SemaphoreType.DMA((2, count)),
            pltpu.SemaphoreType.DMA((2, 2)),
            pltpu.SemaphoreType.DMA((2, 3, 2)),
        ],
        compiler_params=ring_params(2),
        cost_estimate=pl.CostEstimate(
            flops=2 * slots * model * model + 6 * slots * model * inner, bytes_accessed=300 << 20,
            transcendentals=slots * inner,
        ),
    )(mixed, w_out, tokens, gain, w_gate, w_up, w_down, cotangent)


def norm_back(inputs, scale, gain, grad_normed):
    weighted = gain * grad_normed
    inner = jnp.mean(weighted * inputs, axis=1, keepdims=True)
    unit = inputs * scale
    return scale * weighted - unit * (scale * scale * inner), grad_normed * unit


JOBS = 8


def ffn_back_kernel(
    count, groups, rows, grad_gate_in, grad_up_in, hidden_in, w_gate_in, w_up_in, resid_in, cotangent_in, gain, inputs, cotangents,
    grad_resid, full, grad_gain, sum_gate, sum_up, sum_down,
    slots, low, gw_gate, gw_up, gw_down, boxes, box_sems, hidden, resid, cotangent, grad_gate, grad_up, w_gate, w_up, load_sems, *rest,
):
    ring = Ring(count)
    sends, recvs, sends_two, recvs_two, local = rest[:5]
    sums = GroupSum(
        ring, groups, (gw_gate, gw_up, gw_down), rest[5:8], rest[8:11], (sum_gate, sum_up, sum_down), *rest[11:]
    )
    wide = boxes.shape[2]

    def box_copy(job, source):
        at = pl.multiple_of(job % (JOBS // 2) * wide, wide)
        return pltpu.make_async_copy(
            source.at[:, pl.ds(at, wide)], boxes.at[job % 2], box_sems.at[job % 2]
        )

    def fetch(job):
        @pl.when(job < JOBS // 2)
        def _():
            box_copy(job, inputs).start()

        @pl.when(job >= JOBS // 2)
        def _():
            box_copy(job, cotangents).start()

    loads = [
        pltpu.make_async_copy(source, target, load_sems.at[k])
        for k, (source, target) in enumerate(
            (
                (w_gate_in, w_gate), (w_up_in, w_up), (grad_gate_in, grad_gate), (grad_up_in, grad_up),
                (hidden_in, hidden), (resid_in, resid), (cotangent_in, cotangent),
            )
        )
    ]
    for load in loads[:4]:
        load.start()
    fetch(0)
    for load in loads[4:]:
        load.start()
    greet(ring, sums.peers())
    for load in loads[:4]:
        load.wait()
    grad_gain[...] = jnp.zeros_like(grad_gain)
    half = rows // 2

    def partial(first, second, step):
        gates = jnp.concatenate([grad_gate[pl.ds(first, half), :], grad_gate[pl.ds(second, half), :]], 0)
        ups = jnp.concatenate([grad_up[pl.ds(first, half), :], grad_up[pl.ds(second, half), :]], 0)
        return mm(gates, w_gate[...]) + mm(ups, w_up[...])

    def finish(start, size, grad):
        value = resid[start : start + size, :]
        scale = lax.rsqrt(jnp.mean(value * value, axis=1, keepdims=True) + 1e-6)
        through, pieces = norm_back(value, scale, gain[...].astype(F32).reshape(1, -1), grad)
        result = cotangent[start : start + size, :].astype(F32) + through
        grad_resid[start : start + size, :] = result
        grad_gain[...] += jnp.sum(pieces, axis=0, keepdims=True)
        low[start : start + size, :] = result.astype(BF16)

    def work(job, carry):
        box_copy(job, inputs).wait()

        @pl.when(job + 1 < JOBS)
        def _():
            fetch(job + 1)

        at = pl.ds(pl.multiple_of(job % (JOBS // 2) * wide, wide), wide)

        @pl.when(job < JOBS // 2)
        def _():
            box = boxes[job % 2]
            gw_gate[:, at] = mm(grad_gate[...], box, (0, 0)).astype(BF16)
            gw_up[:, at] = mm(grad_up[...], box, (0, 0)).astype(BF16)

        @pl.when(job >= JOBS // 2)
        def _():
            gw_down[:, at] = mm(hidden[...], boxes[job % 2], (0, 0)).astype(BF16)

        return carry

    each = JOBS // 4

    def beside_scatter(step):
        @pl.when(step == 2)
        def _():
            for load in loads[4:]:
                load.wait()

        @pl.when(step == 3)
        def _():
            sums.second((0, 1))

        @pl.when(step < 4)
        def _():
            lax.fori_loop(step * each, step * each + each, work, 0)

        @pl.when(step == 1)
        def _():
            sums.first((0, 1))

        @pl.when(step == 3)
        def _():
            sums.first((2,))

        @pl.when(step == 5)
        def _():
            sums.second((2,))

    def beside_gather(step):
        @pl.when(step == count - 3)
        def _():
            sums.third((0, 1))

        @pl.when(step == count - 2)
        def _():
            sums.third((2,))

    gather = Gather(ring, row_own(low), row_view(full, rows), sends_two, recvs_two, rows)
    start = lambda way, sub: gather.copy(way, sub, 0, ring.me, True).start()
    ring_scatter(Scatter(ring, partial, slots, sends, recvs, rows, finish, start), beside_scatter)
    keep = pltpu.make_async_copy(low, full.at[pl.ds(pl.multiple_of(ring.me * rows, rows), rows), :], local)
    keep.start()
    ring_gather(gather, beside_gather, True)
    keep.wait()
    sums.last()


def ffn_back(grad_gate, grad_up, hidden, w_gate, w_up, resid, cotangent, gain, inputs, cotangents, count, groups):
    rows, model = resid.shape
    slots, inner = grad_up.shape
    shapes = [(inner, model)] * 3
    return pl.pallas_call(
        functools.partial(ffn_back_kernel, count, groups, rows),
        name="ffn_back",
        out_shape=[
            jax.ShapeDtypeStruct((rows, model), F32),
            jax.ShapeDtypeStruct((slots, model), BF16),
            jax.ShapeDtypeStruct((1, model), F32),
        ]
        + [jax.ShapeDtypeStruct(shape, BF16) for shape in shapes],
        in_specs=[ANY] * 7 + [VMEM] + [ANY] * 2,
        out_specs=[VMEM, ANY, VMEM] + [ANY] * 3,
        scratch_shapes=[ring_slots(count, rows, model), pltpu.VMEM((rows, model), BF16)]
        + [pltpu.VMEM(shape, BF16) for shape in shapes]
        + [pltpu.VMEM((2, slots, model // (JOBS // 2)), BF16), pltpu.SemaphoreType.DMA((2,))]
        + [pltpu.VMEM((slots, inner), BF16), pltpu.VMEM((rows, model), F32), pltpu.VMEM((rows, model), BF16)]
        + [pltpu.VMEM((slots, inner), BF16)] * 2
        + [pltpu.VMEM((inner, model), BF16)] * 2
        + [pltpu.SemaphoreType.DMA((7,))]
        + ring_semaphores(count) * 2
        + [pltpu.SemaphoreType.DMA]
        + sum_scratch(shapes, groups),
        compiler_params=ring_params(3),
        cost_estimate=pl.CostEstimate(
            flops=10 * slots * model * inner, bytes_accessed=600 << 20, transcendentals=0
        ),
    )(grad_gate, grad_up, hidden, w_gate, w_up, resid, cotangent, gain, inputs, cotangents)


def last_kernel(
    count, groups, rows, terms, tokens_in, grad_resid_in, gain, small, *rest,
):
    grads_in, rest = rest[:5], rest[5:]
    grad_tokens, total = rest[:2]
    targets, rest = rest[2:7], rest[7:]
    slots, first_box, slice_own, spread, second_box, second_own, boxes, box_sems, tokens, grad_resid, load_sems = rest[:11]
    sends, recvs, first_sends, first_recvs, spread_sends, spread_recvs, second_sends, second_recvs = rest[11:19]
    ring = Ring(count)
    grads, grad_sems = rest[33:38], rest[38]
    sums = GroupSum(ring, groups, grads, rest[19:24], rest[24:29], targets, *rest[29:33])
    loads = [
        pltpu.make_async_copy(tokens_in, tokens, load_sems.at[0]),
        pltpu.make_async_copy(grad_resid_in, grad_resid, load_sems.at[1]),
    ]
    fills = [
        pltpu.make_async_copy(source, target, grad_sems.at[k])
        for k, (source, target) in enumerate(zip(grads_in, grads))
    ]
    half = rows // 2

    def box_copy(way, start, slot):
        return pltpu.make_async_copy(
            terms.at[pl.ds(start, half), :], boxes.at[slot, way], box_sems.at[slot, way]
        )

    def fetch(step):
        for way, owner in ((0, ring.at(-1 - step)), (1, ring.at(1 + step))):
            box_copy(way, pl.multiple_of(owner * rows + way * half, half), step % 2).start()

    fetch(0)
    for fill in fills:
        fill.start()
    for load in loads:
        load.start()
    me, group = ring.me, ring.group
    first_peers = [(group, (me + k) % count) for k in range(1, count)]
    second_peers = [((group + k) % groups, me) for k in range(1, groups)]
    barrier = pltpu.get_barrier_semaphore()
    for peer in first_peers + second_peers:
        pl.semaphore_signal(barrier, inc=1, device_id=peer, device_id_type=MESH)
    pl.semaphore_wait(barrier, count + groups - 2)

    lanes = small.shape[1] // count

    def lanes_of(device):
        return pl.ds(pl.multiple_of(device * lanes, lanes), lanes)

    def first(k):
        peer = first_peers[k]
        return pltpu.make_async_remote_copy(
            src_ref=small.at[0:8, lanes_of(peer[1])], dst_ref=first_box.at[k], send_sem=first_sends.at[k],
            recv_sem=first_recvs.at[k], device_id=peer, device_id_type=MESH,
        )

    def share(k):
        return pltpu.make_async_remote_copy(
            src_ref=slice_own, dst_ref=spread.at[:, lanes_of(me)], send_sem=spread_sends.at[k],
            recv_sem=spread_recvs.at[k], device_id=first_peers[k], device_id_type=MESH,
        )

    def second(k):
        return pltpu.make_async_remote_copy(
            src_ref=second_own, dst_ref=second_box.at[k], send_sem=second_sends.at[k],
            recv_sem=second_recvs.at[k], device_id=second_peers[k], device_id_type=MESH,
        )

    every = range(len(grads))
    for fill in fills:
        fill.wait()
    sums.first(every)
    for k in range(count - 1):
        first(k).start()
    def partial(first, second, step):
        for way, start in ((0, first), (1, second)):
            box_copy(way, start, step % 2).wait()

        @pl.when(step + 1 < count)
        def _():
            fetch(step + 1)

        return jnp.concatenate([boxes[step % 2, 0], boxes[step % 2, 1]], 0).astype(F32)

    def finish(start, size, grad):
        value = tokens[start : start + size, :].astype(F32)
        scale = lax.rsqrt(jnp.mean(value * value, axis=1, keepdims=True) + 1e-6)
        through, pieces = norm_back(value, scale, gain[...].astype(F32).reshape(1, -1), grad)
        grad_tokens[start : start + size, :] = grad_resid[start : start + size, :] + through

    def early():
        sums.second(every)
        for k in range(count - 1):
            first(k).wait()
        mine = small[0:8, lanes_of(me)]
        for k in range(count - 1):
            mine = mine + first_box[k]
        slice_own[...] = mine
        spread[:, lanes_of(me)] = mine
        for k in range(count - 1):
            share(k).start()

    def soon():
        for k in range(count - 1):
            share(k).wait()
        second_own[0:8] = spread[...]
        second_own[8:] = small[8:]
        for k in range(groups - 1):
            second(k).start()

    def late():
        for k in range(groups - 1):
            second(k).wait()
        mine = second_own[...]
        for k in range(groups - 1):
            mine = mine + second_box[k]
        total[...] = mine
        for load in loads:
            load.wait()

    def beside(step):
        pl.when(step == 0)(early)
        pl.when(step == 1)(soon)
        for i in every:
            pl.when(step == count - 1 - len(every) + i)(lambda i=i: sums.third((i,)))
        pl.when(step == count - 2)(late)

    ring_scatter(Scatter(ring, partial, slots, sends, recvs, rows, finish), beside)
    sums.last()


def last_step(terms, tokens, grad_resid, gain, small, grads, count, groups):
    rows, model = tokens.shape
    return pl.pallas_call(
        functools.partial(last_kernel, count, groups, rows),
        name="last_step",
        out_shape=[jax.ShapeDtypeStruct((rows, model), F32), jax.ShapeDtypeStruct(small.shape, F32)]
        + [jax.ShapeDtypeStruct(g.shape, BF16) for g in grads],
        in_specs=[ANY] * 3 + [VMEM] * 2 + [ANY] * len(grads),
        out_specs=[VMEM, VMEM] + [ANY] * len(grads),
        scratch_shapes=[
            ring_slots(count, rows, model),
            pltpu.VMEM((count - 1, 8, model // count), F32),
            pltpu.VMEM((8, model // count), F32),
            pltpu.VMEM((8, model), F32),
            pltpu.VMEM((groups - 1,) + small.shape, F32),
            pltpu.VMEM(small.shape, F32),
            pltpu.VMEM((2, 2, rows // 2, model), BF16),
            pltpu.SemaphoreType.DMA((2, 2)),
            pltpu.VMEM((rows, model), BF16),
            pltpu.VMEM((rows, model), F32),
            pltpu.SemaphoreType.DMA((2,)),
        ]
        + ring_semaphores(count)
        + [pltpu.SemaphoreType.DMA((count - 1,))] * 4
        + [pltpu.SemaphoreType.DMA((groups - 1,))] * 2
        + sum_scratch([g.shape for g in grads], groups)
        + [pltpu.VMEM(g.shape, BF16) for g in grads]
        + [pltpu.SemaphoreType.DMA((len(grads),))],
        compiler_params=ring_params(4),
        cost_estimate=pl.CostEstimate(flops=0, bytes_accessed=300 << 20, transcendentals=0),
    )(terms, tokens, grad_resid, gain, small, *grads)


def results_kernel(heads, taps, wide, width, total, *refs):
    number = (len(refs) - 7) // 2
    for source, target in zip(refs[:number], refs[number : 2 * number]):
        target[...] = source[...].astype(target.dtype)
    g_first, g_second, g_head, gt_query, gt_key, gt_value, g_beta = refs[2 * number :]

    @pl.when(pl.program_id(0) == 0)
    def _():
        g_first[...] = total[0:1, :]
        g_second[...] = total[1:2, :]
        g_head[...] = total[2:3, 0:width]
        row = 8 + heads
        for place, target in enumerate((gt_query, gt_key, gt_value)):
            target[...] = total[row : row + taps, place * wide : (place + 1) * wide]
        g_beta[...] = total[8 : 8 + heads, :]


def results(total, arrays, heads, taps, wide, width):
    model = total.shape[1]
    steps = next(n for n in (2, 1) if all(a.shape[0] % (8 * n) == 0 for a, _ in arrays))
    small = [(1, model), (1, model), (1, width)] + [(taps, wide)] * 3 + [(heads, model)]
    piece = lambda a: pl.BlockSpec((a.shape[0] // steps, a.shape[1]), lambda n: (n, 0))
    whole = lambda shape: pl.BlockSpec(shape, lambda n: (0, 0))
    return pl.pallas_call(
        functools.partial(results_kernel, heads, taps, wide, width),
        name="results",
        grid=(steps,),
        out_shape=[jax.ShapeDtypeStruct(a.shape, kind) for a, kind in arrays]
        + [jax.ShapeDtypeStruct(shape, F32) for shape in small],
        in_specs=[whole(total.shape)] + [piece(a) for a, _ in arrays],
        out_specs=[piece(a) for a, _ in arrays] + [whole(shape) for shape in small],
        compiler_params=pltpu.CompilerParams(vmem_limit_bytes=56 << 20),
        cost_estimate=pl.CostEstimate(flops=0, bytes_accessed=48 << 20, transcendentals=0),
    )(total, *[a for a, _ in arrays])


def spread_hops(step, chunks, count, hop, start=0):
    each = -(-(count - 1) // (chunks - 1))
    for place in range(each):
        number = step * each + place

        @pl.when((number >= start) & (number < count - 1))
        def _():
            hop(number)


def plan_hops(chunks, hops, latency=0.8, segment=2.5):
    now, link, due, done, table = 0.0, 0.0, {}, {}, []

    def send(chunk):
        nonlocal link
        link = max(now, link) + 1.0
        done[chunk] = done.get(chunk, -1) + 1
        due[chunk] = link + latency

    for step in range(chunks):
        for half in range(2):
            ready, moves = True, []
            while ready:
                ready = sorted((due[c], c) for c in due if due[c] <= now and done[c] < hops - 1)
                if ready:
                    send(ready[0][1])
                    moves.append((ready[0][1], done[ready[0][1]]))
            table.append(moves)
            now += segment
        send(step)
    return table, [done[chunk] for chunk in range(chunks)]


def forward_kernel(
    heads, width, seqs, count, groups, chunks,
    starts, lengths, tokens, w_query_in, w_key_in, w_value_in, w_gate_in, w_beta,
    taps_query, taps_key, taps_value, gain, gain_first, w_out,
    mixed_full, w_full, mixed, p_query, p_key, p_value, p_gate, p_beta, z_query, z_key, z_value,
    delta_out, change_out, inverse_out, state_out,
    tail_query, tail_key, tail_value, state, stage, sends, recvs, keeps,
    w_sends, w_recvs, w_keep, w_far, w_near, w_query, w_key, w_value, w_gate, load_sems,
):
    step = pl.program_id(0)
    size = tokens.shape[0]
    first = step * size

    @pl.when(step == 0)
    def _():
        for tail in (tail_query, tail_key, tail_value):
            tail[...] = jnp.zeros_like(tail)
        state[...] = jnp.zeros_like(state)

    ring = Ring(count)

    def chunk_gather(chunk):
        return Gather(
            ring,
            lambda start, length: stage.at[chunk, pl.ds(start, length), :],
            lambda origin, start, length: mixed_full.at[
                origin, pl.ds(pl.multiple_of(chunk * size + start, length), length), :
            ],
            sends.at[chunk], recvs.at[chunk], size, 1,
        )

    def keep(chunk):
        return pltpu.make_async_copy(
            stage.at[chunk],
            mixed_full.at[ring.me, pl.ds(pl.multiple_of(chunk * size, size), size), :],
            keeps.at[chunk],
        )

    weight = WholeWeight(ring, groups, w_out, w_full, w_sends, w_recvs, w_keep, w_far, w_near)
    each = -(-(count - 1) // (chunks - 1))

    def weight_hops(late=0):
        for place in range(each):
            number = (2 * step + late) * each + place
            pl.when((number > 0) & (number < count - 1))(lambda: weight.hop(number))
            pl.when(number == count - 1)(weight.exchange)

    table, done = plan_hops(chunks, count - 1)

    def chunk_hops(half):
        for place, moves in enumerate(table[half::2]):
            if moves:
                @pl.when(step == place)
                def _():
                    for chunk, hop in moves:
                        chunk_gather(chunk).hop(hop)

    @pl.when(step == 0)
    def _():
        loads = [
            pltpu.make_async_copy(source, target, load_sems.at[k])
            for k, (source, target) in enumerate(
                ((w_query_in, w_query), (w_key_in, w_key), (w_value_in, w_value), (w_gate_in, w_gate))
            )
        ]
        for load in loads:
            load.start()
        greet(ring, weight.peers())
        weight.begin()
        for load in loads:
            load.wait()

    weight_hops()
    chunk_hops(0)
    rows, seg_rows, seg_columns, before, last = chunk_masks(starts, lengths, seqs, first, size)
    same = seg_rows == seg_columns
    i = lax.broadcasted_iota(jnp.int32, (size, size), 0)
    j = lax.broadcasted_iota(jnp.int32, (size, size), 1)
    strict = jnp.where(same & (i > j), 1.0, 0.0)
    inclusive = jnp.where(same & (i >= j), 1.0, 0.0)
    carried = jnp.where(seg_rows == before, 1.0, 0.0)
    ending = jnp.where(seg_rows == last, 1.0, 0.0)
    kept = jnp.where(before == last, 1.0, 0.0)
    live = jnp.where(seg_rows % 2 == 1, 1.0, 0.0)
    joined = [
        jnp.where(segment_at(rows - offset, starts, lengths, seqs) == seg_rows, 1.0, 0.0)
        for offset in range(1, taps_query.shape[0])
    ]
    inputs = normed_rows(tokens, gain_first)[0].astype(BF16)

    def feature(weight, taps, tail, p_out, z_out):
        projected = jnp.dot(inputs, weight[...], preferred_element_type=F32)
        p_out[...] = projected
        tail[8:, :] = projected
        tap = taps[...].astype(F32)
        result = projected * tap[0:1]
        for offset in range(1, tap.shape[0]):
            result = result + tail[8 - offset : 8 - offset + size, :] * tap[offset : offset + 1] * joined[offset - 1]
        tail[0:8, :] = projected[size - 8 :, :]
        z_out[...] = result
        return result * sigmoid(result)

    u_query = feature(w_query, taps_query, tail_query, p_query, z_query)
    u_key = feature(w_key, taps_key, tail_key, p_key, z_key)
    u_value = feature(w_value, taps_value, tail_value, p_value, z_value)
    gate = jnp.dot(inputs, w_gate[...], preferred_element_type=F32)
    p_gate[...] = gate
    beta_pre = mm(inputs, w_beta[...], (1, 1))
    p_beta[...] = beta_pre
    strength = sigmoid(beta_pre)
    opened = gate * sigmoid(gate)
    scale = width ** (-0.5)
    head_gain = gain[...].astype(F32)
    for h in range(heads):
        if h == heads // 2:
            weight_hops(1)
            chunk_hops(1)
        cols = slice(h * width, (h + 1) * width)
        uq, uk = u_query[:, cols], u_key[:, cols]
        query = (uq * lax.rsqrt(jnp.sum(uq * uq, axis=1, keepdims=True) + 1e-6)).astype(BF16)
        key = (uk * lax.rsqrt(jnp.sum(uk * uk, axis=1, keepdims=True) + 1e-6)).astype(BF16)
        value = u_value[:, cols].astype(BF16).astype(F32)
        beta = strength[:, h : h + 1]
        memory = state[h]
        low_memory = memory.astype(BF16)
        state_out[0, h] = low_memory
        lower = mm(key, key, (1, 1)) * strict * beta
        inverse = inverse_unit_lower(lower, size).astype(BF16)
        inverse_out[0, h] = inverse
        within = mm(query, key, (1, 1)) * inclusive
        change = mm(inverse, beta * (value - carried * mm(key, low_memory)))
        low_change = change.astype(BF16)
        change_out[:, cols] = low_change
        out = scale * (carried * mm(query, low_memory) + mm(within, low_change))
        state[h] = kept * memory + mm(key, ending * change, (0, 0))
        delta_out[:, cols] = out
        normal = out * lax.rsqrt(jnp.mean(out * out, axis=1, keepdims=True) + 1e-5) * head_gain
        low_mixed = (normal * opened[:, cols] * live).astype(BF16)
        mixed[:, cols] = low_mixed
        stage[step, :, cols] = low_mixed

    chunk_gather(step).begin()
    keep(step).start()

    @pl.when(step == chunks - 1)
    def _():
        def finish(number, carry):
            pl.when(number == (count - 1) // 2)(weight.back)
            for chunk in range(chunks):
                if done[chunk] < count - 2:
                    pl.when(done[chunk] + number < count - 1)(
                        lambda chunk=chunk: chunk_gather(chunk).hop(done[chunk] + number)
                    )
            return carry

        lax.fori_loop(1, count - 1, finish, 0)

        def settle(chunk, carry):
            chunk_gather(chunk).arrived(count - 1)
            chunk_gather(chunk).end()
            keep(chunk).wait()
            return carry

        lax.fori_loop(0, chunks, settle, 0)
        weight.end()


def forward_mixer(tokens, w_query, w_key, w_value, w_gate, w_beta, taps_query, taps_key, taps_value, gain, gain_first, starts, lengths, w_out, count, groups):
    slots, model = tokens.shape
    wide = w_query.shape[1]
    width = gain.shape[0]
    heads = wide // width
    seqs = starts.shape[1]
    chunks = slots // CHUNK
    taps = taps_query.shape[0]
    part = w_out.shape[0] // groups
    smem = pl.BlockSpec(memory_space=pltpu.SMEM)
    whole = lambda shape: pl.BlockSpec(shape, lambda n: (0,) * len(shape))
    piece = lambda shape: pl.BlockSpec(shape, lambda n: (n,) + (0,) * (len(shape) - 1))
    outs = [
        ((slots, wide), BF16), ((slots, wide), F32), ((slots, wide), F32), ((slots, wide), F32), ((slots, wide), F32),
        ((slots, w_beta.shape[0]), F32), ((slots, wide), F32), ((slots, wide), F32), ((slots, wide), F32),
        ((slots, wide), F32), ((slots, wide), BF16),
    ]
    return pl.pallas_call(
        functools.partial(forward_kernel, heads, width, seqs, count, groups, chunks),
        name="mixer_forward",
        grid=(chunks,),
        out_shape=[
            jax.ShapeDtypeStruct((count, slots, wide), BF16),
            jax.ShapeDtypeStruct((count, groups, part, model), BF16),
        ]
        + [jax.ShapeDtypeStruct(s, d) for s, d in outs]
        + [
            jax.ShapeDtypeStruct((chunks, heads, CHUNK, CHUNK), BF16),
            jax.ShapeDtypeStruct((chunks, heads, width, width), BF16),
        ],
        in_specs=[smem, smem, piece((CHUNK, model))]
        + [ANY] * 4
        + [whole(w_beta.shape)]
        + [whole((taps, wide))] * 3
        + [whole((1, width)), VMEM, ANY],
        out_specs=[ANY, ANY]
        + [piece((CHUNK, s[1])) for s, d in outs]
        + [piece((1, heads, CHUNK, CHUNK)), piece((1, heads, width, width))],
        scratch_shapes=[pltpu.VMEM((CHUNK + 8, wide), F32)] * 3
        + [pltpu.VMEM((heads, width, width), F32), pltpu.VMEM((chunks, CHUNK, wide), BF16)]
        + [pltpu.SemaphoreType.DMA((chunks, 2, 1, count - 1))] * 2
        + [pltpu.SemaphoreType.DMA((chunks,))]
        + ring_semaphores(count, 1)
        + [
            pltpu.SemaphoreType.DMA,
            pltpu.SemaphoreType.DMA((2, groups // 2 - 1, 2, count)),
            pltpu.SemaphoreType.DMA((2, groups // 2)),
        ]
        + [pltpu.VMEM((model, wide), BF16)] * 4
        + [pltpu.SemaphoreType.DMA((4,))],
        compiler_params=ring_params(5),
        cost_estimate=pl.CostEstimate(
            flops=2 * slots * model * wide * 4 + slots * heads * CHUNK * 2 * CHUNK * 20,
            bytes_accessed=slots * model * 2 + 4 * model * wide * 2 + slots * wide * 36,
            transcendentals=slots * wide * 4,
        ),
    )(starts, lengths, tokens, w_query, w_key, w_value, w_gate, w_beta, taps_query, taps_key, taps_value, gain.reshape(1, width), gain_first, w_out)


def small_rows(heads, taps):
    return -(-(8 + heads + taps) // 8) * 8


def backward_kernel(
    heads, width, seqs, chunks, count, rows_own,
    starts, lengths, tokens, grad_attended, mixed, p_query, p_key, p_value, p_gate, p_beta,
    z_query, z_key, z_value, delta_out, change_in, inverse_in, state_in,
    w_query_in, w_key_in, w_value_in, w_gate_in, w_beta, w_out_in, taps_query, taps_key, taps_value, gain, gain_first,
    hidden_in, w_down_in, resid_in, g_second, grad_normed, gw_query, gw_key, gw_value, gw_gate, gw_out,
    small, output,
    a_query, a_key, a_value, a_gate, a_out, head_query, head_key, head_value, flow,
    w_query, w_key, w_value, w_gate, resid, w_out, hidden, w_down, load_sems, slots, sends, recvs,
):
    step = pl.program_id(0)
    size = tokens.shape[0]
    first = (chunks - 1 - step) * size

    @pl.when(step == 0)
    def _():
        for ref in (a_query, a_key, a_value, a_gate, a_out, small, flow):
            ref[...] = jnp.zeros_like(ref)
        small[1:2, :] = g_second[...]
        for ref in (head_query, head_key, head_value):
            ref[size:, :] = jnp.zeros((8, ref.shape[1]), F32)

    half = rows_own // 2

    def partial(one, two, number):
        return mm(jnp.concatenate([hidden[pl.ds(one, half), :], hidden[pl.ds(two, half), :]], 0), w_down[...])

    def finish(start, length, down):
        output[start : start + length, :] = (resid[start : start + length, :] + down).astype(BF16)

    ring = Ring(count)
    scatter = Scatter(ring, partial, slots, sends, recvs, rows_own, finish)
    loads = [
        pltpu.make_async_copy(source, target, load_sems.at[k])
        for k, (source, target) in enumerate(
            ((w_query_in, w_query), (w_key_in, w_key), (w_value_in, w_value), (w_gate_in, w_gate), (resid_in, resid),
             (w_out_in, w_out), (hidden_in, hidden), (w_down_in, w_down))
        )
    ]

    @pl.when(step == 0)
    def _():
        for load in reversed(loads):
            load.start()
        greet(ring)
        for load in loads[6:]:
            load.wait()

    spread_hops(step, chunks, count, scatter.hop)

    @pl.when(step == 0)
    def _():
        loads[5].wait()

    rows, seg_rows, seg_columns, before, last = chunk_masks(starts, lengths, seqs, first, size)
    same = seg_rows == seg_columns
    i = lax.broadcasted_iota(jnp.int32, (size, size), 0)
    j = lax.broadcasted_iota(jnp.int32, (size, size), 1)
    strict = jnp.where(same & (i > j), 1.0, 0.0)
    inclusive = jnp.where(same & (i >= j), 1.0, 0.0)
    carried = jnp.where(seg_rows == before, 1.0, 0.0)
    ending = jnp.where(seg_rows == last, 1.0, 0.0)
    kept = jnp.where(before == last, 1.0, 0.0)
    live = jnp.where(seg_rows % 2 == 1, 1.0, 0.0)
    taps = taps_query.shape[0]
    joined = [
        jnp.where(segment_at(rows + offset, starts, lengths, seqs) == seg_rows, 1.0, 0.0)
        for offset in range(1, taps)
    ]
    normal_rows, unit_rows = normed_rows(tokens, gain_first)
    inputs = normal_rows.astype(BF16)
    grad_rows = grad_attended[...]
    grad_mixed = mm(grad_rows, w_out[...], (1, 1))
    a_out[...] += mm(mixed[...], grad_rows, (0, 0))
    strength = sigmoid(p_beta[...])
    scale = width ** (-0.5)
    head_gain = gain[...].astype(F32)

    grads_query, grads_key, grads_value, grads_gate, grads_beta = [], [], [], [], []
    for h in range(heads):
        cols = slice(h * width, (h + 1) * width)
        out = delta_out[:, cols]
        gate = p_gate[:, cols]
        sig_gate = sigmoid(gate)
        silu_gate = gate * sig_gate
        root = lax.rsqrt(jnp.mean(out * out, axis=1, keepdims=True) + 1e-5)
        grad = grad_mixed[:, cols] * live
        unit = out * root
        grads_gate.append(grad * unit * head_gain * (sig_gate * (1.0 + gate * (1.0 - sig_gate))))
        grad_normal = grad * silu_gate
        small[2:3, 0:width] += jnp.sum(grad_normal * unit, axis=0, keepdims=True)
        push = grad_normal * head_gain
        grad_out = scale * root * (push - unit * jnp.mean(push * unit, axis=1, keepdims=True))

        zq, zk, zv = z_query[:, cols], z_key[:, cols], z_value[:, cols]
        sq, sk, sv = sigmoid(zq), sigmoid(zk), sigmoid(zv)
        uq, uk = zq * sq, zk * sk
        nq = lax.rsqrt(jnp.sum(uq * uq, axis=1, keepdims=True) + 1e-6)
        nk = lax.rsqrt(jnp.sum(uk * uk, axis=1, keepdims=True) + 1e-6)
        unit_q, unit_k = uq * nq, uk * nk
        query, key = unit_q.astype(BF16), unit_k.astype(BF16)
        beta = strength[:, h : h + 1]
        change = change_in[:, cols]
        inverse = inverse_in[0, h]
        memory = state_in[0, h]
        flowing = flow[h]
        low_flow = flowing.astype(BF16)
        low_out = grad_out.astype(BF16)

        within = mm(query, key, (1, 1)) * inclusive
        grad_within = (mm(low_out, change, (1, 1)) * inclusive).astype(BF16)
        grad_change = mm(within, low_out, (0, 0)) + ending * mm(key, low_flow)
        grad_mid = mm(inverse, grad_change, (0, 0))
        grad_value = beta * grad_mid
        low_value = grad_value.astype(BF16)
        cross = (mm(low_value, change, (1, 1)) * strict).astype(BF16)
        grad_query = carried * mm(low_out, memory, (1, 1)) + mm(grad_within, key)
        grad_key = (
            mm(grad_within, query, (0, 0))
            + ending * mm(change, low_flow, (1, 1))
            - carried * mm(low_value, memory, (1, 1))
            - mm(cross, key)
            - mm(cross, key, (0, 0))
        )
        flow[h] = (
            kept * flowing
            + mm(query, carried * grad_out, (0, 0))
            - mm(key, carried * grad_value, (0, 0))
        )
        grads_beta.append((1.0 - beta) * jnp.sum(grad_mid * change.astype(F32), axis=1, keepdims=True))
        du_q = nq * (grad_query - unit_q * jnp.sum(grad_query * unit_q, axis=1, keepdims=True))
        du_k = nk * (grad_key - unit_k * jnp.sum(grad_key * unit_k, axis=1, keepdims=True))
        grads_query.append(du_q * sq * (1.0 + zq * (1.0 - sq)))
        grads_key.append(du_k * sk * (1.0 + zk * (1.0 - sk)))
        grads_value.append(grad_value * sv * (1.0 + zv * (1.0 - sv)))

    tap_row = 8 + heads
    wide = heads * width

    def unconv(parts, taps_ref, head, projected, place):
        lanes = slice(place * wide, (place + 1) * wide)
        grad = jnp.concatenate(parts, axis=1)
        head[0:size, :] = grad
        tap = taps_ref[...].astype(F32)
        p = projected[...]
        result = grad * tap[0:1]
        small[tap_row : tap_row + 1, lanes] += jnp.sum(p * grad, axis=0, keepdims=True)
        for offset in range(1, taps):
            moved = head[offset : offset + size, :] * joined[offset - 1]
            result = result + moved * tap[offset : offset + 1]
            row = tap_row + offset
            small[row : row + 1, lanes] += jnp.sum(p * moved, axis=0, keepdims=True)
        head[size:, :] = grad[0:8, :]
        return result.astype(BF16)

    d_query = unconv(grads_query, taps_query, head_query, p_query, 0)
    d_key = unconv(grads_key, taps_key, head_key, p_key, 1)
    d_value = unconv(grads_value, taps_value, head_value, p_value, 2)
    d_gate = jnp.concatenate(grads_gate, axis=1).astype(BF16)
    spare = [jnp.zeros((size, 1), F32)] * (w_beta.shape[0] - heads)
    d_beta = jnp.concatenate(grads_beta + spare, axis=1).astype(BF16)

    @pl.when(step == 0)
    def _():
        for load in loads[:5]:
            load.wait()

    grad_inputs = (
        mm(d_query, w_query[...], (1, 1))
        + mm(d_key, w_key[...], (1, 1))
        + mm(d_value, w_value[...], (1, 1))
        + mm(d_gate, w_gate[...], (1, 1))
        + mm(d_beta, w_beta[...])
    )
    grad_normed[...] = grad_inputs.astype(BF16)
    small[0:1, :] += jnp.sum(grad_inputs * unit_rows, axis=0, keepdims=True)
    a_query[...] += mm(inputs, d_query, (0, 0))
    a_key[...] += mm(inputs, d_key, (0, 0))
    a_value[...] += mm(inputs, d_value, (0, 0))
    a_gate[...] += mm(inputs, d_gate, (0, 0))
    small[8 : 8 + heads, :] += mm(d_beta, inputs, (0, 0))[:heads]

    @pl.when(step == chunks - 1)
    def _():
        for target, source in (
            (gw_query, a_query), (gw_key, a_key), (gw_value, a_value), (gw_gate, a_gate),
            (gw_out, a_out),
        ):
            target[...] = source[...].astype(target.dtype)
        scatter.end()


def backward_mixer(tokens, grad_attended, saved, w_query, w_key, w_value, w_gate, w_beta, w_out, taps_query, taps_key, taps_value, gain, gain_first, starts, lengths, hidden, w_down, resid, g_second, count):
    slots, model = tokens.shape
    wide = w_query.shape[1]
    width = gain.shape[0]
    heads = wide // width
    seqs = starts.shape[1]
    chunks = slots // CHUNK
    taps = taps_query.shape[0]
    smem = pl.BlockSpec(memory_space=pltpu.SMEM)
    fixed = lambda shape: pl.BlockSpec(shape, lambda n: (0,) * len(shape), pipeline_mode=pl.Buffered(1))
    piece = lambda shape: pl.BlockSpec(shape, lambda n: (chunks - 1 - n,) + (0,) * (len(shape) - 1))
    rows = lambda a: piece((CHUNK, a.shape[1]))
    outs = (
        [((slots, model), BF16)] + [((model, wide), BF16)] * 4 + [((wide, model), BF16)]
        + [((small_rows(heads, taps), model), F32), (resid.shape, BF16)]
    )
    return pl.pallas_call(
        functools.partial(backward_kernel, heads, width, seqs, chunks, count, slots // count),
        name="mixer_backward",
        grid=(chunks,),
        out_shape=[jax.ShapeDtypeStruct(s, d) for s, d in outs],
        in_specs=[smem, smem, rows(tokens), rows(grad_attended)]
        + [rows(a) for a in saved[:11]]
        + [piece((1, heads, CHUNK, CHUNK)), piece((1, heads, width, width))]
        + [ANY] * 4
        + [fixed(w_beta.shape), ANY]
        + [fixed((taps, wide))] * 3
        + [fixed((1, width)), VMEM, ANY, ANY, ANY, fixed(g_second.shape)],
        out_specs=[piece((CHUNK, model))] + [fixed(s) for s, d in outs[1:]],
        scratch_shapes=[pltpu.VMEM((model, wide), F32)] * 4
        + [pltpu.VMEM((wide, model), F32)]
        + [pltpu.VMEM((CHUNK + 8, wide), F32)] * 3
        + [pltpu.VMEM((heads, width, width), F32)]
        + [pltpu.VMEM((model, wide), BF16)] * 4
        + [pltpu.VMEM(resid.shape, F32)]
        + [pltpu.VMEM(a.shape, BF16) for a in (w_out, hidden, w_down)]
        + [pltpu.SemaphoreType.DMA((8,)), ring_slots(count, slots // count, model)]
        + ring_semaphores(count),
        compiler_params=ring_params(6),
        cost_estimate=pl.CostEstimate(
            flops=2 * slots * model * wide * 10 + slots * heads * CHUNK * 2 * CHUNK * 8,
            bytes_accessed=slots * model * 6 + 10 * model * wide * 2 + slots * wide * 36,
            transcendentals=slots * wide * 8,
        ),
    )(starts, lengths, tokens, grad_attended, *saved, w_query, w_key, w_value, w_gate, w_beta, w_out, taps_query, taps_key, taps_value, gain.reshape(1, width), gain_first, hidden, w_down, resid, g_second)


def make_shards(groups, count):
    def shards(
        tokens, attn_gain, w_query, w_key, w_value, conv_query, conv_key, conv_value, w_beta, w_gate_out,
        head_gain, w_out, ffn_gain, w_gate, w_up, w_down, seq_starts, seq_lengths, cotangent,
    ):
        model = tokens.shape[1]
        heads = w_beta.shape[1]
        beta_rows = w_beta.T if heads > 1 else jnp.pad(w_beta.T, ((0, 1), (0, 0)))
        tokens_full = gather_tokens(tokens, count)
        mixed_full, w_out_full, *saved = forward_mixer(
            tokens_full, w_query, w_key, w_value, w_gate_out, beta_rows,
            conv_query, conv_key, conv_value, head_gain, attn_gain, seq_starts, seq_lengths, w_out, count, groups,
        )
        w_out_full = w_out_full.reshape(-1, tokens.shape[1])
        resid, ffn_full, hidden, grad_gate, grad_up, grad_full = attend(
            mixed_full, w_out_full, tokens_full, ffn_gain, w_gate.T, w_up.T, w_down, cotangent, count
        )
        grad_resid, grad_attended, g_second, *ffn_grads = ffn_back(
            grad_gate, grad_up, hidden, w_gate.T, w_up.T, resid, cotangent, ffn_gain, ffn_full, grad_full,
            count, groups,
        )
        pulled = backward_mixer(
            tokens_full, grad_attended, saved, w_query, w_key, w_value, w_gate_out, beta_rows, w_out,
            conv_query, conv_key, conv_value, head_gain, attn_gain, seq_starts, seq_lengths,
            hidden, w_down, resid, g_second, count,
        )
        terms, gw_query, gw_key, gw_value, gw_gate_out, gw_out, small, output = pulled
        grad_tokens, total, *mixer_grads = last_step(
            terms, tokens, grad_resid, attn_gain, small,
            (gw_query, gw_key, gw_value, gw_gate_out, gw_out), count, groups,
        )
        taps, wide = conv_query.shape
        output, grad_tokens, *rest = results(
            total,
            [(output, BF16), (grad_tokens, F32)] + [(g, F32) for g in (*mixer_grads, *ffn_grads)],
            heads, taps, wide, head_gain.shape[0],
        )
        grads, (g_first, g_second, g_head, gt_query, gt_key, gt_value, g_beta) = rest[:8], rest[8:]
        return (
            output,
            grad_tokens,
            g_first[0],
            grads[0],
            grads[1],
            grads[2],
            gt_query,
            gt_key,
            gt_value,
            g_beta.T,
            grads[3],
            g_head[0],
            grads[4],
            g_second[0],
            grads[5].T,
            grads[6].T,
            grads[7],
        )

    return shards


def solution(mesh):
    placed = (
        P(("dp", "tensor"), None),
        P(),
        P(None, "tensor"),
        P(None, "tensor"),
        P(None, "tensor"),
        P(None, "tensor"),
        P(None, "tensor"),
        P(None, "tensor"),
        P(None, "tensor"),
        P(None, "tensor"),
        P(),
        P("tensor", None),
        P(),
        P(None, "tensor"),
        P(None, "tensor"),
        P("tensor", None),
        P("dp", None),
        P("dp", None),
        P(("dp", "tensor"), None),
    )
    return jax.shard_map(
        make_shards(mesh.shape["dp"], mesh.shape["tensor"]),
        mesh=mesh,
        in_specs=placed,
        out_specs=(
            P(("dp", "tensor"), None),
            P(("dp", "tensor"), None),
            P(),
            P(None, "tensor"),
            P(None, "tensor"),
            P(None, "tensor"),
            P(None, "tensor"),
            P(None, "tensor"),
            P(None, "tensor"),
            P(None, "tensor"),
            P(None, "tensor"),
            P(),
            P("tensor", None),
            P(),
            P(None, "tensor"),
            P(None, "tensor"),
            P("tensor", None),
        ),
        check_vma=False,
    )
```
